32 devices in a mesh: batch: 8 (over z, x), tok: 4 (over y, core).
Axes of the slice: x: 2, y: 2, z: 4, core: 2. Of those that a mesh axis runs over, the one named last changes fastest.
Arguments:
- patches: bfloat16 [24, 1024, 768], P('batch', 'tok'), may hold values from -6 to 6
- image_ids: int32 [24, 1024], P('batch', 'tok'), may hold values from -1 to 3, as said below
- cotangent: bfloat16 [24, 1024, 768], P('batch', 'tok'), may hold values from -6 to 6
- norm_gain: float32 [768], replicated, may hold values from 0.25 to 1.75
- query_gain: float32 [64], replicated, may hold values from 0.25 to 1.75
- key_gain: float32 [64], replicated, may hold values from 0.25 to 1.75
- in_weight: bfloat16 [768, 5376], P(('batch', 'tok')), may hold values from -0.21875 to 0.21875
- out_weight: bfloat16 [3840, 768], P(('batch', 'tok')), may hold values from -0.6538492 to 0.6538492
Outputs:
- block_out: bfloat16 [24, 1024, 768], P('batch', 'tok')
- patch_grad: bfloat16 [24, 1024, 768], P('batch', 'tok')
- norm_grad: float32 [768], replicated
- query_grad: float32 [64], replicated
- key_grad: float32 [64], replicated
- in_grad: float32 [768, 5376], P(('batch', 'tok'))
- out_grad: float32 [3840, 768], P(('batch', 'tok'))
The draws below stay inside these ranges and needn't reach their ends.
Inputs may be any that keep to these rules, and one draw needn't show every extreme that they name: `image_ids`: in each sequence the ids of the live tokens run 0, 1, 2, 3 in contiguous non-decreasing runs (a run may be empty; the last image is never empty), followed by at least one padding slot of -1 at the end of the sequence.
All inputs are finite; a program needn't handle non-finite values.
Results may differ from the reference program's by a relative error of at most 0.0097.
Values may be sent and summed in bfloat16 or wider, within the bound.
No kernel may reach another device: no remote copies, remote signals or barrier semaphores. Data moves between devices by JAX's collectives and lax.ppermute only.
A program may use at most 192 MiB of HBM per device.

```python
import math
import jax
import jax.numpy as jnp
from jax import lax

D = 768
H = 12
HD = 64
FF = 3072
LEN = 1024
NSEQ = 24


def draw_image_ids(key, part):
    cut_key = jax.random.fold_in(key, 11)
    pad_key = jax.random.fold_in(key, 12)
    cut_points = jax.random.randint(cut_key, (NSEQ, 3), 1, LEN * 3 // 4)
    pad_lengths = jax.random.randint(pad_key, (NSEQ, 1), 1, LEN // 4 + 1)
    positions = jnp.arange(LEN, dtype=jnp.int32)[None, :]
    labels = jnp.sum((positions[:, :, None] >= cut_points[:, None, :]).astype(jnp.int32), axis=-1)
    return jnp.where(positions < LEN - pad_lengths, labels, -1).astype(jnp.int32)


def draw_out_weight(key, part):
    row_index = jnp.arange(D + FF)[:, None]
    row_scale = jnp.where(row_index < D, 6.0 / math.sqrt(D), 1.0 / math.sqrt(FF)).astype(jnp.float32)
    base = jnp.clip(jax.random.normal(key, (D + FF, D), jnp.float32), -3.0, 3.0)
    return (base * row_scale).astype(jnp.bfloat16)


def block_levels(key, dims, pieces, least, largest):
    def one(position, blocks):
        draws = jax.random.uniform(jax.random.fold_in(jax.random.fold_in(key, 6), position), (blocks,), jnp.float32, least / len(pieces), largest / len(pieces))
        return jnp.repeat(jnp.exp(draws), dims[position] // blocks).reshape((-1,) + (1,) * (len(dims) - position - 1))

    gain = one(*pieces[0])
    for cut in pieces[1:]:
        gain = gain * one(*cut)
    return gain


def noise(stream_key, extent, scale, bound, shards=(), kind=jnp.bfloat16):
    gain = block_levels(stream_key, extent, shards, -0.22, 0.18) if shards else 1.0
    drawn = jax.random.normal(stream_key, extent, jnp.float32) * scale * gain
    return jnp.minimum(jnp.maximum(drawn, -bound), bound).astype(kind)


def setup_inputs(seed: int = 0) -> dict:
    keys = jax.random.split(jax.random.key(seed), 9)
    patches = noise(keys[0], (NSEQ, LEN, D), 1.0, 6.0, ((0, 8), (1, 4)))
    image_ids = draw_image_ids(jax.random.fold_in(keys[8], 71), 0)
    cotangent = noise(keys[2], (NSEQ, LEN, D), 1.0, 6.0, ((0, 8), (1, 4)))
    norm_gain = jnp.clip(1.0 + 0.15 * jax.random.normal(keys[3], (D,), jnp.float32), 0.25, 1.75)
    query_gain = jnp.clip(1.0 + 0.15 * jax.random.normal(keys[4], (HD,), jnp.float32), 0.25, 1.75)
    key_gain = jnp.clip(1.0 + 0.15 * jax.random.normal(keys[5], (HD,), jnp.float32), 0.25, 1.75)
    in_weight = noise(keys[6], (D, 3 * D + FF), D ** -0.5, 0.21875, ((0, 32),))
    out_weight = draw_out_weight(jax.random.fold_in(keys[8], 71), 0)
    return dict(patches=patches, image_ids=image_ids, cotangent=cotangent, norm_gain=norm_gain, query_gain=query_gain, key_gain=key_gain, in_weight=in_weight, out_weight=out_weight)


highest = lax.Precision.HIGHEST
mask_fill = -1000000000.0

@jax.custom_vjp
def low(v):
    return lax.optimization_barrier(v.astype(jnp.bfloat16)).astype(jnp.float32)

@jax.custom_vjp
def low_back(v):
    return v

def low_keep(v):
    return (low(v), None)

def low_pass(kept, grad):
    return (grad,)

def back_keep(v):
    return (v, None)

def back_low(kept, grad):
    return (low(grad),)
low.defvjp(low_keep, low_pass)
low_back.defvjp(back_keep, back_low)

def layer_norm(values, scales):
    center = values - lax.optimization_barrier(jnp.mean(values, axis=-1, keepdims=True))
    return center * lax.rsqrt(lax.optimization_barrier(jnp.mean(center * center, axis=-1, keepdims=True)) + 1e-06) * scales

def attend(inputs):
    queries, key_block, value_block, seq_ids = inputs
    score_scale = 1.0 / math.sqrt(queries.shape[-1])
    scores = jnp.einsum('qhd,khd->hqk', queries, key_block, precision=highest) * score_scale
    allowed = (seq_ids[:, None] == seq_ids[None, :]) & (seq_ids[:, None] >= 0)
    scores = low_back(jnp.where(allowed[None], scores, mask_fill))
    probabilities = low(jax.nn.softmax(scores, axis=-1))
    outputs = jnp.einsum('hqk,khd->qhd', probabilities, value_block, precision=highest)
    return low(low_back(outputs))

def forward(patch_rows, norm_gain, query_gain, key_gain, in_weight, out_weight, seq_ids):
    group_size, length, feature_width = patch_rows.shape
    live_rows = (seq_ids >= 0).astype(patch_rows.dtype)[..., None]
    normed = low(layer_norm(patch_rows, norm_gain))
    merged = low_back(jnp.einsum('gtd,de->gte', normed, in_weight, precision=highest))
    head_shape = (group_size, length, H, HD)
    queries = low(low_back(layer_norm(merged[..., :feature_width].reshape(head_shape), query_gain)))
    key_block = low(low_back(layer_norm(merged[..., feature_width:2 * feature_width].reshape(head_shape), key_gain)))
    value_block = low(low_back(merged[..., 2 * feature_width:3 * feature_width].reshape(head_shape)))
    hidden = low(jax.nn.gelu(merged[..., 3 * feature_width:]))
    heads = lax.map(jax.checkpoint(attend), (queries, key_block, value_block, seq_ids))
    combined = jnp.concatenate([heads.reshape(group_size, length, feature_width), hidden], axis=-1)
    branch = jnp.einsum('gtc,cd->gtd', combined, out_weight, precision=highest)
    return live_rows * (patch_rows + branch)

def reference(patches, image_ids, cotangent, norm_gain, query_gain, key_gain, in_weight, out_weight):
    group_size = math.gcd(NSEQ, max(1, 4096 // LEN))
    group_count = NSEQ // group_size
    params = (norm_gain.astype(jnp.float32), query_gain.astype(jnp.float32), key_gain.astype(jnp.float32), in_weight.astype(jnp.float32), out_weight.astype(jnp.float32))
    patch_groups = patches.astype(jnp.float32).reshape(group_count, group_size, LEN, D)
    id_groups = image_ids.reshape(group_count, group_size, LEN)
    cot_groups = cotangent.astype(jnp.float32).reshape(group_count, group_size, LEN, D)

    def one_group(totals, inputs):
        patch_part, id_part, cot_part = inputs

        def closed(patch_rows, *weights):
            return forward(patch_rows, *weights, id_part)
        result, pull = jax.vjp(closed, patch_part, *params)
        grads = pull(cot_part)
        totals = tuple((running + fresh for running, fresh in zip(totals, grads[1:])))
        return (totals, (result.astype(jnp.bfloat16), grads[0].astype(jnp.bfloat16)))
    initial = tuple((jnp.zeros_like(weight_value) for weight_value in params))
    totals, (outputs, input_grads) = lax.scan(one_group, initial, (patch_groups, id_groups, cot_groups))
    return (outputs.reshape(NSEQ, LEN, D), input_grads.reshape(NSEQ, LEN, D), totals[0], totals[1], totals[2], totals[3], totals[4])
```

```python
import functools
import math

import jax
import jax.numpy as jnp
import numpy as np
from jax import lax
from jax.experimental import pallas as pl
from jax.experimental.pallas import tpu as pltpu
from jax.sharding import PartitionSpec as P

H = 12
HD = 64
EPS = 1e-06
BIG = 2048.0
LOG2E = 1.4426950408889634
BF = jnp.bfloat16
F32 = jnp.float32
NT = (((1,), (1,)), ((), ()))
TN = (((0,), (0,)), ((), ()))


def mm(a, b, dims=(((1,), (0,)), ((), ()))):
    return lax.dot_general(a, b, dims, preferred_element_type=F32)


def normalize(values):
    center = values - jnp.mean(values, axis=-1, keepdims=True)
    inverse = lax.rsqrt(jnp.mean(center * center, axis=-1, keepdims=True) + EPS)
    return center * inverse, inverse


def norm_back(grad_unit, unit_rows, inverse):
    return inverse * (
        grad_unit
        - jnp.mean(grad_unit, axis=-1, keepdims=True)
        - unit_rows * jnp.mean(grad_unit * unit_rows, axis=-1, keepdims=True)
    )


def attention_kernel(
    heads, block,
    normed_ref, gb_ref, wqkv_ref, wo_ref, idc_ref, idr_ref, qg_ref, kg_ref,
    o_ref, grad_ref, sums_ref,
    raw_ref, do_ref, e_ref, qa_ref, ka_ref, va_ref, ob_ref, dq_ref, dk_ref, dv_ref,
):
    length = normed_ref.shape[0]
    width = heads * HD
    raw_ref[...] = mm(normed_ref[...], wqkv_ref[...])
    do_ref[...] = mm(gb_ref[...], wo_ref[...], NT)
    idc = idc_ref[...]
    lanes = lax.broadcasted_iota(jnp.int32, (length, HD), 1)
    same = lanes == idc + 1
    k_tail = jnp.where(same, 1.0, 0.0).astype(BF)
    q_tail = jnp.where((same & (idc >= 0)) | (lanes > 4), 0.0, -BIG).astype(BF)
    v_tail = jnp.where(lanes < 3, 1.0, 0.0).astype(BF)
    pad = jnp.where(idc < 0, 1.0, 0.0)
    gain_q = qg_ref[...]
    gain_k = kg_ref[...]
    for h in range(heads):
        q_raw = raw_ref[:, h * HD : (h + 1) * HD]
        k_raw = raw_ref[:, width + h * HD : width + (h + 1) * HD]
        q_unit, q_inv = normalize(q_raw)
        k_unit, k_inv = normalize(k_raw)
        qa_ref[:, :HD] = (q_unit * gain_q).astype(BF)
        qa_ref[:, HD:] = q_tail
        ka_ref[:, :HD] = (k_unit * gain_k).astype(BF)
        ka_ref[:, HD:] = k_tail
        va = raw_ref[:, 2 * width + h * HD : 2 * width + (h + 1) * HD].astype(BF)
        va_ref[:, :HD] = va
        va_ref[:, HD:] = v_tail
        v_mean = jnp.mean(va.astype(F32), axis=0, keepdims=True)
        dk_ref[...] = jnp.zeros_like(dk_ref)
        dv_ref[...] = jnp.zeros_like(dv_ref)

        def step(i, carry):
            rows = pl.ds(pl.multiple_of(i * block, block), block)
            qb = qa_ref[rows, :]
            s = mm(qb, ka_ref[...], NT)
            e = jnp.exp2(s * (LOG2E / math.sqrt(HD)))
            eb = e.astype(BF)
            oa = mm(eb, va_ref[...])
            padb = jnp.where(idc_ref[rows, :] < 0, 1.0, 0.0)
            inv = 1.0 / (oa[:, HD : HD + 1] + padb)
            ob = oa[:, :HD] * inv
            dob = do_ref[rows, h * HD : (h + 1) * HD].astype(BF).astype(F32)
            dos = (dob * inv).astype(BF)
            delta = jnp.sum(dos.astype(F32) * ob, axis=-1, keepdims=True)
            d0 = delta.astype(BF)
            d1 = (delta - d0.astype(F32)).astype(BF)
            ln = lax.broadcasted_iota(jnp.int32, (block, HD), 1)
            tail = jnp.where(ln == 0, -d0.astype(F32), jnp.where(ln == 1, -d1.astype(F32), 0.0)).astype(BF)
            doa = jnp.concatenate([dos, tail], axis=1)
            dp = mm(doa, va_ref[...], NT)
            ds = (e * dp).astype(BF)
            ob_ref[rows, :] = jnp.where(padb > 0, v_mean, ob)
            dq_ref[rows, :] = mm(ds, ka_ref[...])[:, :HD]
            dk_ref[...] += mm(ds, qb, TN)
            dv_ref[...] += mm(eb, doa, TN)
            return carry

        lax.fori_loop(0, length // block, step, 0)
        o_ref[:, h * HD : (h + 1) * HD] = ob_ref[...].astype(BF)
        scale = 1.0 / math.sqrt(HD)
        gq = (dq_ref[...] * scale).astype(BF).astype(F32)
        gk = (dk_ref[:, :HD] * scale).astype(BF).astype(F32)
        sq = jnp.sum(gq * q_unit, axis=0, keepdims=True)
        sk = jnp.sum(gk * k_unit, axis=0, keepdims=True)
        if h == 0:
            sums_ref[0:1, :] = sq
            sums_ref[1:2, :] = sk
        else:
            sums_ref[0:1, :] += sq
            sums_ref[1:2, :] += sk
        grad_ref[:, h * HD : (h + 1) * HD] = norm_back(gq * gain_q, q_unit, q_inv).astype(BF)
        grad_ref[:, width + h * HD : width + (h + 1) * HD] = norm_back(gk * gain_k, k_unit, k_inv).astype(BF)
        grad_ref[:, 2 * width + h * HD : 2 * width + (h + 1) * HD] = dv_ref[:, :HD].astype(BF)


def attention(normed, gb, wqkv, wo, idc, idr, qg, kg):
    length, dim = normed.shape
    width = wo.shape[0]
    heads = width // HD
    block = 256
    flops = 2 * length * dim * width * 4 + heads * 6 * 2 * length * length * 2 * HD
    return pl.pallas_call(
        functools.partial(attention_kernel, heads, block),
        out_shape=(
            jax.ShapeDtypeStruct((length, width), BF),
            jax.ShapeDtypeStruct((length, 3 * width), BF),
            jax.ShapeDtypeStruct((2, HD), F32),
        ),
        in_specs=[pl.BlockSpec(memory_space=pltpu.VMEM)] * 8,
        out_specs=[pl.BlockSpec(memory_space=pltpu.VMEM)] * 3,
        scratch_shapes=[
            pltpu.VMEM((length, 3 * width), F32),
            pltpu.VMEM((length, width), F32),
            pltpu.VMEM((block, length), F32),
            pltpu.VMEM((length, 2 * HD), BF),
            pltpu.VMEM((length, 2 * HD), BF),
            pltpu.VMEM((length, 2 * HD), BF),
            pltpu.VMEM((length, HD), F32),
            pltpu.VMEM((length, HD), F32),
            pltpu.VMEM((length, 2 * HD), F32),
            pltpu.VMEM((length, 2 * HD), F32),
        ],
        cost_estimate=pl.CostEstimate(flops=flops * 2, transcendentals=heads * length * length, bytes_accessed=2 * length * dim * 2 * 2),
        compiler_params=pltpu.CompilerParams(vmem_limit_bytes=48 << 20),
        name="attention",
    )(normed, gb, wqkv, wo, idc, idr, qg, kg)


def ffn_kernel(normed_ref, gb_ref, wup_ref, wff_ref, hid_ref, gup_ref):
    up = mm(normed_ref[...], wup_ref[...])
    gh = mm(gb_ref[...], wff_ref[...], NT)
    c0 = math.sqrt(2.0 / math.pi)
    c1 = 0.044715
    sq = up * up
    t = jnp.tanh(c0 * up * (1.0 + c1 * sq))
    half = 0.5 * (1.0 + t)
    hid_ref[...] = (up * half).astype(BF)
    gup_ref[...] = (gh * (half + 0.5 * up * (1.0 - t * t) * (c0 * (1.0 + 3.0 * c1 * sq)))).astype(BF)


def ffn(normed, gb, wup, wff):
    length, dim = normed.shape
    units = wup.shape[1]
    bm = 256
    return pl.pallas_call(
        ffn_kernel,
        grid=(length // bm,),
        out_shape=(jax.ShapeDtypeStruct((length, units), BF),) * 2,
        in_specs=[
            pl.BlockSpec((bm, dim), lambda i: (i, 0)),
            pl.BlockSpec((bm, dim), lambda i: (i, 0)),
            pl.BlockSpec((dim, units), lambda i: (0, 0)),
            pl.BlockSpec((units, dim), lambda i: (0, 0)),
        ],
        out_specs=[pl.BlockSpec((bm, units), lambda i: (i, 0))] * 2,
        cost_estimate=pl.CostEstimate(flops=4 * length * dim * units, transcendentals=length * units, bytes_accessed=length * dim * 8 + 4 * dim * units),
        compiler_params=pltpu.CompilerParams(vmem_limit_bytes=40 << 20),
        name="ffn",
    )(normed, gb, wup, wff)


def out_kernel(o_ref, hid_ref, wo_ref, wff_ref, gq_ref, gu_ref, wqkv_ref, wup_ref, br_ref, gn_ref):
    br_ref[...] = (mm(o_ref[...], wo_ref[...]) + mm(hid_ref[...], wff_ref[...])).astype(BF)
    gn_ref[...] = (mm(gq_ref[...], wqkv_ref[...], NT) + mm(gu_ref[...], wup_ref[...], NT)).astype(BF)


def outputs(o, hid, wo, wff, gq, gu, wqkv, wup):
    length = o.shape[0]
    dim = wo.shape[1]
    bm = 256
    row = lambda a: pl.BlockSpec((bm, a.shape[1]), lambda i: (i, 0))
    whole = lambda a: pl.BlockSpec(a.shape, lambda i: (0, 0))
    return pl.pallas_call(
        out_kernel,
        grid=(length // bm,),
        out_shape=(jax.ShapeDtypeStruct((length, dim), BF),) * 2,
        in_specs=[row(o), row(hid), whole(wo), whole(wff), row(gq), row(gu), whole(wqkv), whole(wup)],
        out_specs=[pl.BlockSpec((bm, dim), lambda i: (i, 0))] * 2,
        cost_estimate=pl.CostEstimate(
            flops=2 * length * dim * (o.shape[1] + hid.shape[1] + gq.shape[1] + gu.shape[1]),
            transcendentals=0, bytes_accessed=length * dim * 10),
        compiler_params=pltpu.CompilerParams(vmem_limit_bytes=40 << 20),
        name="outputs",
    )(o, hid, wo, wff, gq, gu, wqkv, wup)


def swap(value, axis, count, mask):
    return lax.ppermute(value, axis, [(i, i ^ mask) for i in range(count)])


def bit_groups(count):
    bits = list(range(count.bit_length() - 1))[::-1]
    groups = []
    while bits:
        take = 2 if len(bits) > 1 else 1
        groups.append(bits[:take])
        bits = bits[take:]
    return groups


def gather_batch(block, me, count):
    shape = block.shape
    held = block[None]
    for bits in bit_groups(count):
        low, size = bits[-1], 1 << len(bits)
        mine = (me >> low) & (size - 1)
        parts = [held] + [swap(held, "batch", count, s << low) for s in range(1, size)]
        done = held.shape[0]
        grown = jnp.zeros((done, size) + shape, block.dtype)
        for s, part in enumerate(parts):
            grown = lax.dynamic_update_slice(
                grown, part[:, None], (0, mine ^ s) + (0,) * len(shape)
            )
        held = grown.reshape((done * size,) + shape)
    return held


def scatter_batch(whole, me, count):
    held = whole
    for bits in bit_groups(count)[::-1]:
        low, size = bits[-1], 1 << len(bits)
        mine = (me >> low) & (size - 1)
        held = held.reshape((held.shape[0] // size, size) + held.shape[1:])
        pick = lambda s: lax.dynamic_index_in_dim(held, mine ^ s, 1, keepdims=False)
        total = pick(0)
        for s in range(1, size):
            total = total + swap(pick(s).astype(BF), "batch", count, s << low).astype(F32)
        held = total
    return held[0]


def gather_tok(block, count):
    parts = {0: block}
    far = count >> 1
    while far:
        for s in list(parts):
            pass
        new = {}
        for s, part in parts.items():
            new[s ^ far] = swap(part, "tok", count, far)
        parts.update(new)
        far >>= 1
    return jnp.concatenate([parts[s] for s in range(count)], axis=0)


def scatter_tok(parts, count):
    near = 1
    parts = dict(enumerate(parts))
    while near < count:
        kept = {}
        for s, part in parts.items():
            if not s & near:
                kept[s] = part + swap(parts[s | near].astype(BF), "tok", count, near).astype(F32)
        parts = kept
        near <<= 1
    return parts[0]


def matchings(edges, devices, per_device):
    left = [[] for _ in range(devices)]
    for e, (source, _, _) in enumerate(edges):
        left[source].append(e)
    rounds = []
    for _ in range(per_device):
        owner = [-1] * devices

        def place(source, seen):
            for e in left[source]:
                target = edges[e][1]
                if target in seen:
                    continue
                seen.add(target)
                if owner[target] < 0 or place(edges[owner[target]][0], seen):
                    owner[target] = e
                    return True
            return False

        for source in range(devices):
            place(source, set())
        rounds.append(list(owner))
        for e in owner:
            left[edges[e][0]].remove(e)
    return rounds


def unit_plan(nb, nt, rows, width, hidden):
    unit = math.gcd(math.gcd(rows, width // nt), hidden // nt)
    per = rows // unit
    head_units, hid_units = width // nt // unit, hidden // nt // unit
    assert head_units % nb == 0 and hid_units % nb == 0
    a, c = head_units // nb, hid_units // nb
    edges = []
    for t in range(nt):
        for b in range(nb):
            want = [t * head_units + b * a + i for i in range(a)]
            want += [nt * head_units + t * hid_units + b * c + i for i in range(c)]
            for slot, u in enumerate(want):
                edges.append((u // per, b * nt + t, (u % per, slot)))
    rounds = matchings(edges, nb * nt, per)
    plan = []
    for owner in rounds:
        perm = [(edges[e][0], edges[e][1]) for e in owner]
        source_slot = np.zeros(nb * nt, np.int32)
        target_slot = np.zeros(nb * nt, np.int32)
        for e in owner:
            source_slot[edges[e][0]] = edges[e][2][0]
            target_slot[edges[e][1]] = edges[e][2][1]
        plan.append((perm, source_slot, target_slot))
    return unit, per, a, plan


def per_device(
    nb, nt, patches, image_ids, cotangent, norm_gain, query_gain, key_gain, in_weight, out_weight
):
    seqs, part, dim = patches.shape
    width = H * HD
    local = width // nt
    hidden = in_weight.shape[1] - 3 * width
    units = hidden // nt
    both = ("batch", "tok")
    me_b = lax.axis_index("batch")
    me_t = lax.axis_index("tok")
    me = me_b * nt + me_t

    rows_in = in_weight.shape[0]
    w_qkv = in_weight[:, : 3 * width].reshape(rows_in, 3, nt, local)
    w_qkv = w_qkv.transpose(2, 0, 1, 3).reshape(nt, rows_in, 3 * local)
    w_up = in_weight[:, 3 * width :].reshape(rows_in, nt, units).transpose(1, 0, 2)
    w_in = lax.all_to_all(
        jnp.concatenate([w_qkv, w_up], axis=2), "tok", split_axis=0, concat_axis=0, tiled=True
    ).reshape(nt * rows_in, 3 * local + units)
    unit, per, head_slots, plan = unit_plan(nb, nt, out_weight.shape[0], width, hidden)
    w_units = out_weight.reshape(per, unit, dim)
    held = jnp.zeros_like(w_units)
    for perm, source_slot, target_slot in plan:
        sent = lax.dynamic_index_in_dim(w_units, jnp.asarray(source_slot)[me], 0, keepdims=True)
        held = lax.dynamic_update_slice(
            held, lax.ppermute(sent, both, perm), (jnp.asarray(target_slot)[me], 0, 0)
        )
    wqkv = gather_batch(w_in[:, : 3 * local], me_b, nb).reshape(dim, 3 * local)
    wo = gather_batch(held[:head_slots], me_b, nb).reshape(local, dim)
    wup = gather_batch(w_in[:, 3 * local :], me_b, nb).reshape(dim, units)
    wff = gather_batch(held[head_slots:], me_b, nb).reshape(units, dim)

    live = (image_ids >= 0).astype(F32)[..., None]
    x = patches.astype(F32)
    unit_rows, inverse = normalize(x)
    normed = (unit_rows * norm_gain).astype(BF)
    grad_branch = (live * cotangent.astype(F32)).astype(BF)
    ids = [gather_tok(image_ids[s], nt) for s in range(seqs)]
    normed_s = [gather_tok(normed[s], nt) for s in range(seqs)]
    gb_s = [gather_tok(grad_branch[s], nt) for s in range(seqs)]

    qg = query_gain.reshape(1, HD)
    kg = key_gain.reshape(1, HD)
    heads_s, gqkv_s, hid_s, gup_s, branch_s, gn_s = [], [], [], [], [], []
    sums = 0.0
    for s in range(seqs):
        heads, gqkv, part_sums = attention(
            normed_s[s], gb_s[s], wqkv, wo, ids[s].reshape(-1, 1), ids[s].reshape(1, -1), qg, kg
        )
        hid, gup = ffn(normed_s[s], gb_s[s], wup, wff)
        branch, gn = outputs(heads, hid, wo, wff, gqkv, gup, wqkv, wup)
        split = lambda a: [a[i * part : (i + 1) * part].astype(F32) for i in range(nt)]
        branch_s.append(scatter_tok(split(branch), nt))
        gn_s.append(scatter_tok(split(gn), nt))
        heads_s.append(heads)
        gqkv_s.append(gqkv)
        hid_s.append(hid)
        gup_s.append(gup)
        sums = sums + part_sums

    def weight_grad(lefts, rights):
        return sum(mm(a, b, TN) for a, b in zip(lefts, rights))

    g_up = weight_grad(normed_s, gup_s)
    g_ff = weight_grad(hid_s, gb_s)
    g_qkv = weight_grad(normed_s, gqkv_s)
    g_o = weight_grad(heads_s, gb_s)
    norm_part = (
        jnp.sum(wqkv.astype(F32) * g_qkv, axis=1) + jnp.sum(wup.astype(F32) * g_up, axis=1)
    ) / norm_gain
    small = jnp.concatenate([norm_part, sums.reshape(-1)])
    for bit in range(nt.bit_length() - 1):
        small = small + swap(small, "tok", nt, 1 << bit)
    for bit in range(nb.bit_length() - 1):
        small = small + swap(small, "batch", nb, 1 << bit)
    norm_grad = small[:dim]
    query_grad = small[dim : dim + HD]
    key_grad = small[dim + HD :]

    def finish_in(g):
        mine = scatter_batch(g.reshape(nb, nt * rows_in, g.shape[1]), me_b, nb)
        return lax.all_to_all(
            mine.reshape(nt, rows_in, g.shape[1]), "tok", split_axis=0, concat_axis=0, tiled=True
        )

    in_up = finish_in(g_up).transpose(1, 0, 2).reshape(rows_in, hidden)
    in_qkv = (
        finish_in(g_qkv)
        .reshape(nt, rows_in, 3, local)
        .transpose(1, 2, 0, 3)
        .reshape(rows_in, 3 * width)
    )
    in_grad = jnp.concatenate([in_qkv, in_up], axis=1)
    o_mine = scatter_batch(g_o.reshape(nb, head_slots * unit, dim), me_b, nb)
    f_mine = scatter_batch(g_ff.reshape(nb, (per - head_slots) * unit, dim), me_b, nb)
    mine = jnp.concatenate([o_mine, f_mine], axis=0).reshape(per, unit, dim)
    back = jnp.zeros_like(mine)
    for perm, source_slot, target_slot in plan:
        sent = lax.dynamic_index_in_dim(mine, jnp.asarray(target_slot)[me], 0, keepdims=True)
        back = lax.dynamic_update_slice(
            back,
            lax.ppermute(sent, both, [(b, a) for a, b in perm]),
            (jnp.asarray(source_slot)[me], 0, 0),
        )
    out_grad = back.reshape(per * unit, dim)

    branch = jnp.stack(branch_s)
    gn = jnp.stack(gn_s)
    block_out = (live * (x + branch)).astype(BF)
    patch_grad = (
        grad_branch.astype(F32) + norm_back(gn * norm_gain, unit_rows, inverse)
    ).astype(BF)
    return (block_out, patch_grad, norm_grad, query_grad, key_grad, in_grad, out_grad)


def solution(mesh):
    rows = P("batch", "tok", None)
    weights = P(("batch", "tok"), None)
    return jax.shard_map(
        functools.partial(per_device, mesh.shape["batch"], mesh.shape["tok"]),
        mesh=mesh,
        in_specs=(rows, P("batch", "tok"), rows, P(), P(), P(), weights, weights),
        out_specs=(rows, rows, P(), P(), P(), weights, weights),
        check_vma=False,
    )
```

```python
import functools
import math

import jax
import jax.numpy as jnp
import numpy as np
from jax import lax
from jax.experimental import pallas as pl
from jax.experimental.pallas import tpu as pltpu
from jax.sharding import PartitionSpec as P

H = 12
HD = 64
SLOTS = 4
EPS = 1e-06
BIG = 2048.0
LOG2E = 1.4426950408889634
BF = jnp.bfloat16
F32 = jnp.float32
NN = (((1,), (0,)), ((), ()))
NT = (((1,), (1,)), ((), ()))
TN = (((0,), (0,)), ((), ()))
MIB = 1 << 20

VMEM = pl.BlockSpec(memory_space=pltpu.VMEM)
SMEM = pl.BlockSpec(memory_space=pltpu.SMEM)
ANY = pl.BlockSpec(memory_space=pl.ANY)


def mm(a, b, dims=NN):
    return lax.dot_general(a, b, dims, preferred_element_type=F32)


def normalize(values):
    center = values - jnp.mean(values, axis=-1, keepdims=True)
    inverse = lax.rsqrt(jnp.mean(center * center, axis=-1, keepdims=True) + EPS)
    return center * inverse, inverse


def norm_back(grad_unit, unit_rows, inverse):
    return inverse * (
        grad_unit
        - jnp.mean(grad_unit, axis=-1, keepdims=True)
        - unit_rows * jnp.mean(grad_unit * unit_rows, axis=-1, keepdims=True)
    )


def column(row):
    return jnp.broadcast_to(row, (8, row.shape[1])).T[:, 0:1]


def before_kernel(ids_ref, x_ref, cot_ref, gain_ref, *pay_refs):
    for s, pay in enumerate(pay_refs):
        unit, _ = normalize(x_ref[s].astype(F32))
        live = column(jnp.where(ids_ref[s : s + 1, :] >= 0, 1.0, 0.0))
        pay[0] = (unit * gain_ref[...]).astype(BF)
        pay[1] = (live * cot_ref[s].astype(F32)).astype(BF)


def before(ids, x, cot, gain):
    seqs, part, dim = x.shape
    return pl.pallas_call(
        before_kernel,
        out_shape=[jax.ShapeDtypeStruct((2, part, dim), BF)] * seqs,
        in_specs=[VMEM] * 4,
        out_specs=[VMEM] * seqs,
        cost_estimate=pl.CostEstimate(flops=x.size * 8, transcendentals=0, bytes_accessed=x.size * 8),
        compiler_params=pltpu.CompilerParams(vmem_limit_bytes=32 * MIB),
        name="before",
    )(ids, x, cot, gain)


def after_kernel(s, ids_ref, x_ref, cot_ref, gain_ref, keep_ref, near_ref, far_ref, *rest):
    out_ref, grad_ref = rest[-2:]
    unit, inverse = normalize(x_ref[0].astype(F32))
    live = column(jnp.where(ids_ref[s : s + 1, :] >= 0, 1.0, 0.0))
    both = keep_ref[0].astype(F32) + near_ref[0].astype(F32) + far_ref[...].astype(F32)
    out_ref[0] = (live * (x_ref[0].astype(F32) + both[0])).astype(BF)
    grad_ref[0] = (
        live * cot_ref[0].astype(F32) + norm_back(both[1] * gain_ref[...], unit, inverse)
    ).astype(BF)


def after(s, ids, x, cot, gain, keep, near, far, earlier):
    seqs, part, dim = x.shape
    one = pl.BlockSpec((1, part, dim), lambda i: (s, 0, 0))
    pair = pl.BlockSpec((1, 2, part, dim), lambda i: (0, 0, 0, 0))
    fixed = lambda a: pl.BlockSpec(a.shape, lambda i: (0,) * a.ndim)
    return pl.pallas_call(
        functools.partial(after_kernel, s),
        grid=(1,),
        out_shape=[jax.ShapeDtypeStruct(x.shape, BF)] * 2,
        in_specs=[fixed(ids), one, one, fixed(gain), pair, pair, fixed(far)] + [ANY] * len(earlier),
        out_specs=[one, one],
        input_output_aliases={7 + i: i for i in range(len(earlier))},
        cost_estimate=pl.CostEstimate(flops=part * dim * 20, transcendentals=0, bytes_accessed=part * dim * 20),
        compiler_params=pltpu.CompilerParams(vmem_limit_bytes=32 * MIB),
        name="after",
    )(ids, x, cot, gain, keep, near, far, *earlier)


def split_rows(odd, grad, send_ref, keep_ref, parts, rows, store):
    for z in range(parts):
        low = grad[2 * z * rows : (2 * z + 1) * rows]
        high = grad[(2 * z + 1) * rows : (2 * z + 2) * rows]
        store(send_ref, z, jnp.where(odd, low, high).astype(BF))
        store(keep_ref, z, jnp.where(odd, high, low))


def attention_kernel(
    heads, block, first, last,
    odd_ref, ids_ref, wqkv_ref, wo_ref, qg_ref, kg_ref, *refs,
):
    pays, refs = refs[:SLOTS], refs[SLOTS:]
    if not first:
        (accq_ref, acco_ref, acc_sums_ref), refs = refs[:3], refs[3:]
    if last:
        (o_ref, grad_ref, sums_ref, send_ref, keep_ref, np_ref), refs = refs[:6], refs[6:]
    else:
        (o_ref, grad_ref, sums_ref, newq_ref, newo_ref), refs = refs[:5], refs[5:]
    (norm_ref, gb_ref, raw_ref, do_ref, qa_ref, ka_ref, va_ref, ob_ref, dq_ref, dk_ref, dv_ref, sem) = refs
    length, dim = norm_ref.shape
    part = length // SLOTS
    width = heads * HD
    copies = []
    for j in range(2):
        for i, pay in enumerate(pays):
            to = (norm_ref, gb_ref)[j].at[pl.ds(i * part, part), :]
            copies.append(pltpu.make_async_copy(pay.at[j], to, sem.at[j * SLOTS + i]))
            copies[-1].start()
    idr = ids_ref[...]
    marks = lax.broadcasted_iota(jnp.int32, (HD, length), 0)
    same = marks == idr + 1
    k_tail = jnp.where(same, 1.0, 0.0).T.astype(BF)
    q_tail = jnp.where((same & (idr >= 0)) | (marks > 4), 0.0, -BIG).T.astype(BF)
    pad = jnp.where(idr < 0, 1.0, 0.0)
    pad_ref = dq_ref
    lanes = lax.broadcasted_iota(jnp.int32, (length, HD), 1)
    v_tail = jnp.where(lanes < 2, 1.0, 0.0).astype(BF)
    pad_col = column(pad)
    for i in range(SLOTS):
        copies[i].wait()
    raw_ref[...] = mm(norm_ref[...], wqkv_ref[...])
    for i in range(SLOTS):
        copies[SLOTS + i].wait()
    do_ref[...] = mm(gb_ref[...], wo_ref[...], NT)
    gain_q = qg_ref[...]
    gain_k = kg_ref[...]
    for h in range(heads):
        q_raw = raw_ref[:, h * HD : (h + 1) * HD]
        k_raw = raw_ref[:, width + h * HD : width + (h + 1) * HD]
        q_unit, q_inv = normalize(q_raw)
        k_unit, k_inv = normalize(k_raw)
        qa_ref[:, :HD] = (q_unit * gain_q).astype(BF)
        qa_ref[:, HD:] = q_tail
        ka_ref[:, :HD] = (k_unit * gain_k).astype(BF)
        ka_ref[:, HD:] = k_tail
        va = raw_ref[:, 2 * width + h * HD : 2 * width + (h + 1) * HD].astype(BF)
        va_ref[:, :HD] = va
        va_ref[:, HD:] = v_tail
        v_mean = jnp.mean(va.astype(F32), axis=0, keepdims=True)
        dk_ref[...] = jnp.zeros_like(dk_ref)
        dv_ref[...] = jnp.zeros_like(dv_ref)
        ob_ref[:, HD:] = jnp.broadcast_to(pad_col, (length, HD))

        def step(i, carry):
            rows = pl.ds(pl.multiple_of(i * block, block), block)
            qb = qa_ref[rows, :]
            s = mm(qb, ka_ref[...], NT)
            e = jnp.exp2(s * (LOG2E / math.sqrt(HD)))
            eb = e.astype(BF)
            oa = mm(eb, va_ref[...])
            padb = ob_ref[rows, HD : HD + 1]
            inv = 1.0 / (oa[:, HD : HD + 1] + padb)
            ob = oa[:, :HD] * inv
            dob = do_ref[rows, h * HD : (h + 1) * HD].astype(BF).astype(F32)
            dos = (dob * inv).astype(BF)
            delta = jnp.sum(dos.astype(F32) * ob, axis=-1, keepdims=True)
            d0 = delta.astype(BF).astype(F32)
            d1 = delta - d0
            ln = lax.broadcasted_iota(jnp.int32, (block, HD), 1)
            tail = jnp.where(ln == 0, -d0, jnp.where(ln == 1, -d1, 0.0)).astype(BF)
            doa = jnp.concatenate([dos, tail], axis=1)
            dp = mm(doa, va_ref[...], NT)
            ds = (e * dp).astype(BF)
            ob_ref[rows, :HD] = jnp.where(padb > 0, v_mean, ob)
            dq_ref[rows, :] = mm(ds, ka_ref[...])[:, :HD]
            dk_ref[...] += mm(ds, qb, TN)
            dv_ref[...] += mm(eb, doa, TN)
            return carry

        lax.fori_loop(0, length // block, step, 0)
        o_ref[:, h * HD : (h + 1) * HD] = ob_ref[:, :HD].astype(BF)
        scale = 1.0 / math.sqrt(HD)
        gq = (dq_ref[...] * scale).astype(BF).astype(F32)
        gk = (dk_ref[:, :HD] * scale).astype(BF).astype(F32)
        both = jnp.concatenate(
            [jnp.sum(gq * q_unit, axis=0, keepdims=True), jnp.sum(gk * k_unit, axis=0, keepdims=True)], axis=0
        )
        if h == 0 and first:
            sums_ref[...] = both
        elif h == 0:
            sums_ref[...] = acc_sums_ref[...] + both
        else:
            sums_ref[...] += both
        grad_ref[:, h * HD : (h + 1) * HD] = norm_back(gq * gain_q, q_unit, q_inv).astype(BF)
        grad_ref[:, width + h * HD : width + (h + 1) * HD] = norm_back(gk * gain_k, k_unit, k_inv).astype(BF)
        grad_ref[:, 2 * width + h * HD : 2 * width + (h + 1) * HD] = dv_ref[:, :HD].astype(BF)
    g_q = mm(norm_ref[...], grad_ref[...], TN)
    g_o = mm(o_ref[...], gb_ref[...], TN)
    if not first:
        g_q = g_q + accq_ref[...]
        g_o = g_o + acco_ref[...]
    if not last:
        newq_ref[...] = g_q
        newo_ref[...] = g_o
        return
    np_ref[...] = jnp.sum(wqkv_ref[...].astype(F32) * g_q, axis=1, keepdims=True)
    odd = odd_ref[0] > 0
    parts, rows, _ = send_ref.shape
    unit = width // (2 * parts)

    def put_q(ref, z, value):
        ref[z, :, : 3 * width] = value

    def put_o(ref, z, value):
        for c in range(dim // width):
            ref[z, c * unit : (c + 1) * unit, 3 * width :] = value[:, c * width : (c + 1) * width]

    split_rows(odd, g_q, send_ref, keep_ref, parts, rows, put_q)
    split_rows(odd, g_o, send_ref, keep_ref, parts, unit, put_o)


def attention(odd, ids, wqkv, wo, qg, kg, pays, acc, last, halves):
    dim, wide = wqkv.shape
    width = wo.shape[0]
    heads = width // HD
    length = pays[0].shape[1] * SLOTS
    block = 256
    first = acc is None
    ins = [odd, ids, wqkv, wo, qg, kg, *pays] + ([] if first else list(acc))
    specs = [SMEM] + [VMEM] * 5 + [ANY] * SLOTS + ([] if first else [VMEM] * 3)
    outs = [
        jax.ShapeDtypeStruct((length, width), BF),
        jax.ShapeDtypeStruct((length, wide), BF),
        jax.ShapeDtypeStruct((2, HD), F32),
    ]
    if last:
        rows = dim // (2 * halves)
        outs += [
            jax.ShapeDtypeStruct((halves, rows, wide + width), BF),
            jax.ShapeDtypeStruct((halves, rows, wide + width), F32),
            jax.ShapeDtypeStruct((dim, 1), F32),
        ]
    else:
        outs += [jax.ShapeDtypeStruct((dim, wide), F32), jax.ShapeDtypeStruct((width, dim), F32)]
    flops = 2 * length * dim * width * 8 + heads * 6 * 2 * length * length * HD
    return pl.pallas_call(
        functools.partial(attention_kernel, heads, block, first, last),
        out_shape=outs,
        in_specs=specs,
        out_specs=[VMEM] * len(outs),
        scratch_shapes=[
            pltpu.VMEM((length, dim), BF),
            pltpu.VMEM((length, dim), BF),
            pltpu.VMEM((length, wide), F32),
            pltpu.VMEM((length, width), F32),
            pltpu.VMEM((length, 2 * HD), BF),
            pltpu.VMEM((length, 2 * HD), BF),
            pltpu.VMEM((length, 2 * HD), BF),
            pltpu.VMEM((length, 2 * HD), F32),
            pltpu.VMEM((length, HD), F32),
            pltpu.VMEM((length, 2 * HD), F32),
            pltpu.VMEM((length, 2 * HD), F32),
            pltpu.SemaphoreType.DMA((2 * SLOTS,)),
        ],
        cost_estimate=pl.CostEstimate(flops=flops * 3, transcendentals=heads * length * length, bytes_accessed=8 * length * dim),
        compiler_params=pltpu.CompilerParams(vmem_limit_bytes=56 * MIB),
        name="attention",
    )(*ins)


def ffn_kernel(count, odd_ref, wup_ref, wff_ref, *refs):
    pays, refs = refs[:count], refs[count:]
    (hid_ref, gup_ref, send_ref, keep_ref, np_ref), refs = refs[:5], refs[5:]
    pay_ref, hidv_ref, gupv_ref, gin_ref, gff_ref, sem, out_sem = refs
    part = pay_ref.shape[2]
    for i, pay in enumerate(pays):
        pltpu.make_async_copy(pay, pay_ref.at[i], sem.at[i]).start()
    gin_ref[...] = jnp.zeros_like(gin_ref)
    gff_ref[...] = jnp.zeros_like(gff_ref)
    c0 = math.sqrt(2.0 / math.pi)
    c1 = 0.044715

    def outs(i):
        return (
            pltpu.make_async_copy(hidv_ref.at[i], hid_ref.at[i], out_sem.at[0, i]),
            pltpu.make_async_copy(gupv_ref.at[i], gup_ref.at[i], out_sem.at[1, i]),
        )

    def step(i, carry):
        pltpu.make_async_copy(pays[0], pay_ref.at[i], sem.at[i]).wait()
        normed = pay_ref[i, 0]
        gb = pay_ref[i, 1]
        up = mm(normed, wup_ref[...])
        gh = mm(gb, wff_ref[...], NT)
        sq = up * up
        t = jnp.tanh(up * (c0 + (c0 * c1) * sq))
        half = 0.5 + 0.5 * t
        hid = (up * half).astype(BF)
        gup = (gh * (half + (0.5 * up) * (1.0 - t * t) * (c0 + (3.0 * c0 * c1) * sq))).astype(BF)
        hidv_ref[i] = hid
        gupv_ref[i] = gup
        for copy in outs(i):
            copy.start()
        gin_ref[...] += mm(normed, gup, TN)
        gff_ref[...] += mm(hid, gb, TN)
        return carry

    lax.fori_loop(0, count, step, 0)
    odd = odd_ref[0] > 0
    _, parts, rows, _ = send_ref.shape
    np_ref[...] = jnp.sum(wup_ref[...].astype(F32) * gin_ref[...], axis=1, keepdims=True)
    for k, g in enumerate((gin_ref, gff_ref)):

        def put(ref, z, value, k=k):
            ref[k, z] = value

        split_rows(odd, g[...], send_ref, keep_ref, parts, rows, put)

    def drain(i, carry):
        for copy in outs(i):
            copy.wait()
        return carry

    lax.fori_loop(0, count, drain, 0)


def ffn(odd, wup, wff, pays, halves):
    dim, units = wup.shape
    part = pays[0].shape[1]
    count = len(pays)
    rows = dim // (2 * halves)
    assert units == dim
    act = jax.ShapeDtypeStruct((count, part, units), BF)
    return pl.pallas_call(
        functools.partial(ffn_kernel, count),
        out_shape=[
            act,
            act,
            jax.ShapeDtypeStruct((2, halves, rows, dim), BF),
            jax.ShapeDtypeStruct((2, halves, rows, dim), F32),
            jax.ShapeDtypeStruct((dim, 1), F32),
        ],
        in_specs=[SMEM, VMEM, VMEM] + [ANY] * count,
        out_specs=[ANY, ANY, VMEM, VMEM, VMEM],
        scratch_shapes=[
            pltpu.VMEM((count, 2, part, dim), BF),
            pltpu.VMEM((count, part, units), BF),
            pltpu.VMEM((count, part, units), BF),
            pltpu.VMEM((dim, units), F32),
            pltpu.VMEM((units, dim), F32),
            pltpu.SemaphoreType.DMA((count,)),
            pltpu.SemaphoreType.DMA((2, count)),
        ],
        cost_estimate=pl.CostEstimate(
            flops=8 * count * part * dim * units, transcendentals=count * part * units, bytes_accessed=count * part * dim * 8
        ),
        compiler_params=pltpu.CompilerParams(vmem_limit_bytes=58 * MIB),
        name="ffn",
    )(odd, wup, wff, *pays)


def out_kernel(o_ref, hid_ref, gq_ref, gu_ref, wo_ref, wff_ref, wqkv_ref, wup_ref, keep_ref, send_ref):
    branch = (mm(o_ref[...], wo_ref[...]) + mm(hid_ref[0], wff_ref[...])).astype(BF)
    gn = (mm(gq_ref[...], wqkv_ref[...], NT) + mm(gu_ref[0], wup_ref[...], NT)).astype(BF)
    away = pl.program_id(0) % 2

    @pl.when(away == 0)
    def _():
        keep_ref[0, 0] = branch
        keep_ref[0, 1] = gn

    @pl.when(away == 1)
    def _():
        send_ref[0, 0] = branch
        send_ref[0, 1] = gn


def outputs(s, o, hid, gq, gu, wo, wff, wqkv, wup):
    part, dim = hid.shape[1], wo.shape[1]
    row = lambda a: pl.BlockSpec((part, a.shape[1]), lambda i: (i, 0))
    act = pl.BlockSpec((1, part, hid.shape[2]), lambda i: (s * SLOTS + i, 0, 0))
    whole = lambda a: pl.BlockSpec(a.shape, lambda i: (0, 0), pipeline_mode=pl.Buffered(1))
    out = pl.BlockSpec((1, 2, part, dim), lambda i: (i // 2, 0, 0, 0))
    return pl.pallas_call(
        out_kernel,
        grid=(SLOTS,),
        out_shape=[jax.ShapeDtypeStruct((SLOTS // 2, 2, part, dim), BF)] * 2,
        in_specs=[row(o), act, row(gq), act, whole(wo), whole(wff), whole(wqkv), whole(wup)],
        out_specs=[out, out],
        cost_estimate=pl.CostEstimate(
            flops=2 * SLOTS * part * dim * (o.shape[1] + 2 * hid.shape[2] + gq.shape[1]),
            transcendentals=0, bytes_accessed=SLOTS * part * dim * 10),
        compiler_params=pltpu.CompilerParams(vmem_limit_bytes=40 * MIB),
        name="outputs",
    )(o, hid, gq, gu, wo, wff, wqkv, wup)


def swap(value, axis, count, mask):
    return lax.ppermute(value, axis, [(i, i ^ mask) for i in range(count)])


def bit_groups(count):
    bits = list(range(count.bit_length() - 1))[::-1]
    groups = []
    while bits:
        take = 2 if len(bits) > 1 else 1
        groups.append(bits[:take])
        bits = bits[take:]
    assert len(groups[-1]) == 1
    return groups


def gather_batch(block, me, count):
    shape = block.shape
    held = block[None]
    for bits in bit_groups(count):
        low, size = bits[-1], 1 << len(bits)
        mine = (me >> low) & (size - 1)
        parts = [held] + [swap(held, "batch", count, s << low) for s in range(1, size)]
        blocks = []
        for j in range(size):
            value = parts[0]
            for s in range(1, size):
                value = jnp.where((mine ^ s) == j, parts[s], value)
            blocks.append(value)
        held = jnp.stack(blocks, axis=1).reshape((-1,) + shape)
    return held


def scatter_rest(held, axis, me, count):
    for bits in bit_groups(count)[::-1][1:]:
        low, size = bits[-1], 1 << len(bits)
        mine = (me >> low) & (size - 1)
        held = held.reshape(held.shape[:axis] + (held.shape[axis] // size, size) + held.shape[axis + 1 :])
        pick = lambda s: lax.dynamic_index_in_dim(held, mine ^ s, axis + 1, keepdims=False)
        total = pick(0)
        for s in range(1, size):
            total = total + swap(pick(s).astype(BF), "batch", count, s << low).astype(F32)
        held = total
    return jnp.squeeze(held, axis)


def matchings(edges, devices, per_device):
    left = [[] for _ in range(devices)]
    for e, (source, _, _) in enumerate(edges):
        left[source].append(e)
    rounds = []
    for _ in range(per_device):
        owner = [-1] * devices

        def place(source, seen):
            for e in left[source]:
                target = edges[e][1]
                if target in seen:
                    continue
                seen.add(target)
                if owner[target] < 0 or place(edges[owner[target]][0], seen):
                    owner[target] = e
                    return True
            return False

        for source in range(devices):
            place(source, set())
        rounds.append(list(owner))
        for e in owner:
            left[edges[e][0]].remove(e)
    return rounds


def unit_plan(nb, nt, rows, width, hidden):
    unit = math.gcd(math.gcd(rows, width // nt), hidden // nt)
    per = rows // unit
    head_units, hid_units = width // nt // unit, hidden // nt // unit
    assert head_units == nb and hid_units % nb == 0
    c = hid_units // nb
    edges = []
    for t in range(nt):
        for b in range(nb):
            want = [t * head_units + b]
            want += [nt * head_units + t * hid_units + b * c + i for i in range(c)]
            for slot, u in enumerate(want):
                edges.append((u // per, b * nt + t, (u % per, slot)))
    table = np.zeros((nb * nt, 2 * per), np.int32)
    perms = []
    for k, owner in enumerate(matchings(edges, nb * nt, per)):
        perms.append([(edges[e][0], edges[e][1]) for e in owner])
        for e in owner:
            table[edges[e][0], k] = edges[e][2][0]
            table[edges[e][1], per + k] = edges[e][2][1]
    return unit, per, perms, table


def move_units(units, perms, source_slot, target_slot):
    count = len(units)
    got = []
    for k, perm in enumerate(perms):
        value = units[0]
        for j in range(1, count):
            value = jnp.where(source_slot[k] == j, units[j], value)
        got.append(lax.ppermute(value, ("batch", "tok"), perm))
    placed = []
    for j in range(count):
        value = got[0]
        for k in range(1, count):
            value = jnp.where(target_slot[k] == j, got[k], value)
        placed.append(value)
    return placed


def per_device(
    nb, nt, patches, image_ids, cotangent, norm_gain, query_gain, key_gain, in_weight, out_weight
):
    seqs, part, dim = patches.shape
    width = H * HD
    local = width // nt
    hidden = in_weight.shape[1] - 3 * width
    units = hidden // nt
    halves = nb // 2
    assert nt == SLOTS
    me_b = lax.axis_index("batch")
    me_t = lax.axis_index("tok")
    me = me_b * nt + me_t
    odd = (me_b & 1).reshape(1)
    gain = norm_gain.reshape(1, dim)

    rows_in = in_weight.shape[0]
    w_qkv = in_weight[:, : 3 * width].reshape(rows_in, 3, nt, local)
    w_qkv = w_qkv.transpose(2, 0, 1, 3).reshape(nt, rows_in, 3 * local)
    w_up = in_weight[:, 3 * width :].reshape(rows_in, nt, units).transpose(1, 0, 2)
    id_row = jnp.pad(image_ids.reshape(1, 1, seqs * part).astype(BF), ((0, 0), (0, 0), (0, 3 * local + units - seqs * part)))
    w_in = lax.all_to_all(
        jnp.concatenate(
            [jnp.concatenate([w_qkv, w_up], axis=2), jnp.broadcast_to(id_row, (nt, 1, 3 * local + units))], axis=1
        ),
        "tok", split_axis=0, concat_axis=0, tiled=True,
    )
    id_rows = w_in[:, rows_in, : seqs * part].astype(jnp.int32)
    id_slots = []
    for s in range(nt):
        value = id_rows[0]
        for t in range(1, nt):
            value = jnp.where((me_t ^ s) == t, id_rows[t], value)
        id_slots.append(value.reshape(seqs, part))
    ids = jnp.stack(id_slots, axis=1).reshape(seqs, 1, nt * part)
    w_in = w_in[:, :rows_in]

    unit, per, perms, table = unit_plan(nb, nt, out_weight.shape[0], width, hidden)
    row = lax.dynamic_slice(jnp.asarray(table), (me, 0), (1, 2 * per))[0]
    slots_a = [row[k] for k in range(per)]
    slots_b = [row[per + k] for k in range(per)]
    held = move_units([out_weight[k * unit : (k + 1) * unit] for k in range(per)], perms, slots_a, slots_b)
    packs = dim // local
    wo_pack = held[0].reshape(unit, packs, local).transpose(1, 0, 2).reshape(packs * unit, local)
    assert packs * unit == nt * rows_in
    chunk_a = jnp.concatenate([w_in[:, :, : 3 * local].reshape(nt * rows_in, 3 * local), wo_pack], axis=1)
    chunk_b = jnp.stack(
        [w_in[:, :, 3 * local :].reshape(nt * rows_in, units), jnp.concatenate(held[1:], axis=0)]
    )

    pays = before(image_ids, patches, cotangent, gain)
    pay_s = []
    for s in range(seqs):
        far = swap(pays[s], "tok", nt, 2)
        pay_s.append([pays[s], swap(pays[s], "tok", nt, 1), far, swap(far, "tok", nt, 1)])

    full_a = gather_batch(chunk_a, me_b, nb).reshape(dim, 4 * local)
    wqkv = full_a[:, : 3 * local]
    wo = full_a[:, 3 * local :].reshape(nb, packs, unit, local).transpose(0, 2, 1, 3).reshape(local, dim)
    full_b = gather_batch(chunk_b, me_b, nb)
    wup = full_b[:, 0].reshape(dim, units)
    wff = full_b[:, 1].reshape(units, dim)

    qg = query_gain.reshape(1, HD)
    kg = key_gain.reshape(1, HD)
    acc = None
    atts = []
    for s in range(seqs):
        last = s == seqs - 1
        if last:
            hid, gup, f_send, f_keep, f_np = ffn(odd, wup, wff, [p for q in pay_s for p in q], halves)
        att = attention(odd, ids[s], wqkv, wo, qg, kg, pay_s[s], acc, last, halves)
        acc = (att[3], att[4], att[2]) if not last else None
        atts.append(att)
    _, _, sums, a_send, a_keep, a_np = atts[-1]

    earlier = []
    for s in range(seqs):
        keep, send = outputs(s, atts[s][0], hid, atts[s][1], gup, wo, wff, wqkv, wup)
        near = swap(send, "tok", nt, 1)
        far = swap((keep[1].astype(F32) + near[1].astype(F32)).astype(BF), "tok", nt, 2)
        earlier = after(s, image_ids, patches, cotangent, gain, keep, near, far, earlier)
    block_out, patch_grad = earlier

    small = jnp.concatenate([(a_np + f_np)[:, 0] / norm_gain, sums.reshape(-1)])
    for bit in range(nt.bit_length() - 1):
        small = small + swap(small, "tok", nt, 1 << bit)
    for bit in range(nb.bit_length() - 1):
        small = small + swap(small, "batch", nb, 1 << bit)
    norm_grad = small[:dim]
    query_grad = small[dim : dim + HD]
    key_grad = small[dim + HD :]

    def to_rows(mine):
        return lax.all_to_all(
            mine.reshape(nt, rows_in, mine.shape[1]), "tok", split_axis=0, concat_axis=0, tiled=True
        )

    f_sum = f_keep + swap(f_send, "batch", nb, 1).astype(F32)
    f_mine = scatter_rest(f_sum, 1, me_b, nb)
    in_up = to_rows(f_mine[0]).transpose(1, 0, 2).reshape(rows_in, hidden)
    a_sum = a_keep + swap(a_send, "batch", nb, 1).astype(F32)
    a_mine = scatter_rest(a_sum, 0, me_b, nb)
    in_qkv = to_rows(a_mine[:, : 3 * local])
    in_qkv = in_qkv.reshape(nt, rows_in, 3, local).transpose(1, 2, 0, 3).reshape(rows_in, 3 * width)
    in_grad = jnp.concatenate([in_qkv, in_up], axis=1)
    o_mine = a_mine[:, 3 * local :].reshape(packs, unit, local).transpose(1, 0, 2).reshape(unit, dim)
    mine = [o_mine] + [f_mine[1, k * unit : (k + 1) * unit] for k in range(per - 1)]
    back = move_units(mine, [[(b, a) for a, b in perm] for perm in perms], slots_b, slots_a)
    out_grad = jnp.concatenate(back, axis=0)
    return (block_out, patch_grad, norm_grad, query_grad, key_grad, in_grad, out_grad)


def solution(mesh):
    rows = P("batch", "tok", None)
    weights = P(("batch", "tok"), None)
    return jax.shard_map(
        functools.partial(per_device, mesh.shape["batch"], mesh.shape["tok"]),
        mesh=mesh,
        in_specs=(rows, P("batch", "tok"), rows, P(), P(), P(), weights, weights),
        out_specs=(rows, rows, P(), P(), P(), weights, weights),
        check_vma=False,
    )
```

```python
import functools
import math

import jax
import jax.numpy as jnp
import numpy as np
from jax import lax
from jax.experimental import pallas as pl
from jax.experimental.pallas import tpu as pltpu
from jax.sharding import PartitionSpec as P

H = 12
HD = 64
SLOTS = 4
EPS = 1e-06
BIG = 2048.0
LOG2E = 1.4426950408889634
BF = jnp.bfloat16
F32 = jnp.float32
NN = (((1,), (0,)), ((), ()))
NT = (((1,), (1,)), ((), ()))
TN = (((0,), (0,)), ((), ()))
MIB = 1 << 20

VMEM = pl.BlockSpec(memory_space=pltpu.VMEM)
SMEM = pl.BlockSpec(memory_space=pltpu.SMEM)
ANY = pl.BlockSpec(memory_space=pl.ANY)


def mm(a, b, dims=NN):
    return lax.dot_general(a, b, dims, preferred_element_type=F32)


def normalize(values):
    center = values - jnp.mean(values, axis=-1, keepdims=True)
    inverse = lax.rsqrt(jnp.mean(center * center, axis=-1, keepdims=True) + EPS)
    return center * inverse, inverse


def norm_back(grad_unit, unit_rows, inverse):
    return inverse * (
        grad_unit
        - jnp.mean(grad_unit, axis=-1, keepdims=True)
        - unit_rows * jnp.mean(grad_unit * unit_rows, axis=-1, keepdims=True)
    )


def column(row):
    return jnp.broadcast_to(row, (8, row.shape[1])).T[:, 0:1]


def before_kernel(at_ref, table_ref, ids_ref, x_ref, cot_ref, gain_ref, win_ref, wout_ref, *outs):
    seqs, part, _ = x_ref.shape
    pays, (src_ref, *unit_refs) = outs[:seqs], outs[seqs:]
    nt, rows = src_ref.shape[0], win_ref.shape[0]
    local = H * HD // nt
    units = (win_ref.shape[1] - 3 * H * HD) // nt
    for k, ref in enumerate(unit_refs):
        ref[...] = wout_ref[table_ref[at_ref[0], k]]
    for t in range(nt):
        for k in range(3):
            src_ref[t, :rows, k * local : (k + 1) * local] = win_ref[:, k * H * HD + t * local : k * H * HD + (t + 1) * local]
        src_ref[t, :rows, 3 * local :] = win_ref[:, 3 * H * HD + t * units : 3 * H * HD + (t + 1) * units]
        for s in range(seqs):
            src_ref[t, rows:, s * part : (s + 1) * part] = ids_ref[s : s + 1, :].astype(F32).astype(BF)
        src_ref[t, rows:, seqs * part :] = jnp.zeros((1, 3 * local + units - seqs * part), BF)
    for s, pay in enumerate(pays):
        unit, _ = normalize(x_ref[s].astype(F32))
        live = column(jnp.where(ids_ref[s : s + 1, :] >= 0, 1.0, 0.0))
        pay[0] = (unit * gain_ref[...]).astype(BF)
        pay[1] = (live * cot_ref[s].astype(F32)).astype(BF)


def before(at, table, ids, x, cot, gain, w_in, w_out):
    seqs, part, dim = x.shape
    per, unit, _ = w_out.shape
    rows, wide = w_in.shape
    outs = [jax.ShapeDtypeStruct((2, part, dim), BF)] * seqs
    outs += [jax.ShapeDtypeStruct((SLOTS, rows + 1, wide // SLOTS), BF)]
    outs += [jax.ShapeDtypeStruct((unit, dim), BF)] * per
    return pl.pallas_call(
        before_kernel,
        out_shape=outs,
        in_specs=[SMEM] * 2 + [VMEM] * 6,
        out_specs=[VMEM] * len(outs),
        cost_estimate=pl.CostEstimate(flops=x.size * 8, transcendentals=0, bytes_accessed=x.size * 8),
        compiler_params=pltpu.CompilerParams(vmem_limit_bytes=32 * MIB),
        name="before",
    )(at, table, ids, x, cot, gain, w_in, w_out)


def pack_kernel(at_ref, table_ref, win_ref, *refs):
    got, (a_ref, b_ref, ids_ref) = refs[:-3], refs[-3:]
    nt, rows = a_ref.shape[:2]
    per = len(got)
    local = a_ref.shape[2] // 4
    seqs, _, length = ids_ref.shape
    part = length // nt
    for t in range(nt):
        a_ref[t, :, : 3 * local] = win_ref[t, :rows, : 3 * local]
        b_ref[0, t] = win_ref[t, :rows, 3 * local :]
        row = win_ref[at_ref[1] ^ t, rows:, : seqs * part].astype(F32).astype(jnp.int32)
        for s in range(seqs):
            ids_ref[s, :, t * part : (t + 1) * part] = row[:, s * part : (s + 1) * part]
    for k, ref in enumerate(got):
        slot = table_ref[at_ref[0], per + k]

        @pl.when(slot == 0)
        def _():
            for c in range(nt):
                a_ref[c, :, 3 * local :] = ref[:, c * local : (c + 1) * local]

        @pl.when(slot > 0)
        def _():
            b_ref[1, jnp.maximum(slot, 1) - 1] = ref[...]


def pack(at, table, w_in, got, seqs, part):
    unit, dim = got[0].shape
    return pl.pallas_call(
        pack_kernel,
        out_shape=[
            jax.ShapeDtypeStruct((SLOTS, unit, dim), BF),
            jax.ShapeDtypeStruct((2, SLOTS, unit, dim), BF),
            jax.ShapeDtypeStruct((seqs, 1, SLOTS * part), jnp.int32),
        ],
        in_specs=[SMEM] * 2 + [VMEM] * (1 + len(got)),
        out_specs=[VMEM] * 3,
        cost_estimate=pl.CostEstimate(flops=1000, transcendentals=0, bytes_accessed=unit * dim * 60),
        name="pack",
    )(at, table, w_in, *got)


def join_kernel(at_ref, here_ref, there_ref, wqkv_ref, wo_ref, all_ref):
    halves, nt, unit, dim = here_ref.shape
    local = dim // nt
    high, low = at_ref[2] >> 1, at_ref[2] & 1
    for i in range(halves):
        all_ref[((high ^ i) << 1) | low] = here_ref[i]
        all_ref[((high ^ i) << 1) | (1 - low)] = there_ref[i]
    whole = all_ref[...]
    wqkv_ref[...] = whole.reshape(dim, dim)[:, : 3 * local].T
    for c in range(nt):
        wo_ref[:, c * local : (c + 1) * local] = whole[:, c, :, 3 * local :].reshape(2 * halves * unit, local)


def join(at, here, there):
    halves, nt, unit, dim = here.shape
    local = dim // nt
    return pl.pallas_call(
        join_kernel,
        out_shape=[jax.ShapeDtypeStruct((3 * local, dim), BF), jax.ShapeDtypeStruct((local, dim), BF)],
        in_specs=[SMEM, VMEM, VMEM],
        out_specs=[VMEM] * 2,
        scratch_shapes=[pltpu.VMEM((2 * halves, nt, unit, dim), BF)],
        cost_estimate=pl.CostEstimate(flops=1000, transcendentals=0, bytes_accessed=dim * dim * 8),
        compiler_params=pltpu.CompilerParams(vmem_limit_bytes=32 * MIB),
        name="join",
    )(at, here, there)


def resplit(total, rows):
    first = total[rows : rows + 1] + total[rows + 1 : rows + 2]
    second = total[rows + 2 : rows + 3] + total[rows + 3 : rows + 4]
    return term_rows(first, second)


def term_rows(first, second):
    def terms(v):
        hi = v.astype(BF).astype(F32)
        return [hi, (v - hi).astype(BF).astype(F32)]

    return jnp.concatenate(terms(first) + terms(second) + [jnp.zeros((4, first.shape[1]), F32)], axis=0)


def fold(rows, low, at, keep, got):
    n, high, dim = keep.shape

    def kernel(at_ref, keep_ref, *refs):
        got_refs, (own_ref, *send_refs) = refs[: len(got)], refs[len(got) :]
        mine = (at_ref[2] >> low) & 3
        for i in range(n // 4):
            for s, to in enumerate([own_ref] + send_refs):
                at_block = i * 4 + (mine ^ s)
                total = keep_ref[at_block]
                for ref in got_refs:
                    total = total + ref[at_block].astype(F32)
                if rows:
                    to[i, :rows] = total[:rows].astype(to.dtype)
                    to[i, rows:] = resplit(total, rows).astype(to.dtype)
                else:
                    to[i] = total.astype(to.dtype)

    out = lambda t: jax.ShapeDtypeStruct((n // 4, high, dim), t)
    return pl.pallas_call(
        kernel,
        out_shape=[out(F32)] + [out(BF)] * 3,
        in_specs=[SMEM] + [VMEM] * (1 + len(got)),
        out_specs=[VMEM] * 4,
        cost_estimate=pl.CostEstimate(flops=keep.size, transcendentals=0, bytes_accessed=keep.size * 8),
        compiler_params=pltpu.CompilerParams(vmem_limit_bytes=48 * MIB),
        name="fold",
    )(at, keep, *got)


def leave(at, table, a_parts, f_units, local):
    own = a_parts[0]
    per = f_units.shape[0] + 1
    _, unit, dim = f_units.shape
    rows = SLOTS * unit
    width = 3 * local

    def kernel(at_ref, table_ref, p0, p1, p2, p3, f_ref, src_ref, *outs):
        out_refs, (all_ref,) = outs[:-1], outs[-1:]
        total = (p0[0] + p1[0].astype(F32)) + (p2[0].astype(F32) + p3[0].astype(F32))
        first = total[rows : rows + 1] + total[rows + 1 : rows + 2]
        second = total[rows + 2 : rows + 3] + total[rows + 3 : rows + 4]
        for t in range(SLOTS):
            src_ref[t, :unit] = total[t * unit : (t + 1) * unit, :width]
            src_ref[t, unit : unit + 1] = first[:, :width]
            src_ref[t, unit + 1 : unit + 2] = jnp.concatenate(
                [first[:, width:], second[:, :128], jnp.zeros((1, 2 * width - dim - 128), F32)], axis=1
            )
        for c in range(SLOTS):
            all_ref[0, :, c * local : (c + 1) * local] = total[c * unit : (c + 1) * unit, width:]
        for k in range(per - 1):
            all_ref[k + 1] = f_ref[k]
        for k, ref in enumerate(out_refs):
            ref[...] = all_ref[table_ref[at_ref[0], per + k]]

    return pl.pallas_call(
        kernel,
        out_shape=[jax.ShapeDtypeStruct((SLOTS, unit + 2, width), F32)] + [jax.ShapeDtypeStruct((unit, dim), F32)] * per,
        in_specs=[SMEM] * 2 + [VMEM] * 5,
        out_specs=[VMEM] * (1 + per),
        scratch_shapes=[pltpu.VMEM((per, unit, dim), F32)],
        cost_estimate=pl.CostEstimate(flops=own.size, transcendentals=0, bytes_accessed=own.size * 20),
        name="leave",
    )(at, table, *a_parts, f_units)


def place(at, table, qkv, up, got):
    nt, high, width = qkv.shape
    unit, dim = got[0].shape
    per = len(got)
    local = width // 3
    wide = nt * (width + up.shape[2])

    def kernel(at_ref, table_ref, qkv_ref, up_ref, *refs):
        got_refs, (in_ref, out_ref, small_ref) = refs[:per], refs[per:]
        for t in range(nt):
            for k in range(3):
                in_ref[:, k * nt * local + t * local : k * nt * local + (t + 1) * local] = qkv_ref[t, :unit, k * local : (k + 1) * local]
            in_ref[:, nt * width + t * dim : nt * width + (t + 1) * dim] = up_ref[t]
        for k, ref in enumerate(got_refs):
            out_ref[table_ref[at_ref[0], k]] = ref[...]
        total = qkv_ref[0, unit:]
        for t in range(1, nt):
            total = total + qkv_ref[t, unit:]
        small_ref[:, :width] = total[0:1]
        small_ref[:, width:] = total[1:2, : dim + 128 - width]

    return pl.pallas_call(
        kernel,
        out_shape=[
            jax.ShapeDtypeStruct((unit, wide), F32),
            jax.ShapeDtypeStruct((per, unit, dim), F32),
            jax.ShapeDtypeStruct((1, dim + 128), F32),
        ],
        in_specs=[SMEM] * 2 + [VMEM] * (2 + per),
        out_specs=[VMEM] * 3,
        cost_estimate=pl.CostEstimate(flops=1000, transcendentals=0, bytes_accessed=unit * wide * 16),
        name="place",
    )(at, table, qkv, up, *got)


def after_kernel(s, ids_ref, x_ref, cot_ref, gain_ref, keep_ref, near_ref, far_ref, *rest):
    out_ref, grad_ref = rest[-2:]
    unit, inverse = normalize(x_ref[0].astype(F32))
    live = column(jnp.where(ids_ref[s : s + 1, :] >= 0, 1.0, 0.0))
    both = keep_ref[0].astype(F32) + near_ref[0].astype(F32) + far_ref[...].astype(F32)
    out_ref[0] = (live * (x_ref[0].astype(F32) + both[0])).astype(BF)
    grad_ref[0] = (
        live * cot_ref[0].astype(F32) + norm_back(both[1] * gain_ref[...], unit, inverse)
    ).astype(BF)


def after(s, ids, x, cot, gain, keep, near, far, earlier):
    seqs, part, dim = x.shape
    one = pl.BlockSpec((1, part, dim), lambda i: (s, 0, 0))
    pair = pl.BlockSpec((1, 2, part, dim), lambda i: (0, 0, 0, 0))
    fixed = lambda a: pl.BlockSpec(a.shape, lambda i: (0,) * a.ndim)
    return pl.pallas_call(
        functools.partial(after_kernel, s),
        grid=(1,),
        out_shape=[jax.ShapeDtypeStruct(x.shape, BF)] * 2,
        in_specs=[fixed(ids), one, one, fixed(gain), pair, pair, fixed(far)] + [ANY] * len(earlier),
        out_specs=[one, one],
        input_output_aliases={7 + i: i for i in range(len(earlier))},
        cost_estimate=pl.CostEstimate(flops=part * dim * 20, transcendentals=0, bytes_accessed=part * dim * 20),
        compiler_params=pltpu.CompilerParams(vmem_limit_bytes=32 * MIB),
        name="after",
    )(ids, x, cot, gain, keep, near, far, *earlier)


def split_rows(odd, grad, send_ref, keep_ref, parts, rows, store):
    for z in range(parts):
        low = grad[2 * z * rows : (2 * z + 1) * rows]
        high = grad[(2 * z + 1) * rows : (2 * z + 2) * rows]
        store(send_ref, z, jnp.where(odd, low, high).astype(BF))
        store(keep_ref, z, jnp.where(odd, high, low))


def attention_kernel(
    heads, block, first, last,
    odd_ref, ids_ref, wqkv_ref, wo_ref, qg_ref, kg_ref, *refs,
):
    pays, refs = refs[:SLOTS], refs[SLOTS:]
    if not first:
        (accq_ref, acco_ref, acc_sums_ref), refs = refs[:3], refs[3:]
    if last:
        (fnp_ref, gain_ref, o_ref, grad_ref, send_ref, keep_ref, sums_ref), refs = refs[:7], refs[7:]
    else:
        (o_ref, grad_ref, sums_ref, newq_ref, newo_ref), refs = refs[:5], refs[5:]
    norm_ref, gb_ref, raw_ref, qt_ref, qn_ref, kt_ref, ka_ref, vt_ref, va_ref, do_ref, dq_ref, dk_ref, dv_ref, pad_ref, vm_ref, sem = refs
    length, dim = norm_ref.shape
    part = length // SLOTS
    width = heads * HD
    blocks = length // block
    copies = []
    for j in range(2):
        for i, pay in enumerate(pays):
            to = (norm_ref, gb_ref)[j].at[pl.ds(i * part, part), :]
            copies.append(pltpu.make_async_copy(pay.at[j], to, sem.at[j * SLOTS + i]))
            copies[-1].start()
    ids = ids_ref[...]
    marks = lax.broadcasted_iota(jnp.int32, (HD, length), 0)
    same = marks == ids + 1
    k_tail = jnp.where(same, 1.0, 0.0).T.astype(BF)
    q_tail = jnp.where((same & (ids >= 0)) | (marks > 4), 0.0, -BIG).astype(BF)
    v_tail = jnp.where(lax.broadcasted_iota(jnp.int32, (length, HD), 1) < 2, 1.0, 0.0).astype(BF)
    ones = jnp.where(lax.broadcasted_iota(jnp.int32, (16, length), 0) == 0, 1.0, 0.0).astype(BF)
    pad = jnp.where(ids < 0, 1.0, 0.0)
    cut = lambda a, i: a[:, i * block : (i + 1) * block]
    for i in range(blocks):
        pad_ref[i] = cut(pad, i)
    for i in range(SLOTS):
        copies[i].wait()
    raw_ref[...] = mm(wqkv_ref[...], norm_ref[...], NT)
    for i in range(SLOTS):
        copies[SLOTS + i].wait()
    do_all = mm(wo_ref[...], gb_ref[...], NT).astype(BF)
    for h in range(heads):
        for i in range(blocks):
            do_ref[h * blocks + i] = cut(do_all[h * HD : (h + 1) * HD], i)
    gain_q = qg_ref[...]
    gain_k = kg_ref[...]

    def unit_of(row):
        raw = raw_ref[pl.ds(pl.multiple_of(row, HD), HD), :]
        center = raw - jnp.mean(raw, axis=0, keepdims=True)
        inverse = lax.rsqrt(jnp.mean(center * center, axis=0, keepdims=True) + EPS)
        return center * inverse, inverse

    def prepare(h, carry):
        q_unit, _ = unit_of(h * HD)
        q = q_unit * gain_q
        qn = q.T.astype(BF)
        for i in range(blocks):
            qt_ref[h * blocks + i, :HD] = cut(q, i).astype(BF)
            qt_ref[h * blocks + i, HD:] = cut(q_tail, i)
            qn_ref[h * blocks + i] = qn[i * block : (i + 1) * block]
        k_unit, _ = unit_of(width + h * HD)
        k = k_unit * gain_k
        kt_ref[h] = k.astype(BF)
        ka_ref[h, :, :HD] = k.T.astype(BF)
        ka_ref[h, :, HD:] = k_tail
        v = raw_ref[pl.ds(pl.multiple_of(2 * width + h * HD, HD), HD), :]
        vb = v.astype(BF)
        vt_ref[h, :HD] = vb
        vt_ref[h, HD:] = ones
        va_ref[h, :, :HD] = v.T.astype(BF)
        va_ref[h, :, HD:] = v_tail
        vm_ref[h] = jnp.mean(vb.astype(F32), axis=1, keepdims=True)
        dk_ref[h] = jnp.zeros(dk_ref.shape[1:], F32)
        dv_ref[h] = jnp.zeros(dv_ref.shape[1:], F32)
        return carry

    lax.fori_loop(0, heads, prepare, 0)
    spot = lax.broadcasted_iota(jnp.int32, (HD, block), 0)

    def step(n, carry):
        h = n // blocks
        padb = pad_ref[n % blocks]
        e = jnp.exp2(mm(ka_ref[h], qt_ref[n]) * (LOG2E / math.sqrt(HD)))
        eb = e.astype(BF)
        oa = mm(vt_ref[h], eb)
        inv = 1.0 / (oa[HD : HD + 1] + padb)
        o = oa[:HD] * inv
        dos = (do_ref[n].astype(F32) * inv).astype(BF)
        delta = jnp.sum(dos.astype(F32) * o, axis=0, keepdims=True)
        d0 = delta.astype(BF).astype(F32)
        tail = jnp.where(spot == 0, -d0, jnp.where(spot == 1, d0 - delta, 0.0))
        doa = jnp.concatenate([dos.astype(F32), tail], axis=0)
        ds = (e * mm(va_ref[h], doa.astype(BF))).astype(BF)
        dq_ref[n] = mm(kt_ref[h], ds)
        dk_ref[h] += mm(ds, qn_ref[n])
        dv_ref[h] += mm(eb, doa.T.astype(BF))
        do_ref[n] = jnp.where(padb > 0, vm_ref[h], o).astype(BF)
        return carry

    lax.fori_loop(0, heads * blocks, step, 0)
    scale = 1.0 / math.sqrt(HD)

    def lanes(a):
        total = a[:, :128]
        for i in range(1, length // 128):
            total = total + a[:, i * 128 : (i + 1) * 128]
        return total

    def finish(h, carry):
        rows = lambda at: pl.ds(pl.multiple_of(at + h * HD, HD), HD)
        gq = jnp.concatenate([dq_ref[h * blocks + i] for i in range(blocks)], axis=1)
        gk = dk_ref[h].T
        for k, (g, gain_col) in enumerate(((gq, gain_q), (gk, gain_k))):
            unit, inverse = unit_of(k * width + h * HD)
            g = (g * scale).astype(BF).astype(F32)
            sums_ref[k] += lanes(g * unit)
            g = g * gain_col
            back = inverse * (
                g - jnp.mean(g, axis=0, keepdims=True) - unit * jnp.mean(g * unit, axis=0, keepdims=True)
            )
            grad_ref[rows(k * width), :] = back.astype(BF)
        grad_ref[rows(2 * width), :] = dv_ref[h].T[:HD].astype(BF)
        for i in range(blocks):
            o_ref[rows(0), pl.ds(i * block, block)] = do_ref[h * blocks + i]
        return carry

    sums_ref[...] = jnp.zeros_like(sums_ref) if first else acc_sums_ref[...]
    lax.fori_loop(0, heads, finish, 0)
    g_q = mm(grad_ref[...], norm_ref[...])
    g_o = mm(o_ref[...], gb_ref[...])
    if not first:
        g_q = g_q + accq_ref[...]
        g_o = g_o + acco_ref[...]
    if not last:
        newq_ref[...] = g_q
        newo_ref[...] = g_o
        return
    first_row = (jnp.sum(wqkv_ref[...].astype(F32) * g_q, axis=0, keepdims=True) + fnp_ref[...]) / gain_ref[...]
    second_row = jnp.concatenate(
        [jnp.sum(sums_ref[k].T, axis=0, keepdims=True) for k in range(2)] + [jnp.zeros((1, dim - 2 * HD), F32)], axis=1
    )
    g_q = g_q.T
    odd = odd_ref[0] > 0
    parts, rows, _ = send_ref.shape
    rows = rows - 8
    extra = term_rows(first_row, second_row)
    for z in range(parts):
        send_ref[z, rows:] = extra.astype(BF)
        keep_ref[z, rows:] = extra
    unit = width // (2 * parts)

    def put_q(ref, z, value):
        ref[z, :rows, : 3 * width] = value

    def put_o(ref, z, value):
        for c in range(dim // width):
            ref[z, c * unit : (c + 1) * unit, 3 * width :] = value[:, c * width : (c + 1) * width]

    split_rows(odd, g_q, send_ref, keep_ref, parts, rows, put_q)
    split_rows(odd, g_o, send_ref, keep_ref, parts, unit, put_o)


def attention(odd, ids, wqkv, wo, qg, kg, pays, acc, last, halves, more=()):
    wide, dim = wqkv.shape
    width = wo.shape[0]
    heads = width // HD
    length = pays[0].shape[1] * SLOTS
    block = 512
    blocks = length // block
    first = acc is None
    ins = [odd, ids, wqkv, wo, qg, kg, *pays] + ([] if first else list(acc)) + list(more)
    specs = [SMEM] + [VMEM] * 5 + [ANY] * SLOTS + ([] if first else [VMEM] * 3) + [VMEM] * len(more)
    outs = [jax.ShapeDtypeStruct((width, length), BF), jax.ShapeDtypeStruct((wide, length), BF)]
    scratch = []
    if last:
        rows = dim // (2 * halves)
        outs += [
            jax.ShapeDtypeStruct((halves, rows + 8, wide + width), BF),
            jax.ShapeDtypeStruct((halves, rows + 8, wide + width), F32),
        ]
        scratch = [pltpu.VMEM((2, HD, 128), F32)]
    else:
        outs += [
            jax.ShapeDtypeStruct((2, HD, 128), F32),
            jax.ShapeDtypeStruct((wide, dim), F32),
            jax.ShapeDtypeStruct((width, dim), F32),
        ]
    flops = 2 * length * dim * width * 8 + heads * 6 * 2 * length * length * HD
    return pl.pallas_call(
        functools.partial(attention_kernel, heads, block, first, last),
        out_shape=outs,
        in_specs=specs,
        out_specs=[VMEM] * len(outs),
        scratch_shapes=scratch
        + [
            pltpu.VMEM((length, dim), BF),
            pltpu.VMEM((length, dim), BF),
            pltpu.VMEM((wide, length), F32),
            pltpu.VMEM((heads * blocks, 2 * HD, block), BF),
            pltpu.VMEM((heads * blocks, block, HD), BF),
            pltpu.VMEM((heads, HD, length), BF),
            pltpu.VMEM((heads, length, 2 * HD), BF),
            pltpu.VMEM((heads, HD + 16, length), BF),
            pltpu.VMEM((heads, length, 2 * HD), BF),
            pltpu.VMEM((heads * blocks, HD, block), BF),
            pltpu.VMEM((heads * blocks, HD, block), F32),
            pltpu.VMEM((heads, length, HD), F32),
            pltpu.VMEM((heads, length, 2 * HD), F32),
            pltpu.VMEM((blocks, 1, block), F32),
            pltpu.VMEM((heads, HD, 1), F32),
            pltpu.SemaphoreType.DMA((2 * SLOTS,)),
        ],
        cost_estimate=pl.CostEstimate(flops=flops * 3, transcendentals=heads * length * length, bytes_accessed=8 * length * dim),
        compiler_params=pltpu.CompilerParams(vmem_limit_bytes=56 * MIB),
        name="attention",
    )(*ins)


def ffn_kernel(count, at_ref, here_ref, there_ref, *refs):
    pays, refs = refs[:count], refs[count:]
    (hid_ref, gup_ref, send_ref, keep_ref, np_ref, wup_ref, wff_ref), refs = refs[:7], refs[7:]
    pay_ref, hidv_ref, gupv_ref, gin_ref, gff_ref, sem, out_sem, w_sem = refs
    dim = wup_ref.shape[0]
    halves = here_ref.shape[0]
    unit = dim // (2 * halves * SLOTS)
    copies = []
    for i in range(halves):
        for j, ref in enumerate((here_ref, there_ref)):
            b = (((at_ref[2] >> 1) ^ i) << 1) | ((at_ref[2] & 1) ^ j)
            for k, to in enumerate((wup_ref, wff_ref)):
                start = pl.multiple_of(b * SLOTS * unit, SLOTS * unit)
                copies.append(pltpu.make_async_copy(ref.at[i, k], to.at[pl.ds(start, SLOTS * unit), :], w_sem.at[(i * 2 + j) * 2 + k]))
                copies[-1].start()
    for i, pay in enumerate(pays):
        pltpu.make_async_copy(pay, pay_ref.at[i], sem.at[i]).start()
    for copy in copies:
        copy.wait()
    gin_ref[...] = jnp.zeros_like(gin_ref)
    gff_ref[...] = jnp.zeros_like(gff_ref)
    c0 = math.sqrt(2.0 / math.pi)
    c1 = 0.044715

    def outs(i):
        return (
            pltpu.make_async_copy(hidv_ref.at[i], hid_ref.at[i], out_sem.at[0, i]),
            pltpu.make_async_copy(gupv_ref.at[i], gup_ref.at[i], out_sem.at[1, i]),
        )

    def step(i, carry):
        pltpu.make_async_copy(pays[0], pay_ref.at[i], sem.at[i]).wait()
        normed = pay_ref[i, 0]
        gb = pay_ref[i, 1]
        up = mm(normed, wup_ref[...])
        gh = mm(gb, wff_ref[...], NT)
        sq = up * up
        t = jnp.tanh(up * (c0 + (c0 * c1) * sq))
        half = 0.5 + 0.5 * t
        hid = (up * half).astype(BF)
        gup = (gh * (half + (0.5 * up) * (1.0 - t * t) * (c0 + (3.0 * c0 * c1) * sq))).astype(BF)
        hidv_ref[i] = hid
        gupv_ref[i] = gup
        for copy in outs(i):
            copy.start()
        gin_ref[...] += mm(normed, gup, TN)
        gff_ref[...] += mm(hid, gb, TN)
        return carry

    lax.fori_loop(0, count, step, 0)
    odd = (at_ref[2] & 1) > 0
    parts, _, rows, _ = send_ref.shape
    line = jnp.sum(wup_ref[...].astype(F32) * gin_ref[...], axis=1, keepdims=True)
    np_ref[...] = jnp.broadcast_to(line, (dim, 128)).T[0:1]
    for k, g in enumerate((gin_ref, gff_ref)):

        def put(ref, z, value, k=k):
            ref[z, k] = value

        split_rows(odd, g[...], send_ref, keep_ref, parts, rows, put)

    def drain(i, carry):
        for copy in outs(i):
            copy.wait()
        return carry

    lax.fori_loop(0, count, drain, 0)


def ffn(at, here, there, pays):
    _, part, dim = pays[0].shape
    units = dim
    halves = here.shape[0]
    count = len(pays)
    rows = dim // (2 * halves)
    act = jax.ShapeDtypeStruct((count, part, units), BF)
    return pl.pallas_call(
        functools.partial(ffn_kernel, count),
        out_shape=[
            act,
            act,
            jax.ShapeDtypeStruct((halves, 2, rows, dim), BF),
            jax.ShapeDtypeStruct((halves, 2, rows, dim), F32),
            jax.ShapeDtypeStruct((1, dim), F32),
            jax.ShapeDtypeStruct((dim, units), BF),
            jax.ShapeDtypeStruct((units, dim), BF),
        ],
        in_specs=[SMEM] + [ANY] * (2 + count),
        out_specs=[ANY, ANY] + [VMEM] * 5,
        scratch_shapes=[
            pltpu.VMEM((count, 2, part, dim), BF),
            pltpu.VMEM((count, part, units), BF),
            pltpu.VMEM((count, part, units), BF),
            pltpu.VMEM((dim, units), F32),
            pltpu.VMEM((units, dim), F32),
            pltpu.SemaphoreType.DMA((count,)),
            pltpu.SemaphoreType.DMA((2, count)),
            pltpu.SemaphoreType.DMA((4 * halves,)),
        ],
        cost_estimate=pl.CostEstimate(
            flops=8 * count * part * dim * units, transcendentals=count * part * units, bytes_accessed=count * part * dim * 8
        ),
        compiler_params=pltpu.CompilerParams(vmem_limit_bytes=58 * MIB),
        name="ffn",
    )(at, here, there, *pays)


def out_kernel(o_ref, hid_ref, gq_ref, gu_ref, wo_ref, wff_ref, wqkv_ref, wup_ref, keep_ref, send_ref):
    branch = (mm(o_ref[...], wo_ref[...], TN) + mm(hid_ref[0], wff_ref[...])).astype(BF)
    gn = (mm(gq_ref[...], wqkv_ref[...], TN) + mm(gu_ref[0], wup_ref[...], NT)).astype(BF)
    away = pl.program_id(0) % 2

    @pl.when(away == 0)
    def _():
        keep_ref[0, 0] = branch
        keep_ref[0, 1] = gn

    @pl.when(away == 1)
    def _():
        send_ref[0, 0] = branch
        send_ref[0, 1] = gn


def outputs(s, o, hid, gq, gu, wo, wff, wqkv, wup):
    part, dim = hid.shape[1], wo.shape[1]
    row = lambda a: pl.BlockSpec((a.shape[0], part), lambda i: (0, i))
    act = pl.BlockSpec((1, part, hid.shape[2]), lambda i: (s * SLOTS + i, 0, 0))
    whole = lambda a: pl.BlockSpec(a.shape, lambda i: (0, 0), pipeline_mode=pl.Buffered(1))
    out = pl.BlockSpec((1, 2, part, dim), lambda i: (i // 2, 0, 0, 0))
    return pl.pallas_call(
        out_kernel,
        grid=(SLOTS,),
        out_shape=[jax.ShapeDtypeStruct((SLOTS // 2, 2, part, dim), BF)] * 2,
        in_specs=[row(o), act, row(gq), act, whole(wo), whole(wff), whole(wqkv), whole(wup)],
        out_specs=[out, out],
        cost_estimate=pl.CostEstimate(
            flops=2 * SLOTS * part * dim * (o.shape[0] + 2 * hid.shape[2] + gq.shape[0]),
            transcendentals=0, bytes_accessed=SLOTS * part * dim * 10),
        compiler_params=pltpu.CompilerParams(vmem_limit_bytes=40 * MIB),
        name="outputs",
    )(o, hid, gq, gu, wo, wff, wqkv, wup)


def swap(value, axis, count, mask):
    return lax.ppermute(value, axis, [(i, i ^ mask) for i in range(count)])


def bit_groups(count):
    bits = list(range(count.bit_length() - 1))[::-1]
    groups = []
    while bits:
        take = 2 if len(bits) > 1 else 1
        groups.append(bits[:take])
        bits = bits[take:]
    assert len(groups[-1]) == 1
    return groups


def tie(value, *after):
    return lax.optimization_barrier((value,) + after)[0]


def gather_high(block, count, bits):
    low = bits[-1]
    return [block] + [swap(block, "batch", count, s << low) for s in range(1, 1 << len(bits))]


def matchings(edges, devices, per_device):
    left = [[] for _ in range(devices)]
    for e, (source, _, _) in enumerate(edges):
        left[source].append(e)
    rounds = []
    for _ in range(per_device):
        owner = [-1] * devices

        def place(source, seen):
            for e in left[source]:
                target = edges[e][1]
                if target in seen:
                    continue
                seen.add(target)
                if owner[target] < 0 or place(edges[owner[target]][0], seen):
                    owner[target] = e
                    return True
            return False

        for source in range(devices):
            place(source, set())
        rounds.append(list(owner))
        for e in owner:
            left[edges[e][0]].remove(e)
    return rounds


def unit_plan(nb, nt, rows, width, hidden):
    unit = math.gcd(math.gcd(rows, width // nt), hidden // nt)
    per = rows // unit
    head_units, hid_units = width // nt // unit, hidden // nt // unit
    assert head_units == nb and hid_units % nb == 0
    c = hid_units // nb
    edges = []
    for t in range(nt):
        for b in range(nb):
            want = [t * head_units + b]
            want += [nt * head_units + t * hid_units + b * c + i for i in range(c)]
            for slot, u in enumerate(want):
                edges.append((u // per, b * nt + t, (u % per, slot)))
    table = np.zeros((nb * nt, 2 * per), np.int32)
    perms = []
    for k, owner in enumerate(matchings(edges, nb * nt, per)):
        perms.append([(edges[e][0], edges[e][1]) for e in owner])
        for e in owner:
            table[edges[e][0], k] = edges[e][2][0]
            table[edges[e][1], per + k] = edges[e][2][1]
    return unit, per, perms, table


def per_device(
    nb, nt, patches, image_ids, cotangent, norm_gain, query_gain, key_gain, in_weight, out_weight
):
    seqs, part, dim = patches.shape
    width = H * HD
    local = width // nt
    units = (in_weight.shape[1] - 3 * width) // nt
    halves = nb // 2
    rows_in = in_weight.shape[0]
    unit, per, perms, table = unit_plan(nb, nt, out_weight.shape[0], width, units * nt)
    assert nt == SLOTS and units == dim and unit == rows_in and dim == nt * local and per == nt + 1
    both = ("batch", "tok")
    me_b = lax.axis_index("batch")
    me_t = lax.axis_index("tok")
    at = jnp.stack([me_b * nt + me_t, me_t, me_b])
    odd = (me_b & 1).reshape(1)
    table = jnp.asarray(table)
    gain = norm_gain.reshape(1, dim)
    groups = bit_groups(nb)

    outs = before(at, table, image_ids, patches, cotangent, gain, in_weight, out_weight.reshape(per, unit, dim))
    pays, a2a_src, unit_sends = outs[:seqs], outs[seqs], outs[seqs + 1 :]
    far = [swap(pays[0], "tok", nt, 2)]
    w_in = lax.all_to_all(a2a_src, "tok", split_axis=0, concat_axis=0, tiled=True)
    got = [lax.ppermute(value, both, perm) for value, perm in zip(unit_sends, perms)]
    chunk_a, chunk_b, ids = pack(at, table, w_in, got, seqs, part)

    chunk_b = chunk_b.reshape(2, nt * unit, dim)
    held_a, held_b = chunk_a[None], chunk_b[None]
    for bits in groups[:-1]:
        parts = gather_high(held_a, nb, bits)
        held_a = jnp.stack(parts, axis=1).reshape((-1,) + chunk_a.shape)
        held_b = tie(held_b, parts[-1])
        parts = gather_high(held_b, nb, bits)
        held_b = jnp.stack(parts, axis=1).reshape((-1,) + chunk_b.shape)
    there_a = swap(held_a, "batch", nb, 1)
    there_b = swap(tie(held_b, there_a), "batch", nb, 1)
    wqkv, wo = join(at, held_a, there_a)

    pay_s = []
    for s in range(seqs):
        if s:
            far.append(swap(tie(pays[s], far[s - 1]), "tok", nt, 2))
        pay_s.append([pays[s], swap(pays[s], "tok", nt, 1), far[s], swap(far[s], "tok", nt, 1)])

    qg = query_gain.reshape(HD, 1)
    kg = key_gain.reshape(HD, 1)
    acc = None
    earlier = []
    behind = None
    for s in range(seqs):
        last = s == seqs - 1
        own = pay_s[s] if behind is None else [tie(pay_s[s][0], behind)] + pay_s[s][1:]
        att = attention(odd, ids[s], wqkv, wo, qg, kg, own, acc, last, halves, (f_np, gain) if last else ())
        if not last:
            acc = (att[3], att[4], att[2])
        if s == 0:
            pieces = [p for q in pay_s for p in q]
            pieces[0] = tie(pieces[0], att[0])
            hid, gup, f_send, f_keep, f_np, wup, wff = ffn(at, held_b, there_b, pieces)
        keep, send = outputs(s, att[0], hid, att[1], gup, wo, wff, wqkv, wup)
        behind = keep
        near = swap(send, "tok", nt, 1)
        away = swap((keep[1].astype(F32) + near[1].astype(F32)).astype(BF), "tok", nt, 2)
        earlier = after(s, image_ids, patches, cotangent, gain, keep, near, away, earlier)
    block_out, patch_grad = earlier
    _, _, a_send, a_keep = att

    def reduce_batch(send, keep, rows):
        flat = lambda a: a.reshape((a.shape[0], -1, dim))
        parts = [flat(keep), flat(swap(send, "batch", nb, 1))]
        for bits in groups[:-1][::-1]:
            own, *sends = fold(rows, bits[-1], at, parts[0], parts[1:])
            parts = [own] + [swap(value, "batch", nb, (s + 1) << bits[-1]) for s, value in enumerate(sends)]
        return parts

    f_parts = reduce_batch(f_send, f_keep, 0)
    f_mine = f_parts[0] + sum(p.astype(F32) for p in f_parts[1:])
    f_mine = f_mine.reshape(2, nt, unit, dim)
    up = lax.all_to_all(f_mine[0], "tok", split_axis=0, concat_axis=0, tiled=True)
    a_parts = reduce_batch(a_send, a_keep, nt * unit)
    src, *sends = leave(at, table, a_parts, f_mine[1], local)
    qkv = lax.all_to_all(src, "tok", split_axis=0, concat_axis=0, tiled=True)
    got = [lax.ppermute(v, both, [(b, a) for a, b in perm]) for v, perm in zip(sends, perms)]
    in_grad, out_grad, small = place(at, table, qkv, up, got)
    small = small[0]
    return (
        block_out,
        patch_grad,
        small[:dim],
        small[dim : dim + HD],
        small[dim + HD :],
        in_grad,
        out_grad.reshape(per * unit, dim),
    )


def solution(mesh):
    rows = P("batch", "tok", None)
    weights = P(("batch", "tok"), None)
    return jax.shard_map(
        functools.partial(per_device, mesh.shape["batch"], mesh.shape["tok"]),
        mesh=mesh,
        in_specs=(rows, P("batch", "tok"), rows, P(), P(), P(), weights, weights),
        out_specs=(rows, rows, P(), P(), P(), weights, weights),
        check_vma=False,
    )
```

```python
import functools
import math

import jax
import jax.numpy as jnp
import numpy as np
from jax import lax
from jax.experimental import pallas as pl
from jax.experimental.pallas import tpu as pltpu
from jax.sharding import PartitionSpec as P

H = 12
HD = 64
SLOTS = 4
EPS = 1e-06
BIG = 2048.0
LOG2E = 1.4426950408889634
BF = jnp.bfloat16
F32 = jnp.float32
NN = (((1,), (0,)), ((), ()))
NT = (((1,), (1,)), ((), ()))
TN = (((0,), (0,)), ((), ()))
MIB = 1 << 20

VMEM = pl.BlockSpec(memory_space=pltpu.VMEM)
SMEM = pl.BlockSpec(memory_space=pltpu.SMEM)
ANY = pl.BlockSpec(memory_space=pl.ANY)


def mm(a, b, dims=NN):
    return lax.dot_general(a, b, dims, preferred_element_type=F32)


def normalize(values):
    center = values - jnp.mean(values, axis=-1, keepdims=True)
    inverse = lax.rsqrt(jnp.mean(center * center, axis=-1, keepdims=True) + EPS)
    return center * inverse, inverse


def norm_back(grad_unit, unit_rows, inverse):
    return inverse * (
        grad_unit
        - jnp.mean(grad_unit, axis=-1, keepdims=True)
        - unit_rows * jnp.mean(grad_unit * unit_rows, axis=-1, keepdims=True)
    )


def column(row):
    return jnp.broadcast_to(row, (8, row.shape[1])).T[:, 0:1]


def before_kernel(at_ref, table_ref, ids_ref, gain_ref, x_hbm, cot_hbm, win_hbm, wout_hbm, *refs):
    outs, (x_ref, cot_ref, win_ref, wout_ref, pay_ref, in_sem, out_sem) = refs[:-7], refs[-7:]
    seqs, part, _ = x_ref.shape
    pays, (src_ref, *unit_refs) = outs[:2], outs[2:]
    ins = [
        pltpu.make_async_copy(a, b, in_sem.at[i])
        for i, (a, b) in enumerate(((win_hbm, win_ref), (wout_hbm, wout_ref), (x_hbm, x_ref), (cot_hbm, cot_ref)))
    ]
    for copy in ins:
        copy.start()
    nt, rows = src_ref.shape[0], win_ref.shape[0]
    local = H * HD // nt
    units = (win_ref.shape[1] - 3 * H * HD) // nt
    ins[0].wait()
    ins[1].wait()
    for k, ref in enumerate(unit_refs):
        ref[...] = wout_ref[table_ref[at_ref[0], k]]
    for t in range(nt):
        for k in range(3):
            src_ref[t, :rows, k * local : (k + 1) * local] = win_ref[:, k * H * HD + t * local : k * H * HD + (t + 1) * local]
        src_ref[t, :rows, 3 * local :] = win_ref[:, 3 * H * HD + t * units : 3 * H * HD + (t + 1) * units]
        for s in range(seqs):
            src_ref[t, rows:, s * part : (s + 1) * part] = ids_ref[s : s + 1, :].astype(F32).astype(BF)
        src_ref[t, rows:, seqs * part :] = jnp.zeros((1, 3 * local + units - seqs * part), BF)
    ins[2].wait()
    ins[3].wait()
    copies = []
    for s in range(seqs):
        unit, _ = normalize(x_ref[s].astype(F32))
        live = column(jnp.where(ids_ref[s : s + 1, :] >= 0, 1.0, 0.0))
        pay_ref[s, 0] = (unit * gain_ref[...]).astype(BF)
        pay_ref[s, 1] = (live * cot_ref[s].astype(F32)).astype(BF)
        copies.append(pltpu.make_async_copy(pay_ref.at[s], pays[0] if s == 0 else pays[1].at[s - 1], out_sem.at[s]))
        copies[-1].start()
    for copy in copies:
        copy.wait()


def before(at, table, ids, gain, x, cot, w_in, w_out):
    seqs, part, dim = x.shape
    per, unit, _ = w_out.shape
    rows, wide = w_in.shape
    outs = [jax.ShapeDtypeStruct((2, part, dim), BF), jax.ShapeDtypeStruct((seqs - 1, 2, part, dim), BF)]
    outs += [jax.ShapeDtypeStruct((SLOTS, rows + 1, wide // SLOTS), BF)]
    outs += [jax.ShapeDtypeStruct((unit, dim), BF)] * per
    return pl.pallas_call(
        before_kernel,
        out_shape=outs,
        in_specs=[SMEM] * 2 + [VMEM] * 2 + [ANY] * 4,
        out_specs=[ANY] * 2 + [VMEM] * (1 + per),
        scratch_shapes=[
            pltpu.VMEM(x.shape, BF),
            pltpu.VMEM(x.shape, BF),
            pltpu.VMEM(w_in.shape, BF),
            pltpu.VMEM(w_out.shape, BF),
            pltpu.VMEM((seqs, 2, part, dim), BF),
            pltpu.SemaphoreType.DMA((4,)),
            pltpu.SemaphoreType.DMA((seqs,)),
        ],
        cost_estimate=pl.CostEstimate(flops=x.size * 8, transcendentals=0, bytes_accessed=x.size * 8),
        compiler_params=pltpu.CompilerParams(vmem_limit_bytes=32 * MIB),
        name="before",
    )(at, table, ids, gain, x, cot, w_in, w_out)


def pack_kernel(at_ref, table_ref, win_ref, *refs):
    got, (a_ref, b_ref, ids_ref) = refs[:-3], refs[-3:]
    nt, rows = a_ref.shape[:2]
    per = len(got)
    local = a_ref.shape[2] // 4
    seqs, _, length = ids_ref.shape
    part = length // nt
    for t in range(nt):
        a_ref[t, :, : 3 * local] = win_ref[t, :rows, : 3 * local]
        b_ref[0, t] = win_ref[t, :rows, 3 * local :]
        row = win_ref[t, rows:, : seqs * part].astype(F32).astype(jnp.int32)
        for s in range(seqs):
            ids_ref[s, :, t * part : (t + 1) * part] = row[:, s * part : (s + 1) * part]
    for k, ref in enumerate(got):
        slot = table_ref[at_ref[0], per + k]

        @pl.when(slot == 0)
        def _():
            for c in range(nt):
                a_ref[c, :, 3 * local :] = ref[:, c * local : (c + 1) * local]

        @pl.when(slot > 0)
        def _():
            b_ref[1, jnp.maximum(slot, 1) - 1] = ref[...]


def pack(at, table, w_in, got, seqs, part):
    unit, dim = got[0].shape
    return pl.pallas_call(
        pack_kernel,
        out_shape=[
            jax.ShapeDtypeStruct((SLOTS, unit, dim), BF),
            jax.ShapeDtypeStruct((2, SLOTS, unit, dim), BF),
            jax.ShapeDtypeStruct((seqs, 1, SLOTS * part), jnp.int32),
        ],
        in_specs=[SMEM] * 2 + [VMEM] * (1 + len(got)),
        out_specs=[VMEM] * 3,
        cost_estimate=pl.CostEstimate(flops=1000, transcendentals=0, bytes_accessed=unit * dim * 60),
        name="pack",
    )(at, table, w_in, *got)


def join_kernel(at_ref, here_ref, there_ref, wqkv_ref, wo_ref, all_ref):
    halves, nt, unit, dim = here_ref.shape
    local = dim // nt
    high, low = at_ref[2] >> 1, at_ref[2] & 1
    for i in range(halves):
        all_ref[((high ^ i) << 1) | low] = here_ref[i]
        all_ref[((high ^ i) << 1) | (1 - low)] = there_ref[i]
    whole = all_ref[...]
    wqkv_ref[...] = whole.reshape(dim, dim)[:, : 3 * local].T
    for c in range(nt):
        wo_ref[:, c * local : (c + 1) * local] = whole[:, c, :, 3 * local :].reshape(2 * halves * unit, local)


def join(at, here, there):
    halves, nt, unit, dim = here.shape
    local = dim // nt
    return pl.pallas_call(
        join_kernel,
        out_shape=[jax.ShapeDtypeStruct((3 * local, dim), BF), jax.ShapeDtypeStruct((local, dim), BF)],
        in_specs=[SMEM, VMEM, VMEM],
        out_specs=[VMEM] * 2,
        scratch_shapes=[pltpu.VMEM((2 * halves, nt, unit, dim), BF)],
        cost_estimate=pl.CostEstimate(flops=1000, transcendentals=0, bytes_accessed=dim * dim * 8),
        compiler_params=pltpu.CompilerParams(vmem_limit_bytes=32 * MIB),
        name="join",
    )(at, here, there)


def resplit(total, rows):
    first = total[rows : rows + 1] + total[rows + 1 : rows + 2]
    second = total[rows + 2 : rows + 3] + total[rows + 3 : rows + 4]
    return term_rows(first, second)


def term_rows(first, second):
    def terms(v):
        hi = v.astype(BF).astype(F32)
        return [hi, (v - hi).astype(BF).astype(F32)]

    return jnp.concatenate(terms(first) + terms(second) + [jnp.zeros((4, first.shape[1]), F32)], axis=0)


def fold(rows, low, at, keep, got):
    n, high, dim = keep.shape

    def kernel(at_ref, keep_ref, *refs):
        got_refs, (own_ref, *send_refs) = refs[: len(got)], refs[len(got) :]
        mine = (at_ref[2] >> low) & 3
        for i in range(n // 4):
            for s, to in enumerate([own_ref] + send_refs):
                at_block = i * 4 + (mine ^ s)
                total = keep_ref[at_block]
                for ref in got_refs:
                    total = total + ref[at_block].astype(F32)
                if rows:
                    to[i, :rows] = total[:rows].astype(to.dtype)
                    to[i, rows:] = resplit(total, rows).astype(to.dtype)
                else:
                    to[i] = total.astype(to.dtype)

    out = lambda t: jax.ShapeDtypeStruct((n // 4, high, dim), t)
    return pl.pallas_call(
        kernel,
        out_shape=[out(F32)] + [out(BF)] * 3,
        in_specs=[SMEM] + [VMEM] * (1 + len(got)),
        out_specs=[VMEM] * 4,
        cost_estimate=pl.CostEstimate(flops=keep.size, transcendentals=0, bytes_accessed=keep.size * 8),
        compiler_params=pltpu.CompilerParams(vmem_limit_bytes=48 * MIB),
        name="fold",
    )(at, keep, *got)


def leave(at, table, a_parts, f_units, local):
    own = a_parts[0]
    per = f_units.shape[0] + 1
    _, unit, dim = f_units.shape
    rows = SLOTS * unit
    width = 3 * local

    def kernel(at_ref, table_ref, p0, p1, p2, p3, f_ref, src_ref, *outs):
        out_refs, (all_ref,) = outs[:-1], outs[-1:]
        total = (p0[0] + p1[0].astype(F32)) + (p2[0].astype(F32) + p3[0].astype(F32))
        first = total[rows : rows + 1] + total[rows + 1 : rows + 2]
        second = total[rows + 2 : rows + 3] + total[rows + 3 : rows + 4]
        for t in range(SLOTS):
            src_ref[t, :unit] = total[t * unit : (t + 1) * unit, :width]
            src_ref[t, unit : unit + 1] = first[:, :width]
            src_ref[t, unit + 1 : unit + 2] = jnp.concatenate(
                [first[:, width:], second[:, :128], jnp.zeros((1, 2 * width - dim - 128), F32)], axis=1
            )
        for c in range(SLOTS):
            all_ref[0, :, c * local : (c + 1) * local] = total[c * unit : (c + 1) * unit, width:]
        for k in range(per - 1):
            all_ref[k + 1] = f_ref[k].astype(F32)
        for k, ref in enumerate(out_refs):
            ref[...] = all_ref[table_ref[at_ref[0], per + k]]

    return pl.pallas_call(
        kernel,
        out_shape=[jax.ShapeDtypeStruct((SLOTS, unit + 2, width), F32)] + [jax.ShapeDtypeStruct((unit, dim), F32)] * per,
        in_specs=[SMEM] * 2 + [VMEM] * 5,
        out_specs=[VMEM] * (1 + per),
        scratch_shapes=[pltpu.VMEM((per, unit, dim), F32)],
        cost_estimate=pl.CostEstimate(flops=own.size, transcendentals=0, bytes_accessed=own.size * 20),
        name="leave",
    )(at, table, *a_parts, f_units)


def place(at, table, qkv, up, got):
    nt, high, width = qkv.shape
    unit, dim = got[0].shape
    per = len(got)
    local = width // 3
    wide = nt * (width + up.shape[2])

    def kernel(at_ref, table_ref, qkv_ref, up_ref, *refs):
        got_refs, (in_ref, out_ref, small_ref) = refs[:per], refs[per:]
        for t in range(nt):
            for k in range(3):
                in_ref[:, k * nt * local + t * local : k * nt * local + (t + 1) * local] = qkv_ref[t, :unit, k * local : (k + 1) * local]
            in_ref[:, nt * width + t * dim : nt * width + (t + 1) * dim] = up_ref[t].astype(F32)
        for k, ref in enumerate(got_refs):
            out_ref[table_ref[at_ref[0], k]] = ref[...]
        total = qkv_ref[0, unit:]
        for t in range(1, nt):
            total = total + qkv_ref[t, unit:]
        small_ref[:, :width] = total[0:1]
        small_ref[:, width:] = total[1:2, : dim + 128 - width]

    return pl.pallas_call(
        kernel,
        out_shape=[
            jax.ShapeDtypeStruct((unit, wide), F32),
            jax.ShapeDtypeStruct((per, unit, dim), F32),
            jax.ShapeDtypeStruct((1, dim + 128), F32),
        ],
        in_specs=[SMEM] * 2 + [VMEM] * (2 + per),
        out_specs=[VMEM] * 3,
        cost_estimate=pl.CostEstimate(flops=1000, transcendentals=0, bytes_accessed=unit * wide * 16),
        name="place",
    )(at, table, qkv, up, *got)


def after_kernel(s, ids_ref, x_ref, cot_ref, gain_ref, keep_ref, near_ref, far_ref, *rest):
    out_ref, grad_ref = rest[-2:]
    unit, inverse = normalize(x_ref[0].astype(F32))
    live = column(jnp.where(ids_ref[s : s + 1, :] >= 0, 1.0, 0.0))
    both = keep_ref[0].astype(F32) + near_ref[0].astype(F32) + far_ref[...].astype(F32)
    out_ref[0] = (live * (x_ref[0].astype(F32) + both[0])).astype(BF)
    grad_ref[0] = (
        live * cot_ref[0].astype(F32) + norm_back(both[1] * gain_ref[...], unit, inverse)
    ).astype(BF)


def after(s, ids, x, cot, gain, keep, near, far, earlier):
    seqs, part, dim = x.shape
    one = pl.BlockSpec((1, part, dim), lambda i: (s, 0, 0))
    pair = pl.BlockSpec((1, 2, part, dim), lambda i: (0, 0, 0, 0))
    fixed = lambda a: pl.BlockSpec(a.shape, lambda i: (0,) * a.ndim)
    return pl.pallas_call(
        functools.partial(after_kernel, s),
        grid=(1,),
        out_shape=[jax.ShapeDtypeStruct(x.shape, BF)] * 2,
        in_specs=[fixed(ids), one, one, fixed(gain), pair, pair, fixed(far)] + [ANY] * len(earlier),
        out_specs=[one, one],
        input_output_aliases={7 + i: i for i in range(len(earlier))},
        cost_estimate=pl.CostEstimate(flops=part * dim * 20, transcendentals=0, bytes_accessed=part * dim * 20),
        compiler_params=pltpu.CompilerParams(vmem_limit_bytes=32 * MIB),
        name="after",
    )(ids, x, cot, gain, keep, near, far, *earlier)


def split_rows(odd, grad, send_ref, keep_ref, parts, rows, store):
    for z in range(parts):
        low = grad[2 * z * rows : (2 * z + 1) * rows]
        high = grad[(2 * z + 1) * rows : (2 * z + 2) * rows]
        store(send_ref, z, jnp.where(odd, low, high).astype(BF))
        store(keep_ref, z, jnp.where(odd, high, low))


def attention_kernel(
    heads, block, first, last,
    lead, odd_ref, ids_ref, qg_ref, kg_ref, wqkv_hbm, wo_hbm, pay_hbm, *refs,
):
    if not first:
        (acc_sums_ref, accq_hbm, acco_hbm), refs = refs[:3], refs[3:]
    if last:
        (fnp_ref, gain_ref, o_hbm, grad_hbm, send_ref, keep_ref, sums_ref), refs = refs[:7], refs[7:]
    else:
        (o_hbm, grad_hbm, sums_ref, newq_hbm, newo_hbm), refs = refs[:5], refs[5:]
    wqkv_ref, wo_ref, o_ref, grad_ref, accq_ref, acco_ref, w_sem, norm_ref, gb_ref, raw_ref, qt_ref, qn_ref, kt_ref, ka_ref, vt_ref, va_ref, do_ref, dq_ref, dk_ref, dv_ref, pad_ref, vm_ref, sem = refs
    length, dim = norm_ref.shape
    part = length // SLOTS
    width = heads * HD
    blocks = length // block
    loads = [pltpu.make_async_copy(wqkv_hbm, wqkv_ref, w_sem.at[0])]
    loads[0].start()
    copies = []
    for j in range(2):
        for i in range(SLOTS):
            to = (norm_ref, gb_ref)[j].at[pl.ds(i * part, part), :]
            copies.append(pltpu.make_async_copy(pay_hbm.at[(i,) + lead + (j,)], to, sem.at[j * SLOTS + i]))
            copies[-1].start()
    loads.append(pltpu.make_async_copy(wo_hbm, wo_ref, w_sem.at[1]))
    loads[1].start()
    if not first:
        loads.append(pltpu.make_async_copy(accq_hbm, accq_ref, w_sem.at[2]))
        loads.append(pltpu.make_async_copy(acco_hbm, acco_ref, w_sem.at[3]))
        loads[2].start()
        loads[3].start()
    ids = ids_ref[...]
    marks = lax.broadcasted_iota(jnp.int32, (HD, length), 0)
    same = marks == ids + 1
    k_tail = jnp.where(same, 1.0, 0.0).T.astype(BF)
    q_tail = jnp.where((same & (ids >= 0)) | (marks > 4), 0.0, -BIG).astype(BF)
    v_tail = jnp.where(lax.broadcasted_iota(jnp.int32, (length, HD), 1) < 2, 1.0, 0.0).astype(BF)
    ones = jnp.where(lax.broadcasted_iota(jnp.int32, (16, length), 0) == 0, 1.0, 0.0).astype(BF)
    pad = jnp.where(ids < 0, 1.0, 0.0)
    cut = lambda a, i: a[:, i * block : (i + 1) * block]
    for i in range(blocks):
        pad_ref[i] = cut(pad, i)
    loads[0].wait()
    for i in range(SLOTS):
        copies[i].wait()
    raw_ref[...] = mm(wqkv_ref[...], norm_ref[...], NT)
    loads[1].wait()
    for i in range(SLOTS):
        copies[SLOTS + i].wait()
    do_all = mm(wo_ref[...], gb_ref[...], NT).astype(BF)
    for h in range(heads):
        for i in range(blocks):
            do_ref[h * blocks + i] = cut(do_all[h * HD : (h + 1) * HD], i)
    gain_q = qg_ref[...]
    gain_k = kg_ref[...]

    def unit_of(row):
        raw = raw_ref[pl.ds(pl.multiple_of(row, HD), HD), :]
        center = raw - jnp.mean(raw, axis=0, keepdims=True)
        inverse = lax.rsqrt(jnp.mean(center * center, axis=0, keepdims=True) + EPS)
        return center * inverse, inverse

    def prepare(h, carry):
        q_unit, _ = unit_of(h * HD)
        q = q_unit * gain_q
        qn = q.T.astype(BF)
        for i in range(blocks):
            qt_ref[h * blocks + i, :HD] = cut(q, i).astype(BF)
            qt_ref[h * blocks + i, HD:] = cut(q_tail, i)
            qn_ref[h * blocks + i] = qn[i * block : (i + 1) * block]
        k_unit, _ = unit_of(width + h * HD)
        k = k_unit * gain_k
        kt_ref[h] = k.astype(BF)
        ka_ref[h, :, :HD] = k.T.astype(BF)
        ka_ref[h, :, HD:] = k_tail
        v = raw_ref[pl.ds(pl.multiple_of(2 * width + h * HD, HD), HD), :]
        vb = v.astype(BF)
        vt_ref[h, :HD] = vb
        vt_ref[h, HD:] = ones
        va_ref[h, :, :HD] = v.T.astype(BF)
        va_ref[h, :, HD:] = v_tail
        vm_ref[h] = jnp.mean(vb.astype(F32), axis=1, keepdims=True)
        dk_ref[h] = jnp.zeros(dk_ref.shape[1:], F32)
        dv_ref[h] = jnp.zeros(dv_ref.shape[1:], F32)
        return carry

    lax.fori_loop(0, heads, prepare, 0)
    spot = lax.broadcasted_iota(jnp.int32, (HD, block), 0)

    def step(n, carry):
        h = n // blocks
        padb = pad_ref[n % blocks]
        e = jnp.exp2(mm(ka_ref[h], qt_ref[n]) * (LOG2E / math.sqrt(HD)))
        eb = e.astype(BF)
        oa = mm(vt_ref[h], eb)
        inv = 1.0 / (oa[HD : HD + 1] + padb)
        o = oa[:HD] * inv
        dos = (do_ref[n].astype(F32) * inv).astype(BF)
        delta = jnp.sum(dos.astype(F32) * o, axis=0, keepdims=True)
        d0 = delta.astype(BF).astype(F32)
        tail = jnp.where(spot == 0, -d0, jnp.where(spot == 1, d0 - delta, 0.0))
        doa = jnp.concatenate([dos.astype(F32), tail], axis=0)
        ds = (e * mm(va_ref[h], doa.astype(BF))).astype(BF)
        dq_ref[n] = mm(kt_ref[h], ds)
        dk_ref[h] += mm(ds, qn_ref[n])
        dv_ref[h] += mm(eb, doa.T.astype(BF))
        do_ref[n] = jnp.where(padb > 0, vm_ref[h], o).astype(BF)
        return carry

    lax.fori_loop(0, heads * blocks, step, 0)
    scale = 1.0 / math.sqrt(HD)

    def lanes(a):
        total = a[:, :128]
        for i in range(1, length // 128):
            total = total + a[:, i * 128 : (i + 1) * 128]
        return total

    def finish(h, carry):
        rows = lambda at: pl.ds(pl.multiple_of(at + h * HD, HD), HD)
        gq = jnp.concatenate([dq_ref[h * blocks + i] for i in range(blocks)], axis=1)
        gk = dk_ref[h].T
        for k, (g, gain_col) in enumerate(((gq, gain_q), (gk, gain_k))):
            unit, inverse = unit_of(k * width + h * HD)
            g = (g * scale).astype(BF).astype(F32)
            sums_ref[k] += lanes(g * unit)
            g = g * gain_col
            back = inverse * (
                g - jnp.mean(g, axis=0, keepdims=True) - unit * jnp.mean(g * unit, axis=0, keepdims=True)
            )
            grad_ref[rows(k * width), :] = back.astype(BF)
        grad_ref[rows(2 * width), :] = dv_ref[h].T[:HD].astype(BF)
        for i in range(blocks):
            o_ref[rows(0), pl.ds(i * block, block)] = do_ref[h * blocks + i]
        return carry

    sums_ref[...] = jnp.zeros_like(sums_ref) if first else acc_sums_ref[...]
    lax.fori_loop(0, heads, finish, 0)
    stores = [pltpu.make_async_copy(o_ref, o_hbm, w_sem.at[4]), pltpu.make_async_copy(grad_ref, grad_hbm, w_sem.at[5])]
    stores[0].start()
    stores[1].start()
    g_q = mm(grad_ref[...], norm_ref[...])
    g_o = mm(o_ref[...], gb_ref[...])
    if not first:
        loads[2].wait()
        loads[3].wait()
        g_q = g_q + accq_ref[...]
        g_o = g_o + acco_ref[...]
    if not last:
        accq_ref[...] = g_q
        acco_ref[...] = g_o
        stores += [pltpu.make_async_copy(accq_ref, newq_hbm, w_sem.at[6]), pltpu.make_async_copy(acco_ref, newo_hbm, w_sem.at[7])]
        stores[2].start()
        stores[3].start()
        for copy in stores:
            copy.wait()
        return
    for copy in stores:
        copy.wait()
    first_row = (jnp.sum(wqkv_ref[...].astype(F32) * g_q, axis=0, keepdims=True) + fnp_ref[...]) / gain_ref[...]
    second_row = jnp.concatenate(
        [jnp.sum(sums_ref[k].T, axis=0, keepdims=True) for k in range(2)] + [jnp.zeros((1, dim - 2 * HD), F32)], axis=1
    )
    g_q = g_q.T
    odd = odd_ref[0] > 0
    parts, rows, _ = send_ref.shape
    rows = rows - 8
    extra = term_rows(first_row, second_row)
    for z in range(parts):
        send_ref[z, rows:] = extra.astype(BF)
        keep_ref[z, rows:] = extra
    unit = width // (2 * parts)

    def put_q(ref, z, value):
        ref[z, :rows, : 3 * width] = value

    def put_o(ref, z, value):
        for c in range(dim // width):
            ref[z, c * unit : (c + 1) * unit, 3 * width :] = value[:, c * width : (c + 1) * width]

    split_rows(odd, g_q, send_ref, keep_ref, parts, rows, put_q)
    split_rows(odd, g_o, send_ref, keep_ref, parts, unit, put_o)


def attention(odd, ids, wqkv, wo, qg, kg, pay, lead, acc, last, halves, more=()):
    wide, dim = wqkv.shape
    width = wo.shape[0]
    heads = width // HD
    length = pay.shape[-2] * SLOTS
    block = 512
    blocks = length // block
    first = acc is None
    ins = [odd, ids, qg, kg, wqkv, wo, pay] + ([] if first else list(acc)) + list(more)
    specs = [SMEM] + [VMEM] * 3 + [ANY] * 3 + ([] if first else [VMEM, ANY, ANY]) + [VMEM] * len(more)
    outs = [jax.ShapeDtypeStruct((width, length), BF), jax.ShapeDtypeStruct((wide, length), BF)]
    scratch = []
    if last:
        rows = dim // (2 * halves)
        outs += [
            jax.ShapeDtypeStruct((halves, rows + 8, wide + width), BF),
            jax.ShapeDtypeStruct((halves, rows + 8, wide + width), F32),
        ]
        scratch = [pltpu.VMEM((2, HD, 128), F32)]
    else:
        outs += [
            jax.ShapeDtypeStruct((2, HD, 128), F32),
            jax.ShapeDtypeStruct((wide, dim), F32),
            jax.ShapeDtypeStruct((width, dim), F32),
        ]
    flops = 2 * length * dim * width * 8 + heads * 6 * 2 * length * length * HD
    return pl.pallas_call(
        functools.partial(attention_kernel, heads, block, first, last, lead),
        out_shape=outs,
        in_specs=specs,
        out_specs=[ANY] * 2 + ([VMEM] * 2 if last else [VMEM, ANY, ANY]),
        scratch_shapes=scratch
        + [
            pltpu.VMEM((wide, dim), BF),
            pltpu.VMEM((width, dim), BF),
            pltpu.VMEM((width, length), BF),
            pltpu.VMEM((wide, length), BF),
            pltpu.VMEM((wide, dim), F32),
            pltpu.VMEM((width, dim), F32),
            pltpu.SemaphoreType.DMA((8,)),
            pltpu.VMEM((length, dim), BF),
            pltpu.VMEM((length, dim), BF),
            pltpu.VMEM((wide, length), F32),
            pltpu.VMEM((heads * blocks, 2 * HD, block), BF),
            pltpu.VMEM((heads * blocks, block, HD), BF),
            pltpu.VMEM((heads, HD, length), BF),
            pltpu.VMEM((heads, length, 2 * HD), BF),
            pltpu.VMEM((heads, HD + 16, length), BF),
            pltpu.VMEM((heads, length, 2 * HD), BF),
            pltpu.VMEM((heads * blocks, HD, block), BF),
            pltpu.VMEM((heads * blocks, HD, block), F32),
            pltpu.VMEM((heads, length, HD), F32),
            pltpu.VMEM((heads, length, 2 * HD), F32),
            pltpu.VMEM((blocks, 1, block), F32),
            pltpu.VMEM((heads, HD, 1), F32),
            pltpu.SemaphoreType.DMA((2 * SLOTS,)),
        ],
        cost_estimate=pl.CostEstimate(flops=flops * 3, transcendentals=heads * length * length, bytes_accessed=8 * length * dim),
        compiler_params=pltpu.CompilerParams(vmem_limit_bytes=56 * MIB),
        name="attention",
    )(*ins)


def ffn_kernel(block, at_ref, here_ref, there_ref, pay0_hbm, pay1_hbm, *refs):
    (hid_hbm, gup_hbm, wup_hbm, wff_hbm, send_ref, np_ref), refs = refs[:6], refs[6:]
    norm_ref, gb_ref, hid_ref, gup_ref, wup_ref, wff_ref, gin_ref, gff_ref, sem, out_sem, w_sem = refs
    dim = wup_ref.shape[0]
    halves = here_ref.shape[0]
    rows = dim // (2 * halves)
    part = pay0_hbm.shape[2]
    seqs = 1 + pay1_hbm.shape[1]
    length = SLOTS * part
    total = norm_ref.shape[0]
    copies = []
    for i in range(halves):
        for j, ref in enumerate((here_ref, there_ref)):
            b = (((at_ref[2] >> 1) ^ i) << 1) | ((at_ref[2] & 1) ^ j)
            for k, to in enumerate((wup_ref, wff_ref)):
                start = pl.multiple_of(b * rows, rows)
                copies.append(pltpu.make_async_copy(ref.at[i, k], to.at[pl.ds(start, rows), :], w_sem.at[(i * 2 + j) * 2 + k]))
                copies[-1].start()
    for s in range(seqs):
        for t in range(SLOTS):
            at_rows = pl.ds((s * SLOTS + t) * part, part)
            for k, to in enumerate((norm_ref, gb_ref)):
                source = pay0_hbm.at[t, k] if s == 0 else pay1_hbm.at[t, s - 1, k]
                pltpu.make_async_copy(source, to.at[at_rows, :], sem.at[s * SLOTS + t]).start()
    gin_ref[...] = jnp.zeros_like(gin_ref)
    gff_ref[...] = jnp.zeros_like(gff_ref)
    for copy in copies:
        copy.wait()
    weights = [pltpu.make_async_copy(wup_ref, wup_hbm, w_sem.at[0]), pltpu.make_async_copy(wff_ref, wff_hbm, w_sem.at[1])]
    for copy in weights:
        copy.start()
    c0 = math.sqrt(2.0 / math.pi)
    c1 = 0.044715

    def outs(i):
        at_rows = pl.ds(pl.multiple_of(i * block, block), block)
        return (
            pltpu.make_async_copy(hid_ref.at[at_rows, :], hid_hbm.at[at_rows, :], out_sem.at[0, i]),
            pltpu.make_async_copy(gup_ref.at[at_rows, :], gup_hbm.at[at_rows, :], out_sem.at[1, i]),
        )

    def step(i, carry):
        for k in range(block // part):
            for to in (norm_ref, gb_ref):
                pltpu.make_async_copy(pay0_hbm.at[0, 0], to.at[pl.ds(0, part), :], sem.at[i * (block // part) + k]).wait()
        at_rows = pl.ds(pl.multiple_of(i * block, block), block)
        up = mm(norm_ref[at_rows, :], wup_ref[...])
        gh = mm(gb_ref[at_rows, :], wff_ref[...], NT)
        sq = up * up
        t = jnp.tanh(up * (c0 + (c0 * c1) * sq))
        half = 0.5 + 0.5 * t
        hid_ref[at_rows, :] = (up * half).astype(BF)
        gup_ref[at_rows, :] = (gh * (half + (0.5 * up) * (1.0 - t * t) * (c0 + (3.0 * c0 * c1) * sq))).astype(BF)
        for copy in outs(i):
            copy.start()
        gin_ref[...] += mm(norm_ref[at_rows, :], gup_ref[at_rows, :], TN)
        gff_ref[...] += mm(hid_ref[at_rows, :], gb_ref[at_rows, :], TN)
        return carry

    lax.fori_loop(0, total // block, step, 0)
    line = jnp.sum(wup_ref[...].astype(F32) * gin_ref[...], axis=1, keepdims=True)
    np_ref[...] = jnp.broadcast_to(line, (dim, 128)).T[0:1]
    for b in range(2 * halves):
        for k, g in enumerate((gin_ref, gff_ref)):
            send_ref[b, k] = g[b * rows : (b + 1) * rows, :].astype(BF)
    for copy in weights:
        copy.wait()

    def drain(i, carry):
        for copy in outs(i):
            copy.wait()
        return carry

    lax.fori_loop(0, total // block, drain, 0)


def ffn(at, here, there, pay0, pay1, block=512):
    _, _, part, dim = pay0.shape
    units = dim
    halves = here.shape[0]
    total = SLOTS * part * (1 + pay1.shape[1])
    rows = dim // (2 * halves)
    act = jax.ShapeDtypeStruct((total, units), BF)
    return pl.pallas_call(
        functools.partial(ffn_kernel, block),
        out_shape=[
            act,
            act,
            jax.ShapeDtypeStruct((dim, units), BF),
            jax.ShapeDtypeStruct((units, dim), BF),
            jax.ShapeDtypeStruct((2 * halves, 2, rows, dim), BF),
            jax.ShapeDtypeStruct((1, dim), F32),
        ],
        in_specs=[SMEM] + [ANY] * 4,
        out_specs=[ANY] * 4 + [VMEM] * 2,
        scratch_shapes=[
            pltpu.VMEM((total, dim), BF),
            pltpu.VMEM((total, dim), BF),
            pltpu.VMEM((total, units), BF),
            pltpu.VMEM((total, units), BF),
            pltpu.VMEM((dim, units), BF),
            pltpu.VMEM((units, dim), BF),
            pltpu.VMEM((dim, units), F32),
            pltpu.VMEM((units, dim), F32),
            pltpu.SemaphoreType.DMA((total // part,)),
            pltpu.SemaphoreType.DMA((2, total // block)),
            pltpu.SemaphoreType.DMA((4 * halves,)),
        ],
        cost_estimate=pl.CostEstimate(flops=8 * total * dim * units, transcendentals=total * units, bytes_accessed=total * dim * 8),
        compiler_params=pltpu.CompilerParams(vmem_limit_bytes=58 * MIB),
        name="ffn",
    )(at, here, there, pay0, pay1)


def out_kernel(at_ref, o_ref, hid_ref, gq_ref, gu_ref, wo_ref, wff_ref, wqkv_ref, wup_ref, keep_ref, send_ref):
    branch = (mm(o_ref[...], wo_ref[...], TN) + mm(hid_ref[...], wff_ref[...])).astype(BF)
    gn = (mm(gq_ref[...], wqkv_ref[...], TN) + mm(gu_ref[...], wup_ref[...], NT)).astype(BF)
    away = pl.program_id(0) % 2

    @pl.when(away == 0)
    def _():
        keep_ref[0, 0] = branch
        keep_ref[0, 1] = gn

    @pl.when(away == 1)
    def _():
        send_ref[0, 0] = branch
        send_ref[0, 1] = gn


def outputs(s, at, o, hid, gq, gu, wo, wff, wqkv, wup):
    dim = wo.shape[1]
    part = o.shape[1] // SLOTS
    row = lambda a: pl.BlockSpec((a.shape[0], part), lambda i, at: (0, at[1] ^ i))
    act = pl.BlockSpec((part, hid.shape[1]), lambda i, at: (s * SLOTS + (at[1] ^ i), 0))
    whole = lambda a: pl.BlockSpec(a.shape, lambda i, at: (0, 0), pipeline_mode=pl.Buffered(1))
    out = pl.BlockSpec((1, 2, part, dim), lambda i, at: (i // 2, 0, 0, 0))
    return pl.pallas_call(
        out_kernel,
        grid_spec=pltpu.PrefetchScalarGridSpec(
            num_scalar_prefetch=1,
            grid=(SLOTS,),
            in_specs=[row(o), act, row(gq), act, whole(wo), whole(wff), whole(wqkv), whole(wup)],
            out_specs=[out, out],
        ),
        out_shape=[jax.ShapeDtypeStruct((SLOTS // 2, 2, part, dim), BF)] * 2,
        cost_estimate=pl.CostEstimate(
            flops=2 * SLOTS * part * dim * (o.shape[0] + 2 * hid.shape[1] + gq.shape[0]),
            transcendentals=0, bytes_accessed=SLOTS * part * dim * 10),
        compiler_params=pltpu.CompilerParams(vmem_limit_bytes=40 * MIB),
        name="outputs",
    )(at, o, hid, gq, gu, wo, wff, wqkv, wup)


def swap(value, axis, count, mask):
    return lax.ppermute(value, axis, [(i, i ^ mask) for i in range(count)])


def bit_groups(count):
    bits = list(range(count.bit_length() - 1))[::-1]
    groups = []
    while bits:
        take = 2 if len(bits) > 1 else 1
        groups.append(bits[:take])
        bits = bits[take:]
    assert len(groups[-1]) == 1
    return groups


def tie(value, *after):
    return lax.optimization_barrier((value,) + after)[0]


def gather_high(block, count, bits):
    low = bits[-1]
    return [block] + [swap(block, "batch", count, s << low) for s in range(1, 1 << len(bits))]


def matchings(edges, devices, per_device):
    left = [[] for _ in range(devices)]
    for e, (source, _, _) in enumerate(edges):
        left[source].append(e)
    rounds = []
    for _ in range(per_device):
        owner = [-1] * devices

        def place(source, seen):
            for e in left[source]:
                target = edges[e][1]
                if target in seen:
                    continue
                seen.add(target)
                if owner[target] < 0 or place(edges[owner[target]][0], seen):
                    owner[target] = e
                    return True
            return False

        for source in range(devices):
            place(source, set())
        rounds.append(list(owner))
        for e in owner:
            left[edges[e][0]].remove(e)
    return rounds


def unit_plan(nb, nt, rows, width, hidden):
    unit = math.gcd(math.gcd(rows, width // nt), hidden // nt)
    per = rows // unit
    head_units, hid_units = width // nt // unit, hidden // nt // unit
    assert head_units == nb and hid_units % nb == 0
    c = hid_units // nb
    edges = []
    for t in range(nt):
        for b in range(nb):
            want = [t * head_units + b]
            want += [nt * head_units + t * hid_units + b * c + i for i in range(c)]
            for slot, u in enumerate(want):
                edges.append((u // per, b * nt + t, (u % per, slot)))
    table = np.zeros((nb * nt, 2 * per), np.int32)
    perms = []
    for k, owner in enumerate(matchings(edges, nb * nt, per)):
        perms.append([(edges[e][0], edges[e][1]) for e in owner])
        for e in owner:
            table[edges[e][0], k] = edges[e][2][0]
            table[edges[e][1], per + k] = edges[e][2][1]
    return unit, per, perms, table


def per_device(
    nb, nt, patches, image_ids, cotangent, norm_gain, query_gain, key_gain, in_weight, out_weight
):
    seqs, part, dim = patches.shape
    width = H * HD
    local = width // nt
    units = (in_weight.shape[1] - 3 * width) // nt
    halves = nb // 2
    rows_in = in_weight.shape[0]
    unit, per, perms, table = unit_plan(nb, nt, out_weight.shape[0], width, units * nt)
    assert nt == SLOTS and units == dim and unit == rows_in and dim == nt * local and per == nt + 1
    both = ("batch", "tok")
    me_b = lax.axis_index("batch")
    me_t = lax.axis_index("tok")
    at = jnp.stack([me_b * nt + me_t, me_t, me_b])
    odd = (me_b & 1).reshape(1)
    table = jnp.asarray(table)
    gain = norm_gain.reshape(1, dim)
    groups = bit_groups(nb)

    pay0, pay1, a2a_src, *unit_sends = before(
        at, table, image_ids, gain, patches, cotangent, in_weight, out_weight.reshape(per, unit, dim)
    )
    full0 = lax.all_gather(pay0, "tok", axis=0)
    full1 = lax.all_gather(pay1, "tok", axis=0)
    w_in = lax.all_to_all(a2a_src, "tok", split_axis=0, concat_axis=0, tiled=True)
    got = [lax.ppermute(value, both, perm) for value, perm in zip(unit_sends, perms)]
    chunk_a, chunk_b, ids = pack(at, table, w_in, got, seqs, part)

    chunk_b = chunk_b.reshape(2, nt * unit, dim)
    held_a, held_b = chunk_a[None], chunk_b[None]
    for bits in groups[:-1]:
        parts = gather_high(held_a, nb, bits)
        held_a = jnp.stack(parts, axis=1).reshape((-1,) + chunk_a.shape)
        held_b = tie(held_b, parts[-1])
        parts = gather_high(held_b, nb, bits)
        held_b = jnp.stack(parts, axis=1).reshape((-1,) + chunk_b.shape)
    there_a = swap(held_a, "batch", nb, 1)
    there_b = swap(tie(held_b, there_a), "batch", nb, 1)
    wqkv, wo = join(at, held_a, there_a)

    qg = query_gain.reshape(HD, 1)
    kg = key_gain.reshape(HD, 1)
    wo_s = wo

    def attend(s, acc, wo_now, more=()):
        last = s == seqs - 1
        return attention(
            odd, ids[s], wqkv, wo_now, qg, kg, full1 if s else full0, (s - 1,) if s else (), acc, last, halves, more
        )

    def leave_core(s, att):
        keep, send = outputs(s, at, att[0], hid, att[1], gup, wo, wff, wqkv, wup)
        return keep, swap(send, "tok", nt, 1)

    def leave_chip(keep, near):
        value = (keep[1].astype(F32) + near[1].astype(F32)).astype(BF)
        return value, swap(value, "tok", nt, 2)

    pending = []
    acc = None
    earlier = []
    for s in range(seqs):
        last = s == seqs - 1
        att = attend(s, acc, wo_s, (f_np, gain) if last else ())
        if not last:
            acc = (att[2], att[3], att[4])
        if s == 0:
            hid, gup, wup, wff, f_grad, f_np = ffn(at, held_b, there_b, tie(full0, att[0]), full1)
            f_mine = lax.psum_scatter(f_grad, "batch", scatter_dimension=0, tiled=True)
        if s:
            value, away = leave_chip(*pending[-1])
            pending[-1] = pending[-1] + (away,)
            att = [tie(att[0], value)] + list(att[1:])
            if s > 1:
                att = [tie(att[0], pending[0][2])] + list(att[1:])
        keep, near = leave_core(s, att)
        pending.append((keep, near))
        wo_s = tie(wo, keep)
    pending[-1] = pending[-1] + (leave_chip(*pending[-1])[1],)
    for s, (keep, near, away) in enumerate(pending):
        earlier = after(s, image_ids, patches, cotangent, gain, keep, near, away, earlier)
    block_out, patch_grad = earlier
    _, _, a_send, a_keep = att

    def reduce_batch(send, keep, rows):
        parts = [keep, swap(send, "batch", nb, 1)]
        for bits in groups[:-1][::-1]:
            own, *sends = fold(rows, bits[-1], at, parts[0], parts[1:])
            parts = [own] + [swap(value, "batch", nb, (s + 1) << bits[-1]) for s, value in enumerate(sends)]
        return parts

    f_mine = f_mine.reshape(2, nt, unit, dim)
    up = lax.all_to_all(f_mine[0], "tok", split_axis=0, concat_axis=0, tiled=True)
    a_parts = reduce_batch(a_send, a_keep, nt * unit)
    src, *sends = leave(at, table, a_parts, f_mine[1], local)
    qkv = lax.all_to_all(src, "tok", split_axis=0, concat_axis=0, tiled=True)
    got = [lax.ppermute(v, both, [(b, a) for a, b in perm]) for v, perm in zip(sends, perms)]
    in_grad, out_grad, small = place(at, table, qkv, up, got)
    small = small[0]
    return (
        block_out,
        patch_grad,
        small[:dim],
        small[dim : dim + HD],
        small[dim + HD :],
        in_grad,
        out_grad.reshape(per * unit, dim),
    )


def solution(mesh):
    rows = P("batch", "tok", None)
    weights = P(("batch", "tok"), None)
    return jax.shard_map(
        functools.partial(per_device, mesh.shape["batch"], mesh.shape["tok"]),
        mesh=mesh,
        in_specs=(rows, P("batch", "tok"), rows, P(), P(), P(), weights, weights),
        out_specs=(rows, rows, P(), P(), P(), weights, weights),
        check_vma=False,
    )
```

```python
import functools
import math

import jax
import jax.numpy as jnp
import numpy as np
from jax import lax
from jax.experimental import pallas as pl
from jax.experimental.pallas import tpu as pltpu
from jax.sharding import PartitionSpec as P

H = 12
HD = 64
SLOTS = 4
EPS = 1e-06
BIG = 2048.0
LOG2E = 1.4426950408889634
BF = jnp.bfloat16
F32 = jnp.float32
NN = (((1,), (0,)), ((), ()))
NT = (((1,), (1,)), ((), ()))
TN = (((0,), (0,)), ((), ()))
MIB = 1 << 20

VMEM = pl.BlockSpec(memory_space=pltpu.VMEM)
SMEM = pl.BlockSpec(memory_space=pltpu.SMEM)
ANY = pl.BlockSpec(memory_space=pl.ANY)
HBM = pl.BlockSpec(memory_space=pltpu.HBM)


def mm(a, b, dims=NN):
    return lax.dot_general(a, b, dims, preferred_element_type=F32)


def normalize(values):
    center = values - jnp.mean(values, axis=-1, keepdims=True)
    inverse = lax.rsqrt(jnp.mean(center * center, axis=-1, keepdims=True) + EPS)
    return center * inverse, inverse


def norm_back(grad_unit, unit_rows, inverse):
    return inverse * (
        grad_unit
        - jnp.mean(grad_unit, axis=-1, keepdims=True)
        - unit_rows * jnp.mean(grad_unit * unit_rows, axis=-1, keepdims=True)
    )


def column(row):
    return jnp.broadcast_to(row, (8, row.shape[1])).T[:, 0:1]


def before_kernel(at_ref, table_ref, ids_ref, gain_ref, x_hbm, cot_hbm, win_hbm, wout_hbm, *refs):
    outs, (x_ref, cot_ref, win_ref, wout_ref, pay_ref, in_sem, out_sem) = refs[:-7], refs[-7:]
    seqs, part, _ = x_ref.shape
    pays, (src_ref, *unit_refs) = outs[:2], outs[2:]
    ins = [
        pltpu.make_async_copy(a, b, in_sem.at[i])
        for i, (a, b) in enumerate(((win_hbm, win_ref), (wout_hbm, wout_ref), (x_hbm, x_ref), (cot_hbm, cot_ref)))
    ]
    for copy in ins:
        copy.start()
    nt, rows = src_ref.shape[0], win_ref.shape[0]
    local = H * HD // nt
    units = (win_ref.shape[1] - 3 * H * HD) // nt
    ins[0].wait()
    ins[1].wait()
    for k, ref in enumerate(unit_refs):
        ref[...] = wout_ref[table_ref[at_ref[0], k]]
    for t in range(nt):
        for k in range(3):
            src_ref[t, :rows, k * local : (k + 1) * local] = win_ref[:, k * H * HD + t * local : k * H * HD + (t + 1) * local]
        src_ref[t, :rows, 3 * local :] = win_ref[:, 3 * H * HD + t * units : 3 * H * HD + (t + 1) * units]
        for s in range(seqs):
            src_ref[t, rows:, s * part : (s + 1) * part] = ids_ref[s : s + 1, :].astype(F32).astype(BF)
        src_ref[t, rows:, seqs * part :] = jnp.zeros((1, 3 * local + units - seqs * part), BF)
    ins[2].wait()
    ins[3].wait()
    copies = []
    for s in range(seqs):
        unit, _ = normalize(x_ref[s].astype(F32))
        live = column(jnp.where(ids_ref[s : s + 1, :] >= 0, 1.0, 0.0))
        pay_ref[s, 0] = (unit * gain_ref[...]).astype(BF)
        pay_ref[s, 1] = (live * cot_ref[s].astype(F32)).astype(BF)
        copies.append(pltpu.make_async_copy(pay_ref.at[s], pays[0].at[s] if s < seqs - 1 else pays[1], out_sem.at[s]))
        copies[-1].start()
    for copy in copies:
        copy.wait()


def before(at, table, ids, gain, x, cot, w_in, w_out):
    seqs, part, dim = x.shape
    per, unit, _ = w_out.shape
    rows, wide = w_in.shape
    outs = [jax.ShapeDtypeStruct((seqs - 1, 2, part, dim), BF), jax.ShapeDtypeStruct((2, part, dim), BF)]
    outs += [jax.ShapeDtypeStruct((SLOTS, rows + 1, wide // SLOTS), BF)]
    outs += [jax.ShapeDtypeStruct((unit, dim), BF)] * per
    return pl.pallas_call(
        before_kernel,
        out_shape=outs,
        in_specs=[SMEM] * 2 + [VMEM] * 2 + [HBM] * 4,
        out_specs=[HBM] * 2 + [VMEM] * (1 + per),
        scratch_shapes=[
            pltpu.VMEM(x.shape, BF),
            pltpu.VMEM(x.shape, BF),
            pltpu.VMEM(w_in.shape, BF),
            pltpu.VMEM(w_out.shape, BF),
            pltpu.VMEM((seqs, 2, part, dim), BF),
            pltpu.SemaphoreType.DMA((4,)),
            pltpu.SemaphoreType.DMA((seqs,)),
        ],
        cost_estimate=pl.CostEstimate(flops=x.size * 8, transcendentals=0, bytes_accessed=x.size * 8),
        compiler_params=pltpu.CompilerParams(vmem_limit_bytes=32 * MIB),
        name="before",
    )(at, table, ids, gain, x, cot, w_in, w_out)


def pack_in(w_in, seqs, part):
    nt, high, wide = w_in.shape
    unit = high - 1
    local = H * HD // nt
    length = nt * part

    def kernel(win_ref, a_ref, u_ref, ids_ref):
        for t in range(nt):
            a_ref[t] = win_ref[t, :unit, : 3 * local]
            u_ref[t] = win_ref[t, :unit, 3 * local :]
            row = win_ref[t, unit:, : seqs * part].astype(F32).astype(jnp.int32)
            for s in range(seqs):
                ids_ref[s, :, t * part : (t + 1) * part] = row[:, s * part : (s + 1) * part]

    return pl.pallas_call(
        kernel,
        out_shape=[
            jax.ShapeDtypeStruct((nt, unit, 3 * local), BF),
            jax.ShapeDtypeStruct((nt, unit, wide - 3 * local), BF),
            jax.ShapeDtypeStruct((seqs, 1, length), jnp.int32),
        ],
        in_specs=[VMEM],
        out_specs=[VMEM] * 3,
        cost_estimate=pl.CostEstimate(flops=1000, transcendentals=0, bytes_accessed=w_in.size * 4),
        name="pack_in",
    )(w_in)


def pack_out(at, table, got):
    unit, dim = got[0].shape
    per = len(got)

    def kernel(at_ref, table_ref, *refs):
        got_refs, (wo_ref, ff_ref, all_ref) = refs[:per], refs[per:]
        for k, ref in enumerate(got_refs):
            all_ref[table_ref[at_ref[0], per + k]] = ref[...]
        wo_ref[...] = all_ref[0]
        for k in range(per - 1):
            ff_ref[k] = all_ref[k + 1]

    return pl.pallas_call(
        kernel,
        out_shape=[jax.ShapeDtypeStruct((unit, dim), BF), jax.ShapeDtypeStruct((per - 1, unit, dim), BF)],
        in_specs=[SMEM] * 2 + [VMEM] * per,
        out_specs=[VMEM] * 2,
        scratch_shapes=[pltpu.VMEM((per, unit, dim), BF)],
        cost_estimate=pl.CostEstimate(flops=1000, transcendentals=0, bytes_accessed=unit * dim * 30),
        name="pack_out",
    )(at, table, *got)


def join(at, qkv_parts, wo_parts):
    nt, unit, wide = qkv_parts[0][0].shape[1:]
    dim = wo_parts[0][0].shape[2]
    count = sum(len(masks) for _, masks in qkv_parts)

    def kernel(at_ref, *refs):
        ins, (wqkv_ref, wo_ref, all_ref) = refs[:-3], refs[-3:]
        for k, (_, masks) in enumerate(qkv_parts + wo_parts):
            to = all_ref if k < len(qkv_parts) else wo_ref
            for i, mask in enumerate(masks):
                to[at_ref[2] ^ mask] = ins[k][i]
        wqkv_ref[...] = all_ref[...].reshape(dim, wide).T

    return pl.pallas_call(
        kernel,
        out_shape=[jax.ShapeDtypeStruct((wide, dim), BF), jax.ShapeDtypeStruct((count, unit, dim), BF)],
        in_specs=[SMEM] + [VMEM] * (len(qkv_parts) + len(wo_parts)),
        out_specs=[VMEM] * 2,
        scratch_shapes=[pltpu.VMEM((count, nt, unit, wide), BF)],
        cost_estimate=pl.CostEstimate(flops=1000, transcendentals=0, bytes_accessed=dim * dim * 8),
        compiler_params=pltpu.CompilerParams(vmem_limit_bytes=32 * MIB),
        name="join",
    )(at, *[a for a, _ in qkv_parts + wo_parts])


def resplit(total, rows):
    first = total[rows : rows + 1] + total[rows + 1 : rows + 2]
    second = total[rows + 2 : rows + 3] + total[rows + 3 : rows + 4]
    return term_rows(first, second)


def term_rows(first, second):
    def terms(v):
        hi = v.astype(BF).astype(F32)
        return [hi, (v - hi).astype(BF).astype(F32)]

    return jnp.concatenate(terms(first) + terms(second) + [jnp.zeros((4, first.shape[1]), F32)], axis=0)


def fold(rows, low, at, keep, got):
    n, high, dim = keep.shape

    def kernel(at_ref, keep_ref, *refs):
        got_refs, (own_ref, *send_refs) = refs[: len(got)], refs[len(got) :]
        mine = (at_ref[2] >> low) & 3
        for i in range(n // 4):
            for s, to in enumerate([own_ref] + send_refs):
                at_block = i * 4 + (mine ^ s)
                total = keep_ref[at_block]
                for ref in got_refs:
                    total = total + ref[at_block].astype(F32)
                if rows:
                    to[i, :rows] = total[:rows].astype(to.dtype)
                    to[i, rows:] = resplit(total, rows).astype(to.dtype)
                else:
                    to[i] = total.astype(to.dtype)

    out = lambda t: jax.ShapeDtypeStruct((n // 4, high, dim), t)
    return pl.pallas_call(
        kernel,
        out_shape=[out(F32)] + [out(BF)] * 3,
        in_specs=[SMEM] + [VMEM] * (1 + len(got)),
        out_specs=[VMEM] * 4,
        cost_estimate=pl.CostEstimate(flops=keep.size, transcendentals=0, bytes_accessed=keep.size * 8),
        compiler_params=pltpu.CompilerParams(vmem_limit_bytes=48 * MIB),
        name="fold",
    )(at, keep, *got)


def leave(at, table, a_parts, f_units, local):
    own = a_parts[0]
    per = f_units.shape[0] + 1
    _, unit, dim = f_units.shape
    rows = SLOTS * unit
    width = 3 * local

    def kernel(at_ref, table_ref, p0, p1, p2, p3, f_ref, src_ref, *outs):
        out_refs, (all_ref,) = outs[:-1], outs[-1:]
        total = (p0[0] + p1[0].astype(F32)) + (p2[0].astype(F32) + p3[0].astype(F32))
        first = total[rows : rows + 1] + total[rows + 1 : rows + 2]
        second = total[rows + 2 : rows + 3] + total[rows + 3 : rows + 4]
        for t in range(SLOTS):
            src_ref[t, :unit] = total[t * unit : (t + 1) * unit, :width]
            src_ref[t, unit : unit + 1] = first[:, :width]
            src_ref[t, unit + 1 : unit + 2] = jnp.concatenate(
                [first[:, width:], second[:, :128], jnp.zeros((1, 2 * width - dim - 128), F32)], axis=1
            )
        for c in range(SLOTS):
            all_ref[0, :, c * local : (c + 1) * local] = total[c * unit : (c + 1) * unit, width:]
        for k in range(per - 1):
            all_ref[k + 1] = f_ref[k].astype(F32)
        for k, ref in enumerate(out_refs):
            ref[...] = all_ref[table_ref[at_ref[0], per + k]]

    return pl.pallas_call(
        kernel,
        out_shape=[jax.ShapeDtypeStruct((SLOTS, unit + 2, width), F32)] + [jax.ShapeDtypeStruct((unit, dim), F32)] * per,
        in_specs=[SMEM] * 2 + [VMEM] * 5,
        out_specs=[VMEM] * (1 + per),
        scratch_shapes=[pltpu.VMEM((per, unit, dim), F32)],
        cost_estimate=pl.CostEstimate(flops=own.size, transcendentals=0, bytes_accessed=own.size * 20),
        name="leave",
    )(at, table, *a_parts, f_units)


def place(at, table, qkv, up, got):
    nt, high, width = qkv.shape
    unit, dim = got[0].shape
    per = len(got)
    local = width // 3
    wide = nt * (width + up.shape[2])

    def kernel(at_ref, table_ref, qkv_ref, up_ref, *refs):
        got_refs, (in_ref, out_ref, norm_ref, q_ref, k_ref) = refs[:per], refs[per:]
        for t in range(nt):
            for k in range(3):
                in_ref[:, k * nt * local + t * local : k * nt * local + (t + 1) * local] = qkv_ref[t, :unit, k * local : (k + 1) * local]
            in_ref[:, nt * width + t * dim : nt * width + (t + 1) * dim] = up_ref[t].astype(F32)
        for k, ref in enumerate(got_refs):
            out_ref[table_ref[at_ref[0], k]] = ref[...]
        total = qkv_ref[0, unit:]
        for t in range(1, nt):
            total = total + qkv_ref[t, unit:]
        norm_ref[:, :width] = total[0:1]
        norm_ref[:, width:] = total[1:2, : dim - width]
        q_ref[...] = total[1:2, dim - width : dim - width + HD]
        k_ref[...] = total[1:2, dim - width + HD : dim - width + 2 * HD]

    return pl.pallas_call(
        kernel,
        out_shape=[
            jax.ShapeDtypeStruct((unit, wide), F32),
            jax.ShapeDtypeStruct((per, unit, dim), F32),
            jax.ShapeDtypeStruct((1, dim), F32),
            jax.ShapeDtypeStruct((1, HD), F32),
            jax.ShapeDtypeStruct((1, HD), F32),
        ],
        in_specs=[SMEM] * 2 + [VMEM] * (2 + per),
        out_specs=[VMEM] * 5,
        cost_estimate=pl.CostEstimate(flops=1000, transcendentals=0, bytes_accessed=unit * wide * 16),
        name="place",
    )(at, table, qkv, up, *got)


def after_kernel(s, ids_ref, x_ref, cot_ref, gain_ref, keep_ref, near_ref, far_ref, *rest):
    out_ref, grad_ref = rest[-2:]
    unit, inverse = normalize(x_ref[0].astype(F32))
    live = column(jnp.where(ids_ref[s : s + 1, :] >= 0, 1.0, 0.0))
    both = keep_ref[0, 0].astype(F32) + near_ref[0, 0].astype(F32) + far_ref[0].astype(F32)
    out_ref[0] = (live * (x_ref[0].astype(F32) + both[0])).astype(BF)
    grad_ref[0] = (
        live * cot_ref[0].astype(F32) + norm_back(both[1] * gain_ref[...], unit, inverse)
    ).astype(BF)


def after(s, i, ids, x, cot, gain, keep, near, far, earlier):
    x, cot, keep, near, far = (pltpu.with_memory_space_constraint(a, pltpu.HBM) for a in (x, cot, keep, near, far))
    seqs, part, dim = x.shape
    one = pl.BlockSpec((1, part, dim), lambda g: (s, 0, 0))
    pair = pl.BlockSpec((1, 1, 2, part, dim), lambda g: (0, i, 0, 0, 0))
    lone = pl.BlockSpec((1, 2, part, dim), lambda g: (i, 0, 0, 0))
    fixed = lambda a: pl.BlockSpec(a.shape, lambda g: (0,) * a.ndim)
    return pl.pallas_call(
        functools.partial(after_kernel, s),
        grid=(1,),
        out_shape=[jax.ShapeDtypeStruct(x.shape, BF)] * 2,
        in_specs=[fixed(ids), one, one, fixed(gain), pair, pair, lone] + [ANY] * len(earlier),
        out_specs=[one, one],
        input_output_aliases={7 + i: i for i in range(len(earlier))},
        cost_estimate=pl.CostEstimate(flops=part * dim * 20, transcendentals=0, bytes_accessed=part * dim * 20),
        compiler_params=pltpu.CompilerParams(vmem_limit_bytes=32 * MIB),
        name="after",
    )(ids, x, cot, gain, keep, near, far, *earlier)


def split_rows(odd, grad, send_ref, keep_ref, parts, rows, store):
    for z in range(parts):
        low = grad[2 * z * rows : (2 * z + 1) * rows]
        high = grad[(2 * z + 1) * rows : (2 * z + 2) * rows]
        store(send_ref, z, jnp.where(odd, low, high).astype(BF))
        store(keep_ref, z, jnp.where(odd, high, low))


def attention_kernel(
    heads, block, last,
    odd_ref, ids_ref, qg_ref, kg_ref, wqkv_hbm, wo_hbm, pay_hbm, *refs,
):
    if last:
        (acc_sums_ref, fnp_ref, gain_ref, accq_hbm, acco_hbm), refs = refs[:5], refs[5:]
        (o_hbm, grad_hbm, send_ref, keep_ref, sums_ref), refs = refs[:5], refs[5:]
    else:
        (o_hbm, grad_hbm, sums_ref, newq_hbm, newo_hbm), refs = refs[:5], refs[5:]
    (
        wqkv_ref, wo_ref, norm_ref, gb_ref, o_ref, grad_ref, gq_ref, go_ref, raw_ref,
        qt_ref, qn_ref, kt_ref, ka_ref, vt_ref, va_ref, do_ref, dq_ref, dk_ref, dv_ref, pad_ref, vm_ref,
        w_sem, sem, out_sem,
    ) = refs
    seqs, length, dim = norm_ref.shape
    part = length // SLOTS
    width = heads * HD
    blocks = length // block
    loads = [pltpu.make_async_copy(wqkv_hbm, wqkv_ref, w_sem.at[0]), pltpu.make_async_copy(wo_hbm, wo_ref, w_sem.at[1])]
    loads[0].start()

    def pay_copy(s, j, t):
        to = (norm_ref, gb_ref)[j].at[s, pl.ds(t * part, part), :]
        return pltpu.make_async_copy(pay_hbm.at[t, s, j], to, sem.at[s, j * SLOTS + t])

    for s in range(seqs):
        for j in range(2):
            for t in range(SLOTS):
                pay_copy(s, j, t).start()
            if s + j == 0:
                loads[1].start()
    if last:
        loads.append(pltpu.make_async_copy(accq_hbm, gq_ref, w_sem.at[2]))
        loads.append(pltpu.make_async_copy(acco_hbm, go_ref, w_sem.at[3]))
        loads[2].start()
        loads[3].start()
        sums_ref[...] = acc_sums_ref[...]
    else:
        gq_ref[...] = jnp.zeros_like(gq_ref)
        go_ref[...] = jnp.zeros_like(go_ref)
        sums_ref[...] = jnp.zeros_like(sums_ref)
    gain_q = qg_ref[...]
    gain_k = kg_ref[...]
    marks = lax.broadcasted_iota(jnp.int32, (HD, length), 0)
    v_tail = jnp.where(lax.broadcasted_iota(jnp.int32, (length, HD), 1) < 2, 1.0, 0.0).astype(BF)
    ones = jnp.where(lax.broadcasted_iota(jnp.int32, (16, length), 0) == 0, 1.0, 0.0).astype(BF)
    spot = lax.broadcasted_iota(jnp.int32, (HD, block), 0)
    scale = 1.0 / math.sqrt(HD)
    cut = lambda a, i: a[:, i * block : (i + 1) * block]

    def unit_of(row):
        raw = raw_ref[pl.ds(pl.multiple_of(row, HD), HD), :]
        center = raw - jnp.mean(raw, axis=0, keepdims=True)
        inverse = lax.rsqrt(jnp.mean(center * center, axis=0, keepdims=True) + EPS)
        return center * inverse, inverse

    def lanes(a):
        total = a[:, :128]
        for i in range(1, length // 128):
            total = total + a[:, i * 128 : (i + 1) * 128]
        return total

    def stores(s):
        return [
            pltpu.make_async_copy(o_ref.at[s], o_hbm.at[s], out_sem.at[s, 0]),
            pltpu.make_async_copy(grad_ref.at[s], grad_hbm.at[s], out_sem.at[s, 1]),
        ]

    loads[0].wait()
    loads[1].wait()

    def sequence(s, carry):
        ids = ids_ref[s]
        same = marks == ids + 1
        k_tail = jnp.where(same, 1.0, 0.0).T.astype(BF)
        q_tail = jnp.where((same & (ids >= 0)) | (marks > 4), 0.0, -BIG).astype(BF)
        pad = jnp.where(ids < 0, 1.0, 0.0)
        for i in range(blocks):
            pad_ref[i] = cut(pad, i)
        for t in range(SLOTS):
            pay_copy(s, 0, t).wait()
        raw_ref[...] = mm(wqkv_ref[...], norm_ref[s], NT)
        for t in range(SLOTS):
            pay_copy(s, 1, t).wait()
        do_all = mm(wo_ref[...], gb_ref[s], NT).astype(BF)
        for h in range(heads):
            for i in range(blocks):
                do_ref[h * blocks + i] = cut(do_all[h * HD : (h + 1) * HD], i)

        def prepare(h, carry):
            q_unit, _ = unit_of(h * HD)
            q = q_unit * gain_q
            qn = q.T.astype(BF)
            for i in range(blocks):
                qt_ref[h * blocks + i, :HD] = cut(q, i).astype(BF)
                qt_ref[h * blocks + i, HD:] = cut(q_tail, i)
                qn_ref[h * blocks + i] = qn[i * block : (i + 1) * block]
            k_unit, _ = unit_of(width + h * HD)
            k = k_unit * gain_k
            kt_ref[h] = k.astype(BF)
            ka_ref[h, :, :HD] = k.T.astype(BF)
            ka_ref[h, :, HD:] = k_tail
            v = raw_ref[pl.ds(pl.multiple_of(2 * width + h * HD, HD), HD), :]
            vb = v.astype(BF)
            vt_ref[h, :HD] = vb
            vt_ref[h, HD:] = ones
            va_ref[h, :, :HD] = v.T.astype(BF)
            va_ref[h, :, HD:] = v_tail
            vm_ref[h] = jnp.mean(vb.astype(F32), axis=1, keepdims=True)
            dk_ref[h] = jnp.zeros(dk_ref.shape[1:], F32)
            dv_ref[h] = jnp.zeros(dv_ref.shape[1:], F32)
            return carry

        lax.fori_loop(0, heads, prepare, 0)

        def step(n, carry):
            h = n // blocks
            padb = pad_ref[n % blocks]
            e = jnp.exp2(mm(ka_ref[h], qt_ref[n]) * (LOG2E * scale))
            eb = e.astype(BF)
            oa = mm(vt_ref[h], eb)
            inv = 1.0 / (oa[HD : HD + 1] + padb)
            o = oa[:HD] * inv
            dos = (do_ref[n].astype(F32) * inv).astype(BF)
            delta = jnp.sum(dos.astype(F32) * o, axis=0, keepdims=True)
            d0 = delta.astype(BF).astype(F32)
            tail = jnp.where(spot == 0, -d0, jnp.where(spot == 1, d0 - delta, 0.0))
            doa = jnp.concatenate([dos.astype(F32), tail], axis=0)
            ds = (e * mm(va_ref[h], doa.astype(BF))).astype(BF)
            dq_ref[n] = mm(kt_ref[h], ds)
            dk_ref[h] += mm(ds, qn_ref[n])
            dv_ref[h] += mm(eb, doa.T.astype(BF))
            do_ref[n] = jnp.where(padb > 0, vm_ref[h], o).astype(BF)
            return carry

        lax.fori_loop(0, heads * blocks, step, 0)

        def finish(h, carry):
            rows = lambda at: pl.ds(pl.multiple_of(at + h * HD, HD), HD)
            gq = jnp.concatenate([dq_ref[h * blocks + i] for i in range(blocks)], axis=1)
            gk = dk_ref[h].T
            for k, (g, gain_col) in enumerate(((gq, gain_q), (gk, gain_k))):
                unit, inverse = unit_of(k * width + h * HD)
                g = (g * scale).astype(BF).astype(F32)
                sums_ref[k] += lanes(g * unit)
                g = g * gain_col
                back = inverse * (
                    g - jnp.mean(g, axis=0, keepdims=True) - unit * jnp.mean(g * unit, axis=0, keepdims=True)
                )
                grad_ref[s, rows(k * width), :] = back.astype(BF)
            grad_ref[s, rows(2 * width), :] = dv_ref[h].T[:HD].astype(BF)
            for i in range(blocks):
                o_ref[s, rows(0), pl.ds(i * block, block)] = do_ref[h * blocks + i]
            return carry

        lax.fori_loop(0, heads, finish, 0)
        for copy in stores(s):
            copy.start()
        if last:
            loads[2].wait()
            loads[3].wait()
        gq_ref[...] += mm(grad_ref[s], norm_ref[s])
        go_ref[...] += mm(o_ref[s], gb_ref[s])
        return carry

    if last:
        assert seqs == 1
        sequence(0, 0)
    else:
        lax.fori_loop(0, seqs, sequence, 0)
        ends = [pltpu.make_async_copy(gq_ref, newq_hbm, w_sem.at[2]), pltpu.make_async_copy(go_ref, newo_hbm, w_sem.at[3])]
        for copy in ends:
            copy.start()
        for copy in ends:
            copy.wait()
    for s in range(seqs):
        for copy in stores(s):
            copy.wait()
    if not last:
        return
    g_q = gq_ref[...]
    first_row = (jnp.sum(wqkv_ref[...].astype(F32) * g_q, axis=0, keepdims=True) + fnp_ref[...]) / gain_ref[...]
    second_row = jnp.concatenate(
        [jnp.sum(sums_ref[k].T, axis=0, keepdims=True) for k in range(2)] + [jnp.zeros((1, dim - 2 * HD), F32)], axis=1
    )
    g_q = g_q.T
    odd = odd_ref[0] > 0
    parts, rows, _ = send_ref.shape
    rows = rows - 8
    extra = term_rows(first_row, second_row)
    for z in range(parts):
        send_ref[z, rows:] = extra.astype(BF)
        keep_ref[z, rows:] = extra
    unit = width // (2 * parts)

    def put_q(ref, z, value):
        ref[z, :rows, : 3 * width] = value

    def put_o(ref, z, value):
        for c in range(dim // width):
            ref[z, c * unit : (c + 1) * unit, 3 * width :] = value[:, c * width : (c + 1) * width]

    split_rows(odd, g_q, send_ref, keep_ref, parts, rows, put_q)
    split_rows(odd, go_ref[...], send_ref, keep_ref, parts, unit, put_o)


def attention(odd, ids, wqkv, wo, qg, kg, pay, halves, more=()):
    wide, dim = wqkv.shape
    width = wo.shape[0]
    heads = width // HD
    seqs, part = pay.shape[1], pay.shape[3]
    length = part * SLOTS
    block = 512
    blocks = length // block
    last = bool(more)
    ins = [odd, ids, qg, kg, wqkv, wo, pay, *more]
    specs = [SMEM] + [VMEM] * 3 + [HBM] * 3 + ([VMEM] * 3 + [HBM] * 2 if last else [])
    outs = [jax.ShapeDtypeStruct((seqs, width, length), BF), jax.ShapeDtypeStruct((seqs, wide, length), BF)]
    scratch = []
    if last:
        rows = dim // (2 * halves)
        outs += [
            jax.ShapeDtypeStruct((halves, rows + 8, wide + width), BF),
            jax.ShapeDtypeStruct((halves, rows + 8, wide + width), F32),
        ]
        scratch = [pltpu.VMEM((2, HD, 128), F32)]
    else:
        outs += [
            jax.ShapeDtypeStruct((2, HD, 128), F32),
            jax.ShapeDtypeStruct((wide, dim), F32),
            jax.ShapeDtypeStruct((width, dim), F32),
        ]
    flops = seqs * (2 * length * dim * width * 8 + heads * 6 * 2 * length * length * HD)
    return pl.pallas_call(
        functools.partial(attention_kernel, heads, block, last),
        out_shape=outs,
        in_specs=specs,
        out_specs=[HBM] * 2 + ([VMEM] * 2 if last else [VMEM, HBM, HBM]),
        scratch_shapes=scratch
        + [
            pltpu.VMEM((wide, dim), BF),
            pltpu.VMEM((width, dim), BF),
            pltpu.VMEM((seqs, length, dim), BF),
            pltpu.VMEM((seqs, length, dim), BF),
            pltpu.VMEM((seqs, width, length), BF),
            pltpu.VMEM((seqs, wide, length), BF),
            pltpu.VMEM((wide, dim), F32),
            pltpu.VMEM((width, dim), F32),
            pltpu.VMEM((wide, length), F32),
            pltpu.VMEM((heads * blocks, 2 * HD, block), BF),
            pltpu.VMEM((heads * blocks, block, HD), BF),
            pltpu.VMEM((heads, HD, length), BF),
            pltpu.VMEM((heads, length, 2 * HD), BF),
            pltpu.VMEM((heads, HD + 16, length), BF),
            pltpu.VMEM((heads, length, 2 * HD), BF),
            pltpu.VMEM((heads * blocks, HD, block), BF),
            pltpu.VMEM((heads * blocks, HD, block), F32),
            pltpu.VMEM((heads, length, HD), F32),
            pltpu.VMEM((heads, length, 2 * HD), F32),
            pltpu.VMEM((blocks, 1, block), F32),
            pltpu.VMEM((heads, HD, 1), F32),
            pltpu.SemaphoreType.DMA((4,)),
            pltpu.SemaphoreType.DMA((seqs, 2 * SLOTS)),
            pltpu.SemaphoreType.DMA((seqs, 2)),
        ],
        cost_estimate=pl.CostEstimate(flops=flops * 3, transcendentals=seqs * heads * length * length, bytes_accessed=8 * seqs * length * dim),
        compiler_params=pltpu.CompilerParams(vmem_limit_bytes=56 * MIB),
        name="attention",
    )(*ins)


def ffn_kernel(block, plan, at_ref, pay0_hbm, pay1_hbm, *refs):
    pieces, refs = refs[: len(plan)], refs[len(plan) :]
    (hid_hbm, gup_hbm, wup_hbm, wff_hbm, send_ref, np_ref), refs = refs[:6], refs[6:]
    norm_ref, gb_ref, hid_ref, gup_ref, wup_ref, wff_ref, gin_ref, gff_ref, sem, out_sem, w_sem = refs
    dim = wup_ref.shape[0]
    rows = send_ref.shape[2]
    part, seqs = pay0_hbm.shape[3], pay0_hbm.shape[1] + 1
    length = SLOTS * part
    total = norm_ref.shape[0]
    copies = []
    for ref, (which, masks) in zip(pieces, plan):
        for i, mask in enumerate(masks):
            start = pl.multiple_of((at_ref[2] ^ mask) * rows, rows)
            to = (wup_ref, wff_ref)[which].at[pl.ds(start, rows), :]
            copies.append(pltpu.make_async_copy(ref.at[i], to, w_sem.at[len(copies)]))
            copies[-1].start()
    for s in range(seqs):
        for t in range(SLOTS):
            at_rows = pl.ds((s * SLOTS + t) * part, part)
            for k, to in enumerate((norm_ref, gb_ref)):
                source = pay0_hbm.at[t, s, k] if s < seqs - 1 else pay1_hbm.at[t, k]
                pltpu.make_async_copy(source, to.at[at_rows, :], sem.at[s * SLOTS + t]).start()
    gin_ref[...] = jnp.zeros_like(gin_ref)
    gff_ref[...] = jnp.zeros_like(gff_ref)
    for copy in copies:
        copy.wait()
    weights = [pltpu.make_async_copy(wup_ref, wup_hbm, w_sem.at[0]), pltpu.make_async_copy(wff_ref, wff_hbm, w_sem.at[1])]
    for copy in weights:
        copy.start()
    c0 = math.sqrt(2.0 / math.pi)
    c1 = 0.044715

    def outs(i):
        at_rows = pl.ds(pl.multiple_of(i * block, block), block)
        return (
            pltpu.make_async_copy(hid_ref.at[at_rows, :], hid_hbm.at[at_rows, :], out_sem.at[0, i]),
            pltpu.make_async_copy(gup_ref.at[at_rows, :], gup_hbm.at[at_rows, :], out_sem.at[1, i]),
        )

    def step(i, carry):
        for k in range(block // part):
            for to in (norm_ref, gb_ref):
                pltpu.make_async_copy(pay1_hbm.at[0, 0], to.at[pl.ds(0, part), :], sem.at[i * (block // part) + k]).wait()
        at_rows = pl.ds(pl.multiple_of(i * block, block), block)
        up = mm(norm_ref[at_rows, :], wup_ref[...])
        gh = mm(gb_ref[at_rows, :], wff_ref[...], NT)
        sq = up * up
        t = jnp.tanh(up * (c0 + (c0 * c1) * sq))
        half = 0.5 + 0.5 * t
        hid_ref[at_rows, :] = (up * half).astype(BF)
        gup_ref[at_rows, :] = (gh * (half + (0.5 * up) * (1.0 - t * t) * (c0 + (3.0 * c0 * c1) * sq))).astype(BF)
        for copy in outs(i):
            copy.start()
        gin_ref[...] += mm(norm_ref[at_rows, :], gup_ref[at_rows, :], TN)
        gff_ref[...] += mm(hid_ref[at_rows, :], gb_ref[at_rows, :], TN)
        return carry

    lax.fori_loop(0, total // block, step, 0)
    line = jnp.sum(wup_ref[...].astype(F32) * gin_ref[...], axis=1, keepdims=True)
    np_ref[...] = jnp.broadcast_to(line, (dim, 128)).T[0:1]
    for b in range(dim // rows):
        for k, g in enumerate((gin_ref, gff_ref)):
            send_ref[b, k] = g[b * rows : (b + 1) * rows, :].astype(BF)
    for copy in weights:
        copy.wait()

    def drain(i, carry):
        for copy in outs(i):
            copy.wait()
        return carry

    lax.fori_loop(0, total // block, drain, 0)


def ffn(at, up_parts, ff_parts, pay0, pay1, count, block=512):
    _, _, part, dim = pay1.shape
    units = dim
    total = SLOTS * part * (1 + pay0.shape[1])
    rows = dim // count
    plan = [(0, masks) for _, masks in up_parts] + [(1, masks) for _, masks in ff_parts]
    pieces = [a for a, _ in up_parts + ff_parts]
    act = jax.ShapeDtypeStruct((total, units), BF)
    return pl.pallas_call(
        functools.partial(ffn_kernel, block, plan),
        out_shape=[
            act,
            act,
            jax.ShapeDtypeStruct((dim, units), BF),
            jax.ShapeDtypeStruct((units, dim), BF),
            jax.ShapeDtypeStruct((count, 2, rows, dim), BF),
            jax.ShapeDtypeStruct((1, dim), F32),
        ],
        in_specs=[SMEM] + [HBM] * (2 + len(pieces)),
        out_specs=[HBM] * 4 + [VMEM] * 2,
        scratch_shapes=[
            pltpu.VMEM((total, dim), BF),
            pltpu.VMEM((total, dim), BF),
            pltpu.VMEM((total, units), BF),
            pltpu.VMEM((total, units), BF),
            pltpu.VMEM((dim, units), BF),
            pltpu.VMEM((units, dim), BF),
            pltpu.VMEM((dim, units), F32),
            pltpu.VMEM((units, dim), F32),
            pltpu.SemaphoreType.DMA((total // part,)),
            pltpu.SemaphoreType.DMA((2, total // block)),
            pltpu.SemaphoreType.DMA((2 * count,)),
        ],
        cost_estimate=pl.CostEstimate(flops=8 * total * dim * units, transcendentals=total * units, bytes_accessed=total * dim * 8),
        compiler_params=pltpu.CompilerParams(vmem_limit_bytes=58 * MIB),
        name="ffn",
    )(at, pay0, pay1, *pieces)


def outputs(start, at, o, hid, gq, gu, wo, wff, wqkv, wup):
    seqs, _, length = o.shape
    dim = wo.shape[1]
    part = length // SLOTS

    def kernel(at_ref, o_hbm, hid_hbm, gq_hbm, gu_hbm, wo_hbm, wff_hbm, wqkv_hbm, wup_hbm, keep_hbm, send_hbm, *scratch):
        o_ref, hid_ref, gq_ref, gu_ref, wo_ref, wff_ref, wqkv_ref, wup_ref, res_ref, w_sem, sem, out_sem = scratch

        def load(k, s):
            rows = pl.ds(pl.multiple_of((start + s) * length, length), length)
            source, to = (
                (hid_hbm.at[rows, :], hid_ref), (o_hbm.at[s], o_ref), (gu_hbm.at[rows, :], gu_ref), (gq_hbm.at[s], gq_ref)
            )[k]
            return pltpu.make_async_copy(source, to.at[s], sem.at[s, k])

        weights = [
            pltpu.make_async_copy(a, b, w_sem.at[k])
            for k, (a, b) in enumerate(((wff_hbm, wff_ref), (wo_hbm, wo_ref), (wup_hbm, wup_ref), (wqkv_hbm, wqkv_ref)))
        ]
        for k in range(4):
            weights[k].start()
            load(k, 0).start()
        for s in range(1, seqs):
            for k in range(4):
                load(k, s).start()

        def leave(s, j, t, act):
            slot = at_ref[1] ^ t
            for to, odd in ((keep_hbm, 0), (send_hbm, 1)):

                @pl.when((slot & 1) == odd)
                def _(to=to):
                    act(pltpu.make_async_copy(res_ref.at[s, j, pl.ds(t * part, part), :], to.at[slot >> 1, s, j], out_sem.at[s, j, t]))

        for copy in weights:
            copy.wait()

        def sequence(s, carry):
            for k in range(2):
                load(k, s).wait()
            res_ref[s, 0] = (mm(o_ref[s], wo_ref[...], TN) + mm(hid_ref[s], wff_ref[...])).astype(BF)
            for t in range(SLOTS):
                leave(s, 0, t, lambda copy: copy.start())
            for k in range(2, 4):
                load(k, s).wait()
            res_ref[s, 1] = (mm(gq_ref[s], wqkv_ref[...], TN) + mm(gu_ref[s], wup_ref[...], NT)).astype(BF)
            for t in range(SLOTS):
                leave(s, 1, t, lambda copy: copy.start())
            return carry

        lax.fori_loop(0, seqs, sequence, 0)
        for s in range(seqs):
            for j in range(2):
                for t in range(SLOTS):
                    leave(s, j, t, lambda copy: copy.wait())

    return pl.pallas_call(
        kernel,
        out_shape=[jax.ShapeDtypeStruct((SLOTS // 2, seqs, 2, part, dim), BF)] * 2,
        in_specs=[SMEM] + [HBM] * 8,
        out_specs=[HBM] * 2,
        scratch_shapes=[
            pltpu.VMEM(o.shape, BF),
            pltpu.VMEM((seqs, length, hid.shape[1]), BF),
            pltpu.VMEM(gq.shape, BF),
            pltpu.VMEM((seqs, length, gu.shape[1]), BF),
            pltpu.VMEM(wo.shape, BF),
            pltpu.VMEM(wff.shape, BF),
            pltpu.VMEM(wqkv.shape, BF),
            pltpu.VMEM(wup.shape, BF),
            pltpu.VMEM((seqs, 2, length, dim), BF),
            pltpu.SemaphoreType.DMA((4,)),
            pltpu.SemaphoreType.DMA((seqs, 4)),
            pltpu.SemaphoreType.DMA((seqs, 2, SLOTS)),
        ],
        cost_estimate=pl.CostEstimate(
            flops=2 * seqs * length * dim * (o.shape[1] + 2 * hid.shape[1] + gq.shape[1]),
            transcendentals=0, bytes_accessed=seqs * length * dim * 10),
        compiler_params=pltpu.CompilerParams(vmem_limit_bytes=48 * MIB),
        name="outputs",
    )(at, o, hid, gq, gu, wo, wff, wqkv, wup)


def swap(value, axis, count, mask):
    return lax.ppermute(value, axis, [(i, i ^ mask) for i in range(count)])


def bit_groups(count):
    bits = list(range(count.bit_length() - 1))[::-1]
    groups = []
    while bits:
        take = 2 if len(bits) > 1 else 1
        groups.append(bits[:take])
        bits = bits[take:]
    assert len(groups[-1]) == 1
    return groups


def tie(value, *after):
    return lax.optimization_barrier((value,) + after)[0]


def gather_batch(block, count, groups, after=None):
    held, masks = block[None], [0]
    for stage, bits in enumerate(groups):
        low = bits[-1]
        if after and after[stage] is not None:
            held = tie(held, after[stage])
        parts = [(held, masks)]
        for s in range(1, 1 << len(bits)):
            parts.append((swap(held, "batch", count, s << low), [m ^ (s << low) for m in masks]))
        yield parts
        held = jnp.concatenate([a for a, _ in parts], axis=0)
        masks = sum((m for _, m in parts), [])


def matchings(edges, devices, per_device):
    left = [[] for _ in range(devices)]
    for e, (source, _, _) in enumerate(edges):
        left[source].append(e)
    rounds = []
    for _ in range(per_device):
        owner = [-1] * devices

        def place(source, seen):
            for e in left[source]:
                target = edges[e][1]
                if target in seen:
                    continue
                seen.add(target)
                if owner[target] < 0 or place(edges[owner[target]][0], seen):
                    owner[target] = e
                    return True
            return False

        for source in range(devices):
            place(source, set())
        rounds.append(list(owner))
        for e in owner:
            left[edges[e][0]].remove(e)
    return rounds


def unit_plan(nb, nt, rows, width, hidden):
    unit = math.gcd(math.gcd(rows, width // nt), hidden // nt)
    per = rows // unit
    head_units, hid_units = width // nt // unit, hidden // nt // unit
    assert head_units == nb and hid_units % nb == 0
    c = hid_units // nb
    edges = []
    for t in range(nt):
        for b in range(nb):
            want = [t * head_units + b]
            want += [nt * head_units + t * hid_units + b * c + i for i in range(c)]
            for slot, u in enumerate(want):
                edges.append((u // per, b * nt + t, (u % per, slot)))
    table = np.zeros((nb * nt, 2 * per), np.int32)
    perms = []
    for k, owner in enumerate(matchings(edges, nb * nt, per)):
        perms.append([(edges[e][0], edges[e][1]) for e in owner])
        for e in owner:
            table[edges[e][0], k] = edges[e][2][0]
            table[edges[e][1], per + k] = edges[e][2][1]
    return unit, per, perms, table


def per_device(
    nb, nt, patches, image_ids, cotangent, norm_gain, query_gain, key_gain, in_weight, out_weight
):
    seqs, part, dim = patches.shape
    width = H * HD
    local = width // nt
    units = (in_weight.shape[1] - 3 * width) // nt
    halves = nb // 2
    rows_in = in_weight.shape[0]
    unit, per, perms, table = unit_plan(nb, nt, out_weight.shape[0], width, units * nt)
    assert nt == SLOTS and units == dim and unit == rows_in and dim == nt * local and per == nt + 1
    both = ("batch", "tok")
    me_b = lax.axis_index("batch")
    me_t = lax.axis_index("tok")
    at = jnp.stack([me_b * nt + me_t, me_t, me_b])
    odd = (me_b & 1).reshape(1)
    table = jnp.asarray(table)
    gain = norm_gain.reshape(1, dim)
    groups = bit_groups(nb)

    pay0, pay1, a2a_src, *unit_sends = before(
        at, table, image_ids, gain, patches, cotangent, in_weight, out_weight.reshape(per, unit, dim)
    )
    full0 = lax.all_gather(pay0, "tok", axis=0)
    full1 = lax.all_gather(pay1, "tok", axis=0)
    w_in = lax.all_to_all(a2a_src, "tok", split_axis=0, concat_axis=0, tiled=True)
    early = 2
    got = [lax.ppermute(v, both, perm) for v, perm in zip(unit_sends[:early], perms)]
    chunk_a, chunk_u, ids = pack_in(tie(w_in, *got), seqs, part)
    got += [lax.ppermute(tie(v, chunk_a), both, perm) for v, perm in zip(unit_sends[early:], perms[early:])]
    chunk_w, chunk_f = pack_out(at, table, got)
    chunk_u = chunk_u.reshape(nt * unit, dim)
    chunk_f = chunk_f.reshape(nt * unit, dim)

    *_, a_parts = gather_batch(chunk_a, nb, groups, [None] * (len(groups) - 1) + [got[-1]])
    *_, w_parts = gather_batch(chunk_w, nb, groups)
    a_there, w_there = a_parts[-1][0], w_parts[-1][0]
    w_high = w_parts[0][0]
    stages = len(groups)
    wqkv, wo = join(at, a_parts, w_parts)
    *_, u_parts = gather_batch(chunk_u, nb, groups, [w_high] + [None] * (stages - 2) + [wqkv])
    *_, f_parts = gather_batch(chunk_f, nb, groups[::-1], [a_there, wqkv] + [None] * (stages - 2))
    wo = wo.reshape(local, dim)

    qg = query_gain.reshape(HD, 1)
    kg = key_gain.reshape(HD, 1)

    def leave_core(start, o, gq):
        keep, send = outputs(start, at, o, hid, gq, gup, wo, wff, wqkv, wup)
        return keep, swap(send, "tok", nt, 1)

    def leave_chip(keep, near):
        value = (keep[1].astype(F32) + near[1].astype(F32)).astype(BF)
        return value, swap(value, "tok", nt, 2)

    o0, gq0, sums, acc_q, acc_o = attention(odd, ids[: seqs - 1], wqkv, wo, qg, kg, full0, halves)
    hid, gup, wup, wff, f_grad, f_np = ffn(at, u_parts, f_parts, full0, tie(full1, o0), nb)
    f_mine = lax.psum_scatter(f_grad, "batch", scatter_dimension=0, tiled=True)
    keep0, near0 = leave_core(0, o0, gq0)
    o1, gq1, a_send, a_keep = attention(
        odd, ids[seqs - 1 :], wqkv, tie(wo, keep0), qg, kg, full1[:, None], halves, (sums, f_np, gain, acc_q, acc_o)
    )

    a_send = swap(a_send, "batch", nb, 1)
    value0, away0 = leave_chip(keep0, near0)
    a_parts = [a_keep, a_send]
    for bits in groups[:-1][::-1]:
        own, *sends = fold(nt * unit, bits[-1], at, a_parts[0], a_parts[1:])
        a_parts = [own] + [swap(value, "batch", nb, (s + 1) << bits[-1]) for s, value in enumerate(sends)]
    keep1, near1 = leave_core(seqs - 1, tie(o1, own), gq1)
    value1, away1 = leave_chip(keep1, near1)

    f_mine = f_mine.reshape(2, nt, unit, dim)
    up = lax.all_to_all(f_mine[0], "tok", split_axis=0, concat_axis=0, tiled=True)
    src, *sends = leave(at, table, a_parts, f_mine[1], local)
    qkv = lax.all_to_all(src, "tok", split_axis=0, concat_axis=0, tiled=True)
    got = [lax.ppermute(v, both, [(b, a) for a, b in perm]) for v, perm in zip(sends, perms)]
    in_grad, out_grad, norm_grad, query_grad, key_grad = place(at, table, qkv, up, got)

    earlier = []
    for s in range(seqs):
        i, group = (s, (keep0, near0, away0)) if s < seqs - 1 else (0, (keep1, near1, away1))
        earlier = after(s, i, image_ids, patches, cotangent, gain, *group, earlier)
    block_out, patch_grad = earlier
    return (
        block_out,
        patch_grad,
        norm_grad.reshape(dim),
        query_grad.reshape(HD),
        key_grad.reshape(HD),
        in_grad,
        out_grad.reshape(per * unit, dim),
    )


def solution(mesh):
    rows = P("batch", "tok", None)
    weights = P(("batch", "tok"), None)
    return jax.shard_map(
        functools.partial(per_device, mesh.shape["batch"], mesh.shape["tok"]),
        mesh=mesh,
        in_specs=(rows, P("batch", "tok"), rows, P(), P(), P(), weights, weights),
        out_specs=(rows, rows, P(), P(), P(), weights, weights),
        check_vma=False,
    )
```

```python
import functools
import math

import jax
import jax.numpy as jnp
import numpy as np
from jax import lax
from jax.experimental import pallas as pl
from jax.experimental.pallas import tpu as pltpu
from jax.sharding import PartitionSpec as P

H = 12
HD = 64
SLOTS = 4
EPS = 1e-06
BIG = 2048.0
LOG2E = 1.4426950408889634
BF = jnp.bfloat16
F32 = jnp.float32
NN = (((1,), (0,)), ((), ()))
NT = (((1,), (1,)), ((), ()))
TN = (((0,), (0,)), ((), ()))
MIB = 1 << 20
SMALL = pl.CostEstimate(flops=1, transcendentals=0, bytes_accessed=1)
LARGE = pl.CostEstimate(flops=60_000_000_000, transcendentals=0, bytes_accessed=1)

VMEM = pl.BlockSpec(memory_space=pltpu.VMEM)
SMEM = pl.BlockSpec(memory_space=pltpu.SMEM)
ANY = pl.BlockSpec(memory_space=pl.ANY)
HBM = pl.BlockSpec(memory_space=pltpu.HBM)


def hbm(*arrays):
    return [pltpu.with_memory_space_constraint(a, pltpu.HBM) for a in arrays]


def mm(a, b, dims=NN):
    return lax.dot_general(a, b, dims, preferred_element_type=F32)


def normalize(values):
    center = values - jnp.mean(values, axis=-1, keepdims=True)
    inverse = lax.rsqrt(jnp.mean(center * center, axis=-1, keepdims=True) + EPS)
    return center * inverse, inverse


def norm_back(grad_unit, unit_rows, inverse):
    return inverse * (
        grad_unit
        - jnp.mean(grad_unit, axis=-1, keepdims=True)
        - unit_rows * jnp.mean(grad_unit * unit_rows, axis=-1, keepdims=True)
    )


def column(row):
    return jnp.broadcast_to(row, (8, row.shape[1])).T[:, 0:1]


def prepare(ids, w_in, nb, nt):
    rows, wide = w_in.shape
    seqs, part = ids.shape
    width = H * HD
    local = width // nt
    units = (wide - 3 * width) // nt

    def kernel(ids_hbm, win_hbm, a_hbm, u_hbm, ids_ref, win_ref, a_ref, u_ref, in_sem, a_sem, u_sem):
        loads = [pltpu.make_async_copy(win_hbm, win_ref, in_sem.at[0]), pltpu.make_async_copy(ids_hbm, ids_ref, in_sem.at[1])]
        for copy in loads:
            copy.start()
        for copy in loads:
            copy.wait()
        row = jnp.concatenate([ids_ref[s : s + 1, :] for s in range(seqs)], axis=1).astype(F32).astype(BF)
        first = 3 * local
        second = jnp.concatenate([row[:, first:].astype(F32), jnp.zeros((1, 2 * first - seqs * part), F32)], axis=1).astype(BF)
        for t in range(nt):
            for k in range(3):
                a_ref[t, :rows, k * local : (k + 1) * local] = win_ref[:, k * width + t * local : k * width + (t + 1) * local]
            a_ref[t, rows : rows + 1] = row[:, :first]
            a_ref[t, rows + 1 :] = second
        for b in range(nb):
            pltpu.make_async_copy(a_ref, a_hbm.at[b], a_sem.at[b]).start()
        for t in range(nt):
            u_ref[t] = win_ref[:, 3 * width + t * units : 3 * width + (t + 1) * units]
        for b in range(nb):
            pltpu.make_async_copy(u_ref, u_hbm.at[b], u_sem.at[b]).start()
        for b in range(nb):
            pltpu.make_async_copy(a_ref, a_hbm.at[b], a_sem.at[b]).wait()
            pltpu.make_async_copy(u_ref, u_hbm.at[b], u_sem.at[b]).wait()

    return pl.pallas_call(
        kernel,
        out_shape=[
            jax.ShapeDtypeStruct((nb, nt, rows + 2, 3 * local), BF),
            jax.ShapeDtypeStruct((nb, nt, rows, units), BF),
        ],
        in_specs=[HBM] * 2,
        out_specs=[HBM] * 2,
        scratch_shapes=[
            pltpu.VMEM(ids.shape, jnp.int32),
            pltpu.VMEM(w_in.shape, BF),
            pltpu.VMEM((nt, rows + 2, 3 * local), BF),
            pltpu.VMEM((nt, rows, units), BF),
            pltpu.SemaphoreType.DMA((2,)),
            pltpu.SemaphoreType.DMA((nb,)),
            pltpu.SemaphoreType.DMA((nb,)),
        ],
        cost_estimate=SMALL,
        compiler_params=pltpu.CompilerParams(vmem_limit_bytes=16 * MIB),
        name="prepare",
    )(*hbm(ids, w_in))


def before_kernel(at_ref, table_hbm, ids_hbm, gain_hbm, x_hbm, cot_hbm, wout_hbm, *refs):
    outs, (table_ref, ids_ref, gain_ref, x_ref, cot_ref, wout_ref, pay_ref, in_sem, out_sem) = refs[:-9], refs[-9:]
    seqs = x_ref.shape[0]
    pays, unit_refs = outs[:2], outs[2:]
    ins = [
        pltpu.make_async_copy(a, b, in_sem.at[i])
        for i, (a, b) in enumerate(
            ((x_hbm, x_ref), (cot_hbm, cot_ref), (ids_hbm, ids_ref), (gain_hbm, gain_ref), (table_hbm, table_ref), (wout_hbm, wout_ref))
        )
    ]
    for copy in ins:
        copy.start()
    for copy in ins:
        copy.wait()
    for k, ref in enumerate(unit_refs):
        ref[...] = wout_ref[table_ref[at_ref[0], k]]
    copies = []
    for s in range(seqs):
        unit, _ = normalize(x_ref[s].astype(F32))
        live = column(jnp.where(ids_ref[s : s + 1, :] >= 0, 1.0, 0.0))
        pay_ref[s, 0] = (unit * gain_ref[...]).astype(BF)
        pay_ref[s, 1] = (live * cot_ref[s].astype(F32)).astype(BF)
        copies.append(pltpu.make_async_copy(pay_ref.at[s], pays[0].at[s] if s < seqs - 1 else pays[1].at[0], out_sem.at[s]))
        copies[-1].start()
    for copy in copies:
        copy.wait()


def before(at, table, ids, gain, x, cot, w_out):
    seqs, part, dim = x.shape
    per, unit, _ = w_out.shape
    outs = [jax.ShapeDtypeStruct((seqs - 1, 2, part, dim), BF), jax.ShapeDtypeStruct((1, 2, part, dim), BF)]
    outs += [jax.ShapeDtypeStruct((unit, dim), BF)] * per
    return pl.pallas_call(
        before_kernel,
        out_shape=outs,
        in_specs=[SMEM] + [HBM] * 6,
        out_specs=[HBM] * 2 + [VMEM] * per,
        scratch_shapes=[
            pltpu.SMEM(table.shape, jnp.int32),
            pltpu.VMEM(ids.shape, jnp.int32),
            pltpu.VMEM(gain.shape, F32),
            pltpu.VMEM(x.shape, BF),
            pltpu.VMEM(x.shape, BF),
            pltpu.VMEM(w_out.shape, BF),
            pltpu.VMEM((seqs, 2, part, dim), BF),
            pltpu.SemaphoreType.DMA((6,)),
            pltpu.SemaphoreType.DMA((seqs,)),
        ],
        cost_estimate=SMALL,
        compiler_params=pltpu.CompilerParams(vmem_limit_bytes=32 * MIB),
        name="before",
    )(at, *hbm(table, ids, gain, x, cot, w_out))


def join(at, got, seqs, part):
    count, high, wide = got.shape
    unit = high - 2
    dim = count * unit

    def kernel(at_ref, got_ref, w_ref, ids_ref, all_ref):
        def move(i, carry):
            all_ref[i] = got_ref[i, :unit]
            return carry

        lax.fori_loop(0, count, move, 0)
        w_ref[...] = all_ref[...].reshape(dim, wide).T
        for slot in range(SLOTS):
            i = at_ref[2] * SLOTS + (at_ref[1] ^ slot)
            row = jnp.concatenate([got_ref[i, unit : unit + 1], got_ref[i, unit + 1 :]], axis=1)
            row = row.astype(F32).astype(jnp.int32)
            for s in range(seqs):
                ids_ref[s, :, slot * part : (slot + 1) * part] = row[:, s * part : (s + 1) * part]

    return pl.pallas_call(
        kernel,
        out_shape=[jax.ShapeDtypeStruct((wide, dim), BF), jax.ShapeDtypeStruct((seqs, 1, SLOTS * part), jnp.int32)],
        in_specs=[SMEM, VMEM],
        out_specs=[VMEM] * 2,
        scratch_shapes=[pltpu.VMEM((count, unit, wide), BF)],
        cost_estimate=SMALL,
        compiler_params=pltpu.CompilerParams(vmem_limit_bytes=32 * MIB),
        name="join",
    )(at, got)


def pack_out(at, table, got, nb):
    unit, dim = got[0].shape
    per = len(got)

    def kernel(at_ref, table_ref, *refs):
        got_refs, (wo_hbm, ff_hbm, all_ref, wo_sem, ff_sem) = refs[:per], refs[per:]
        for k, ref in enumerate(got_refs):
            all_ref[table_ref[at_ref[0], per + k]] = ref[...]
        copies = [pltpu.make_async_copy(all_ref.at[0], wo_hbm.at[b], wo_sem.at[b]) for b in range(nb)]
        copies.append(pltpu.make_async_copy(all_ref.at[pl.ds(1, per - 1)], ff_hbm, ff_sem))
        for copy in copies:
            copy.start()
        for copy in copies:
            copy.wait()

    return pl.pallas_call(
        kernel,
        out_shape=[jax.ShapeDtypeStruct((nb, unit, dim), BF), jax.ShapeDtypeStruct((per - 1, unit, dim), BF)],
        in_specs=[SMEM] * 2 + [VMEM] * per,
        out_specs=[HBM] * 2,
        scratch_shapes=[
            pltpu.VMEM((per, unit, dim), BF),
            pltpu.SemaphoreType.DMA((nb,)),
            pltpu.SemaphoreType.DMA,
        ],
        cost_estimate=SMALL,
        name="pack_out",
    )(at, table, *got)


def add_blocks(ref, count, step, start, rows):
    total = ref[start, rows].astype(F32)
    for i in range(1, count):
        total = total + ref[start + i * step, rows].astype(F32)
    return total


def sum_qkv(up, nt):
    count, unit, dim = up.shape

    def kernel(up_ref, out_ref):
        for t in range(nt):
            out_ref[t] = add_blocks(up_ref, count // nt, nt, t, slice(None))

    return pl.pallas_call(
        kernel,
        out_shape=jax.ShapeDtypeStruct((nt, unit, dim), F32),
        in_specs=[VMEM],
        out_specs=VMEM,
        cost_estimate=SMALL,
        compiler_params=pltpu.CompilerParams(vmem_limit_bytes=32 * MIB),
        name="sum_qkv",
    )(up)


def fold(at, low, keep, got):
    n, high, dim = keep.shape

    def kernel(at_ref, keep_ref, *refs):
        got_refs, (own_ref, *send_refs) = refs[: len(got)], refs[len(got) :]
        mine = (at_ref[2] >> low) & 3
        for i in range(n // 4):
            for s, to in enumerate([own_ref] + send_refs):
                total = keep_ref[i * 4 + (mine ^ s)]
                for ref in got_refs:
                    total = total + ref[i * 4 + (mine ^ s)].astype(F32)
                to[i] = total.astype(to.dtype)

    out = lambda t: jax.ShapeDtypeStruct((n // 4, high, dim), t)
    return pl.pallas_call(
        kernel,
        out_shape=[out(F32)] + [out(BF)] * 3,
        in_specs=[SMEM] + [VMEM] * (1 + len(got)),
        out_specs=[VMEM] * 4,
        cost_estimate=SMALL,
        compiler_params=pltpu.CompilerParams(vmem_limit_bytes=32 * MIB),
        name="fold",
    )(at, keep, *got)


def split_rows(odd, grad, send_ref, keep_ref, start, rows):
    for z in range(send_ref.shape[0]):
        low = grad[2 * z * rows : (2 * z + 1) * rows]
        high = grad[(2 * z + 1) * rows : (2 * z + 2) * rows]
        send_ref[z, start : start + rows] = jnp.where(odd, low, high).astype(BF)
        keep_ref[z, start : start + rows] = jnp.where(odd, high, low)


def leave(at, table, terms):
    per = table.shape[1] // 2
    _, high, dim = terms[0].shape
    unit = high // per

    def kernel(at_ref, table_ref, *refs):
        term_refs, out_refs, all_ref = refs[: len(terms)], refs[len(terms) : -1], refs[-1]
        total = term_refs[0][0]
        for ref in term_refs[1:]:
            total = total + ref[0].astype(F32)
        for k in range(per):
            all_ref[k] = total[k * unit : (k + 1) * unit]
        for k, ref in enumerate(out_refs):
            ref[...] = all_ref[table_ref[at_ref[0], per + k]]

    return pl.pallas_call(
        kernel,
        out_shape=[jax.ShapeDtypeStruct((unit, dim), F32)] * per,
        in_specs=[SMEM] * 2 + [VMEM] * len(terms),
        out_specs=[VMEM] * per,
        scratch_shapes=[pltpu.VMEM((per, unit, dim), F32)],
        cost_estimate=SMALL,
        name="leave",
    )(at, table, *terms)


def place(at, table, qkv, up, got):
    nt, unit, width = qkv.shape
    count, high, dim = up.shape
    per = len(got)
    local = width // 3
    wide = nt * (width + dim)

    def kernel(at_ref, table_ref, qkv_ref, up_ref, *refs):
        got_refs, (in_ref, out_ref, norm_ref, q_ref, k_ref) = refs[:per], refs[per:]
        for t in range(nt):
            for k in range(3):
                to = k * nt * local + t * local
                in_ref[:, to : to + local] = qkv_ref[t, :, k * local : (k + 1) * local]
            to = nt * width + t * dim
            in_ref[:, to : to + dim] = add_blocks(up_ref, count // nt, nt, t, slice(0, unit))
        for k, ref in enumerate(got_refs):
            out_ref[table_ref[at_ref[0], k]] = ref[...]
        small = add_blocks(up_ref, count, 1, 0, slice(unit, high))
        small = small[0:2] + small[2:4]
        norm_ref[...] = small[0:1]
        q_ref[...] = small[1:2, :HD]
        k_ref[...] = small[1:2, HD : 2 * HD]

    return pl.pallas_call(
        kernel,
        out_shape=[
            jax.ShapeDtypeStruct((unit, wide), F32),
            jax.ShapeDtypeStruct((per, unit, dim), F32),
            jax.ShapeDtypeStruct((1, dim), F32),
            jax.ShapeDtypeStruct((1, HD), F32),
            jax.ShapeDtypeStruct((1, HD), F32),
        ],
        in_specs=[SMEM] * 2 + [VMEM] * (2 + per),
        out_specs=[VMEM] * 5,
        cost_estimate=SMALL,
        compiler_params=pltpu.CompilerParams(vmem_limit_bytes=32 * MIB),
        name="place",
    )(at, table, qkv, up, *got)


def after_kernel(s, ids_ref, x_ref, cot_ref, gain_ref, keep_ref, near_ref, far_ref, *rest):
    out_ref, grad_ref = rest[-2:]
    unit, inverse = normalize(x_ref[0].astype(F32))
    live = column(jnp.where(ids_ref[s : s + 1, :] >= 0, 1.0, 0.0))
    both = keep_ref[0, 0].astype(F32) + near_ref[0, 0].astype(F32) + far_ref[0].astype(F32)
    out_ref[0] = (live * (x_ref[0].astype(F32) + both[0])).astype(BF)
    grad_ref[0] = (
        live * cot_ref[0].astype(F32) + norm_back(both[1] * gain_ref[...], unit, inverse)
    ).astype(BF)


def after(s, i, ids, x, cot, gain, keep, near, far, earlier):
    x, cot, keep, near, far = (pltpu.with_memory_space_constraint(a, pltpu.HBM) for a in (x, cot, keep, near, far))
    seqs, part, dim = x.shape
    one = pl.BlockSpec((1, part, dim), lambda g: (s, 0, 0))
    pair = pl.BlockSpec((1, 1, 2, part, dim), lambda g: (0, i, 0, 0, 0))
    lone = pl.BlockSpec((1, 2, part, dim), lambda g: (i, 0, 0, 0))
    fixed = lambda a: pl.BlockSpec(a.shape, lambda g: (0,) * a.ndim)
    return pl.pallas_call(
        functools.partial(after_kernel, s),
        grid=(1,),
        out_shape=[jax.ShapeDtypeStruct(x.shape, BF)] * 2,
        in_specs=[fixed(ids), one, one, fixed(gain), pair, pair, lone] + [ANY] * len(earlier),
        out_specs=[one, one],
        input_output_aliases={7 + i: i for i in range(len(earlier))},
        cost_estimate=SMALL,
        compiler_params=pltpu.CompilerParams(vmem_limit_bytes=32 * MIB),
        name="after",
    )(ids, x, cot, gain, keep, near, far, *earlier)


def attention_kernel(
    heads, block, groups,
    ids_ref, qg_ref, kg_ref, wqkv_hbm, wo_hbm, *refs,
):
    pays, refs = refs[: SLOTS * len(groups)], refs[SLOTS * len(groups) :]
    (o_hbm, grad_hbm, sendq_ref, go_ref, np_ref, sums_ref), refs = refs[:6], refs[6:]
    (
        wqkv_ref, wo_ref, norm_ref, gb_ref, o_ref, grad_ref, gq_ref, acc_ref, raw_ref,
        qt_ref, qn_ref, kt_ref, ka_ref, vt_ref, va_ref, do_ref, dq_ref, dk_ref, dv_ref, pad_ref, vm_ref,
        w_sem, sem, out_sem,
    ) = refs
    seqs, length, dim = norm_ref.shape
    part = length // SLOTS
    width = heads * HD
    blocks = length // block
    loads = [pltpu.make_async_copy(wqkv_hbm, wqkv_ref, w_sem.at[0]), pltpu.make_async_copy(wo_hbm, wo_ref, w_sem.at[1])]
    loads[0].start()

    def pay_copy(s, j, t, source):
        to = (norm_ref, gb_ref)[j].at[s, pl.ds(t * part, part), :]
        return pltpu.make_async_copy(source, to, sem.at[s, j * SLOTS + t])

    s = 0
    for g, size in enumerate(groups):
        for i in range(size):
            for j in range(2):
                for t in range(SLOTS):
                    pay_copy(s, j, t, pays[g * SLOTS + t].at[i, j]).start()
                if s + j == 0:
                    loads[1].start()
            s += 1
    gq_ref[...] = jnp.zeros_like(gq_ref)
    go_ref[...] = jnp.zeros_like(go_ref)
    acc_ref[...] = jnp.zeros_like(acc_ref)
    gain_q = qg_ref[...]
    gain_k = kg_ref[...]
    marks = lax.broadcasted_iota(jnp.int32, (HD, length), 0)
    v_tail = jnp.where(lax.broadcasted_iota(jnp.int32, (length, HD), 1) < 2, 1.0, 0.0).astype(BF)
    ones = jnp.where(lax.broadcasted_iota(jnp.int32, (16, length), 0) == 0, 1.0, 0.0).astype(BF)
    spot = lax.broadcasted_iota(jnp.int32, (HD, block), 0)
    scale = 1.0 / math.sqrt(HD)
    cut = lambda a, i: a[:, i * block : (i + 1) * block]

    def unit_of(row):
        raw = raw_ref[pl.ds(pl.multiple_of(row, HD), HD), :]
        center = raw - jnp.mean(raw, axis=0, keepdims=True)
        inverse = lax.rsqrt(jnp.mean(center * center, axis=0, keepdims=True) + EPS)
        return center * inverse, inverse

    def lanes(a):
        total = a[:, :128]
        for i in range(1, length // 128):
            total = total + a[:, i * 128 : (i + 1) * 128]
        return total

    def stores(s):
        return [
            pltpu.make_async_copy(o_ref.at[s], o_hbm.at[s], out_sem.at[s, 0]),
            pltpu.make_async_copy(grad_ref.at[s], grad_hbm.at[s], out_sem.at[s, 1]),
        ]

    loads[0].wait()
    loads[1].wait()

    def sequence(s, carry):
        ids = ids_ref[s]
        same = marks == ids + 1
        k_tail = jnp.where(same, 1.0, 0.0).T.astype(BF)
        q_tail = jnp.where((same & (ids >= 0)) | (marks > 4), 0.0, -BIG).astype(BF)
        pad = jnp.where(ids < 0, 1.0, 0.0)
        for i in range(blocks):
            pad_ref[i] = cut(pad, i)
        for t in range(SLOTS):
            pay_copy(s, 0, t, pays[0].at[0, 0]).wait()
        raw_ref[...] = mm(wqkv_ref[...], norm_ref[s], NT)
        for t in range(SLOTS):
            pay_copy(s, 1, t, pays[0].at[0, 0]).wait()
        do_all = mm(wo_ref[...], gb_ref[s], NT).astype(BF)
        for h in range(heads):
            for i in range(blocks):
                do_ref[h * blocks + i] = cut(do_all[h * HD : (h + 1) * HD], i)

        def prepare(h, carry):
            q_unit, _ = unit_of(h * HD)
            q = q_unit * gain_q
            qn = q.T.astype(BF)
            for i in range(blocks):
                qt_ref[h * blocks + i, :HD] = cut(q, i).astype(BF)
                qt_ref[h * blocks + i, HD:] = cut(q_tail, i)
                qn_ref[h * blocks + i] = qn[i * block : (i + 1) * block]
            k_unit, _ = unit_of(width + h * HD)
            k = k_unit * gain_k
            kt_ref[h] = k.astype(BF)
            ka_ref[h, :, :HD] = k.T.astype(BF)
            ka_ref[h, :, HD:] = k_tail
            v = raw_ref[pl.ds(pl.multiple_of(2 * width + h * HD, HD), HD), :]
            vb = v.astype(BF)
            vt_ref[h, :HD] = vb
            vt_ref[h, HD:] = ones
            va_ref[h, :, :HD] = v.T.astype(BF)
            va_ref[h, :, HD:] = v_tail
            vm_ref[h] = jnp.mean(vb.astype(F32), axis=1, keepdims=True)
            dk_ref[h] = jnp.zeros(dk_ref.shape[1:], F32)
            dv_ref[h] = jnp.zeros(dv_ref.shape[1:], F32)
            return carry

        lax.fori_loop(0, heads, prepare, 0)

        def step(n, carry):
            h = n // blocks
            padb = pad_ref[n % blocks]
            e = jnp.exp2(mm(ka_ref[h], qt_ref[n]) * (LOG2E * scale))
            eb = e.astype(BF)
            oa = mm(vt_ref[h], eb)
            inv = 1.0 / (oa[HD : HD + 1] + padb)
            o = oa[:HD] * inv
            dos = (do_ref[n].astype(F32) * inv).astype(BF)
            delta = jnp.sum(dos.astype(F32) * o, axis=0, keepdims=True)
            d0 = delta.astype(BF).astype(F32)
            tail = jnp.where(spot == 0, -d0, jnp.where(spot == 1, d0 - delta, 0.0))
            doa = jnp.concatenate([dos.astype(F32), tail], axis=0)
            ds = (e * mm(va_ref[h], doa.astype(BF))).astype(BF)
            dq_ref[n] = mm(kt_ref[h], ds)
            dk_ref[h] += mm(ds, qn_ref[n])
            dv_ref[h] += mm(eb, doa.T.astype(BF))
            do_ref[n] = jnp.where(padb > 0, vm_ref[h], o).astype(BF)
            return carry

        lax.fori_loop(0, heads * blocks, step, 0)

        def finish(h, carry):
            rows = lambda at: pl.ds(pl.multiple_of(at + h * HD, HD), HD)
            gq = jnp.concatenate([dq_ref[h * blocks + i] for i in range(blocks)], axis=1)
            gk = dk_ref[h].T
            for k, (g, gain_col) in enumerate(((gq, gain_q), (gk, gain_k))):
                unit, inverse = unit_of(k * width + h * HD)
                g = (g * scale).astype(BF).astype(F32)
                acc_ref[k] += lanes(g * unit)
                g = g * gain_col
                back = inverse * (
                    g - jnp.mean(g, axis=0, keepdims=True) - unit * jnp.mean(g * unit, axis=0, keepdims=True)
                )
                grad_ref[s, rows(k * width), :] = back.astype(BF)
            grad_ref[s, rows(2 * width), :] = dv_ref[h].T[:HD].astype(BF)
            for i in range(blocks):
                o_ref[s, rows(0), pl.ds(i * block, block)] = do_ref[h * blocks + i]
            return carry

        lax.fori_loop(0, heads, finish, 0)
        for copy in stores(s):
            copy.start()
        gq_ref[...] += mm(grad_ref[s], norm_ref[s])
        go_ref[...] += mm(o_ref[s], gb_ref[s])
        return carry

    lax.fori_loop(0, seqs, sequence, 0)
    g_q = gq_ref[...]
    np_ref[...] = jnp.sum(wqkv_ref[...].astype(F32) * g_q, axis=0, keepdims=True)
    sums_ref[...] = jnp.concatenate([jnp.sum(acc_ref[k].T, axis=0, keepdims=True) for k in range(2)], axis=1)
    g_q = g_q.T.astype(BF)
    count, rows, _ = sendq_ref.shape
    for i in range(count):
        sendq_ref[i] = g_q[i * rows : (i + 1) * rows]
    for s in range(seqs):
        for copy in stores(s):
            copy.wait()


def attention(ids, wqkv, wo, qg, kg, groups, count):
    wide, dim = wqkv.shape
    width = wo.shape[0]
    heads = width // HD
    sizes = [g[0].shape[0] for g in groups]
    seqs, part = sum(sizes), groups[0][0].shape[2]
    length = part * SLOTS
    block = 512
    blocks = length // block
    ins = [ids, qg, kg, *hbm(wqkv, wo, *[p for g in groups for p in g])]
    outs = [
        jax.ShapeDtypeStruct((seqs, width, length), BF),
        jax.ShapeDtypeStruct((seqs, wide, length), BF),
        jax.ShapeDtypeStruct((count, dim // count, wide), BF),
        jax.ShapeDtypeStruct((width, dim), F32),
        jax.ShapeDtypeStruct((1, dim), F32),
        jax.ShapeDtypeStruct((1, 2 * HD), F32),
    ]
    flops = seqs * (2 * length * dim * width * 8 + heads * 6 * 2 * length * length * HD)
    return pl.pallas_call(
        functools.partial(attention_kernel, heads, block, sizes),
        out_shape=outs,
        in_specs=[VMEM] * 3 + [HBM] * (2 + SLOTS * len(groups)),
        out_specs=[HBM] * 2 + [VMEM] * 4,
        scratch_shapes=[
            pltpu.VMEM((wide, dim), BF),
            pltpu.VMEM((width, dim), BF),
            pltpu.VMEM((seqs, length, dim), BF),
            pltpu.VMEM((seqs, length, dim), BF),
            pltpu.VMEM((seqs, width, length), BF),
            pltpu.VMEM((seqs, wide, length), BF),
            pltpu.VMEM((wide, dim), F32),
            pltpu.VMEM((2, HD, 128), F32),
            pltpu.VMEM((wide, length), F32),
            pltpu.VMEM((heads * blocks, 2 * HD, block), BF),
            pltpu.VMEM((heads * blocks, block, HD), BF),
            pltpu.VMEM((heads, HD, length), BF),
            pltpu.VMEM((heads, length, 2 * HD), BF),
            pltpu.VMEM((heads, HD + 16, length), BF),
            pltpu.VMEM((heads, length, 2 * HD), BF),
            pltpu.VMEM((heads * blocks, HD, block), BF),
            pltpu.VMEM((heads * blocks, HD, block), F32),
            pltpu.VMEM((heads, length, HD), F32),
            pltpu.VMEM((heads, length, 2 * HD), F32),
            pltpu.VMEM((blocks, 1, block), F32),
            pltpu.VMEM((heads, HD, 1), F32),
            pltpu.SemaphoreType.DMA((4,)),
            pltpu.SemaphoreType.DMA((seqs, 2 * SLOTS)),
            pltpu.SemaphoreType.DMA((seqs, 2)),
        ],
        cost_estimate=LARGE,
        compiler_params=pltpu.CompilerParams(vmem_limit_bytes=56 * MIB),
        name="attention",
    )(*ins)


def ffn_kernel(block, groups, plan, at_ref, go_ref, anp_ref, sums_ref, gain_ref, wup_hbm, *refs):
    pieces, refs = refs[: len(plan)], refs[len(plan) :]
    pays, refs = refs[: len(groups) * SLOTS], refs[len(groups) * SLOTS :]
    (hid_hbm, gup_hbm, wff_hbm, sendu_ref, sendf_ref, keepf_ref), refs = refs[:6], refs[6:]
    norm_ref, gb_ref, hid_ref, gup_ref, wup_ref, wff_ref, gin_ref, gff_ref, sem, out_sem, w_sem = refs
    dim = wup_ref.shape[0]
    part = pays[0].shape[2]
    total = norm_ref.shape[0]
    weights = [pltpu.make_async_copy(wup_hbm, wup_ref, w_sem.at[0])]
    head_rows = go_ref.shape[0] // (2 * sendf_ref.shape[0])
    rows = sendf_ref.shape[1] - head_rows
    for ref, masks in zip(pieces, plan):
        for i, mask in enumerate(masks):
            to = wff_ref.at[pl.ds(pl.multiple_of((at_ref[2] ^ mask) * rows, rows), rows), :]
            weights.append(pltpu.make_async_copy(ref.at[i], to, w_sem.at[len(weights)]))
    for copy in weights:
        copy.start()
    n = 0
    for g, seqs in enumerate(groups):
        for s in range(seqs):
            for t in range(SLOTS):
                for k, to in enumerate((norm_ref, gb_ref)):
                    source = pays[g * SLOTS + t].at[s, k]
                    pltpu.make_async_copy(source, to.at[pl.ds(n * part, part), :], sem.at[k, n]).start()
                n += 1
    gin_ref[...] = jnp.zeros_like(gin_ref)
    gff_ref[...] = jnp.zeros_like(gff_ref)
    for copy in weights:
        copy.wait()
    joined = pltpu.make_async_copy(wff_ref, wff_hbm, w_sem.at[0])
    joined.start()
    c0 = math.sqrt(2.0 / math.pi)
    c1 = 0.044715

    def outs(i):
        at_rows = pl.ds(pl.multiple_of(i * block, block), block)
        return (
            pltpu.make_async_copy(hid_ref.at[at_rows, :], hid_hbm.at[at_rows, :], out_sem.at[0, i]),
            pltpu.make_async_copy(gup_ref.at[at_rows, :], gup_hbm.at[at_rows, :], out_sem.at[1, i]),
        )

    def step(i, carry):
        for j in range(block // part):
            for k, to in enumerate((norm_ref, gb_ref)):
                pltpu.make_async_copy(pays[0].at[0, 0], to.at[pl.ds(0, part), :], sem.at[k, i * (block // part) + j]).wait()
        at_rows = pl.ds(pl.multiple_of(i * block, block), block)
        up = mm(norm_ref[at_rows, :], wup_ref[...])
        gh = mm(gb_ref[at_rows, :], wff_ref[...], NT)
        sq = up * up
        t = jnp.tanh(up * (c0 + (c0 * c1) * sq))
        half = 0.5 + 0.5 * t
        hid_ref[at_rows, :] = (up * half).astype(BF)
        gup_ref[at_rows, :] = (gh * (half + (0.5 * up) * (1.0 - t * t) * (c0 + (3.0 * c0 * c1) * sq))).astype(BF)
        for copy in outs(i):
            copy.start()
        gin_ref[...] += mm(norm_ref[at_rows, :], gup_ref[at_rows, :], TN)
        gff_ref[...] += mm(hid_ref[at_rows, :], gb_ref[at_rows, :], TN)
        return carry

    lax.fori_loop(0, total // block, step, 0)
    line = jnp.sum(wup_ref[...].astype(F32) * gin_ref[...], axis=1, keepdims=True)
    first = (jnp.broadcast_to(line, (dim, 128)).T[0:1] + anp_ref[...]) / gain_ref[...]
    second = jnp.concatenate([sums_ref[...], jnp.zeros((1, dim - 2 * HD), F32)], axis=1)
    small = jnp.concatenate([first, second], axis=0)
    high = small.astype(BF).astype(F32)
    small = jnp.concatenate([high, small - high], axis=0).astype(BF)
    count, unit, _ = sendu_ref.shape
    unit = unit - 4
    for i in range(count):
        sendu_ref[i, :unit] = gin_ref[i * unit : (i + 1) * unit, :].astype(BF)
        sendu_ref[i, unit:] = small
    odd = (at_ref[2] & 1) > 0
    split_rows(odd, go_ref[...], sendf_ref, keepf_ref, 0, head_rows)
    split_rows(odd, gff_ref[...], sendf_ref, keepf_ref, head_rows, rows)
    joined.wait()

    def drain(i, carry):
        for copy in outs(i):
            copy.wait()
        return carry

    lax.fori_loop(0, total // block, drain, 0)


def ffn(at, go, anp, sums, gain, wup, ff_parts, groups, count, block=512):
    dim, units = wup.shape
    sizes = [g[0].shape[0] for g in groups]
    part = groups[0][0].shape[2]
    total = SLOTS * part * sum(sizes)
    pieces = [p for g in groups for p in g]
    act = jax.ShapeDtypeStruct((total, units), BF)
    return pl.pallas_call(
        functools.partial(ffn_kernel, block, sizes, [masks for _, masks in ff_parts]),
        out_shape=[
            act,
            act,
            jax.ShapeDtypeStruct((units, dim), BF),
            jax.ShapeDtypeStruct((count * SLOTS, dim // (count * SLOTS) + 4, units), BF),
            jax.ShapeDtypeStruct((count // 2, (units + go.shape[0]) // count, dim), BF),
            jax.ShapeDtypeStruct((count // 2, (units + go.shape[0]) // count, dim), F32),
        ],
        in_specs=[SMEM] + [VMEM] * 4 + [HBM] * (1 + len(ff_parts) + len(pieces)),
        out_specs=[HBM] * 3 + [VMEM] * 3,
        scratch_shapes=[
            pltpu.VMEM((total, dim), BF),
            pltpu.VMEM((total, dim), BF),
            pltpu.VMEM((total, units), BF),
            pltpu.VMEM((total, units), BF),
            pltpu.VMEM((dim, units), BF),
            pltpu.VMEM((units, dim), BF),
            pltpu.VMEM((dim, units), F32),
            pltpu.VMEM((units, dim), F32),
            pltpu.SemaphoreType.DMA((2, total // part)),
            pltpu.SemaphoreType.DMA((2, total // block)),
            pltpu.SemaphoreType.DMA((1 + count,)),
        ],
        cost_estimate=LARGE,
        compiler_params=pltpu.CompilerParams(vmem_limit_bytes=58 * MIB),
        name="ffn",
    )(at, go, anp, sums, gain, *hbm(wup, *[a for a, _ in ff_parts], *pieces))


def outputs(start, first, seqs, o, hid, gq, gu, wo, wff, wqkv, wup):
    length = o.shape[2]
    dim = wo.shape[1]
    part = length // SLOTS

    def kernel(o_hbm, hid_hbm, gq_hbm, gu_hbm, wo_hbm, wff_hbm, wqkv_hbm, wup_hbm, keep_hbm, send_hbm, *scratch):
        o_ref, hid_ref, gq_ref, gu_ref, wo_ref, wff_ref, wqkv_ref, wup_ref, res_ref, w_sem, sem, out_sem = scratch

        def load(k, s):
            rows = pl.ds((start + s) * length, length)
            source, to = (
                (hid_hbm.at[rows, :], hid_ref), (o_hbm.at[first + s], o_ref), (gu_hbm.at[rows, :], gu_ref), (gq_hbm.at[first + s], gq_ref)
            )[k]
            return pltpu.make_async_copy(source, to.at[s], sem.at[s, k])

        weights = [
            pltpu.make_async_copy(a, b, w_sem.at[k])
            for k, (a, b) in enumerate(((wff_hbm, wff_ref), (wo_hbm, wo_ref), (wup_hbm, wup_ref), (wqkv_hbm, wqkv_ref)))
        ]
        for k in range(4):
            weights[k].start()
            load(k, 0).start()
        for s in range(1, seqs):
            for k in range(4):
                load(k, s).start()

        weights[0].wait()
        weights[1].wait()
        half = length // 2

        def step(n, carry):
            s, i = n // 2, n % 2
            lanes = pl.ds(pl.multiple_of(i * half, half), half)

            @pl.when(i == 0)
            def _():
                load(0, s).wait()
                load(1, s).wait()

            res_ref[s, 0, lanes, :] = (mm(o_ref[s, :, lanes], wo_ref[...], TN) + mm(hid_ref[s, lanes, :], wff_ref[...])).astype(BF)

            @pl.when(n == 0)
            def _():
                weights[2].wait()
                weights[3].wait()

            @pl.when(i == 0)
            def _():
                load(2, s).wait()
                load(3, s).wait()

            res_ref[s, 1, lanes, :] = (
                mm(gq_ref[s, :, lanes], wqkv_ref[...], TN) + mm(gu_ref[s, lanes, :], wup_ref[...], NT)
            ).astype(BF)
            for copy in moves(s, i):
                copy.start()
            return carry

        def moves(s, i):
            out = []
            for j in range(2):
                for k, to in enumerate((keep_hbm, send_hbm)):
                    rows = pl.ds(pl.multiple_of(i * half + k * part, part), part)
                    out.append(pltpu.make_async_copy(res_ref.at[s, j, rows, :], to.at[i, s, j], out_sem.at[s, j, 2 * i + k]))
            return out

        lax.fori_loop(0, 2 * seqs, step, 0)
        for s in range(seqs):
            for i in range(2):
                for copy in moves(s, i):
                    copy.wait()

    return pl.pallas_call(
        kernel,
        out_shape=[jax.ShapeDtypeStruct((SLOTS // 2, seqs, 2, part, dim), BF)] * 2,
        in_specs=[HBM] * 8,
        out_specs=[HBM] * 2,
        scratch_shapes=[
            pltpu.VMEM((seqs,) + o.shape[1:], BF),
            pltpu.VMEM((seqs, length, hid.shape[1]), BF),
            pltpu.VMEM((seqs,) + gq.shape[1:], BF),
            pltpu.VMEM((seqs, length, gu.shape[1]), BF),
            pltpu.VMEM(wo.shape, BF),
            pltpu.VMEM(wff.shape, BF),
            pltpu.VMEM(wqkv.shape, BF),
            pltpu.VMEM(wup.shape, BF),
            pltpu.VMEM((seqs, 2, length, dim), BF),
            pltpu.SemaphoreType.DMA((4,)),
            pltpu.SemaphoreType.DMA((seqs, 4)),
            pltpu.SemaphoreType.DMA((seqs, 2, SLOTS)),
        ],
        cost_estimate=SMALL,
        compiler_params=pltpu.CompilerParams(vmem_limit_bytes=48 * MIB),
        name="outputs",
    )(*hbm(o, hid, gq, gu, wo, wff, wqkv, wup))


def swap(value, axis, count, mask):
    return lax.ppermute(value, axis, [(i, i ^ mask) for i in range(count)])


def tie(value, *after):
    return lax.optimization_barrier((value,) + after)[0]


def bit_groups(count):
    bits = list(range(count.bit_length() - 1))[::-1]
    groups = []
    while bits:
        take = 2 if len(bits) > 1 else 1
        groups.append(bits[:take])
        bits = bits[take:]
    assert len(groups[-1]) == 1
    return groups


def gather_batch(block, count, groups):
    held, masks = block[None], [0]
    for bits in groups:
        low = bits[-1]
        parts = [(held, masks)]
        for s in range(1, 1 << len(bits)):
            parts.append((swap(held, "batch", count, s << low), [m ^ (s << low) for m in masks]))
        held = jnp.concatenate([a for a, _ in parts], axis=0)
        masks = sum((m for _, m in parts), [])
    return parts


def matchings(edges, devices, per_device):
    left = [[] for _ in range(devices)]
    for e, (source, _, _) in enumerate(edges):
        left[source].append(e)
    rounds = []
    for _ in range(per_device):
        owner = [-1] * devices

        def place(source, seen):
            for e in left[source]:
                target = edges[e][1]
                if target in seen:
                    continue
                seen.add(target)
                if owner[target] < 0 or place(edges[owner[target]][0], seen):
                    owner[target] = e
                    return True
            return False

        for source in range(devices):
            place(source, set())
        rounds.append(list(owner))
        for e in owner:
            left[edges[e][0]].remove(e)
    return rounds


def unit_plan(nb, nt, rows, width, hidden):
    unit = math.gcd(math.gcd(rows, width // nt), hidden // nt)
    per = rows // unit
    head_units, hid_units = width // nt // unit, hidden // nt // unit
    assert head_units == nb and hid_units % nb == 0
    c = hid_units // nb
    edges = []
    for t in range(nt):
        for b in range(nb):
            want = [t * head_units + b]
            want += [nt * head_units + t * hid_units + b * c + i for i in range(c)]
            for slot, u in enumerate(want):
                edges.append((u // per, b * nt + t, (u % per, slot)))
    table = np.zeros((nb * nt, 2 * per), np.int32)
    perms = []
    for k, owner in enumerate(matchings(edges, nb * nt, per)):
        perms.append([(edges[e][0], edges[e][1]) for e in owner])
        for e in owner:
            table[edges[e][0], k] = edges[e][2][0]
            table[edges[e][1], per + k] = edges[e][2][1]
    return unit, per, perms, table


def per_device(
    nb, nt, patches, image_ids, cotangent, norm_gain, query_gain, key_gain, in_weight, out_weight
):
    seqs, part, dim = patches.shape
    width = H * HD
    local = width // nt
    units = (in_weight.shape[1] - 3 * width) // nt
    rows_in = in_weight.shape[0]
    unit, per, perms, table = unit_plan(nb, nt, out_weight.shape[0], width, units * nt)
    assert nt == SLOTS and units == dim and unit == rows_in and dim == nt * local and per == nt + 1
    both = ("batch", "tok")
    me_b = lax.axis_index("batch")
    me_t = lax.axis_index("tok")
    at = jnp.stack([me_b * nt + me_t, me_t, me_b])
    table = jnp.asarray(table)
    gain = norm_gain.reshape(1, dim)

    def exchange(value, axis):
        return lax.all_to_all(value, axis, split_axis=0, concat_axis=0, tiled=True)

    groups = bit_groups(nb)

    a_src, u_src = prepare(image_ids, in_weight, nb, nt)
    a_got = exchange(a_src.reshape(nb * nt, rows_in + 2, 3 * local), both)
    own0, own1, *unit_sends = before(
        at, table, image_ids, gain, tie(patches, a_src), cotangent, out_weight.reshape(per, unit, dim)
    )
    far0 = swap(own0, "tok", nt, 2)
    got = [lax.ppermute(v, both, perm) for v, perm in zip(unit_sends, perms)]
    wo_src, ff_src = pack_out(at, table, got, nb)
    ff_parts = gather_batch(ff_src.reshape((per - 1) * unit, dim), nb, groups[::-1])
    wo = exchange(tie(wo_src, a_got), "batch").reshape(local, dim)
    wqkv, ids = join(at, a_got, seqs, part)
    far1 = swap(tie(own1, far0, wo_src), "tok", nt, 2)
    slots0 = [own0, swap(own0, "tok", nt, 1), far0, swap(tie(far0, wo_src), "tok", nt, 1)]
    slots1 = [own1, swap(own1, "tok", nt, 1), far1, swap(far1, "tok", nt, 1)]
    wup = exchange(tie(u_src, wo).reshape(nb * nt, unit, dim), both).reshape(dim, units)

    qg = query_gain.reshape(HD, 1)
    kg = key_gain.reshape(HD, 1)

    def leave_core(s, i, o, gq):
        keep, send = outputs(s, i, 1, o, hid, gq, gup, wo, wff, wqkv, wup)
        return keep, swap(send, "tok", nt, 1)

    def leave_chip(keep, near):
        value = (keep[1].astype(F32) + near[1].astype(F32)).astype(BF)
        return value, swap(value, "tok", nt, 2)

    o, gq, a_q, go, a_np, sums = attention(ids, wqkv, tie(wo, ff_parts[0][0]), qg, kg, [slots0, slots1], nb * nt)
    a_q = sum_qkv(exchange(a_q, both), nt)
    hid, gup, wff, f_up, f_send, f_keep = ffn(at, go, a_np, sums, gain, wup, ff_parts, [slots0, slots1], nb)
    f_up = exchange(tie(f_up, a_q), both)
    terms = [f_keep, swap(f_send, "batch", nb, 1)]
    group = []
    o = tie(o, a_q)
    for s in range(seqs):
        if s == seqs - 1:
            value, away = leave_chip(*group[0])
            group[0].append(away)
            o = tie(o, value)
            for bits in groups[:-1][::-1]:
                own, *sends = fold(at, bits[-1], terms[0], terms[1:])
                terms = [own] + [swap(v, "batch", nb, (k + 1) << bits[-1]) for k, v in enumerate(sends)]
                o = tie(o, own)
        keep, near = leave_core(s, s, o, gq)
        group.append([keep, near])
        o = tie(o, keep)
    for s in range(1, seqs):
        group[s].append(leave_chip(*group[s])[1])

    sends = leave(at, table, terms)
    got = [lax.ppermute(v, both, [(b, a) for a, b in perm]) for v, perm in zip(sends, perms)]
    in_grad, out_grad, norm_grad, query_grad, key_grad = place(at, table, a_q, f_up, got)

    earlier = []
    for s in range(seqs):
        earlier = after(s, 0, image_ids, patches, cotangent, gain, *group[s], earlier)
    block_out, patch_grad = earlier
    return (
        block_out,
        patch_grad,
        norm_grad.reshape(dim),
        query_grad.reshape(HD),
        key_grad.reshape(HD),
        in_grad,
        out_grad.reshape(per * unit, dim),
    )


def solution(mesh):
    rows = P("batch", "tok", None)
    weights = P(("batch", "tok"), None)
    return jax.shard_map(
        functools.partial(per_device, mesh.shape["batch"], mesh.shape["tok"]),
        mesh=mesh,
        in_specs=(rows, P("batch", "tok"), rows, P(), P(), P(), weights, weights),
        out_specs=(rows, rows, P(), P(), P(), weights, weights),
        check_vma=False,
    )
```

```python
import functools
import math

import jax
import jax.numpy as jnp
import numpy as np
from jax import lax
from jax.experimental import pallas as pl
from jax.experimental.pallas import tpu as pltpu
from jax.sharding import PartitionSpec as P

H = 12
HD = 64
SLOTS = 4
EPS = 1e-06
BIG = 2048.0
LOG2E = 1.4426950408889634
BF = jnp.bfloat16
F32 = jnp.float32
NN = (((1,), (0,)), ((), ()))
NT = (((1,), (1,)), ((), ()))
TN = (((0,), (0,)), ((), ()))
MIB = 1 << 20
SMALL = pl.CostEstimate(flops=1, transcendentals=0, bytes_accessed=1)
LARGE = pl.CostEstimate(flops=60_000_000_000, transcendentals=0, bytes_accessed=1)

VMEM = pl.BlockSpec(memory_space=pltpu.VMEM)
SMEM = pl.BlockSpec(memory_space=pltpu.SMEM)
ANY = pl.BlockSpec(memory_space=pl.ANY)
HBM = pl.BlockSpec(memory_space=pltpu.HBM)


def hbm(*arrays):
    return [pltpu.with_memory_space_constraint(a, pltpu.HBM) for a in arrays]


def mm(a, b, dims=NN):
    return lax.dot_general(a, b, dims, preferred_element_type=F32)


def normalize(values):
    center = values - jnp.mean(values, axis=-1, keepdims=True)
    inverse = lax.rsqrt(jnp.mean(center * center, axis=-1, keepdims=True) + EPS)
    return center * inverse, inverse


def norm_back(grad_unit, unit_rows, inverse):
    return inverse * (
        grad_unit
        - jnp.mean(grad_unit, axis=-1, keepdims=True)
        - unit_rows * jnp.mean(grad_unit * unit_rows, axis=-1, keepdims=True)
    )


def column(row):
    return jnp.broadcast_to(row, (8, row.shape[1])).T[:, 0:1]


def prepare(ids, w_in, nb, nt):
    rows, wide = w_in.shape
    seqs, part = ids.shape
    width = H * HD
    local = width // nt
    units = (wide - 3 * width) // nt

    def kernel(ids_hbm, win_hbm, a_hbm, u_hbm, ids_ref, win_ref, a_ref, u_ref, in_sem, a_sem, u_sem):
        loads = [pltpu.make_async_copy(win_hbm, win_ref, in_sem.at[0]), pltpu.make_async_copy(ids_hbm, ids_ref, in_sem.at[1])]
        for copy in loads:
            copy.start()
        for copy in loads:
            copy.wait()
        row = jnp.concatenate([ids_ref[s : s + 1, :] for s in range(seqs)], axis=1).astype(F32).astype(BF)
        first = 3 * local
        second = jnp.concatenate([row[:, first:].astype(F32), jnp.zeros((1, 2 * first - seqs * part), F32)], axis=1).astype(BF)
        for t in range(nt):
            for k in range(3):
                a_ref[t, :rows, k * local : (k + 1) * local] = win_ref[:, k * width + t * local : k * width + (t + 1) * local]
            a_ref[t, rows : rows + 1] = row[:, :first]
            a_ref[t, rows + 1 :] = second
        for b in range(nb):
            pltpu.make_async_copy(a_ref, a_hbm.at[b], a_sem.at[b]).start()
        for t in range(nt):
            u_ref[t] = win_ref[:, 3 * width + t * units : 3 * width + (t + 1) * units]
        for b in range(nb):
            pltpu.make_async_copy(u_ref, u_hbm.at[b], u_sem.at[b]).start()
        for b in range(nb):
            pltpu.make_async_copy(a_ref, a_hbm.at[b], a_sem.at[b]).wait()
            pltpu.make_async_copy(u_ref, u_hbm.at[b], u_sem.at[b]).wait()

    return pl.pallas_call(
        kernel,
        out_shape=[
            jax.ShapeDtypeStruct((nb, nt, rows + 2, 3 * local), BF),
            jax.ShapeDtypeStruct((nb, nt, rows, units), BF),
        ],
        in_specs=[HBM] * 2,
        out_specs=[HBM] * 2,
        scratch_shapes=[
            pltpu.VMEM(ids.shape, jnp.int32),
            pltpu.VMEM(w_in.shape, BF),
            pltpu.VMEM((nt, rows + 2, 3 * local), BF),
            pltpu.VMEM((nt, rows, units), BF),
            pltpu.SemaphoreType.DMA((2,)),
            pltpu.SemaphoreType.DMA((nb,)),
            pltpu.SemaphoreType.DMA((nb,)),
        ],
        cost_estimate=SMALL,
        compiler_params=pltpu.CompilerParams(vmem_limit_bytes=16 * MIB),
        name="prepare",
    )(*hbm(ids, w_in))


def before(at, table, w_out, ids, gain, x, cot, first):
    seqs, part, dim = x.shape

    per, unit, _ = w_out.shape

    def kernel(at_ref, table_hbm, wout_hbm, ids_hbm, gain_hbm, x_hbm, cot_hbm, out0_hbm, out1_hbm, *refs):
        unit_refs, (table_ref, wout_ref, ids_ref, gain_ref, x_ref, cot_ref, pay_ref, in_sem, x_sem, out_sem) = refs[:per], refs[per:]
        ins = [
            pltpu.make_async_copy(a, b, in_sem.at[i])
            for i, (a, b) in enumerate(((table_hbm, table_ref), (wout_hbm, wout_ref), (ids_hbm, ids_ref), (gain_hbm, gain_ref)))
        ]
        loads = [
            [pltpu.make_async_copy(a.at[s], b.at[s], x_sem.at[s, k]) for k, (a, b) in enumerate(((x_hbm, x_ref), (cot_hbm, cot_ref)))]
            for s in range(seqs)
        ]
        for copy in ins + sum(loads, []):
            copy.start()
        for copy in ins:
            copy.wait()
        for k, ref in enumerate(unit_refs):
            ref[...] = wout_ref[table_ref[at_ref[0], k]]
        copies = []
        for s in range(seqs):
            for copy in loads[s]:
                copy.wait()
            unit, _ = normalize(x_ref[s].astype(F32))
            live = column(jnp.where(ids_ref[s : s + 1, :] >= 0, 1.0, 0.0))
            pay_ref[s, 0] = (unit * gain_ref[...]).astype(BF)
            pay_ref[s, 1] = (live * cot_ref[s].astype(F32)).astype(BF)
            to = out0_hbm.at[s] if s < first else out1_hbm.at[s - first]
            copies.append(pltpu.make_async_copy(pay_ref.at[s], to, out_sem.at[s]))
            copies[-1].start()
        for copy in copies:
            copy.wait()

    return pl.pallas_call(
        kernel,
        out_shape=[jax.ShapeDtypeStruct((n, 2, part, dim), BF) for n in (first, seqs - first)]
        + [jax.ShapeDtypeStruct((unit, dim), BF)] * per,
        in_specs=[SMEM] + [HBM] * 6,
        out_specs=[HBM] * 2 + [VMEM] * per,
        scratch_shapes=[
            pltpu.SMEM(table.shape, jnp.int32),
            pltpu.VMEM(w_out.shape, BF),
            pltpu.VMEM(ids.shape, jnp.int32),
            pltpu.VMEM(gain.shape, F32),
            pltpu.VMEM(x.shape, BF),
            pltpu.VMEM(x.shape, BF),
            pltpu.VMEM((seqs, 2, part, dim), BF),
            pltpu.SemaphoreType.DMA((4,)),
            pltpu.SemaphoreType.DMA((seqs, 2)),
            pltpu.SemaphoreType.DMA((seqs,)),
        ],
        cost_estimate=SMALL,
        compiler_params=pltpu.CompilerParams(vmem_limit_bytes=32 * MIB),
        name="before",
    )(at, *hbm(table, w_out, ids, gain, x, cot))


def join(at, got, wo_parts, seqs, part):
    count, high, wide = got.shape
    unit = high - 2
    dim = count * unit
    nb = count // SLOTS

    def kernel(at_ref, got_ref, *refs):
        ins, (w_ref, wo_ref, ids_ref, all_ref) = refs[:-4], refs[-4:]

        def move(i, carry):
            all_ref[i] = got_ref[i, :unit]
            return carry

        lax.fori_loop(0, count, move, 0)
        w_ref[...] = all_ref[...].reshape(dim, wide).T
        for ref, (_, masks) in zip(ins, wo_parts):
            for i, mask in enumerate(masks):
                wo_ref[at_ref[2] ^ mask] = ref[i]
        for slot in range(SLOTS):
            i = at_ref[2] * SLOTS + (at_ref[1] ^ slot)
            row = jnp.concatenate([got_ref[i, unit : unit + 1], got_ref[i, unit + 1 :]], axis=1)
            row = row.astype(F32).astype(jnp.int32)
            for s in range(seqs):
                ids_ref[s, :, slot * part : (slot + 1) * part] = row[:, s * part : (s + 1) * part]

    return pl.pallas_call(
        kernel,
        out_shape=[
            jax.ShapeDtypeStruct((wide, dim), BF),
            jax.ShapeDtypeStruct((nb,) + wo_parts[0][0].shape[1:], BF),
            jax.ShapeDtypeStruct((seqs, 1, SLOTS * part), jnp.int32),
        ],
        in_specs=[SMEM] + [VMEM] * (1 + len(wo_parts)),
        out_specs=[VMEM] * 3,
        scratch_shapes=[pltpu.VMEM((count, unit, wide), BF)],
        cost_estimate=SMALL,
        compiler_params=pltpu.CompilerParams(vmem_limit_bytes=32 * MIB),
        name="join",
    )(at, got, *[a for a, _ in wo_parts])


def pack_out(at, table, got):
    unit, dim = got[0].shape
    per = len(got)

    def kernel(at_ref, table_ref, *refs):
        got_refs, (wo_ref, ff_ref, all_ref) = refs[:per], refs[per:]
        for k, ref in enumerate(got_refs):
            all_ref[table_ref[at_ref[0], per + k]] = ref[...]
        wo_ref[...] = all_ref[0]
        for k in range(per - 1):
            ff_ref[k] = all_ref[k + 1]

    return pl.pallas_call(
        kernel,
        out_shape=[jax.ShapeDtypeStruct((unit, dim), BF), jax.ShapeDtypeStruct((per - 1, unit, dim), BF)],
        in_specs=[SMEM] * 2 + [VMEM] * per,
        out_specs=[VMEM] * 2,
        scratch_shapes=[pltpu.VMEM((per, unit, dim), BF)],
        cost_estimate=SMALL,
        name="pack_out",
    )(at, table, *got)


def add_blocks(ref, count, step, start, rows):
    total = ref[start, rows].astype(F32)
    for i in range(1, count):
        total = total + ref[start + i * step, rows].astype(F32)
    return total


def sum_up(up, nt):
    count, unit, dim = up.shape

    def kernel(up_ref, out_ref):
        for t in range(nt):
            out_ref[t] = add_blocks(up_ref, count // nt, nt, t, slice(None))

    return pl.pallas_call(
        kernel,
        out_shape=jax.ShapeDtypeStruct((nt, unit, dim), F32),
        in_specs=[VMEM],
        out_specs=VMEM,
        cost_estimate=SMALL,
        compiler_params=pltpu.CompilerParams(vmem_limit_bytes=32 * MIB),
        name="sum_up",
    )(up)


def fold(at, low, keep, got):
    n, high, dim = keep.shape

    def kernel(at_ref, keep_ref, *refs):
        got_refs, (own_ref, *send_refs) = refs[: len(got)], refs[len(got) :]
        mine = (at_ref[2] >> low) & 3
        for i in range(n // 4):
            for s, to in enumerate([own_ref] + send_refs):
                total = keep_ref[i * 4 + (mine ^ s)]
                for ref in got_refs:
                    total = total + ref[i * 4 + (mine ^ s)].astype(F32)
                to[i] = total.astype(to.dtype)

    out = lambda t: jax.ShapeDtypeStruct((n // 4, high, dim), t)
    return pl.pallas_call(
        kernel,
        out_shape=[out(F32)] + [out(BF)] * 3,
        in_specs=[SMEM] + [VMEM] * (1 + len(got)),
        out_specs=[VMEM] * 4,
        cost_estimate=SMALL,
        compiler_params=pltpu.CompilerParams(vmem_limit_bytes=32 * MIB),
        name="fold",
    )(at, keep, *got)


def split_rows(odd, grad, send_ref, keep_ref):
    parts, rows, _ = send_ref.shape
    for z in range(parts):
        low = grad[2 * z * rows : (2 * z + 1) * rows]
        high = grad[(2 * z + 1) * rows : (2 * z + 2) * rows]
        send_ref[z] = jnp.where(odd, low, high).astype(BF)
        keep_ref[z] = jnp.where(odd, high, low)


def leave(at, table, heads, ff):
    _, unit, dim = heads[0].shape
    per = 1 + ff[0].shape[1] // unit

    def kernel(at_ref, table_ref, *refs):
        terms, refs = refs[: 2 * len(heads)], refs[2 * len(heads) :]
        out_refs, (all_ref,) = refs[:-1], refs[-1:]
        for j, group in enumerate((terms[: len(heads)], terms[len(heads) :])):
            total = group[0][0]
            for ref in group[1:]:
                total = total + ref[0].astype(F32)
            if j == 0:
                all_ref[0] = total
            else:
                for k in range(per - 1):
                    all_ref[k + 1] = total[k * unit : (k + 1) * unit]
        for k, ref in enumerate(out_refs):
            ref[...] = all_ref[table_ref[at_ref[0], per + k]]

    return pl.pallas_call(
        kernel,
        out_shape=[jax.ShapeDtypeStruct((unit, dim), F32)] * per,
        in_specs=[SMEM] * 2 + [VMEM] * (2 * len(heads)),
        out_specs=[VMEM] * per,
        scratch_shapes=[pltpu.VMEM((per, unit, dim), F32)],
        cost_estimate=SMALL,
        name="leave",
    )(at, table, *heads, *ff)


def place(at, table, qkv, up, got):
    count, high, width = qkv.shape
    unit, dim = got[0].shape
    nt = up.shape[0]
    nb = count // nt
    per = len(got)
    local = width // 3
    wide = nt * (width + dim)

    def kernel(at_ref, table_ref, qkv_ref, up_ref, *refs):
        got_refs, (in_ref, out_ref, norm_ref, q_ref, k_ref) = refs[:per], refs[per:]
        for t in range(nt):
            total = add_blocks(qkv_ref, nb, nt, t, slice(0, unit))
            for k in range(3):
                in_ref[:, k * nt * local + t * local : k * nt * local + (t + 1) * local] = total[:, k * local : (k + 1) * local]
            in_ref[:, nt * width + t * dim : nt * width + (t + 1) * dim] = up_ref[t]
        for k, ref in enumerate(got_refs):
            out_ref[table_ref[at_ref[0], k]] = ref[...]
        small = add_blocks(qkv_ref, count, 1, 0, slice(unit, high))
        small = small[0:2] + small[2:4]
        norm_ref[:, :width] = small[0:1]
        norm_ref[:, width:] = small[1:2, : dim - width]
        q_ref[...] = small[1:2, dim - width : dim - width + HD]
        k_ref[...] = small[1:2, dim - width + HD : dim - width + 2 * HD]

    return pl.pallas_call(
        kernel,
        out_shape=[
            jax.ShapeDtypeStruct((unit, wide), F32),
            jax.ShapeDtypeStruct((per, unit, dim), F32),
            jax.ShapeDtypeStruct((1, dim), F32),
            jax.ShapeDtypeStruct((1, HD), F32),
            jax.ShapeDtypeStruct((1, HD), F32),
        ],
        in_specs=[SMEM] * 2 + [VMEM] * (2 + per),
        out_specs=[VMEM] * 5,
        cost_estimate=SMALL,
        compiler_params=pltpu.CompilerParams(vmem_limit_bytes=32 * MIB),
        name="place",
    )(at, table, qkv, up, *got)


def after_kernel(s, ids_ref, x_ref, cot_ref, gain_ref, keep_ref, near_ref, far_ref, *rest):
    out_ref, grad_ref = rest[-2:]
    unit, inverse = normalize(x_ref[0].astype(F32))
    live = column(jnp.where(ids_ref[s : s + 1, :] >= 0, 1.0, 0.0))
    both = keep_ref[0, 0].astype(F32) + near_ref[0, 0].astype(F32) + far_ref[0].astype(F32)
    out_ref[0] = (live * (x_ref[0].astype(F32) + both[0])).astype(BF)
    grad_ref[0] = (
        live * cot_ref[0].astype(F32) + norm_back(both[1] * gain_ref[...], unit, inverse)
    ).astype(BF)


def after(s, i, ids, x, cot, gain, keep, near, far, earlier):
    x, cot, keep, near, far = (pltpu.with_memory_space_constraint(a, pltpu.HBM) for a in (x, cot, keep, near, far))
    seqs, part, dim = x.shape
    one = pl.BlockSpec((1, part, dim), lambda g: (s, 0, 0))
    pair = pl.BlockSpec((1, 1, 2, part, dim), lambda g: (0, i, 0, 0, 0))
    lone = pl.BlockSpec((1, 2, part, dim), lambda g: (i, 0, 0, 0))
    fixed = lambda a: pl.BlockSpec(a.shape, lambda g: (0,) * a.ndim)
    return pl.pallas_call(
        functools.partial(after_kernel, s),
        grid=(1,),
        out_shape=[jax.ShapeDtypeStruct(x.shape, BF)] * 2,
        in_specs=[fixed(ids), one, one, fixed(gain), pair, pair, lone] + [ANY] * len(earlier),
        out_specs=[one, one],
        input_output_aliases={7 + i: i for i in range(len(earlier))},
        cost_estimate=SMALL,
        compiler_params=pltpu.CompilerParams(vmem_limit_bytes=32 * MIB),
        name="after",
    )(ids, x, cot, gain, keep, near, far, *earlier)


def attention_kernel(
    heads, block, last,
    at_ref, ids_ref, qg_ref, kg_ref, wqkv_hbm, wo_hbm, *refs,
):
    pays, refs = refs[:SLOTS], refs[SLOTS:]
    if last:
        (acc_sums_ref, fnp_ref, gain_ref, accq_hbm, acco_hbm, hid_hbm, gup_hbm, wff_hbm, wup_hbm), refs = refs[:9], refs[9:]
        (keep_hbm, leave_hbm, sendq_ref, sendo_ref, keepo_ref, sums_ref), refs = refs[:6], refs[6:]
        (hid_ref, gup_ref, wff_ref, wup_ref, res_ref, res_sem, act_sem), refs = refs[:7], refs[7:]
    else:
        (o_hbm, grad_hbm, sums_ref, newq_hbm, newo_hbm), refs = refs[:5], refs[5:]
    (
        wqkv_ref, wo_ref, norm_ref, gb_ref, o_ref, grad_ref, gq_ref, go_ref, raw_ref,
        qt_ref, qn_ref, kt_ref, ka_ref, vt_ref, va_ref, do_ref, dq_ref, dk_ref, dv_ref, pad_ref, vm_ref,
        w_sem, sem, out_sem,
    ) = refs
    seqs, length, dim = norm_ref.shape
    part = length // SLOTS
    width = heads * HD
    blocks = length // block
    loads = [pltpu.make_async_copy(wqkv_hbm, wqkv_ref, w_sem.at[0]), pltpu.make_async_copy(wo_hbm, wo_ref, w_sem.at[1])]
    loads[0].start()

    def pay_copy(s, j, t):
        to = (norm_ref, gb_ref)[j].at[s, pl.ds(t * part, part), :]
        return pltpu.make_async_copy(pays[t].at[s, j], to, sem.at[s, j * SLOTS + t])

    for s in range(seqs):
        for j in range(2):
            for t in range(SLOTS):
                pay_copy(s, j, t).start()
            if s + j == 0:
                loads[1].start()
    if last:
        loads.append(pltpu.make_async_copy(accq_hbm, gq_ref, w_sem.at[2]))
        loads.append(pltpu.make_async_copy(acco_hbm, go_ref, w_sem.at[3]))
        loads.append(pltpu.make_async_copy(wff_hbm, wff_ref, act_sem.at[2 * seqs]))
        loads.append(pltpu.make_async_copy(wup_hbm, wup_ref, act_sem.at[2 * seqs + 1]))
        for copy in loads[2:]:
            copy.start()
        skip = hid_hbm.shape[0] // length - seqs

        def act_copies(s):
            rows = pl.ds(pl.multiple_of((skip + s) * length, length), length)
            return [
                pltpu.make_async_copy(hid_hbm.at[rows, :], hid_ref.at[s], act_sem.at[2 * s]),
                pltpu.make_async_copy(gup_hbm.at[rows, :], gup_ref.at[s], act_sem.at[2 * s + 1]),
            ]

        for s in range(seqs):
            for copy in act_copies(s):
                copy.start()
        outs = Outputs(keep_hbm, leave_hbm, res_ref, res_sem, wo_ref, wff_ref, wqkv_ref, wup_ref)
        sums_ref[...] = acc_sums_ref[...]
    else:
        gq_ref[...] = jnp.zeros_like(gq_ref)
        go_ref[...] = jnp.zeros_like(go_ref)
        sums_ref[...] = jnp.zeros_like(sums_ref)
    gain_q = qg_ref[...]
    gain_k = kg_ref[...]
    marks = lax.broadcasted_iota(jnp.int32, (HD, length), 0)
    v_tail = jnp.where(lax.broadcasted_iota(jnp.int32, (length, HD), 1) < 2, 1.0, 0.0).astype(BF)
    ones = jnp.where(lax.broadcasted_iota(jnp.int32, (16, length), 0) == 0, 1.0, 0.0).astype(BF)
    spot = lax.broadcasted_iota(jnp.int32, (HD, block), 0)
    scale = 1.0 / math.sqrt(HD)
    cut = lambda a, i: a[:, i * block : (i + 1) * block]

    def unit_of(row):
        raw = raw_ref[pl.ds(pl.multiple_of(row, HD), HD), :]
        center = raw - jnp.mean(raw, axis=0, keepdims=True)
        inverse = lax.rsqrt(jnp.mean(center * center, axis=0, keepdims=True) + EPS)
        return center * inverse, inverse

    def lanes(a):
        total = a[:, :128]
        for i in range(1, length // 128):
            total = total + a[:, i * 128 : (i + 1) * 128]
        return total

    def stores(s):
        return [
            pltpu.make_async_copy(o_ref.at[s], o_hbm.at[s], out_sem.at[s, 0]),
            pltpu.make_async_copy(grad_ref.at[s], grad_hbm.at[s], out_sem.at[s, 1]),
        ]

    loads[0].wait()
    loads[1].wait()

    def sequence(s, carry):
        ids = ids_ref[s]
        same = marks == ids + 1
        k_tail = jnp.where(same, 1.0, 0.0).T.astype(BF)
        q_tail = jnp.where((same & (ids >= 0)) | (marks > 4), 0.0, -BIG).astype(BF)
        pad = jnp.where(ids < 0, 1.0, 0.0)
        for i in range(blocks):
            pad_ref[i] = cut(pad, i)
        for t in range(SLOTS):
            pay_copy(s, 0, t).wait()
        raw_ref[...] = mm(wqkv_ref[...], norm_ref[s], NT)
        for t in range(SLOTS):
            pay_copy(s, 1, t).wait()
        do_all = mm(wo_ref[...], gb_ref[s], NT).astype(BF)
        for h in range(heads):
            for i in range(blocks):
                do_ref[h * blocks + i] = cut(do_all[h * HD : (h + 1) * HD], i)

        def prepare(h, carry):
            q_unit, _ = unit_of(h * HD)
            q = q_unit * gain_q
            qn = q.T.astype(BF)
            for i in range(blocks):
                qt_ref[h * blocks + i, :HD] = cut(q, i).astype(BF)
                qt_ref[h * blocks + i, HD:] = cut(q_tail, i)
                qn_ref[h * blocks + i] = qn[i * block : (i + 1) * block]
            k_unit, _ = unit_of(width + h * HD)
            k = k_unit * gain_k
            kt_ref[h] = k.astype(BF)
            ka_ref[h, :, :HD] = k.T.astype(BF)
            ka_ref[h, :, HD:] = k_tail
            v = raw_ref[pl.ds(pl.multiple_of(2 * width + h * HD, HD), HD), :]
            vb = v.astype(BF)
            vt_ref[h, :HD] = vb
            vt_ref[h, HD:] = ones
            va_ref[h, :, :HD] = v.T.astype(BF)
            va_ref[h, :, HD:] = v_tail
            vm_ref[h] = jnp.mean(vb.astype(F32), axis=1, keepdims=True)
            dk_ref[h] = jnp.zeros(dk_ref.shape[1:], F32)
            dv_ref[h] = jnp.zeros(dv_ref.shape[1:], F32)
            return carry

        lax.fori_loop(0, heads, prepare, 0)

        def step(n, carry):
            h = n // blocks
            padb = pad_ref[n % blocks]
            e = jnp.exp2(mm(ka_ref[h], qt_ref[n]) * (LOG2E * scale))
            eb = e.astype(BF)
            oa = mm(vt_ref[h], eb)
            inv = 1.0 / (oa[HD : HD + 1] + padb)
            o = oa[:HD] * inv
            dos = (do_ref[n].astype(F32) * inv).astype(BF)
            delta = jnp.sum(dos.astype(F32) * o, axis=0, keepdims=True)
            d0 = delta.astype(BF).astype(F32)
            tail = jnp.where(spot == 0, -d0, jnp.where(spot == 1, d0 - delta, 0.0))
            doa = jnp.concatenate([dos.astype(F32), tail], axis=0)
            ds = (e * mm(va_ref[h], doa.astype(BF))).astype(BF)
            dq_ref[n] = mm(kt_ref[h], ds)
            dk_ref[h] += mm(ds, qn_ref[n])
            dv_ref[h] += mm(eb, doa.T.astype(BF))
            do_ref[n] = jnp.where(padb > 0, vm_ref[h], o).astype(BF)
            return carry

        lax.fori_loop(0, heads * blocks, step, 0)

        def finish(h, carry):
            rows = lambda at: pl.ds(pl.multiple_of(at + h * HD, HD), HD)
            gq = jnp.concatenate([dq_ref[h * blocks + i] for i in range(blocks)], axis=1)
            gk = dk_ref[h].T
            for k, (g, gain_col) in enumerate(((gq, gain_q), (gk, gain_k))):
                unit, inverse = unit_of(k * width + h * HD)
                g = (g * scale).astype(BF).astype(F32)
                sums_ref[k] += lanes(g * unit)
                g = g * gain_col
                back = inverse * (
                    g - jnp.mean(g, axis=0, keepdims=True) - unit * jnp.mean(g * unit, axis=0, keepdims=True)
                )
                grad_ref[s, rows(k * width), :] = back.astype(BF)
            grad_ref[s, rows(2 * width), :] = dv_ref[h].T[:HD].astype(BF)
            for i in range(blocks):
                o_ref[s, rows(0), pl.ds(i * block, block)] = do_ref[h * blocks + i]
            return carry

        lax.fori_loop(0, heads, finish, 0)
        if last:

            @pl.when(s == 0)
            def _():
                for copy in loads[2:]:
                    copy.wait()

            for copy in act_copies(s):
                copy.wait()
            outs.compute(s, o_ref.at[s], hid_ref.at[s], grad_ref.at[s], gup_ref.at[s])
        else:
            for copy in stores(s):
                copy.start()
        gq_ref[...] += mm(grad_ref[s], norm_ref[s])
        go_ref[...] += mm(o_ref[s], gb_ref[s])
        return carry

    lax.fori_loop(0, seqs, sequence, 0)
    if not last:
        ends = [pltpu.make_async_copy(gq_ref, newq_hbm, w_sem.at[2]), pltpu.make_async_copy(go_ref, newo_hbm, w_sem.at[3])]
        for copy in ends:
            copy.start()
        for copy in ends:
            copy.wait()
        for s in range(seqs):
            for copy in stores(s):
                copy.wait()
        return
    outs.wait()
    g_q = gq_ref[...]
    first_row = (jnp.sum(wqkv_ref[...].astype(F32) * g_q, axis=0, keepdims=True) + fnp_ref[...]) / gain_ref[...]
    second_row = jnp.concatenate([jnp.sum(sums_ref[k].T, axis=0, keepdims=True) for k in range(2)], axis=1)
    wide = 3 * width
    line = jnp.concatenate([first_row[:, wide:], second_row, jnp.zeros((1, 2 * wide - dim - 2 * HD), F32)], axis=1)
    small = jnp.concatenate([first_row[:, :wide], line], axis=0)
    high = small.astype(BF)
    small = jnp.concatenate([high.astype(F32), small - high.astype(F32)], axis=0).astype(BF)
    g_q = g_q.T.astype(BF)
    count, rows, _ = sendq_ref.shape
    rows = rows - 4
    for i in range(count):
        sendq_ref[i, :rows] = g_q[i * rows : (i + 1) * rows]
        sendq_ref[i, rows:] = small
    split_rows((at_ref[2] & 1) > 0, go_ref[...], sendo_ref, keepo_ref)


def attention(at, ids, wqkv, wo, qg, kg, pays, count, more=()):
    wide, dim = wqkv.shape
    width = wo.shape[0]
    heads = width // HD
    seqs, _, part, _ = pays[0].shape
    length = part * SLOTS
    block = 512
    blocks = length // block
    last = bool(more)
    ins = [at, ids, qg, kg, *hbm(wqkv, wo, *pays), *more[:3], *hbm(*more[3:])]
    specs = [SMEM] + [VMEM] * 3 + [HBM] * (2 + SLOTS) + ([VMEM] * 3 + [HBM] * 6 if last else [])
    scratch = []
    if last:
        outs = [jax.ShapeDtypeStruct((SLOTS // 2, seqs, 2, part, dim), BF)] * 2
        outs += [jax.ShapeDtypeStruct((count, dim // count + 4, wide), BF)]
        outs += [jax.ShapeDtypeStruct((count // (2 * SLOTS), SLOTS * width // count, dim), t) for t in (BF, F32)]
        scratch = [pltpu.VMEM((2, HD, 128), F32)]
        scratch += [pltpu.VMEM((seqs, length, dim), BF)] * 2 + [pltpu.VMEM((dim, dim), BF)] * 2
        scratch += Outputs.scratch(seqs, length, dim) + [pltpu.SemaphoreType.DMA((2 * seqs + 2,))]
    else:
        outs = [jax.ShapeDtypeStruct((seqs, width, length), BF), jax.ShapeDtypeStruct((seqs, wide, length), BF)]
        outs += [
            jax.ShapeDtypeStruct((2, HD, 128), F32),
            jax.ShapeDtypeStruct((wide, dim), F32),
            jax.ShapeDtypeStruct((width, dim), F32),
        ]
    flops = seqs * (2 * length * dim * width * 8 + heads * 6 * 2 * length * length * HD)
    return pl.pallas_call(
        functools.partial(attention_kernel, heads, block, last),
        out_shape=outs,
        in_specs=specs,
        out_specs=[HBM] * 2 + ([VMEM] * 3 if last else [VMEM, HBM, HBM]),
        scratch_shapes=scratch
        + [
            pltpu.VMEM((wide, dim), BF),
            pltpu.VMEM((width, dim), BF),
            pltpu.VMEM((seqs, length, dim), BF),
            pltpu.VMEM((seqs, length, dim), BF),
            pltpu.VMEM((seqs, width, length), BF),
            pltpu.VMEM((seqs, wide, length), BF),
            pltpu.VMEM((wide, dim), F32),
            pltpu.VMEM((width, dim), F32),
            pltpu.VMEM((wide, length), F32),
            pltpu.VMEM((heads * blocks, 2 * HD, block), BF),
            pltpu.VMEM((heads * blocks, block, HD), BF),
            pltpu.VMEM((heads, HD, length), BF),
            pltpu.VMEM((heads, length, 2 * HD), BF),
            pltpu.VMEM((heads, HD + 16, length), BF),
            pltpu.VMEM((heads, length, 2 * HD), BF),
            pltpu.VMEM((heads * blocks, HD, block), BF),
            pltpu.VMEM((heads * blocks, HD, block), F32),
            pltpu.VMEM((heads, length, HD), F32),
            pltpu.VMEM((heads, length, 2 * HD), F32),
            pltpu.VMEM((blocks, 1, block), F32),
            pltpu.VMEM((heads, HD, 1), F32),
            pltpu.SemaphoreType.DMA((4,)),
            pltpu.SemaphoreType.DMA((seqs, 2 * SLOTS)),
            pltpu.SemaphoreType.DMA((seqs, 2)),
        ],
        cost_estimate=LARGE,
        compiler_params=pltpu.CompilerParams(vmem_limit_bytes=56 * MIB),
        name="attention",
    )(*ins)


def ffn_kernel(block, groups, plan, at_ref, wup_hbm, wqkv_hbm, wo_hbm, o_hbm, gq_hbm, *refs):
    pieces, refs = refs[: len(plan)], refs[len(plan) :]
    pays, refs = refs[: len(groups) * SLOTS], refs[len(groups) * SLOTS :]
    (hid_hbm, gup_hbm, wff_hbm, keep_hbm, leave_hbm, sendu_ref, sendf_ref, keepf_ref, np_ref), refs = refs[:9], refs[9:]
    norm_ref, gb_ref, hid_ref, gup_ref, wup_ref, wff_ref, gin_ref, gff_ref, sem, out_sem, w_sem, *refs = refs
    wqkv_ref, wo_ref, o_ref, gq_ref, res_ref, res_sem, late_sem = refs
    dim = wup_ref.shape[0]
    part = pays[0].shape[2]
    total = norm_ref.shape[0]
    weights = [pltpu.make_async_copy(wup_hbm, wup_ref, w_sem.at[0])]
    rows = sendf_ref.shape[1]
    for ref, masks in zip(pieces, plan):
        for i, mask in enumerate(masks):
            to = wff_ref.at[pl.ds(pl.multiple_of((at_ref[2] ^ mask) * rows, rows), rows), :]
            weights.append(pltpu.make_async_copy(ref.at[i], to, w_sem.at[len(weights)]))
    for copy in weights:
        copy.start()
    n = 0
    for g, seqs in enumerate(groups):
        for s in range(seqs):
            for t in range(SLOTS):
                for k, to in enumerate((norm_ref, gb_ref)):
                    source = pays[g * SLOTS + t].at[s, k]
                    pltpu.make_async_copy(source, to.at[pl.ds(n * part, part), :], sem.at[k, n]).start()
                n += 1
    late = [
        pltpu.make_async_copy(a, b, late_sem.at[i])
        for i, (a, b) in enumerate(((wqkv_hbm, wqkv_ref), (wo_hbm, wo_ref), (o_hbm, o_ref), (gq_hbm, gq_ref)))
    ]
    for copy in late:
        copy.start()
    gin_ref[...] = jnp.zeros_like(gin_ref)
    gff_ref[...] = jnp.zeros_like(gff_ref)
    for copy in weights:
        copy.wait()
    joined = pltpu.make_async_copy(wff_ref, wff_hbm, w_sem.at[0])
    joined.start()
    c0 = math.sqrt(2.0 / math.pi)
    c1 = 0.044715

    def outs(i):
        at_rows = pl.ds(pl.multiple_of(i * block, block), block)
        return (
            pltpu.make_async_copy(hid_ref.at[at_rows, :], hid_hbm.at[at_rows, :], out_sem.at[0, i]),
            pltpu.make_async_copy(gup_ref.at[at_rows, :], gup_hbm.at[at_rows, :], out_sem.at[1, i]),
        )

    def step(i, carry):
        for j in range(block // part):
            for k, to in enumerate((norm_ref, gb_ref)):
                pltpu.make_async_copy(pays[0].at[0, 0], to.at[pl.ds(0, part), :], sem.at[k, i * (block // part) + j]).wait()
        at_rows = pl.ds(pl.multiple_of(i * block, block), block)
        up = mm(norm_ref[at_rows, :], wup_ref[...])
        gh = mm(gb_ref[at_rows, :], wff_ref[...], NT)
        sq = up * up
        t = jnp.tanh(up * (c0 + (c0 * c1) * sq))
        half = 0.5 + 0.5 * t
        hid_ref[at_rows, :] = (up * half).astype(BF)
        gup_ref[at_rows, :] = (gh * (half + (0.5 * up) * (1.0 - t * t) * (c0 + (3.0 * c0 * c1) * sq))).astype(BF)
        for copy in outs(i):
            copy.start()
        gin_ref[...] += mm(norm_ref[at_rows, :], gup_ref[at_rows, :], TN)
        gff_ref[...] += mm(hid_ref[at_rows, :], gb_ref[at_rows, :], TN)
        return carry

    lax.fori_loop(0, total // block, step, 0)
    for copy in late:
        copy.wait()
    results = Outputs(keep_hbm, leave_hbm, res_ref, res_sem, wo_ref, wff_ref, wqkv_ref, wup_ref)
    length = SLOTS * part
    for s in range(results.seqs):
        rows_s = pl.ds(s * length, length)
        results.compute(s, o_ref.at[s], hid_ref.at[rows_s, :], gq_ref.at[s], gup_ref.at[rows_s, :])
    line = jnp.sum(wup_ref[...].astype(F32) * gin_ref[...], axis=1, keepdims=True)
    np_ref[...] = jnp.broadcast_to(line, (dim, 128)).T[0:1]
    sendu_ref[...] = gin_ref[...].astype(BF)
    split_rows((at_ref[2] & 1) > 0, gff_ref[...], sendf_ref, keepf_ref)
    joined.wait()
    results.wait()

    def drain(i, carry):
        for copy in outs(i):
            copy.wait()
        return carry

    lax.fori_loop(0, total // block, drain, 0)


def ffn(at, wup, ff_parts, groups, count, wqkv, wo, o, gq, block=512):
    dim, units = wup.shape
    sizes = [g[0].shape[0] for g in groups]
    part = groups[0][0].shape[2]
    total = SLOTS * part * sum(sizes)
    pieces = [p for g in groups for p in g]
    act = jax.ShapeDtypeStruct((total, units), BF)
    return pl.pallas_call(
        functools.partial(ffn_kernel, block, sizes, [masks for _, masks in ff_parts]),
        out_shape=[
            act,
            act,
            jax.ShapeDtypeStruct((units, dim), BF),
            *[jax.ShapeDtypeStruct((SLOTS // 2, o.shape[0], 2, part, dim), BF)] * 2,
            jax.ShapeDtypeStruct((dim, units), BF),
            jax.ShapeDtypeStruct((count // 2, units // count, dim), BF),
            jax.ShapeDtypeStruct((count // 2, units // count, dim), F32),
            jax.ShapeDtypeStruct((1, dim), F32),
        ],
        in_specs=[SMEM] + [HBM] * (5 + len(ff_parts) + len(pieces)),
        out_specs=[HBM] * 5 + [VMEM] * 4,
        scratch_shapes=[
            pltpu.VMEM((total, dim), BF),
            pltpu.VMEM((total, dim), BF),
            pltpu.VMEM((total, units), BF),
            pltpu.VMEM((total, units), BF),
            pltpu.VMEM((dim, units), BF),
            pltpu.VMEM((units, dim), BF),
            pltpu.VMEM((dim, units), F32),
            pltpu.VMEM((units, dim), F32),
            pltpu.SemaphoreType.DMA((2, total // part)),
            pltpu.SemaphoreType.DMA((2, total // block)),
            pltpu.SemaphoreType.DMA((1 + count,)),
            *[pltpu.VMEM(a.shape, BF) for a in (wqkv, wo, o, gq)],
            *Outputs.scratch(o.shape[0], SLOTS * part, dim),
            pltpu.SemaphoreType.DMA((4,)),
        ],
        cost_estimate=LARGE,
        compiler_params=pltpu.CompilerParams(vmem_limit_bytes=58 * MIB),
        name="ffn",
    )(at, *hbm(wup, wqkv, wo, o, gq, *[a for a, _ in ff_parts], *pieces))


class Outputs:
    def __init__(self, keep, send, res, sem, wo, wff, wqkv, wup):
        self.keep, self.send, self.res, self.sem = keep, send, res, sem
        self.wo, self.wff, self.wqkv, self.wup = wo, wff, wqkv, wup
        self.seqs, _, self.length, _ = res.shape

    @staticmethod
    def scratch(seqs, length, dim):
        return [pltpu.VMEM((seqs, 2, length, dim), BF), pltpu.SemaphoreType.DMA((seqs, 2, SLOTS))]

    def moves(self, s, i):
        half = self.length // 2
        part = half // 2
        out = []
        for j in range(2):
            for k, to in enumerate((self.keep, self.send)):
                rows = pl.ds(pl.multiple_of(i * half + k * part, part), part)
                out.append(pltpu.make_async_copy(self.res.at[s, j, rows, :], to.at[i, s, j], self.sem.at[s, j, 2 * i + k]))
        return out

    def compute(self, s, o, hid, gq, gu):
        half = self.length // 2

        def step(i, carry):
            rows = pl.ds(pl.multiple_of(i * half, half), half)
            branch = mm(o[:, rows], self.wo[...], TN) + mm(hid[rows, :], self.wff[...])
            self.res[s, 0, rows, :] = branch.astype(BF)
            gn = mm(gq[:, rows], self.wqkv[...], TN) + mm(gu[rows, :], self.wup[...], NT)
            self.res[s, 1, rows, :] = gn.astype(BF)
            for copy in self.moves(s, i):
                copy.start()
            return carry

        lax.fori_loop(0, 2, step, 0)

    def wait(self):
        for s in range(self.seqs):
            for i in range(2):
                for copy in self.moves(s, i):
                    copy.wait()


def swap(value, axis, count, mask):
    return lax.ppermute(value, axis, [(i, i ^ mask) for i in range(count)])


def tie(value, *after):
    return lax.optimization_barrier((value,) + after)[0]


def bit_groups(count):
    bits = list(range(count.bit_length() - 1))[::-1]
    groups = []
    while bits:
        take = 2 if len(bits) > 1 else 1
        groups.append(bits[:take])
        bits = bits[take:]
    assert len(groups[-1]) == 1
    return groups


def gather_batch(block, count, groups):
    held, masks = block[None], [0]
    for bits in groups:
        low = bits[-1]
        parts = [(held, masks)]
        for s in range(1, 1 << len(bits)):
            parts.append((swap(held, "batch", count, s << low), [m ^ (s << low) for m in masks]))
        held = jnp.concatenate([a for a, _ in parts], axis=0)
        masks = sum((m for _, m in parts), [])
    return parts


def matchings(edges, devices, per_device):
    left = [[] for _ in range(devices)]
    for e, (source, _, _) in enumerate(edges):
        left[source].append(e)
    rounds = []
    for _ in range(per_device):
        owner = [-1] * devices

        def place(source, seen):
            for e in left[source]:
                target = edges[e][1]
                if target in seen:
                    continue
                seen.add(target)
                if owner[target] < 0 or place(edges[owner[target]][0], seen):
                    owner[target] = e
                    return True
            return False

        for source in range(devices):
            place(source, set())
        rounds.append(list(owner))
        for e in owner:
            left[edges[e][0]].remove(e)
    return rounds


def unit_plan(nb, nt, rows, width, hidden):
    unit = math.gcd(math.gcd(rows, width // nt), hidden // nt)
    per = rows // unit
    head_units, hid_units = width // nt // unit, hidden // nt // unit
    assert head_units == nb and hid_units % nb == 0
    c = hid_units // nb
    edges = []
    for t in range(nt):
        for b in range(nb):
            want = [t * head_units + b]
            want += [nt * head_units + t * hid_units + b * c + i for i in range(c)]
            for slot, u in enumerate(want):
                edges.append((u // per, b * nt + t, (u % per, slot)))
    table = np.zeros((nb * nt, 2 * per), np.int32)
    perms = []
    for k, owner in enumerate(matchings(edges, nb * nt, per)):
        perms.append([(edges[e][0], edges[e][1]) for e in owner])
        for e in owner:
            table[edges[e][0], k] = edges[e][2][0]
            table[edges[e][1], per + k] = edges[e][2][1]
    return unit, per, perms, table


def per_device(
    nb, nt, patches, image_ids, cotangent, norm_gain, query_gain, key_gain, in_weight, out_weight
):
    seqs, part, dim = patches.shape
    width = H * HD
    local = width // nt
    units = (in_weight.shape[1] - 3 * width) // nt
    rows_in = in_weight.shape[0]
    unit, per, perms, table = unit_plan(nb, nt, out_weight.shape[0], width, units * nt)
    assert nt == SLOTS and units == dim and unit == rows_in and dim == nt * local and per == nt + 1
    both = ("batch", "tok")
    me_b = lax.axis_index("batch")
    me_t = lax.axis_index("tok")
    at = jnp.stack([me_b * nt + me_t, me_t, me_b])
    table = jnp.asarray(table)
    gain = norm_gain.reshape(1, dim)

    def exchange(value, axis):
        return lax.all_to_all(value, axis, split_axis=0, concat_axis=0, tiled=True)

    groups = bit_groups(nb)

    lead = 1
    a_src, u_src = prepare(image_ids, in_weight, nb, nt)
    a_got = exchange(a_src.reshape(nb * nt, rows_in + 2, 3 * local), both)
    own0, own1, *unit_sends = before(
        at, table, out_weight.reshape(per, unit, dim), image_ids, gain, tie(patches, a_src), cotangent, lead
    )
    got = [lax.ppermute(v, both, perm) for v, perm in zip(unit_sends, perms)]
    wo_src, ff_src = pack_out(at, table, got)
    far0 = swap(tie(own0, *got), "tok", nt, 2)
    wo_parts = gather_batch(wo_src, nb, groups)
    ff_parts = gather_batch(ff_src.reshape((per - 1) * unit, dim), nb, groups[::-1])
    wqkv, wo, ids = join(at, a_got, wo_parts, seqs, part)
    wo = wo.reshape(local, dim)
    far1 = swap(tie(own1, far0), "tok", nt, 2)
    slots0 = [own0, swap(own0, "tok", nt, 1), far0, swap(far0, "tok", nt, 1)]
    slots1 = [own1, swap(own1, "tok", nt, 1), far1, swap(far1, "tok", nt, 1)]
    wup = exchange(tie(u_src, a_got).reshape(nb * nt, unit, dim), both).reshape(dim, units)

    qg = query_gain.reshape(HD, 1)
    kg = key_gain.reshape(HD, 1)

    def leave_chip(keep, near, *hold):
        value = (keep[1].astype(F32) + near[1].astype(F32)).astype(BF)
        return value, swap(tie(value, *hold) if hold else value, "tok", nt, 2)

    def reduce_batch(keep, came):
        terms = [keep, came]
        for bits in groups[:-1][::-1]:
            own, *sends = fold(at, bits[-1], terms[0], terms[1:])
            terms = [own] + [swap(value, "batch", nb, (s + 1) << bits[-1]) for s, value in enumerate(sends)]
        return terms

    o0, gq0, sums, acc_q, acc_o = attention(at, ids[:lead], wqkv, tie(wo, ff_parts[0][0]), qg, kg, slots0, nb * nt)
    hid, gup, wff, keep0, send0, f_up, f_send, f_keep, f_np = ffn(
        at, wup, ff_parts, [slots0, slots1], nb, wqkv, wo, o0, gq0
    )
    f_up = exchange(f_up.reshape(nb * nt, unit, dim), both)
    f_came = swap(f_send, "batch", nb, 1)
    near0 = swap(send0, "tok", nt, 1)
    value0, away0 = leave_chip(keep0, near0)
    keep1, send1, a_q, a_send, a_keep = attention(
        at, ids[lead:], wqkv, tie(wo, value0), qg, kg, slots1, nb * nt,
        (sums, f_np, gain, acc_q, acc_o, hid, gup, wff, wup),
    )
    send1, a_q, a_send = (tie(value, f_up, f_came, away0) for value in (send1, a_q, a_send))
    a_q = exchange(a_q, both)
    a_came = swap(a_send, "batch", nb, 1)
    near1 = swap(send1, "tok", nt, 1)
    ff_terms = reduce_batch(f_keep, f_came)
    o_terms = reduce_batch(a_keep, a_came)
    value1, away1 = leave_chip(keep1, tie(near1, a_came))
    up = sum_up(f_up, nt)
    group = [(0, s, keep0, near0, away0) for s in range(lead)]
    group += [(lead, s, keep1, near1, away1) for s in range(lead, seqs)]

    sends = leave(at, table, o_terms, ff_terms)
    got = [lax.ppermute(v, both, [(b, a) for a, b in perm]) for v, perm in zip(sends, perms)]
    in_grad, out_grad, norm_grad, query_grad, key_grad = place(at, table, a_q, up, got)

    earlier = []
    for s in range(seqs):
        start, _, *arrays = group[s]
        earlier = after(s, s - start, image_ids, patches, cotangent, gain, *arrays, earlier)
    block_out, patch_grad = earlier
    return (
        block_out,
        patch_grad,
        norm_grad.reshape(dim),
        query_grad.reshape(HD),
        key_grad.reshape(HD),
        in_grad,
        out_grad.reshape(per * unit, dim),
    )


def solution(mesh):
    rows = P("batch", "tok", None)
    weights = P(("batch", "tok"), None)
    return jax.shard_map(
        functools.partial(per_device, mesh.shape["batch"], mesh.shape["tok"]),
        mesh=mesh,
        in_specs=(rows, P("batch", "tok"), rows, P(), P(), P(), weights, weights),
        out_specs=(rows, rows, P(), P(), P(), weights, weights),
        check_vma=False,
    )
```

```python
import functools
import math

import jax
import jax.numpy as jnp
import numpy as np
from jax import lax
from jax.experimental import pallas as pl
from jax.experimental.pallas import tpu as pltpu
from jax.sharding import PartitionSpec as P

H = 12
HD = 64
SLOTS = 4
EPS = 1e-06
BIG = 2048.0
LOG2E = 1.4426950408889634
BF = jnp.bfloat16
F32 = jnp.float32
NN = (((1,), (0,)), ((), ()))
NT = (((1,), (1,)), ((), ()))
TN = (((0,), (0,)), ((), ()))
MIB = 1 << 20
SMALL = pl.CostEstimate(flops=1, transcendentals=0, bytes_accessed=1)
LARGE = pl.CostEstimate(flops=60_000_000_000, transcendentals=0, bytes_accessed=1)

VMEM = pl.BlockSpec(memory_space=pltpu.VMEM)
SMEM = pl.BlockSpec(memory_space=pltpu.SMEM)
ANY = pl.BlockSpec(memory_space=pl.ANY)
HBM = pl.BlockSpec(memory_space=pltpu.HBM)


def hbm(*arrays):
    return [pltpu.with_memory_space_constraint(a, pltpu.HBM) for a in arrays]


def mm(a, b, dims=NN):
    return lax.dot_general(a, b, dims, preferred_element_type=F32)


def normalize(values):
    center = values - jnp.mean(values, axis=-1, keepdims=True)
    inverse = lax.rsqrt(jnp.mean(center * center, axis=-1, keepdims=True) + EPS)
    return center * inverse, inverse


def norm_back(grad_unit, unit_rows, inverse):
    return inverse * (
        grad_unit
        - jnp.mean(grad_unit, axis=-1, keepdims=True)
        - unit_rows * jnp.mean(grad_unit * unit_rows, axis=-1, keepdims=True)
    )


def column(row):
    return jnp.broadcast_to(row, (8, row.shape[1])).T[:, 0:1]


def prepare(ids, w_in, nb, nt):
    rows, wide = w_in.shape
    seqs, part = ids.shape
    width = H * HD
    local = width // nt
    units = (wide - 3 * width) // nt

    def kernel(ids_hbm, win_hbm, a_hbm, u_hbm, ids_ref, win_ref, a_ref, u_ref, in_sem, a_sem, u_sem):
        loads = [pltpu.make_async_copy(win_hbm, win_ref, in_sem.at[0]), pltpu.make_async_copy(ids_hbm, ids_ref, in_sem.at[1])]
        for copy in loads:
            copy.start()
        for copy in loads:
            copy.wait()
        row = jnp.concatenate([ids_ref[s : s + 1, :] for s in range(seqs)], axis=1).astype(F32).astype(BF)
        first = 3 * local
        second = jnp.concatenate([row[:, first:].astype(F32), jnp.zeros((1, 2 * first - seqs * part), F32)], axis=1).astype(BF)
        for t in range(nt):
            for k in range(3):
                a_ref[t, :rows, k * local : (k + 1) * local] = win_ref[:, k * width + t * local : k * width + (t + 1) * local]
            a_ref[t, rows : rows + 1] = row[:, :first]
            a_ref[t, rows + 1 :] = second
        for b in range(nb):
            pltpu.make_async_copy(a_ref, a_hbm.at[b], a_sem.at[b]).start()
        for t in range(nt):
            u_ref[t] = win_ref[:, 3 * width + t * units : 3 * width + (t + 1) * units]
        for b in range(nb):
            pltpu.make_async_copy(u_ref, u_hbm.at[b], u_sem.at[b]).start()
        for b in range(nb):
            pltpu.make_async_copy(a_ref, a_hbm.at[b], a_sem.at[b]).wait()
            pltpu.make_async_copy(u_ref, u_hbm.at[b], u_sem.at[b]).wait()

    return pl.pallas_call(
        kernel,
        out_shape=[
            jax.ShapeDtypeStruct((nb, nt, rows + 2, 3 * local), BF),
            jax.ShapeDtypeStruct((nb, nt, rows, units), BF),
        ],
        in_specs=[HBM] * 2,
        out_specs=[HBM] * 2,
        scratch_shapes=[
            pltpu.VMEM(ids.shape, jnp.int32),
            pltpu.VMEM(w_in.shape, BF),
            pltpu.VMEM((nt, rows + 2, 3 * local), BF),
            pltpu.VMEM((nt, rows, units), BF),
            pltpu.SemaphoreType.DMA((2,)),
            pltpu.SemaphoreType.DMA((nb,)),
            pltpu.SemaphoreType.DMA((nb,)),
        ],
        cost_estimate=SMALL,
        compiler_params=pltpu.CompilerParams(vmem_limit_bytes=16 * MIB),
        name="prepare",
    )(*hbm(ids, w_in))


def before(at, table, w_out, ids, gain, x, cot, first):
    seqs, part, dim = x.shape

    per, unit, _ = w_out.shape

    def kernel(at_ref, table_hbm, wout_hbm, ids_hbm, gain_hbm, x_hbm, cot_hbm, out0_hbm, out1_hbm, *refs):
        unit_refs, (table_ref, wout_ref, ids_ref, gain_ref, x_ref, cot_ref, pay_ref, in_sem, x_sem, out_sem) = refs[:per], refs[per:]
        ins = [
            pltpu.make_async_copy(a, b, in_sem.at[i])
            for i, (a, b) in enumerate(((table_hbm, table_ref), (wout_hbm, wout_ref), (ids_hbm, ids_ref), (gain_hbm, gain_ref)))
        ]
        loads = [
            [pltpu.make_async_copy(a.at[s], b.at[s], x_sem.at[s, k]) for k, (a, b) in enumerate(((x_hbm, x_ref), (cot_hbm, cot_ref)))]
            for s in range(seqs)
        ]
        for copy in ins + sum(loads, []):
            copy.start()
        for copy in ins:
            copy.wait()
        for k, ref in enumerate(unit_refs):
            ref[...] = wout_ref[table_ref[at_ref[0], k]]
        copies = []
        for s in range(seqs):
            for copy in loads[s]:
                copy.wait()
            unit, _ = normalize(x_ref[s].astype(F32))
            live = column(jnp.where(ids_ref[s : s + 1, :] >= 0, 1.0, 0.0))
            pay_ref[s, 0] = (unit * gain_ref[...]).astype(BF)
            pay_ref[s, 1] = (live * cot_ref[s].astype(F32)).astype(BF)
            to = out0_hbm.at[s] if s < first else out1_hbm.at[s - first]
            copies.append(pltpu.make_async_copy(pay_ref.at[s], to, out_sem.at[s]))
            copies[-1].start()
        for copy in copies:
            copy.wait()

    return pl.pallas_call(
        kernel,
        out_shape=[jax.ShapeDtypeStruct((n, 2, part, dim), BF) for n in (first, seqs - first)]
        + [jax.ShapeDtypeStruct((unit, dim), BF)] * per,
        in_specs=[SMEM] + [HBM] * 6,
        out_specs=[HBM] * 2 + [VMEM] * per,
        scratch_shapes=[
            pltpu.SMEM(table.shape, jnp.int32),
            pltpu.VMEM(w_out.shape, BF),
            pltpu.VMEM(ids.shape, jnp.int32),
            pltpu.VMEM(gain.shape, F32),
            pltpu.VMEM(x.shape, BF),
            pltpu.VMEM(x.shape, BF),
            pltpu.VMEM((seqs, 2, part, dim), BF),
            pltpu.SemaphoreType.DMA((4,)),
            pltpu.SemaphoreType.DMA((seqs, 2)),
            pltpu.SemaphoreType.DMA((seqs,)),
        ],
        cost_estimate=SMALL,
        compiler_params=pltpu.CompilerParams(vmem_limit_bytes=32 * MIB),
        name="before",
    )(at, *hbm(table, w_out, ids, gain, x, cot))


def join(at, got, wo_parts, seqs, part):
    count, high, wide = got.shape
    unit = high - 2
    dim = count * unit
    nb = count // SLOTS

    def kernel(at_ref, got_ref, *refs):
        ins, (w_ref, wo_ref, ids_ref, all_ref) = refs[:-4], refs[-4:]

        def move(i, carry):
            all_ref[i] = got_ref[i, :unit]
            return carry

        lax.fori_loop(0, count, move, 0)
        w_ref[...] = all_ref[...].reshape(dim, wide).T
        for ref, (_, masks) in zip(ins, wo_parts):
            for i, mask in enumerate(masks):
                wo_ref[at_ref[2] ^ mask] = ref[i]
        for slot in range(SLOTS):
            i = at_ref[2] * SLOTS + slot
            row = jnp.concatenate([got_ref[i, unit : unit + 1], got_ref[i, unit + 1 :]], axis=1)
            row = row.astype(F32).astype(jnp.int32)
            for s in range(seqs):
                ids_ref[s, :, slot * part : (slot + 1) * part] = row[:, s * part : (s + 1) * part]

    return pl.pallas_call(
        kernel,
        out_shape=[
            jax.ShapeDtypeStruct((wide, dim), BF),
            jax.ShapeDtypeStruct((nb,) + wo_parts[0][0].shape[1:], BF),
            jax.ShapeDtypeStruct((seqs, 1, SLOTS * part), jnp.int32),
        ],
        in_specs=[SMEM] + [VMEM] * (1 + len(wo_parts)),
        out_specs=[VMEM] * 3,
        scratch_shapes=[pltpu.VMEM((count, unit, wide), BF)],
        cost_estimate=SMALL,
        compiler_params=pltpu.CompilerParams(vmem_limit_bytes=32 * MIB),
        name="join",
    )(at, got, *[a for a, _ in wo_parts])


def pack_out(at, table, got):
    unit, dim = got[0].shape
    per = len(got)

    def kernel(at_ref, table_ref, *refs):
        got_refs, (wo_ref, ff_ref, all_ref) = refs[:per], refs[per:]
        for k, ref in enumerate(got_refs):
            all_ref[table_ref[at_ref[0], per + k]] = ref[...]
        wo_ref[...] = all_ref[0]
        for k in range(per - 1):
            ff_ref[k] = all_ref[k + 1]

    return pl.pallas_call(
        kernel,
        out_shape=[jax.ShapeDtypeStruct((unit, dim), BF), jax.ShapeDtypeStruct((per - 1, unit, dim), BF)],
        in_specs=[SMEM] * 2 + [VMEM] * per,
        out_specs=[VMEM] * 2,
        scratch_shapes=[pltpu.VMEM((per, unit, dim), BF)],
        cost_estimate=SMALL,
        name="pack_out",
    )(at, table, *got)


def add_blocks(ref, count, step, start, rows):
    total = ref[start, rows].astype(F32)
    for i in range(1, count):
        total = total + ref[start + i * step, rows].astype(F32)
    return total


def fold(at, low, terms):
    n, _, dim = terms[0][0].shape
    counts = [len(group) for group in terms]
    rows = [group[0].shape[1] for group in terms]

    def kernel(at_ref, *refs):
        ins, (own_ref, *send_refs) = refs[: sum(counts)], refs[sum(counts) :]
        mine = (at_ref[2] >> low) & 3
        k, start = 0, 0
        for count, high in zip(counts, rows):
            for i in range(n // 4):
                for s, to in enumerate([own_ref] + send_refs):
                    block = i * 4 + (mine ^ s)
                    total = ins[k][block].astype(F32)
                    for ref in ins[k + 1 : k + count]:
                        total = total + ref[block].astype(F32)
                    to[i, start : start + high] = total.astype(to.dtype)
            k += count
            start += high

    out = lambda t: jax.ShapeDtypeStruct((n // 4, sum(rows), dim), t)
    return pl.pallas_call(
        kernel,
        out_shape=[out(F32)] + [out(BF)] * 3,
        in_specs=[SMEM] + [VMEM] * sum(counts),
        out_specs=[VMEM] * 4,
        cost_estimate=SMALL,
        compiler_params=pltpu.CompilerParams(vmem_limit_bytes=32 * MIB),
        name="fold",
    )(at, *sum(terms, []))


def split_rows(odd, grad, send_ref, keep_ref):
    parts, rows, _ = send_ref.shape
    for z in range(parts):
        low = grad[2 * z * rows : (2 * z + 1) * rows]
        high = grad[(2 * z + 1) * rows : (2 * z + 2) * rows]
        send_ref[z] = jnp.where(odd, low, high).astype(BF)
        keep_ref[z] = jnp.where(odd, high, low)


def leave(at, table, heads, ff):
    per_ff, unit, dim = ff.shape
    per = 1 + per_ff

    def kernel(at_ref, table_ref, ff_ref, *refs):
        terms, out_refs, all_ref = refs[: len(heads)], refs[len(heads) : -1], refs[-1]
        total = terms[0][0]
        for ref in terms[1:]:
            total = total + ref[0].astype(F32)
        all_ref[0] = total
        for k in range(per_ff):
            all_ref[k + 1] = ff_ref[k].astype(F32)
        for k, ref in enumerate(out_refs):
            ref[...] = all_ref[table_ref[at_ref[0], per + k]]

    return pl.pallas_call(
        kernel,
        out_shape=[jax.ShapeDtypeStruct((unit, dim), F32)] * per,
        in_specs=[SMEM] * 2 + [VMEM] * (1 + len(heads)),
        out_specs=[VMEM] * per,
        scratch_shapes=[pltpu.VMEM((per, unit, dim), F32)],
        cost_estimate=SMALL,
        name="leave",
    )(at, table, ff, *heads)


def place(at, table, qkv, up, got):
    count, high, width = qkv.shape
    unit, dim = got[0].shape
    nt = up.shape[0]
    nb = count // nt
    per = len(got)
    local = width // 3
    wide = nt * (width + dim)

    def kernel(at_ref, table_ref, qkv_ref, up_ref, *refs):
        got_refs, (in_ref, out_ref, norm_ref, q_ref, k_ref) = refs[:per], refs[per:]
        for t in range(nt):
            total = add_blocks(qkv_ref, nb, nt, t, slice(0, unit))
            for k in range(3):
                in_ref[:, k * nt * local + t * local : k * nt * local + (t + 1) * local] = total[:, k * local : (k + 1) * local]
            in_ref[:, nt * width + t * dim : nt * width + (t + 1) * dim] = up_ref[t].astype(F32)
        for k, ref in enumerate(got_refs):
            out_ref[table_ref[at_ref[0], k]] = ref[...]
        small = add_blocks(qkv_ref, count, 1, 0, slice(unit, high))
        small = small[0:2] + small[2:4]
        norm_ref[:, :width] = small[0:1]
        norm_ref[:, width:] = small[1:2, : dim - width]
        q_ref[...] = small[1:2, dim - width : dim - width + HD]
        k_ref[...] = small[1:2, dim - width + HD : dim - width + 2 * HD]

    return pl.pallas_call(
        kernel,
        out_shape=[
            jax.ShapeDtypeStruct((unit, wide), F32),
            jax.ShapeDtypeStruct((per, unit, dim), F32),
            jax.ShapeDtypeStruct((1, dim), F32),
            jax.ShapeDtypeStruct((1, HD), F32),
            jax.ShapeDtypeStruct((1, HD), F32),
        ],
        in_specs=[SMEM] * 2 + [VMEM] * (2 + per),
        out_specs=[VMEM] * 5,
        cost_estimate=SMALL,
        compiler_params=pltpu.CompilerParams(vmem_limit_bytes=32 * MIB),
        name="place",
    )(at, table, qkv, up, *got)


def after_kernel(s, ids_ref, x_ref, cot_ref, gain_ref, keep_ref, near_ref, far_ref, *rest):
    out_ref, grad_ref = rest[-2:]
    unit, inverse = normalize(x_ref[0].astype(F32))
    live = column(jnp.where(ids_ref[s : s + 1, :] >= 0, 1.0, 0.0))
    both = keep_ref[0, 0].astype(F32) + near_ref[0, 0].astype(F32) + far_ref[0].astype(F32)
    out_ref[0] = (live * (x_ref[0].astype(F32) + both[0])).astype(BF)
    grad_ref[0] = (
        live * cot_ref[0].astype(F32) + norm_back(both[1] * gain_ref[...], unit, inverse)
    ).astype(BF)


def after(s, i, ids, x, cot, gain, keep, near, far, earlier):
    x, cot, keep, near, far = (pltpu.with_memory_space_constraint(a, pltpu.HBM) for a in (x, cot, keep, near, far))
    seqs, part, dim = x.shape
    one = pl.BlockSpec((1, part, dim), lambda g: (s, 0, 0))
    pair = pl.BlockSpec((1, 1, 2, part, dim), lambda g: (0, i, 0, 0, 0))
    lone = pl.BlockSpec((1, 2, part, dim), lambda g: (i, 0, 0, 0))
    fixed = lambda a: pl.BlockSpec(a.shape, lambda g: (0,) * a.ndim)
    return pl.pallas_call(
        functools.partial(after_kernel, s),
        grid=(1,),
        out_shape=[jax.ShapeDtypeStruct(x.shape, BF)] * 2,
        in_specs=[fixed(ids), one, one, fixed(gain), pair, pair, lone] + [ANY] * len(earlier),
        out_specs=[one, one],
        input_output_aliases={7 + i: i for i in range(len(earlier))},
        cost_estimate=SMALL,
        compiler_params=pltpu.CompilerParams(vmem_limit_bytes=32 * MIB),
        name="after",
    )(ids, x, cot, gain, keep, near, far, *earlier)


def attention_kernel(
    heads, block, last,
    at_ref, ids_ref, qg_ref, kg_ref, wqkv_hbm, wo_hbm, *refs,
):
    pays, refs = refs[0], refs[1:]
    if last:
        (acc_sums_ref, fnp_ref, gain_ref, accq_hbm, acco_hbm, hid_hbm, gup_hbm, wff_hbm, wup_hbm), refs = refs[:9], refs[9:]
        (keep_hbm, leave_hbm, sendq_ref, sendo_ref, keepo_ref, sums_ref), refs = refs[:6], refs[6:]
        (hid_ref, gup_ref, wff_ref, wup_ref, res_ref, res_sem, act_sem), refs = refs[:7], refs[7:]
    else:
        (o_hbm, grad_hbm, sums_ref, newq_hbm, newo_hbm), refs = refs[:5], refs[5:]
    (
        wqkv_ref, wo_ref, norm_ref, gb_ref, o_ref, grad_ref, gq_ref, go_ref, raw_ref,
        qt_ref, qn_ref, kt_ref, ka_ref, vt_ref, va_ref, do_ref, dq_ref, dk_ref, dv_ref, pad_ref, vm_ref,
        w_sem, sem, out_sem,
    ) = refs
    seqs, length, dim = norm_ref.shape
    part = length // SLOTS
    width = heads * HD
    blocks = length // block
    loads = [pltpu.make_async_copy(wqkv_hbm, wqkv_ref, w_sem.at[0]), pltpu.make_async_copy(wo_hbm, wo_ref, w_sem.at[1])]
    loads[0].start()

    def pay_copy(s, j, t):
        to = (norm_ref, gb_ref)[j].at[s, pl.ds(t * part, part), :]
        return pltpu.make_async_copy(pays.at[t, s, j], to, sem.at[s, j * SLOTS + t])

    for s in range(seqs):
        for j in range(2):
            for t in range(SLOTS):
                pay_copy(s, j, t).start()
            if s + j == 0:
                loads[1].start()
    if last:
        loads.append(pltpu.make_async_copy(accq_hbm, gq_ref, w_sem.at[2]))
        loads.append(pltpu.make_async_copy(acco_hbm, go_ref, w_sem.at[3]))
        loads.append(pltpu.make_async_copy(wff_hbm, wff_ref, act_sem.at[2 * seqs]))
        loads.append(pltpu.make_async_copy(wup_hbm, wup_ref, act_sem.at[2 * seqs + 1]))
        for copy in loads[2:]:
            copy.start()
        skip = hid_hbm.shape[0] // length - seqs

        def act_copies(s):
            rows = pl.ds(pl.multiple_of((skip + s) * length, length), length)
            return [
                pltpu.make_async_copy(hid_hbm.at[rows, :], hid_ref.at[s], act_sem.at[2 * s]),
                pltpu.make_async_copy(gup_hbm.at[rows, :], gup_ref.at[s], act_sem.at[2 * s + 1]),
            ]

        for s in range(seqs):
            for copy in act_copies(s):
                copy.start()
        outs = Outputs(at_ref[1], keep_hbm, leave_hbm, res_ref, res_sem, wo_ref, wff_ref, wqkv_ref, wup_ref)
        sums_ref[...] = acc_sums_ref[...]
    else:
        gq_ref[...] = jnp.zeros_like(gq_ref)
        go_ref[...] = jnp.zeros_like(go_ref)
        sums_ref[...] = jnp.zeros_like(sums_ref)
    gain_q = qg_ref[...]
    gain_k = kg_ref[...]
    marks = lax.broadcasted_iota(jnp.int32, (HD, length), 0)
    v_tail = jnp.where(lax.broadcasted_iota(jnp.int32, (length, HD), 1) < 2, 1.0, 0.0).astype(BF)
    ones = jnp.where(lax.broadcasted_iota(jnp.int32, (16, length), 0) == 0, 1.0, 0.0).astype(BF)
    spot = lax.broadcasted_iota(jnp.int32, (HD, block), 0)
    scale = 1.0 / math.sqrt(HD)
    cut = lambda a, i: a[:, i * block : (i + 1) * block]

    def unit_of(row):
        raw = raw_ref[pl.ds(pl.multiple_of(row, HD), HD), :]
        center = raw - jnp.mean(raw, axis=0, keepdims=True)
        inverse = lax.rsqrt(jnp.mean(center * center, axis=0, keepdims=True) + EPS)
        return center * inverse, inverse

    def lanes(a):
        total = a[:, :128]
        for i in range(1, length // 128):
            total = total + a[:, i * 128 : (i + 1) * 128]
        return total

    def stores(s):
        return [
            pltpu.make_async_copy(o_ref.at[s], o_hbm.at[s], out_sem.at[s, 0]),
            pltpu.make_async_copy(grad_ref.at[s], grad_hbm.at[s], out_sem.at[s, 1]),
        ]

    loads[0].wait()
    loads[1].wait()

    def sequence(s, carry):
        ids = ids_ref[s]
        same = marks == ids + 1
        k_tail = jnp.where(same, 1.0, 0.0).T.astype(BF)
        q_tail = jnp.where((same & (ids >= 0)) | (marks > 4), 0.0, -BIG).astype(BF)
        pad = jnp.where(ids < 0, 1.0, 0.0)
        for i in range(blocks):
            pad_ref[i] = cut(pad, i)
        for t in range(SLOTS):
            pay_copy(s, 0, t).wait()
        raw_ref[...] = mm(wqkv_ref[...], norm_ref[s], NT)
        for t in range(SLOTS):
            pay_copy(s, 1, t).wait()
        do_all = mm(wo_ref[...], gb_ref[s], NT).astype(BF)
        for h in range(heads):
            for i in range(blocks):
                do_ref[h * blocks + i] = cut(do_all[h * HD : (h + 1) * HD], i)

        def prepare(h, carry):
            q_unit, _ = unit_of(h * HD)
            q = q_unit * gain_q
            qn = q.T.astype(BF)
            for i in range(blocks):
                qt_ref[h * blocks + i, :HD] = cut(q, i).astype(BF)
                qt_ref[h * blocks + i, HD:] = cut(q_tail, i)
                qn_ref[h * blocks + i] = qn[i * block : (i + 1) * block]
            k_unit, _ = unit_of(width + h * HD)
            k = k_unit * gain_k
            kt_ref[h] = k.astype(BF)
            ka_ref[h, :, :HD] = k.T.astype(BF)
            ka_ref[h, :, HD:] = k_tail
            v = raw_ref[pl.ds(pl.multiple_of(2 * width + h * HD, HD), HD), :]
            vb = v.astype(BF)
            vt_ref[h, :HD] = vb
            vt_ref[h, HD:] = ones
            va_ref[h, :, :HD] = v.T.astype(BF)
            va_ref[h, :, HD:] = v_tail
            vm_ref[h] = jnp.mean(vb.astype(F32), axis=1, keepdims=True)
            dk_ref[h] = jnp.zeros(dk_ref.shape[1:], F32)
            dv_ref[h] = jnp.zeros(dv_ref.shape[1:], F32)
            return carry

        lax.fori_loop(0, heads, prepare, 0)

        def step(n, carry):
            h = n // blocks
            padb = pad_ref[n % blocks]
            e = jnp.exp2(mm(ka_ref[h], qt_ref[n]) * (LOG2E * scale))
            eb = e.astype(BF)
            oa = mm(vt_ref[h], eb)
            inv = 1.0 / (oa[HD : HD + 1] + padb)
            o = oa[:HD] * inv
            dos = (do_ref[n].astype(F32) * inv).astype(BF)
            delta = jnp.sum(dos.astype(F32) * o, axis=0, keepdims=True)
            d0 = delta.astype(BF).astype(F32)
            tail = jnp.where(spot == 0, -d0, jnp.where(spot == 1, d0 - delta, 0.0))
            doa = jnp.concatenate([dos.astype(F32), tail], axis=0)
            ds = (e * mm(va_ref[h], doa.astype(BF))).astype(BF)
            dq_ref[n] = mm(kt_ref[h], ds)
            dk_ref[h] += mm(ds, qn_ref[n])
            dv_ref[h] += mm(eb, doa.T.astype(BF))
            do_ref[n] = jnp.where(padb > 0, vm_ref[h], o).astype(BF)
            return carry

        lax.fori_loop(0, heads * blocks, step, 0)

        def finish(h, carry):
            rows = lambda at: pl.ds(pl.multiple_of(at + h * HD, HD), HD)
            gq = jnp.concatenate([dq_ref[h * blocks + i] for i in range(blocks)], axis=1)
            gk = dk_ref[h].T
            for k, (g, gain_col) in enumerate(((gq, gain_q), (gk, gain_k))):
                unit, inverse = unit_of(k * width + h * HD)
                g = (g * scale).astype(BF).astype(F32)
                sums_ref[k] += lanes(g * unit)
                g = g * gain_col
                back = inverse * (
                    g - jnp.mean(g, axis=0, keepdims=True) - unit * jnp.mean(g * unit, axis=0, keepdims=True)
                )
                grad_ref[s, rows(k * width), :] = back.astype(BF)
            grad_ref[s, rows(2 * width), :] = dv_ref[h].T[:HD].astype(BF)
            for i in range(blocks):
                o_ref[s, rows(0), pl.ds(i * block, block)] = do_ref[h * blocks + i]
            return carry

        lax.fori_loop(0, heads, finish, 0)
        if last:

            @pl.when(s == 0)
            def _():
                for copy in loads[2:]:
                    copy.wait()

            for copy in act_copies(s):
                copy.wait()
            outs.compute(s, o_ref.at[s], hid_ref.at[s], grad_ref.at[s], gup_ref.at[s])
        else:
            for copy in stores(s):
                copy.start()
        gq_ref[...] += mm(grad_ref[s], norm_ref[s])
        go_ref[...] += mm(o_ref[s], gb_ref[s])
        return carry

    lax.fori_loop(0, seqs, sequence, 0)
    if not last:
        ends = [pltpu.make_async_copy(gq_ref, newq_hbm, w_sem.at[2]), pltpu.make_async_copy(go_ref, newo_hbm, w_sem.at[3])]
        for copy in ends:
            copy.start()
        for copy in ends:
            copy.wait()
        for s in range(seqs):
            for copy in stores(s):
                copy.wait()
        return
    outs.wait()
    g_q = gq_ref[...]
    first_row = (jnp.sum(wqkv_ref[...].astype(F32) * g_q, axis=0, keepdims=True) + fnp_ref[...]) / gain_ref[...]
    second_row = jnp.concatenate([jnp.sum(sums_ref[k].T, axis=0, keepdims=True) for k in range(2)], axis=1)
    wide = 3 * width
    line = jnp.concatenate([first_row[:, wide:], second_row, jnp.zeros((1, 2 * wide - dim - 2 * HD), F32)], axis=1)
    small = jnp.concatenate([first_row[:, :wide], line], axis=0)
    high = small.astype(BF)
    small = jnp.concatenate([high.astype(F32), small - high.astype(F32)], axis=0).astype(BF)
    g_q = g_q.T.astype(BF)
    count, rows, _ = sendq_ref.shape
    rows = rows - 4
    for i in range(count):
        sendq_ref[i, :rows] = g_q[i * rows : (i + 1) * rows]
        sendq_ref[i, rows:] = small
    split_rows((at_ref[2] & 1) > 0, go_ref[...], sendo_ref, keepo_ref)


def attention(at, ids, wqkv, wo, qg, kg, pays, count, more=()):
    wide, dim = wqkv.shape
    width = wo.shape[0]
    heads = width // HD
    _, seqs, _, part, _ = pays.shape
    length = part * SLOTS
    block = 512
    blocks = length // block
    last = bool(more)
    ins = [at, ids, qg, kg, *hbm(wqkv, wo, pays), *more[:3], *hbm(*more[3:])]
    specs = [SMEM] + [VMEM] * 3 + [HBM] * 3 + ([VMEM] * 3 + [HBM] * 6 if last else [])
    scratch = []
    if last:
        outs = [jax.ShapeDtypeStruct((SLOTS // 2, seqs, 2, part, dim), BF)] * 2
        outs += [jax.ShapeDtypeStruct((count, dim // count + 4, wide), BF)]
        outs += [jax.ShapeDtypeStruct((count // (2 * SLOTS), SLOTS * width // count, dim), t) for t in (BF, F32)]
        scratch = [pltpu.VMEM((2, HD, 128), F32)]
        scratch += [pltpu.VMEM((seqs, length, dim), BF)] * 2 + [pltpu.VMEM((dim, dim), BF)] * 2
        scratch += Outputs.scratch(seqs, length, dim) + [pltpu.SemaphoreType.DMA((2 * seqs + 2,))]
    else:
        outs = [jax.ShapeDtypeStruct((seqs, width, length), BF), jax.ShapeDtypeStruct((seqs, wide, length), BF)]
        outs += [
            jax.ShapeDtypeStruct((2, HD, 128), F32),
            jax.ShapeDtypeStruct((wide, dim), F32),
            jax.ShapeDtypeStruct((width, dim), F32),
        ]
    flops = seqs * (2 * length * dim * width * 8 + heads * 6 * 2 * length * length * HD)
    return pl.pallas_call(
        functools.partial(attention_kernel, heads, block, last),
        out_shape=outs,
        in_specs=specs,
        out_specs=[HBM] * 2 + ([VMEM] * 3 if last else [VMEM, HBM, HBM]),
        scratch_shapes=scratch
        + [
            pltpu.VMEM((wide, dim), BF),
            pltpu.VMEM((width, dim), BF),
            pltpu.VMEM((seqs, length, dim), BF),
            pltpu.VMEM((seqs, length, dim), BF),
            pltpu.VMEM((seqs, width, length), BF),
            pltpu.VMEM((seqs, wide, length), BF),
            pltpu.VMEM((wide, dim), F32),
            pltpu.VMEM((width, dim), F32),
            pltpu.VMEM((wide, length), F32),
            pltpu.VMEM((heads * blocks, 2 * HD, block), BF),
            pltpu.VMEM((heads * blocks, block, HD), BF),
            pltpu.VMEM((heads, HD, length), BF),
            pltpu.VMEM((heads, length, 2 * HD), BF),
            pltpu.VMEM((heads, HD + 16, length), BF),
            pltpu.VMEM((heads, length, 2 * HD), BF),
            pltpu.VMEM((heads * blocks, HD, block), BF),
            pltpu.VMEM((heads * blocks, HD, block), F32),
            pltpu.VMEM((heads, length, HD), F32),
            pltpu.VMEM((heads, length, 2 * HD), F32),
            pltpu.VMEM((blocks, 1, block), F32),
            pltpu.VMEM((heads, HD, 1), F32),
            pltpu.SemaphoreType.DMA((4,)),
            pltpu.SemaphoreType.DMA((seqs, 2 * SLOTS)),
            pltpu.SemaphoreType.DMA((seqs, 2)),
        ],
        cost_estimate=LARGE,
        compiler_params=pltpu.CompilerParams(vmem_limit_bytes=56 * MIB),
        name="attention",
    )(*ins)


def ffn_kernel(block, groups, plan, at_ref, wup_hbm, wqkv_hbm, wo_hbm, o_hbm, gq_hbm, *refs):
    pieces, refs = refs[: len(plan)], refs[len(plan) :]
    pays, refs = refs[: len(groups)], refs[len(groups) :]
    (hid_hbm, gup_hbm, wff_hbm, keep_hbm, leave_hbm, send_ref, np_ref), refs = refs[:7], refs[7:]
    norm_ref, gb_ref, hid_ref, gup_ref, wup_ref, wff_ref, gin_ref, gff_ref, sem, out_sem, w_sem, *refs = refs
    wqkv_ref, wo_ref, o_ref, gq_ref, res_ref, res_sem, late_sem = refs
    dim = wup_ref.shape[0]
    part = pays[0].shape[3]
    total = norm_ref.shape[0]
    weights = [pltpu.make_async_copy(wup_hbm, wup_ref, w_sem.at[0])]
    rows = send_ref.shape[2]
    for ref, masks in zip(pieces, plan):
        for i, mask in enumerate(masks):
            to = wff_ref.at[pl.ds(pl.multiple_of((at_ref[2] ^ mask) * rows, rows), rows), :]
            weights.append(pltpu.make_async_copy(ref.at[i], to, w_sem.at[len(weights)]))
    for copy in weights:
        copy.start()
    n = 0
    for g, seqs in enumerate(groups):
        for s in range(seqs):
            for t in range(SLOTS):
                for k, to in enumerate((norm_ref, gb_ref)):
                    source = pays[g].at[t, s, k]
                    pltpu.make_async_copy(source, to.at[pl.ds(n * part, part), :], sem.at[k, n]).start()
                n += 1
    late = [
        pltpu.make_async_copy(a, b, late_sem.at[i])
        for i, (a, b) in enumerate(((wqkv_hbm, wqkv_ref), (wo_hbm, wo_ref), (o_hbm, o_ref), (gq_hbm, gq_ref)))
    ]
    for copy in late:
        copy.start()
    gin_ref[...] = jnp.zeros_like(gin_ref)
    gff_ref[...] = jnp.zeros_like(gff_ref)
    for copy in weights:
        copy.wait()
    joined = pltpu.make_async_copy(wff_ref, wff_hbm, w_sem.at[0])
    joined.start()
    c0 = math.sqrt(2.0 / math.pi)
    c1 = 0.044715

    def outs(i):
        at_rows = pl.ds(pl.multiple_of(i * block, block), block)
        return (
            pltpu.make_async_copy(hid_ref.at[at_rows, :], hid_hbm.at[at_rows, :], out_sem.at[0, i]),
            pltpu.make_async_copy(gup_ref.at[at_rows, :], gup_hbm.at[at_rows, :], out_sem.at[1, i]),
        )

    def step(i, carry):
        for j in range(block // part):
            for k, to in enumerate((norm_ref, gb_ref)):
                pltpu.make_async_copy(pays[0].at[0, 0, 0], to.at[pl.ds(0, part), :], sem.at[k, i * (block // part) + j]).wait()
        at_rows = pl.ds(pl.multiple_of(i * block, block), block)
        up = mm(norm_ref[at_rows, :], wup_ref[...])
        gh = mm(gb_ref[at_rows, :], wff_ref[...], NT)
        sq = up * up
        t = jnp.tanh(up * (c0 + (c0 * c1) * sq))
        half = 0.5 + 0.5 * t
        hid_ref[at_rows, :] = (up * half).astype(BF)
        gup_ref[at_rows, :] = (gh * (half + (0.5 * up) * (1.0 - t * t) * (c0 + (3.0 * c0 * c1) * sq))).astype(BF)
        for copy in outs(i):
            copy.start()
        gin_ref[...] += mm(norm_ref[at_rows, :], gup_ref[at_rows, :], TN)
        gff_ref[...] += mm(hid_ref[at_rows, :], gb_ref[at_rows, :], TN)
        return carry

    lax.fori_loop(0, total // block, step, 0)
    for copy in late:
        copy.wait()
    results = Outputs(at_ref[1], keep_hbm, leave_hbm, res_ref, res_sem, wo_ref, wff_ref, wqkv_ref, wup_ref)
    length = SLOTS * part
    for s in range(results.seqs):
        rows_s = pl.ds(s * length, length)
        results.compute(s, o_ref.at[s], hid_ref.at[rows_s, :], gq_ref.at[s], gup_ref.at[rows_s, :])
    line = jnp.sum(wup_ref[...].astype(F32) * gin_ref[...], axis=1, keepdims=True)
    np_ref[...] = jnp.broadcast_to(line, (dim, 128)).T[0:1]
    for b in range(dim // rows):
        for k, g in enumerate((gin_ref, gff_ref)):
            send_ref[b, k] = g[b * rows : (b + 1) * rows, :].astype(BF)
    joined.wait()
    results.wait()

    def drain(i, carry):
        for copy in outs(i):
            copy.wait()
        return carry

    lax.fori_loop(0, total // block, drain, 0)


def ffn(at, wup, ff_parts, groups, count, wqkv, wo, o, gq, block=512):
    dim, units = wup.shape
    sizes = [g.shape[1] for g in groups]
    part = groups[0].shape[3]
    total = SLOTS * part * sum(sizes)
    pieces = groups
    act = jax.ShapeDtypeStruct((total, units), BF)
    return pl.pallas_call(
        functools.partial(ffn_kernel, block, sizes, [masks for _, masks in ff_parts]),
        out_shape=[
            act,
            act,
            jax.ShapeDtypeStruct((units, dim), BF),
            *[jax.ShapeDtypeStruct((SLOTS // 2, o.shape[0], 2, part, dim), BF)] * 2,
            jax.ShapeDtypeStruct((count, 2, units // count, dim), BF),
            jax.ShapeDtypeStruct((1, dim), F32),
        ],
        in_specs=[SMEM] + [HBM] * (5 + len(ff_parts) + len(pieces)),
        out_specs=[HBM] * 5 + [VMEM] * 2,
        scratch_shapes=[
            pltpu.VMEM((total, dim), BF),
            pltpu.VMEM((total, dim), BF),
            pltpu.VMEM((total, units), BF),
            pltpu.VMEM((total, units), BF),
            pltpu.VMEM((dim, units), BF),
            pltpu.VMEM((units, dim), BF),
            pltpu.VMEM((dim, units), F32),
            pltpu.VMEM((units, dim), F32),
            pltpu.SemaphoreType.DMA((2, total // part)),
            pltpu.SemaphoreType.DMA((2, total // block)),
            pltpu.SemaphoreType.DMA((1 + count,)),
            *[pltpu.VMEM(a.shape, BF) for a in (wqkv, wo, o, gq)],
            *Outputs.scratch(o.shape[0], SLOTS * part, dim),
            pltpu.SemaphoreType.DMA((4,)),
        ],
        cost_estimate=LARGE,
        compiler_params=pltpu.CompilerParams(vmem_limit_bytes=58 * MIB),
        name="ffn",
    )(at, *hbm(wup, wqkv, wo, o, gq, *[a for a, _ in ff_parts], *pieces))


class Outputs:
    def __init__(self, me, keep, send, res, sem, wo, wff, wqkv, wup):
        self.me = me
        self.keep, self.send, self.res, self.sem = keep, send, res, sem
        self.wo, self.wff, self.wqkv, self.wup = wo, wff, wqkv, wup
        self.seqs, _, self.length, _ = res.shape

    @staticmethod
    def scratch(seqs, length, dim):
        return [pltpu.VMEM((seqs, 2, length, dim), BF), pltpu.SemaphoreType.DMA((seqs, 2, SLOTS))]

    def moves(self, s, i):
        half = self.length // 2
        part = half // 2
        out = []
        for j in range(2):
            for k, to in enumerate((self.keep, self.send)):
                rows = pl.ds(pl.multiple_of(i * half + (k ^ (self.me & 1)) * part, part), part)
                source = self.res.at[s, j, rows, :]
                out.append(pltpu.make_async_copy(source, to.at[i ^ (self.me >> 1), s, j], self.sem.at[s, j, 2 * i + k]))
        return out

    def compute(self, s, o, hid, gq, gu):
        half = self.length // 2

        def step(i, carry):
            rows = pl.ds(pl.multiple_of(i * half, half), half)
            branch = mm(o[:, rows], self.wo[...], TN) + mm(hid[rows, :], self.wff[...])
            self.res[s, 0, rows, :] = branch.astype(BF)
            gn = mm(gq[:, rows], self.wqkv[...], TN) + mm(gu[rows, :], self.wup[...], NT)
            self.res[s, 1, rows, :] = gn.astype(BF)
            for copy in self.moves(s, i):
                copy.start()
            return carry

        lax.fori_loop(0, 2, step, 0)

    def wait(self):
        for s in range(self.seqs):
            for i in range(2):
                for copy in self.moves(s, i):
                    copy.wait()


def swap(value, axis, count, mask):
    return lax.ppermute(value, axis, [(i, i ^ mask) for i in range(count)])


def tie(value, *after):
    return lax.optimization_barrier((value,) + after)[0]


def bit_groups(count):
    bits = list(range(count.bit_length() - 1))[::-1]
    groups = []
    while bits:
        take = 2 if len(bits) > 1 else 1
        groups.append(bits[:take])
        bits = bits[take:]
    assert len(groups[-1]) == 1
    return groups


def gather_batch(block, count, groups):
    held, masks = block[None], [0]
    for bits in groups:
        low = bits[-1]
        parts = [(held, masks)]
        for s in range(1, 1 << len(bits)):
            parts.append((swap(held, "batch", count, s << low), [m ^ (s << low) for m in masks]))
        held = jnp.concatenate([a for a, _ in parts], axis=0)
        masks = sum((m for _, m in parts), [])
    return parts


def matchings(edges, devices, per_device):
    left = [[] for _ in range(devices)]
    for e, (source, _, _) in enumerate(edges):
        left[source].append(e)
    rounds = []
    for _ in range(per_device):
        owner = [-1] * devices

        def place(source, seen):
            for e in left[source]:
                target = edges[e][1]
                if target in seen:
                    continue
                seen.add(target)
                if owner[target] < 0 or place(edges[owner[target]][0], seen):
                    owner[target] = e
                    return True
            return False

        for source in range(devices):
            place(source, set())
        rounds.append(list(owner))
        for e in owner:
            left[edges[e][0]].remove(e)
    return rounds


def unit_plan(nb, nt, rows, width, hidden):
    unit = math.gcd(math.gcd(rows, width // nt), hidden // nt)
    per = rows // unit
    head_units, hid_units = width // nt // unit, hidden // nt // unit
    assert head_units == nb and hid_units % nb == 0
    c = hid_units // nb
    edges = []
    for t in range(nt):
        for b in range(nb):
            want = [t * head_units + b]
            want += [nt * head_units + t * hid_units + b * c + i for i in range(c)]
            for slot, u in enumerate(want):
                edges.append((u // per, b * nt + t, (u % per, slot)))
    table = np.zeros((nb * nt, 2 * per), np.int32)
    perms = []
    for k, owner in enumerate(matchings(edges, nb * nt, per)):
        perms.append([(edges[e][0], edges[e][1]) for e in owner])
        for e in owner:
            table[edges[e][0], k] = edges[e][2][0]
            table[edges[e][1], per + k] = edges[e][2][1]
    return unit, per, perms, table


def per_device(
    nb, nt, patches, image_ids, cotangent, norm_gain, query_gain, key_gain, in_weight, out_weight
):
    seqs, part, dim = patches.shape
    width = H * HD
    local = width // nt
    units = (in_weight.shape[1] - 3 * width) // nt
    rows_in = in_weight.shape[0]
    unit, per, perms, table = unit_plan(nb, nt, out_weight.shape[0], width, units * nt)
    assert nt == SLOTS and units == dim and unit == rows_in and dim == nt * local and per == nt + 1
    both = ("batch", "tok")
    me_b = lax.axis_index("batch")
    me_t = lax.axis_index("tok")
    at = jnp.stack([me_b * nt + me_t, me_t, me_b])
    table = jnp.asarray(table)
    gain = norm_gain.reshape(1, dim)

    def exchange(value, axis):
        return lax.all_to_all(value, axis, split_axis=0, concat_axis=0, tiled=True)

    groups = bit_groups(nb)

    lead = 2
    a_src, u_src = prepare(image_ids, in_weight, nb, nt)
    a_got = exchange(a_src.reshape(nb * nt, rows_in + 2, 3 * local), both)
    own0, own1, *unit_sends = before(
        at, table, out_weight.reshape(per, unit, dim), image_ids, gain, tie(patches, a_src), cotangent, lead
    )
    got = [lax.ppermute(v, both, perm) for v, perm in zip(unit_sends, perms)]
    wo_src, ff_src = pack_out(at, table, tie(got, a_got))
    slots0 = lax.all_gather(own0, "tok", axis=0)
    slots1 = lax.all_gather(own1, "tok", axis=0)
    wo_parts = gather_batch(wo_src, nb, groups)
    ff_parts = gather_batch(ff_src.reshape((per - 1) * unit, dim), nb, groups[::-1])
    wqkv, wo, ids = join(at, a_got, wo_parts, seqs, part)
    wo = wo.reshape(local, dim)
    wup = exchange(tie(u_src, a_got).reshape(nb * nt, unit, dim), both).reshape(dim, units)

    qg = query_gain.reshape(HD, 1)
    kg = key_gain.reshape(HD, 1)

    def leave_chip(keep, near, *hold):
        value = (keep[1].astype(F32) + near[1].astype(F32)).astype(BF)
        return value, swap(tie(value, *hold) if hold else value, "tok", nt, 2)

    o0, gq0, sums, acc_q, acc_o = attention(at, ids[:lead], wqkv, tie(wo, ff_parts[0][0]), qg, kg, slots0, nb * nt)
    hid, gup, wff, keep0, send0, f_grad, f_np = ffn(
        at, tie(wup, o0), ff_parts, [slots0, slots1], nb, wqkv, wo, o0, gq0
    )
    f_mine = lax.psum_scatter(f_grad, "batch", scatter_dimension=0, tiled=True).reshape(2, nt, unit, dim)
    near0 = swap(send0, "tok", nt, 1)
    value0, away0 = leave_chip(keep0, near0)
    keep1, send1, a_q, a_send, a_keep = attention(
        at, ids[lead:], wqkv, tie(wo, value0), qg, kg, slots1, nb * nt,
        (sums, f_np, gain, acc_q, acc_o, hid, gup, wff, wup),
    )
    a_came = swap(a_send, "batch", nb, 1)
    terms = [a_keep, a_came]
    for bits in groups[:-1][::-1]:
        own, *sends = fold(at, bits[-1], [terms])
        terms = [own] + [swap(value, "batch", nb, (s + 1) << bits[-1]) for s, value in enumerate(sends)]
    near1 = swap(tie(send1, away0, *terms[1:]), "tok", nt, 1)
    a_q = exchange(tie(a_q, *terms[1:]), both)
    value1, away1 = leave_chip(keep1, near1)
    up = exchange(tie(f_mine[0], a_q), "tok")
    group = [(0, s, keep0, near0, away0) for s in range(lead)]
    group += [(lead, s, keep1, near1, away1) for s in range(lead, seqs)]

    sends = leave(at, table, terms, f_mine[1])
    got = [lax.ppermute(v, both, [(b, a) for a, b in perm]) for v, perm in zip(sends, perms)]
    in_grad, out_grad, norm_grad, query_grad, key_grad = place(at, table, a_q, up, got)

    earlier = []
    for s in range(seqs):
        start, _, *arrays = group[s]
        earlier = after(s, s - start, image_ids, patches, cotangent, gain, *arrays, earlier)
    block_out, patch_grad = earlier
    return (
        block_out,
        patch_grad,
        norm_grad.reshape(dim),
        query_grad.reshape(HD),
        key_grad.reshape(HD),
        in_grad,
        out_grad.reshape(per * unit, dim),
    )


def solution(mesh):
    rows = P("batch", "tok", None)
    weights = P(("batch", "tok"), None)
    return jax.shard_map(
        functools.partial(per_device, mesh.shape["batch"], mesh.shape["tok"]),
        mesh=mesh,
        in_specs=(rows, P("batch", "tok"), rows, P(), P(), P(), weights, weights),
        out_specs=(rows, rows, P(), P(), P(), weights, weights),
        check_vma=False,
    )
```

```python
import functools
import math

import jax
import jax.numpy as jnp
import numpy as np
from jax import lax
from jax.experimental import pallas as pl
from jax.experimental.pallas import tpu as pltpu
from jax.sharding import PartitionSpec as P

H = 12
HD = 64
SLOTS = 4
EPS = 1e-06
BIG = 2048.0
LOG2E = 1.4426950408889634
BF = jnp.bfloat16
F32 = jnp.float32
NN = (((1,), (0,)), ((), ()))
NT = (((1,), (1,)), ((), ()))
TN = (((0,), (0,)), ((), ()))
MIB = 1 << 20
SMALL = pl.CostEstimate(flops=1, transcendentals=0, bytes_accessed=1)
LARGE = pl.CostEstimate(flops=60_000_000_000, transcendentals=0, bytes_accessed=1)

VMEM = pl.BlockSpec(memory_space=pltpu.VMEM)
SMEM = pl.BlockSpec(memory_space=pltpu.SMEM)
ANY = pl.BlockSpec(memory_space=pl.ANY)
HBM = pl.BlockSpec(memory_space=pltpu.HBM)


def hbm(*arrays):
    return [pltpu.with_memory_space_constraint(a, pltpu.HBM) for a in arrays]


def mm(a, b, dims=NN):
    return lax.dot_general(a, b, dims, preferred_element_type=F32)


def normalize(values):
    center = values - jnp.mean(values, axis=-1, keepdims=True)
    inverse = lax.rsqrt(jnp.mean(center * center, axis=-1, keepdims=True) + EPS)
    return center * inverse, inverse


def norm_back(grad_unit, unit_rows, inverse):
    return inverse * (
        grad_unit
        - jnp.mean(grad_unit, axis=-1, keepdims=True)
        - unit_rows * jnp.mean(grad_unit * unit_rows, axis=-1, keepdims=True)
    )


def as_row(ref):
    return ref[...].reshape(1, ref.shape[0])


def column(row):
    return jnp.broadcast_to(row, (8, row.shape[1])).T[:, 0:1]


def prepare(ids, w_in, nb, nt):
    rows, wide = w_in.shape
    seqs, part = ids.shape
    width = H * HD
    local = width // nt
    units = (wide - 3 * width) // nt

    def kernel(ids_hbm, win_hbm, a_hbm, u_hbm, ids_ref, win_ref, a_ref, u_ref, in_sem, a_sem, u_sem):
        loads = [pltpu.make_async_copy(win_hbm, win_ref, in_sem.at[0]), pltpu.make_async_copy(ids_hbm, ids_ref, in_sem.at[1])]
        for copy in loads:
            copy.start()
        for copy in loads:
            copy.wait()
        row = jnp.concatenate([ids_ref[s : s + 1, :] for s in range(seqs)], axis=1).astype(F32).astype(BF)
        first = 3 * local
        second = jnp.concatenate([row[:, first:].astype(F32), jnp.zeros((1, 2 * first - seqs * part), F32)], axis=1).astype(BF)
        for t in range(nt):
            for k in range(3):
                a_ref[t, :rows, k * local : (k + 1) * local] = win_ref[:, k * width + t * local : k * width + (t + 1) * local]
            a_ref[t, rows : rows + 1] = row[:, :first]
            a_ref[t, rows + 1 :] = second
        for b in range(nb):
            pltpu.make_async_copy(a_ref, a_hbm.at[b], a_sem.at[b]).start()
        for t in range(nt):
            u_ref[t] = win_ref[:, 3 * width + t * units : 3 * width + (t + 1) * units]
        for b in range(nb):
            pltpu.make_async_copy(u_ref, u_hbm.at[b], u_sem.at[b]).start()
        for b in range(nb):
            pltpu.make_async_copy(a_ref, a_hbm.at[b], a_sem.at[b]).wait()
            pltpu.make_async_copy(u_ref, u_hbm.at[b], u_sem.at[b]).wait()

    return pl.pallas_call(
        kernel,
        out_shape=[
            jax.ShapeDtypeStruct((nb, nt, rows + 2, 3 * local), BF),
            jax.ShapeDtypeStruct((nb, nt, rows, units), BF),
        ],
        in_specs=[HBM] * 2,
        out_specs=[HBM] * 2,
        scratch_shapes=[
            pltpu.VMEM(ids.shape, jnp.int32),
            pltpu.VMEM(w_in.shape, BF),
            pltpu.VMEM((nt, rows + 2, 3 * local), BF),
            pltpu.VMEM((nt, rows, units), BF),
            pltpu.SemaphoreType.DMA((2,)),
            pltpu.SemaphoreType.DMA((nb,)),
            pltpu.SemaphoreType.DMA((nb,)),
        ],
        cost_estimate=SMALL,
        compiler_params=pltpu.CompilerParams(vmem_limit_bytes=16 * MIB),
        name="prepare",
    )(*hbm(ids, w_in))


def before(at, table, w_out, ids, gain, x, cot, first):
    seqs, part, dim = x.shape

    per, unit, _ = w_out.shape

    def kernel(at_ref, table_hbm, wout_hbm, ids_hbm, gain_hbm, x_hbm, cot_hbm, out0_hbm, out1_hbm, *refs):
        unit_refs, (table_ref, wout_ref, ids_ref, gain_ref, x_ref, cot_ref, pay_ref, in_sem, x_sem, out_sem) = refs[:per], refs[per:]
        ins = [
            pltpu.make_async_copy(a, b, in_sem.at[i])
            for i, (a, b) in enumerate(((table_hbm, table_ref), (wout_hbm, wout_ref), (ids_hbm, ids_ref), (gain_hbm, gain_ref)))
        ]
        loads = [
            [pltpu.make_async_copy(a.at[s], b.at[s], x_sem.at[s, k]) for k, (a, b) in enumerate(((x_hbm, x_ref), (cot_hbm, cot_ref)))]
            for s in range(seqs)
        ]
        for copy in ins + sum(loads, []):
            copy.start()
        for copy in ins:
            copy.wait()
        for k, ref in enumerate(unit_refs):
            ref[...] = wout_ref[table_ref[at_ref[0], k]]
        copies = []
        for s in range(seqs):
            for copy in loads[s]:
                copy.wait()
            unit, _ = normalize(x_ref[s].astype(F32))
            live = column(jnp.where(ids_ref[s : s + 1, :] >= 0, 1.0, 0.0))
            pay_ref[s, 0] = (unit * as_row(gain_ref)).astype(BF)
            pay_ref[s, 1] = (live * cot_ref[s].astype(F32)).astype(BF)
            to = out0_hbm.at[s] if s < first else out1_hbm.at[s - first]
            copies.append(pltpu.make_async_copy(pay_ref.at[s], to, out_sem.at[s]))
            copies[-1].start()
        for copy in copies:
            copy.wait()

    return pl.pallas_call(
        kernel,
        out_shape=[jax.ShapeDtypeStruct((n, 2, part, dim), BF) for n in (first, seqs - first)]
        + [jax.ShapeDtypeStruct((unit, dim), BF)] * per,
        in_specs=[SMEM] + [HBM] * 6,
        out_specs=[HBM] * 2 + [VMEM] * per,
        scratch_shapes=[
            pltpu.SMEM(table.shape, jnp.int32),
            pltpu.VMEM(w_out.shape, BF),
            pltpu.VMEM(ids.shape, jnp.int32),
            pltpu.VMEM(gain.shape, F32),
            pltpu.VMEM(x.shape, BF),
            pltpu.VMEM(x.shape, BF),
            pltpu.VMEM((seqs, 2, part, dim), BF),
            pltpu.SemaphoreType.DMA((4,)),
            pltpu.SemaphoreType.DMA((seqs, 2)),
            pltpu.SemaphoreType.DMA((seqs,)),
        ],
        cost_estimate=SMALL,
        compiler_params=pltpu.CompilerParams(vmem_limit_bytes=32 * MIB),
        name="before",
    )(at, *hbm(table, w_out, ids, gain, x, cot))


def join(at, got, wo_parts, seqs, part):
    count, high, wide = got.shape
    unit = high - 2
    dim = count * unit
    nb = count // SLOTS

    def kernel(at_ref, got_ref, *refs):
        ins, (w_ref, wo_ref, ids_ref, all_ref) = refs[:-4], refs[-4:]

        def move(i, carry):
            all_ref[i] = got_ref[i, :unit]
            return carry

        lax.fori_loop(0, count, move, 0)
        w_ref[...] = all_ref[...].reshape(dim, wide).T
        for ref, (_, masks) in zip(ins, wo_parts):
            for i, mask in enumerate(masks):
                wo_ref[at_ref[2] ^ mask] = ref[i]
        for slot in range(SLOTS):
            i = at_ref[2] * SLOTS + slot
            row = jnp.concatenate([got_ref[i, unit : unit + 1], got_ref[i, unit + 1 :]], axis=1)
            row = row.astype(F32).astype(jnp.int32)
            for s in range(seqs):
                ids_ref[s, :, slot * part : (slot + 1) * part] = row[:, s * part : (s + 1) * part]

    return pl.pallas_call(
        kernel,
        out_shape=[
            jax.ShapeDtypeStruct((wide, dim), BF),
            jax.ShapeDtypeStruct((nb,) + wo_parts[0][0].shape[1:], BF),
            jax.ShapeDtypeStruct((seqs, 1, SLOTS * part), jnp.int32),
        ],
        in_specs=[SMEM] + [VMEM] * (1 + len(wo_parts)),
        out_specs=[VMEM] * 3,
        scratch_shapes=[pltpu.VMEM((count, unit, wide), BF)],
        cost_estimate=SMALL,
        compiler_params=pltpu.CompilerParams(vmem_limit_bytes=32 * MIB),
        name="join",
    )(at, got, *[a for a, _ in wo_parts])


def pack_out(at, table, got):
    unit, dim = got[0].shape
    per = len(got)

    def kernel(at_ref, table_ref, *refs):
        got_refs, (wo_ref, ff_ref, all_ref) = refs[:per], refs[per:]
        for k, ref in enumerate(got_refs):
            all_ref[table_ref[at_ref[0], per + k]] = ref[...]
        wo_ref[...] = all_ref[0]
        for k in range(per - 1):
            ff_ref[k] = all_ref[k + 1]

    return pl.pallas_call(
        kernel,
        out_shape=[jax.ShapeDtypeStruct((unit, dim), BF), jax.ShapeDtypeStruct((per - 1, unit, dim), BF)],
        in_specs=[SMEM] * 2 + [VMEM] * per,
        out_specs=[VMEM] * 2,
        scratch_shapes=[pltpu.VMEM((per, unit, dim), BF)],
        cost_estimate=SMALL,
        name="pack_out",
    )(at, table, *got)


def add_blocks(ref, count, step, start, rows):
    total = ref[start, rows].astype(F32)
    for i in range(1, count):
        total = total + ref[start + i * step, rows].astype(F32)
    return total


def fold(at, low, terms):
    n, _, dim = terms[0][0].shape
    counts = [len(group) for group in terms]
    rows = [group[0].shape[1] for group in terms]

    def kernel(at_ref, *refs):
        ins, (own_ref, *send_refs) = refs[: sum(counts)], refs[sum(counts) :]
        mine = (at_ref[2] >> low) & 3
        k, start = 0, 0
        for count, high in zip(counts, rows):
            for i in range(n // 4):
                for s, to in enumerate([own_ref] + send_refs):
                    block = i * 4 + (mine ^ s)
                    total = ins[k][block].astype(F32)
                    for ref in ins[k + 1 : k + count]:
                        total = total + ref[block].astype(F32)
                    to[i, start : start + high] = total.astype(to.dtype)
            k += count
            start += high

    out = lambda t: jax.ShapeDtypeStruct((n // 4, sum(rows), dim), t)
    return pl.pallas_call(
        kernel,
        out_shape=[out(F32)] + [out(BF)] * 3,
        in_specs=[SMEM] + [VMEM] * sum(counts),
        out_specs=[VMEM] * 4,
        cost_estimate=SMALL,
        compiler_params=pltpu.CompilerParams(vmem_limit_bytes=32 * MIB),
        name="fold",
    )(at, *sum(terms, []))


def split_rows(odd, grad, send_ref, keep_ref):
    parts, rows, _ = send_ref.shape
    for z in range(parts):
        low = grad[2 * z * rows : (2 * z + 1) * rows]
        high = grad[(2 * z + 1) * rows : (2 * z + 2) * rows]
        send_ref[z] = jnp.where(odd, low, high).astype(BF)
        keep_ref[z] = jnp.where(odd, high, low)


def leave(at, table, heads, ffn):
    _, per_ff, unit, dim = ffn.shape
    per = 1 + per_ff

    def kernel(at_ref, table_ref, ffn_ref, *refs):
        terms, outs, all_ref = refs[: len(heads)], refs[len(heads) : -1], refs[-1]
        total = terms[0][0]
        for ref in terms[1:]:
            total = total + ref[0].astype(F32)
        all_ref[0] = total.astype(all_ref.dtype)
        for k in range(per_ff):
            all_ref[k + 1] = ffn_ref[1, k].astype(all_ref.dtype)
        for k in range(per):
            outs[k][...] = all_ref[table_ref[at_ref[0], per + k]]
        for s in range(SLOTS):
            outs[per + s][...] = ffn_ref[0, at_ref[1] ^ s]

    return pl.pallas_call(
        kernel,
        out_shape=[jax.ShapeDtypeStruct((unit, dim), F32)] * per + [jax.ShapeDtypeStruct((unit, dim), BF)] * SLOTS,
        in_specs=[SMEM] * 2 + [VMEM] * (1 + len(heads)),
        out_specs=[VMEM] * (per + SLOTS),
        scratch_shapes=[pltpu.VMEM((per, unit, dim), F32)],
        cost_estimate=SMALL,
        name="leave",
    )(at, table, ffn, *heads)


def place(at, table, qkv, up, got):
    count, high, width = qkv.shape
    unit, dim = got[0].shape
    nt = len(up)
    nb = count // nt
    per = len(got)
    local = width // 3
    wide = nt * (width + dim)

    def kernel(at_ref, table_ref, qkv_ref, *refs):
        up_refs, got_refs, (in_ref, out_ref, norm_ref, q_ref, k_ref) = refs[:nt], refs[nt : nt + per], refs[nt + per :]
        for s, ref in enumerate(up_refs):
            to = pl.multiple_of(nt * width + (at_ref[1] ^ s) * dim, 128)
            in_ref[:, pl.ds(to, dim)] = ref[...].astype(F32)
        for t in range(nt):
            total = add_blocks(qkv_ref, nb, nt, t, slice(0, unit))
            for k in range(3):
                in_ref[:, k * nt * local + t * local : k * nt * local + (t + 1) * local] = total[:, k * local : (k + 1) * local]
        for k, ref in enumerate(got_refs):
            out_ref[table_ref[at_ref[0], k]] = ref[...]
        small = add_blocks(qkv_ref, count, 1, 0, slice(unit, high))
        small = small[0:2] + small[2:4]
        norm_ref[:, :width] = small[0:1]
        norm_ref[:, width:] = small[1:2, : dim - width]
        q_ref[...] = small[1:2, dim - width : dim - width + HD]
        k_ref[...] = small[1:2, dim - width + HD : dim - width + 2 * HD]

    return pl.pallas_call(
        kernel,
        out_shape=[
            jax.ShapeDtypeStruct((unit, wide), F32),
            jax.ShapeDtypeStruct((per, unit, dim), F32),
            jax.ShapeDtypeStruct((1, dim), F32),
            jax.ShapeDtypeStruct((1, HD), F32),
            jax.ShapeDtypeStruct((1, HD), F32),
        ],
        in_specs=[SMEM] * 2 + [VMEM] * (1 + nt + per),
        out_specs=[VMEM] * 5,
        cost_estimate=SMALL,
        compiler_params=pltpu.CompilerParams(vmem_limit_bytes=32 * MIB),
        name="place",
    )(at, table, qkv, *up, *got)


def after(start, ids, x, cot, gain, keep, near, far, earlier):
    seqs, part, dim = x.shape
    count = far.shape[0]

    def kernel(ids_ref, x_ref, cot_ref, gain_ref, keep_ref, near_ref, far_ref, *rest):
        out_ref, grad_ref = rest[-2:]
        unit, inverse = normalize(x_ref[0].astype(F32))
        live = column(jnp.where(ids_ref[0] >= 0, 1.0, 0.0))
        branch, gn = (keep_ref[0, 0, j].astype(F32) + near_ref[0, 0, j].astype(F32) + far_ref[0, j].astype(F32) for j in range(2))
        out_ref[0] = (live * (x_ref[0].astype(F32) + branch)).astype(BF)
        grad_ref[0] = (live * cot_ref[0].astype(F32) + norm_back(gn * as_row(gain_ref), unit, inverse)).astype(BF)

    one = pl.BlockSpec((1, part, dim), lambda g: (start + g, 0, 0))
    pair = pl.BlockSpec((1, 1, 2, part, dim), lambda g: (0, g, 0, 0, 0))
    lone = pl.BlockSpec((1, 2, part, dim), lambda g: (g, 0, 0, 0))
    return pl.pallas_call(
        kernel,
        grid=(count,),
        out_shape=[jax.ShapeDtypeStruct(x.shape, BF)] * 2,
        in_specs=[
            pl.BlockSpec((1, 1, part), lambda g: (start + g, 0, 0)), one, one,
            pl.BlockSpec(gain.shape, lambda g: (0,)), pair, pair, lone,
        ]
        + [ANY] * len(earlier),
        out_specs=[one, one],
        input_output_aliases={7 + i: i for i in range(len(earlier))},
        cost_estimate=SMALL,
        compiler_params=pltpu.CompilerParams(vmem_limit_bytes=32 * MIB),
        name="after",
    )(ids.reshape(seqs, 1, part), *hbm(x, cot), gain, *hbm(keep, near, far), *earlier)


def attention_kernel(
    heads, block, last, start,
    at_ref, ids_ref, qg_ref, kg_ref, wqkv_hbm, wo_hbm, *refs,
):
    pays, refs = refs[0], refs[1:]
    if last:
        (acc_sums_ref, fnp_ref, gain_ref, accq_hbm, acco_hbm, hid_hbm, gup_hbm, wff_hbm, wup_hbm), refs = refs[:9], refs[9:]
        (keep_hbm, leave_hbm, sendq_ref, sendo_ref, keepo_ref, sums_ref), refs = refs[:6], refs[6:]
        (hid_ref, gup_ref, wff_ref, wup_ref, res_ref, res_sem, act_sem), refs = refs[:7], refs[7:]
    else:
        (o_hbm, grad_hbm, sums_ref, newq_hbm, newo_hbm), refs = refs[:5], refs[5:]
    (
        wqkv_ref, wo_ref, norm_ref, gb_ref, o_ref, grad_ref, gq_ref, go_ref, raw_ref,
        qt_ref, qn_ref, kt_ref, ka_ref, vt_ref, va_ref, do_ref, dq_ref, dk_ref, dv_ref, pad_ref, vm_ref,
        w_sem, sem, out_sem,
    ) = refs
    seqs, length, dim = norm_ref.shape
    part = length // SLOTS
    width = heads * HD
    blocks = length // block
    loads = [pltpu.make_async_copy(wqkv_hbm, wqkv_ref, w_sem.at[0]), pltpu.make_async_copy(wo_hbm, wo_ref, w_sem.at[1])]
    loads[0].start()

    def pay_copy(s, j, t):
        to = (norm_ref, gb_ref)[j].at[s, pl.ds(t * part, part), :]
        return pltpu.make_async_copy(pays.at[t, s, j], to, sem.at[s, j * SLOTS + t])

    for s in range(seqs):
        for j in range(2):
            for t in range(SLOTS):
                pay_copy(s, j, t).start()
            if s + j == 0:
                loads[1].start()
    if last:
        loads.append(pltpu.make_async_copy(accq_hbm, gq_ref, w_sem.at[2]))
        loads.append(pltpu.make_async_copy(acco_hbm, go_ref, w_sem.at[3]))
        loads.append(pltpu.make_async_copy(wff_hbm, wff_ref, act_sem.at[2 * seqs]))
        loads.append(pltpu.make_async_copy(wup_hbm, wup_ref, act_sem.at[2 * seqs + 1]))
        for copy in loads[2:]:
            copy.start()
        skip = hid_hbm.shape[0] // length - seqs

        def act_copies(s):
            rows = pl.ds(pl.multiple_of((skip + s) * length, length), length)
            return [
                pltpu.make_async_copy(hid_hbm.at[rows, :], hid_ref.at[s], act_sem.at[2 * s]),
                pltpu.make_async_copy(gup_hbm.at[rows, :], gup_ref.at[s], act_sem.at[2 * s + 1]),
            ]

        for s in range(seqs):
            for copy in act_copies(s):
                copy.start()
        outs = Outputs(at_ref[1], keep_hbm, leave_hbm, res_ref, res_sem, wo_ref, wff_ref, wqkv_ref, wup_ref)
        sums_ref[...] = acc_sums_ref[...]
    else:
        gq_ref[...] = jnp.zeros_like(gq_ref)
        go_ref[...] = jnp.zeros_like(go_ref)
        sums_ref[...] = jnp.zeros_like(sums_ref)
    gain_q = column(as_row(qg_ref))
    gain_k = column(as_row(kg_ref))
    marks = lax.broadcasted_iota(jnp.int32, (HD, length), 0)
    v_tail = jnp.where(lax.broadcasted_iota(jnp.int32, (length, HD), 1) < 2, 1.0, 0.0).astype(BF)
    ones = jnp.where(lax.broadcasted_iota(jnp.int32, (16, length), 0) == 0, 1.0, 0.0).astype(BF)
    spot = lax.broadcasted_iota(jnp.int32, (HD, block), 0)
    scale = 1.0 / math.sqrt(HD)
    cut = lambda a, i: a[:, i * block : (i + 1) * block]

    def unit_of(row):
        raw = raw_ref[pl.ds(pl.multiple_of(row, HD), HD), :]
        center = raw - jnp.mean(raw, axis=0, keepdims=True)
        inverse = lax.rsqrt(jnp.mean(center * center, axis=0, keepdims=True) + EPS)
        return center * inverse, inverse

    def lanes(a):
        total = a[:, :128]
        for i in range(1, length // 128):
            total = total + a[:, i * 128 : (i + 1) * 128]
        return total

    def stores(s):
        return [
            pltpu.make_async_copy(o_ref.at[s], o_hbm.at[s], out_sem.at[s, 0]),
            pltpu.make_async_copy(grad_ref.at[s], grad_hbm.at[s], out_sem.at[s, 1]),
        ]

    loads[0].wait()
    loads[1].wait()

    def sequence(s, carry):
        ids = ids_ref[start + s]
        same = marks == ids + 1
        k_tail = jnp.where(same, 1.0, 0.0).T.astype(BF)
        q_tail = jnp.where((same & (ids >= 0)) | (marks > 4), 0.0, -BIG).astype(BF)
        pad = jnp.where(ids < 0, 1.0, 0.0)
        for i in range(blocks):
            pad_ref[i] = cut(pad, i)
        for t in range(SLOTS):
            pay_copy(s, 0, t).wait()
        raw_ref[...] = mm(wqkv_ref[...], norm_ref[s], NT)
        for t in range(SLOTS):
            pay_copy(s, 1, t).wait()
        do_all = mm(wo_ref[...], gb_ref[s], NT).astype(BF)
        for h in range(heads):
            for i in range(blocks):
                do_ref[h * blocks + i] = cut(do_all[h * HD : (h + 1) * HD], i)

        def prepare(h, carry):
            q_unit, _ = unit_of(h * HD)
            q = q_unit * gain_q
            qn = q.T.astype(BF)
            for i in range(blocks):
                qt_ref[h * blocks + i, :HD] = cut(q, i).astype(BF)
                qt_ref[h * blocks + i, HD:] = cut(q_tail, i)
                qn_ref[h * blocks + i] = qn[i * block : (i + 1) * block]
            k_unit, _ = unit_of(width + h * HD)
            k = k_unit * gain_k
            kt_ref[h] = k.astype(BF)
            ka_ref[h, :, :HD] = k.T.astype(BF)
            ka_ref[h, :, HD:] = k_tail
            v = raw_ref[pl.ds(pl.multiple_of(2 * width + h * HD, HD), HD), :]
            vb = v.astype(BF)
            vt_ref[h, :HD] = vb
            vt_ref[h, HD:] = ones
            va_ref[h, :, :HD] = v.T.astype(BF)
            va_ref[h, :, HD:] = v_tail
            vm_ref[h] = jnp.mean(vb.astype(F32), axis=1, keepdims=True)
            dk_ref[h] = jnp.zeros(dk_ref.shape[1:], F32)
            dv_ref[h] = jnp.zeros(dv_ref.shape[1:], F32)
            return carry

        lax.fori_loop(0, heads, prepare, 0)

        def step(n, carry):
            h = n // blocks
            padb = pad_ref[n % blocks]
            e = jnp.exp2(mm(ka_ref[h], qt_ref[n]) * (LOG2E * scale))
            eb = e.astype(BF)
            oa = mm(vt_ref[h], eb)
            inv = 1.0 / (oa[HD : HD + 1] + padb)
            o = oa[:HD] * inv
            dos = (do_ref[n].astype(F32) * inv).astype(BF)
            delta = jnp.sum(dos.astype(F32) * o, axis=0, keepdims=True)
            d0 = delta.astype(BF).astype(F32)
            tail = jnp.where(spot == 0, -d0, jnp.where(spot == 1, d0 - delta, 0.0))
            doa = jnp.concatenate([dos.astype(F32), tail], axis=0)
            ds = (e * mm(va_ref[h], doa.astype(BF))).astype(BF)
            dq_ref[n] = mm(kt_ref[h], ds)
            dk_ref[h] += mm(ds, qn_ref[n])
            dv_ref[h] += mm(eb, doa.T.astype(BF))
            do_ref[n] = jnp.where(padb > 0, vm_ref[h], o).astype(BF)
            return carry

        lax.fori_loop(0, heads * blocks, step, 0)

        def finish(h, carry):
            rows = lambda at: pl.ds(pl.multiple_of(at + h * HD, HD), HD)
            gq = jnp.concatenate([dq_ref[h * blocks + i] for i in range(blocks)], axis=1)
            gk = dk_ref[h].T
            for k, (g, gain_col) in enumerate(((gq, gain_q), (gk, gain_k))):
                unit, inverse = unit_of(k * width + h * HD)
                g = (g * scale).astype(BF).astype(F32)
                sums_ref[k] += lanes(g * unit)
                g = g * gain_col
                back = inverse * (
                    g - jnp.mean(g, axis=0, keepdims=True) - unit * jnp.mean(g * unit, axis=0, keepdims=True)
                )
                grad_ref[s, rows(k * width), :] = back.astype(BF)
            grad_ref[s, rows(2 * width), :] = dv_ref[h].T[:HD].astype(BF)
            for i in range(blocks):
                o_ref[s, rows(0), pl.ds(i * block, block)] = do_ref[h * blocks + i]
            return carry

        lax.fori_loop(0, heads, finish, 0)
        if last:

            @pl.when(s == 0)
            def _():
                for copy in loads[2:]:
                    copy.wait()

            for copy in act_copies(s):
                copy.wait()
            outs.compute(s, o_ref.at[s], hid_ref.at[s], grad_ref.at[s], gup_ref.at[s])
        else:
            for copy in stores(s):
                copy.start()
        gq_ref[...] += mm(grad_ref[s], norm_ref[s])
        go_ref[...] += mm(o_ref[s], gb_ref[s])
        return carry

    lax.fori_loop(0, seqs, sequence, 0)
    if not last:
        ends = [pltpu.make_async_copy(gq_ref, newq_hbm, w_sem.at[2]), pltpu.make_async_copy(go_ref, newo_hbm, w_sem.at[3])]
        for copy in ends:
            copy.start()
        for copy in ends:
            copy.wait()
        for s in range(seqs):
            for copy in stores(s):
                copy.wait()
        return
    outs.wait()
    g_q = gq_ref[...]
    first_row = (jnp.sum(wqkv_ref[...].astype(F32) * g_q, axis=0, keepdims=True) + fnp_ref[...]) / as_row(gain_ref)
    second_row = jnp.concatenate([jnp.sum(sums_ref[k].T, axis=0, keepdims=True) for k in range(2)], axis=1)
    wide = 3 * width
    line = jnp.concatenate([first_row[:, wide:], second_row, jnp.zeros((1, 2 * wide - dim - 2 * HD), F32)], axis=1)
    small = jnp.concatenate([first_row[:, :wide], line], axis=0)
    high = small.astype(BF)
    small = jnp.concatenate([high.astype(F32), small - high.astype(F32)], axis=0).astype(BF)
    g_q = g_q.T.astype(BF)
    count, rows, _ = sendq_ref.shape
    rows = rows - 4
    for i in range(count):
        sendq_ref[i, :rows] = g_q[i * rows : (i + 1) * rows]
        sendq_ref[i, rows:] = small
    split_rows((at_ref[2] & 1) > 0, go_ref[...], sendo_ref, keepo_ref)


def attention(at, start, ids, wqkv, wo, qg, kg, pays, count, more=()):
    wide, dim = wqkv.shape
    width = wo.shape[0]
    heads = width // HD
    _, seqs, _, part, _ = pays.shape
    length = part * SLOTS
    block = 512
    blocks = length // block
    last = bool(more)
    ins = [at, ids, qg, kg, *hbm(wqkv, wo, pays), *more[:3], *hbm(*more[3:])]
    specs = [SMEM] + [VMEM] * 3 + [HBM] * 3 + ([VMEM] * 3 + [HBM] * 6 if last else [])
    scratch = []
    if last:
        outs = [jax.ShapeDtypeStruct((SLOTS // 2, seqs, 2, part, dim), BF)] * 2
        outs += [jax.ShapeDtypeStruct((count, dim // count + 4, wide), BF)]
        outs += [jax.ShapeDtypeStruct((count // (2 * SLOTS), SLOTS * width // count, dim), t) for t in (BF, F32)]
        scratch = [pltpu.VMEM((2, HD, 128), F32)]
        scratch += [pltpu.VMEM((seqs, length, dim), BF)] * 2 + [pltpu.VMEM((dim, dim), BF)] * 2
        scratch += Outputs.scratch(seqs, length, dim) + [pltpu.SemaphoreType.DMA((2 * seqs + 2,))]
    else:
        outs = [jax.ShapeDtypeStruct((seqs, width, length), BF), jax.ShapeDtypeStruct((seqs, wide, length), BF)]
        outs += [
            jax.ShapeDtypeStruct((2, HD, 128), F32),
            jax.ShapeDtypeStruct((wide, dim), F32),
            jax.ShapeDtypeStruct((width, dim), F32),
        ]
    flops = seqs * (2 * length * dim * width * 8 + heads * 6 * 2 * length * length * HD)
    return pl.pallas_call(
        functools.partial(attention_kernel, heads, block, last, start),
        out_shape=outs,
        in_specs=specs,
        out_specs=[HBM] * 2 + ([VMEM] * 3 if last else [VMEM, HBM, HBM]),
        scratch_shapes=scratch
        + [
            pltpu.VMEM((wide, dim), BF),
            pltpu.VMEM((width, dim), BF),
            pltpu.VMEM((seqs, length, dim), BF),
            pltpu.VMEM((seqs, length, dim), BF),
            pltpu.VMEM((seqs, width, length), BF),
            pltpu.VMEM((seqs, wide, length), BF),
            pltpu.VMEM((wide, dim), F32),
            pltpu.VMEM((width, dim), F32),
            pltpu.VMEM((wide, length), F32),
            pltpu.VMEM((heads * blocks, 2 * HD, block), BF),
            pltpu.VMEM((heads * blocks, block, HD), BF),
            pltpu.VMEM((heads, HD, length), BF),
            pltpu.VMEM((heads, length, 2 * HD), BF),
            pltpu.VMEM((heads, HD + 16, length), BF),
            pltpu.VMEM((heads, length, 2 * HD), BF),
            pltpu.VMEM((heads * blocks, HD, block), BF),
            pltpu.VMEM((heads * blocks, HD, block), F32),
            pltpu.VMEM((heads, length, HD), F32),
            pltpu.VMEM((heads, length, 2 * HD), F32),
            pltpu.VMEM((blocks, 1, block), F32),
            pltpu.VMEM((heads, HD, 1), F32),
            pltpu.SemaphoreType.DMA((4,)),
            pltpu.SemaphoreType.DMA((seqs, 2 * SLOTS)),
            pltpu.SemaphoreType.DMA((seqs, 2)),
        ],
        cost_estimate=LARGE,
        compiler_params=pltpu.CompilerParams(vmem_limit_bytes=56 * MIB),
        name="attention",
    )(*ins)


def ffn_kernel(block, groups, plan, at_ref, wup_hbm, wqkv_hbm, wo_hbm, o_hbm, gq_hbm, *refs):
    pieces, refs = refs[: len(plan)], refs[len(plan) :]
    pays, refs = refs[: len(groups)], refs[len(groups) :]
    (hid_hbm, gup_hbm, wff_hbm, keep_hbm, leave_hbm, send_ref, np_ref), refs = refs[:7], refs[7:]
    norm_ref, gb_ref, hid_ref, gup_ref, wup_ref, wff_ref, gin_ref, gff_ref, sem, out_sem, w_sem, *refs = refs
    wqkv_ref, wo_ref, o_ref, gq_ref, res_ref, res_sem, late_sem = refs
    dim = wup_ref.shape[0]
    part = pays[0].shape[3]
    total = norm_ref.shape[0]
    weights = [pltpu.make_async_copy(wup_hbm, wup_ref, w_sem.at[0])]
    rows = send_ref.shape[2]
    for ref, masks in zip(pieces, plan):
        for i, mask in enumerate(masks):
            to = wff_ref.at[pl.ds(pl.multiple_of((at_ref[2] ^ mask) * rows, rows), rows), :]
            weights.append(pltpu.make_async_copy(ref.at[i], to, w_sem.at[len(weights)]))
    for copy in weights:
        copy.start()
    n = 0
    for g, seqs in enumerate(groups):
        for s in range(seqs):
            for t in range(SLOTS):
                for k, to in enumerate((norm_ref, gb_ref)):
                    source = pays[g].at[t, s, k]
                    pltpu.make_async_copy(source, to.at[pl.ds(n * part, part), :], sem.at[k, n]).start()
                n += 1
    late = [
        pltpu.make_async_copy(a, b, late_sem.at[i])
        for i, (a, b) in enumerate(((wqkv_hbm, wqkv_ref), (wo_hbm, wo_ref), (o_hbm, o_ref), (gq_hbm, gq_ref)))
    ]
    for copy in late:
        copy.start()
    gin_ref[...] = jnp.zeros_like(gin_ref)
    gff_ref[...] = jnp.zeros_like(gff_ref)
    for copy in weights:
        copy.wait()
    joined = pltpu.make_async_copy(wff_ref, wff_hbm, w_sem.at[0])
    joined.start()
    c0 = math.sqrt(2.0 / math.pi)
    c1 = 0.044715

    def outs(i):
        at_rows = pl.ds(pl.multiple_of(i * block, block), block)
        return (
            pltpu.make_async_copy(hid_ref.at[at_rows, :], hid_hbm.at[at_rows, :], out_sem.at[0, i]),
            pltpu.make_async_copy(gup_ref.at[at_rows, :], gup_hbm.at[at_rows, :], out_sem.at[1, i]),
        )

    def step(i, carry):
        for j in range(block // part):
            for k, to in enumerate((norm_ref, gb_ref)):
                pltpu.make_async_copy(pays[0].at[0, 0, 0], to.at[pl.ds(0, part), :], sem.at[k, i * (block // part) + j]).wait()
        at_rows = pl.ds(pl.multiple_of(i * block, block), block)
        up = mm(norm_ref[at_rows, :], wup_ref[...])
        gh = mm(gb_ref[at_rows, :], wff_ref[...], NT)
        sq = up * up
        t = jnp.tanh(up * (c0 + (c0 * c1) * sq))
        half = 0.5 + 0.5 * t
        hid_ref[at_rows, :] = (up * half).astype(BF)
        gup_ref[at_rows, :] = (gh * (half + (0.5 * up) * (1.0 - t * t) * (c0 + (3.0 * c0 * c1) * sq))).astype(BF)
        for copy in outs(i):
            copy.start()
        gin_ref[...] += mm(norm_ref[at_rows, :], gup_ref[at_rows, :], TN)
        gff_ref[...] += mm(hid_ref[at_rows, :], gb_ref[at_rows, :], TN)
        return carry

    lax.fori_loop(0, total // block, step, 0)
    for copy in late:
        copy.wait()
    results = Outputs(at_ref[1], keep_hbm, leave_hbm, res_ref, res_sem, wo_ref, wff_ref, wqkv_ref, wup_ref)
    length = SLOTS * part
    for s in range(results.seqs):
        rows_s = pl.ds(s * length, length)
        results.compute(s, o_ref.at[s], hid_ref.at[rows_s, :], gq_ref.at[s], gup_ref.at[rows_s, :])
    line = jnp.sum(wup_ref[...].astype(F32) * gin_ref[...], axis=1, keepdims=True)
    np_ref[...] = jnp.broadcast_to(line, (dim, 128)).T[0:1]
    for b in range(dim // rows):
        for k, g in enumerate((gin_ref, gff_ref)):
            send_ref[b, k] = g[b * rows : (b + 1) * rows, :].astype(BF)
    joined.wait()
    results.wait()

    def drain(i, carry):
        for copy in outs(i):
            copy.wait()
        return carry

    lax.fori_loop(0, total // block, drain, 0)


def ffn(at, wup, ff_parts, groups, count, wqkv, wo, o, gq, block=512):
    dim, units = wup.shape
    sizes = [g.shape[1] for g in groups]
    part = groups[0].shape[3]
    total = SLOTS * part * sum(sizes)
    pieces = groups
    act = jax.ShapeDtypeStruct((total, units), BF)
    return pl.pallas_call(
        functools.partial(ffn_kernel, block, sizes, [masks for _, masks in ff_parts]),
        out_shape=[
            act,
            act,
            jax.ShapeDtypeStruct((units, dim), BF),
            *[jax.ShapeDtypeStruct((SLOTS // 2, o.shape[0], 2, part, dim), BF)] * 2,
            jax.ShapeDtypeStruct((count, 2, units // count, dim), BF),
            jax.ShapeDtypeStruct((1, dim), F32),
        ],
        in_specs=[SMEM] + [HBM] * (5 + len(ff_parts) + len(pieces)),
        out_specs=[HBM] * 5 + [VMEM] * 2,
        scratch_shapes=[
            pltpu.VMEM((total, dim), BF),
            pltpu.VMEM((total, dim), BF),
            pltpu.VMEM((total, units), BF),
            pltpu.VMEM((total, units), BF),
            pltpu.VMEM((dim, units), BF),
            pltpu.VMEM((units, dim), BF),
            pltpu.VMEM((dim, units), F32),
            pltpu.VMEM((units, dim), F32),
            pltpu.SemaphoreType.DMA((2, total // part)),
            pltpu.SemaphoreType.DMA((2, total // block)),
            pltpu.SemaphoreType.DMA((1 + count,)),
            *[pltpu.VMEM(a.shape, BF) for a in (wqkv, wo, o, gq)],
            *Outputs.scratch(o.shape[0], SLOTS * part, dim),
            pltpu.SemaphoreType.DMA((4,)),
        ],
        cost_estimate=LARGE,
        compiler_params=pltpu.CompilerParams(vmem_limit_bytes=58 * MIB),
        name="ffn",
    )(at, *hbm(wup, wqkv, wo, o, gq, *[a for a, _ in ff_parts], *pieces))


class Outputs:
    def __init__(self, me, keep, send, res, sem, wo, wff, wqkv, wup):
        self.me = me
        self.keep, self.send, self.res, self.sem = keep, send, res, sem
        self.wo, self.wff, self.wqkv, self.wup = wo, wff, wqkv, wup
        self.seqs, _, self.length, _ = res.shape

    @staticmethod
    def scratch(seqs, length, dim):
        return [pltpu.VMEM((seqs, 2, length, dim), BF), pltpu.SemaphoreType.DMA((seqs, 2, SLOTS))]

    def moves(self, s, i):
        half = self.length // 2
        part = half // 2
        out = []
        for j in range(2):
            for k, to in enumerate((self.keep, self.send)):
                rows = pl.ds(pl.multiple_of(i * half + (k ^ (self.me & 1)) * part, part), part)
                source = self.res.at[s, j, rows, :]
                out.append(pltpu.make_async_copy(source, to.at[i ^ (self.me >> 1), s, j], self.sem.at[s, j, 2 * i + k]))
        return out

    def compute(self, s, o, hid, gq, gu):
        half = self.length // 2

        def step(i, carry):
            rows = pl.ds(pl.multiple_of(i * half, half), half)
            branch = mm(o[:, rows], self.wo[...], TN) + mm(hid[rows, :], self.wff[...])
            self.res[s, 0, rows, :] = branch.astype(BF)
            gn = mm(gq[:, rows], self.wqkv[...], TN) + mm(gu[rows, :], self.wup[...], NT)
            self.res[s, 1, rows, :] = gn.astype(BF)
            for copy in self.moves(s, i):
                copy.start()
            return carry

        lax.fori_loop(0, 2, step, 0)

    def wait(self):
        for s in range(self.seqs):
            for i in range(2):
                for copy in self.moves(s, i):
                    copy.wait()


def swap(value, axis, count, mask):
    return lax.ppermute(value, axis, [(i, i ^ mask) for i in range(count)])


def tie(value, *after):
    return lax.optimization_barrier((value,) + after)[0]


def bit_groups(count):
    bits = list(range(count.bit_length() - 1))[::-1]
    groups = []
    while bits:
        take = 2 if len(bits) > 1 else 1
        groups.append(bits[:take])
        bits = bits[take:]
    assert len(groups[-1]) == 1
    return groups


def gather_batch(block, count, groups, hold=None):
    held, masks = block[None], [0]
    for bits in groups:
        low = bits[-1]
        if hold is not None and bits is groups[-1]:
            held = tie(held, hold)
        parts = [(held, masks)]
        for s in range(1, 1 << len(bits)):
            parts.append((swap(held, "batch", count, s << low), [m ^ (s << low) for m in masks]))
        held = jnp.concatenate([a for a, _ in parts], axis=0)
        masks = sum((m for _, m in parts), [])
    return parts


def matchings(edges, devices, per_device):
    left = [[] for _ in range(devices)]
    for e, (source, _, _) in enumerate(edges):
        left[source].append(e)
    rounds = []
    for _ in range(per_device):
        owner = [-1] * devices

        def place(source, seen):
            for e in left[source]:
                target = edges[e][1]
                if target in seen:
                    continue
                seen.add(target)
                if owner[target] < 0 or place(edges[owner[target]][0], seen):
                    owner[target] = e
                    return True
            return False

        for source in range(devices):
            place(source, set())
        rounds.append(list(owner))
        for e in owner:
            left[edges[e][0]].remove(e)
    return rounds


def unit_plan(nb, nt, rows, width, hidden):
    unit = math.gcd(math.gcd(rows, width // nt), hidden // nt)
    per = rows // unit
    head_units, hid_units = width // nt // unit, hidden // nt // unit
    assert head_units == nb and hid_units % nb == 0
    c = hid_units // nb
    edges = []
    for t in range(nt):
        for b in range(nb):
            want = [t * head_units + b]
            want += [nt * head_units + t * hid_units + b * c + i for i in range(c)]
            for slot, u in enumerate(want):
                edges.append((u // per, b * nt + t, (u % per, slot)))
    table = np.zeros((nb * nt, 2 * per), np.int32)
    perms = []
    for k, owner in enumerate(matchings(edges, nb * nt, per)):
        perms.append([(edges[e][0], edges[e][1]) for e in owner])
        for e in owner:
            table[edges[e][0], k] = edges[e][2][0]
            table[edges[e][1], per + k] = edges[e][2][1]
    return unit, per, perms, table


def per_device(
    nb, nt, patches, image_ids, cotangent, norm_gain, query_gain, key_gain, in_weight, out_weight
):
    seqs, part, dim = patches.shape
    width = H * HD
    local = width // nt
    units = (in_weight.shape[1] - 3 * width) // nt
    rows_in = in_weight.shape[0]
    unit, per, perms, table = unit_plan(nb, nt, out_weight.shape[0], width, units * nt)
    assert nt == SLOTS and units == dim and unit == rows_in and dim == nt * local and per == nt + 1
    both = ("batch", "tok")
    me_b = lax.axis_index("batch")
    me_t = lax.axis_index("tok")
    at = jnp.stack([me_b * nt + me_t, me_t, me_b])
    table = jnp.asarray(table)
    gain = norm_gain

    def exchange(value, axis):
        return lax.all_to_all(value, axis, split_axis=0, concat_axis=0, tiled=True)

    groups = bit_groups(nb)

    lead = 2
    a_src, u_src = prepare(image_ids, in_weight, nb, nt)
    a_got = exchange(a_src.reshape(nb * nt, rows_in + 2, 3 * local), both)
    own0, own1, *unit_sends = before(
        at, table, out_weight.reshape(per, unit, dim), image_ids, gain, tie(patches, a_src), cotangent, lead
    )
    got = [lax.ppermute(v, both, perm) for v, perm in zip(unit_sends, perms)]
    wo_src, ff_src = pack_out(at, table, got)
    slots0 = lax.all_gather(own0, "tok", axis=0)
    slots1 = lax.all_gather(own1, "tok", axis=0)
    wo_parts = gather_batch(wo_src, nb, groups, a_got)
    ff_parts = gather_batch(ff_src.reshape((per - 1) * unit, dim), nb, groups[::-1])
    wqkv, wo, ids = join(at, a_got, wo_parts, seqs, part)
    wo = wo.reshape(local, dim)
    wup = exchange(tie(u_src, a_got).reshape(nb * nt, unit, dim), both).reshape(dim, units)

    qg, kg = query_gain, key_gain

    def leave_chip(keep, near, *hold):
        value = (keep[1].astype(F32) + near[1].astype(F32)).astype(BF)
        return value, swap(tie(value, *hold) if hold else value, "tok", nt, 2)

    o0, gq0, sums, acc_q, acc_o = attention(at, 0, ids, wqkv, tie(wo, ff_parts[0][0]), qg, kg, slots0, nb * nt)
    hid, gup, wff, keep0, send0, f_grad, f_np = ffn(
        at, tie(wup, o0), ff_parts, [slots0, slots1], nb, wqkv, wo, o0, gq0
    )
    f_mine = lax.psum_scatter(f_grad, "batch", scatter_dimension=0, tiled=True).reshape(2, nt, unit, dim)
    near0 = swap(send0, "tok", nt, 1)
    value0, away0 = leave_chip(keep0, near0)
    keep1, send1, a_q, a_send, a_keep = attention(
        at, lead, ids, wqkv, tie(wo, value0), qg, kg, slots1, nb * nt,
        (sums, f_np, gain, acc_q, acc_o, hid, gup, wff, wup),
    )
    a_came = swap(a_send, "batch", nb, 1)
    terms = [a_keep, a_came]
    for bits in groups[:-1][::-1]:
        own, *sends = fold(at, bits[-1], [terms])
        terms = [own] + [swap(value, "batch", nb, (s + 1) << bits[-1]) for s, value in enumerate(sends)]
    near1 = swap(tie(send1, away0, *terms[1:]), "tok", nt, 1)
    a_q = exchange(a_q, both)
    value1, away1 = leave_chip(keep1, near1)
    earlier = after(0, image_ids, patches, cotangent, gain, keep0, near0, away0, [])
    outs = leave(at, table, terms, tie(f_mine, *earlier))
    sends, up = outs[:per], outs[per:]
    up = [up[0]] + [swap(up[s], "tok", nt, s) for s in range(1, nt)]
    got = [lax.ppermute(v, both, [(b, a) for a, b in perm]) for v, perm in zip(sends, perms)]
    in_grad, out_grad, norm_grad, query_grad, key_grad = place(at, table, a_q, up, got)

    earlier = after(lead, image_ids, patches, cotangent, gain, keep1, near1, away1, earlier)
    block_out, patch_grad = earlier
    return (
        block_out,
        patch_grad,
        norm_grad.reshape(dim),
        query_grad.reshape(HD),
        key_grad.reshape(HD),
        in_grad,
        out_grad.reshape(per * unit, dim),
    )


def solution(mesh):
    rows = P("batch", "tok", None)
    weights = P(("batch", "tok"), None)
    return jax.shard_map(
        functools.partial(per_device, mesh.shape["batch"], mesh.shape["tok"]),
        mesh=mesh,
        in_specs=(rows, P("batch", "tok"), rows, P(), P(), P(), weights, weights),
        out_specs=(rows, rows, P(), P(), P(), weights, weights),
        check_vma=False,
    )
```

```python
import functools
import math

import jax
import jax.numpy as jnp
import numpy as np
from jax import lax
from jax.experimental import pallas as pl
from jax.experimental.pallas import tpu as pltpu
from jax.sharding import PartitionSpec as P

H = 12
HD = 64
SLOTS = 4
EPS = 1e-06
BIG = 2048.0
LOG2E = 1.4426950408889634
BF = jnp.bfloat16
F32 = jnp.float32
NN = (((1,), (0,)), ((), ()))
NT = (((1,), (1,)), ((), ()))
TN = (((0,), (0,)), ((), ()))
MIB = 1 << 20
SMALL = pl.CostEstimate(flops=1, transcendentals=0, bytes_accessed=1)
LARGE = pl.CostEstimate(flops=60_000_000_000, transcendentals=0, bytes_accessed=1)

VMEM = pl.BlockSpec(memory_space=pltpu.VMEM)
SMEM = pl.BlockSpec(memory_space=pltpu.SMEM)
ANY = pl.BlockSpec(memory_space=pl.ANY)
HBM = pl.BlockSpec(memory_space=pltpu.HBM)


def hbm(*arrays):
    return [pltpu.with_memory_space_constraint(a, pltpu.HBM) for a in arrays]


def mm(a, b, dims=NN):
    return lax.dot_general(a, b, dims, preferred_element_type=F32)


def normalize(values):
    center = values - jnp.mean(values, axis=-1, keepdims=True)
    inverse = lax.rsqrt(jnp.mean(center * center, axis=-1, keepdims=True) + EPS)
    return center * inverse, inverse


def norm_back(grad_unit, unit_rows, inverse):
    return inverse * (
        grad_unit
        - jnp.mean(grad_unit, axis=-1, keepdims=True)
        - unit_rows * jnp.mean(grad_unit * unit_rows, axis=-1, keepdims=True)
    )


def as_row(ref):
    return ref[...].reshape(1, ref.shape[0])


def column(row):
    return jnp.broadcast_to(row, (8, row.shape[1])).T[:, 0:1]


def prepare(ids, w_in, nb, nt):
    rows, wide = w_in.shape
    seqs, part = ids.shape
    width = H * HD
    local = width // nt
    units = (wide - 3 * width) // nt

    def kernel(ids_hbm, win_hbm, a_hbm, u_hbm, ids_ref, win_ref, a_ref, u_ref, in_sem, a_sem, u_sem):
        loads = [pltpu.make_async_copy(win_hbm, win_ref, in_sem.at[0]), pltpu.make_async_copy(ids_hbm, ids_ref, in_sem.at[1])]
        for copy in loads:
            copy.start()
        for copy in loads:
            copy.wait()
        row = jnp.concatenate([ids_ref[s : s + 1, :] for s in range(seqs)], axis=1).astype(F32).astype(BF)
        first = 3 * local
        second = jnp.concatenate([row[:, first:].astype(F32), jnp.zeros((1, 2 * first - seqs * part), F32)], axis=1).astype(BF)
        for t in range(nt):
            for k in range(3):
                a_ref[t, :rows, k * local : (k + 1) * local] = win_ref[:, k * width + t * local : k * width + (t + 1) * local]
            a_ref[t, rows : rows + 1] = row[:, :first]
            a_ref[t, rows + 1 :] = second
        for b in range(nb):
            pltpu.make_async_copy(a_ref, a_hbm.at[b], a_sem.at[b]).start()
        for t in range(nt):
            u_ref[t] = win_ref[:, 3 * width + t * units : 3 * width + (t + 1) * units]
        for b in range(nb):
            pltpu.make_async_copy(u_ref, u_hbm.at[b], u_sem.at[b]).start()
        for b in range(nb):
            pltpu.make_async_copy(a_ref, a_hbm.at[b], a_sem.at[b]).wait()
            pltpu.make_async_copy(u_ref, u_hbm.at[b], u_sem.at[b]).wait()

    return pl.pallas_call(
        kernel,
        out_shape=[
            jax.ShapeDtypeStruct((nb, nt, rows + 2, 3 * local), BF),
            jax.ShapeDtypeStruct((nb, nt, rows, units), BF),
        ],
        in_specs=[HBM] * 2,
        out_specs=[HBM] * 2,
        scratch_shapes=[
            pltpu.VMEM(ids.shape, jnp.int32),
            pltpu.VMEM(w_in.shape, BF),
            pltpu.VMEM((nt, rows + 2, 3 * local), BF),
            pltpu.VMEM((nt, rows, units), BF),
            pltpu.SemaphoreType.DMA((2,)),
            pltpu.SemaphoreType.DMA((nb,)),
            pltpu.SemaphoreType.DMA((nb,)),
        ],
        cost_estimate=SMALL,
        compiler_params=pltpu.CompilerParams(vmem_limit_bytes=16 * MIB),
        name="prepare",
    )(*hbm(ids, w_in))


def before(at, table, w_out, ids, gain, x, cot, first):
    seqs, part, dim = x.shape

    per, unit, _ = w_out.shape

    def kernel(at_ref, table_hbm, wout_hbm, ids_hbm, gain_hbm, x_hbm, cot_hbm, out0_hbm, out1_hbm, *refs):
        unit_refs, (table_ref, wout_ref, ids_ref, gain_ref, x_ref, cot_ref, pay_ref, in_sem, x_sem, out_sem) = refs[:per], refs[per:]
        ins = [
            pltpu.make_async_copy(a, b, in_sem.at[i])
            for i, (a, b) in enumerate(((table_hbm, table_ref), (wout_hbm, wout_ref), (ids_hbm, ids_ref), (gain_hbm, gain_ref)))
        ]
        loads = [
            [pltpu.make_async_copy(a.at[s], b.at[s], x_sem.at[s, k]) for k, (a, b) in enumerate(((x_hbm, x_ref), (cot_hbm, cot_ref)))]
            for s in range(seqs)
        ]
        for copy in ins + sum(loads, []):
            copy.start()
        for copy in ins:
            copy.wait()
        for k, ref in enumerate(unit_refs):
            ref[...] = wout_ref[table_ref[at_ref[0], k]]
        copies = []
        for s in range(seqs):
            for copy in loads[s]:
                copy.wait()
            unit, _ = normalize(x_ref[s].astype(F32))
            live = column(jnp.where(ids_ref[s : s + 1, :] >= 0, 1.0, 0.0))
            pay_ref[s, 0] = (unit * as_row(gain_ref)).astype(BF)
            pay_ref[s, 1] = (live * cot_ref[s].astype(F32)).astype(BF)
            to = out0_hbm.at[s] if s < first else out1_hbm.at[s - first]
            copies.append(pltpu.make_async_copy(pay_ref.at[s], to, out_sem.at[s]))
            copies[-1].start()
        for copy in copies:
            copy.wait()

    return pl.pallas_call(
        kernel,
        out_shape=[jax.ShapeDtypeStruct((n, 2, part, dim), BF) for n in (first, seqs - first)]
        + [jax.ShapeDtypeStruct((unit, dim), BF)] * per,
        in_specs=[SMEM] + [HBM] * 6,
        out_specs=[HBM] * 2 + [VMEM] * per,
        scratch_shapes=[
            pltpu.SMEM(table.shape, jnp.int32),
            pltpu.VMEM(w_out.shape, BF),
            pltpu.VMEM(ids.shape, jnp.int32),
            pltpu.VMEM(gain.shape, F32),
            pltpu.VMEM(x.shape, BF),
            pltpu.VMEM(x.shape, BF),
            pltpu.VMEM((seqs, 2, part, dim), BF),
            pltpu.SemaphoreType.DMA((4,)),
            pltpu.SemaphoreType.DMA((seqs, 2)),
            pltpu.SemaphoreType.DMA((seqs,)),
        ],
        cost_estimate=SMALL,
        compiler_params=pltpu.CompilerParams(vmem_limit_bytes=32 * MIB),
        name="before",
    )(at, *hbm(table, w_out, ids, gain, x, cot))


def join(at, got, wo_parts, seqs, part):
    count, high, wide = got.shape
    unit = high - 2
    dim = count * unit
    nb = count // SLOTS

    def kernel(at_ref, got_ref, *refs):
        ins, (w_ref, wo_ref, ids_ref, all_ref) = refs[:-4], refs[-4:]

        def move(i, carry):
            all_ref[i] = got_ref[i, :unit]
            return carry

        lax.fori_loop(0, count, move, 0)
        w_ref[...] = all_ref[...].reshape(dim, wide).T
        for ref, (_, masks) in zip(ins, wo_parts):
            for i, mask in enumerate(masks):
                wo_ref[at_ref[2] ^ mask] = ref[i]
        for slot in range(SLOTS):
            i = at_ref[2] * SLOTS + slot
            row = jnp.concatenate([got_ref[i, unit : unit + 1], got_ref[i, unit + 1 :]], axis=1)
            row = row.astype(F32).astype(jnp.int32)
            for s in range(seqs):
                ids_ref[s, :, slot * part : (slot + 1) * part] = row[:, s * part : (s + 1) * part]

    return pl.pallas_call(
        kernel,
        out_shape=[
            jax.ShapeDtypeStruct((wide, dim), BF),
            jax.ShapeDtypeStruct((nb,) + wo_parts[0][0].shape[1:], BF),
            jax.ShapeDtypeStruct((seqs, 1, SLOTS * part), jnp.int32),
        ],
        in_specs=[SMEM] + [VMEM] * (1 + len(wo_parts)),
        out_specs=[VMEM] * 3,
        scratch_shapes=[pltpu.VMEM((count, unit, wide), BF)],
        cost_estimate=SMALL,
        compiler_params=pltpu.CompilerParams(vmem_limit_bytes=32 * MIB),
        name="join",
    )(at, got, *[a for a, _ in wo_parts])


def pack_out(at, table, got):
    unit, dim = got[0].shape
    per = len(got)

    def kernel(at_ref, table_ref, *refs):
        got_refs, (wo_ref, ff_ref, all_ref) = refs[:per], refs[per:]
        for k, ref in enumerate(got_refs):
            all_ref[table_ref[at_ref[0], per + k]] = ref[...]
        wo_ref[...] = all_ref[0]
        for k in range(per - 1):
            ff_ref[k] = all_ref[k + 1]

    return pl.pallas_call(
        kernel,
        out_shape=[jax.ShapeDtypeStruct((unit, dim), BF), jax.ShapeDtypeStruct((per - 1, unit, dim), BF)],
        in_specs=[SMEM] * 2 + [VMEM] * per,
        out_specs=[VMEM] * 2,
        scratch_shapes=[pltpu.VMEM((per, unit, dim), BF)],
        cost_estimate=SMALL,
        name="pack_out",
    )(at, table, *got)


def add_blocks(ref, count, step, start, rows):
    total = ref[start, rows].astype(F32)
    for i in range(1, count):
        total = total + ref[start + i * step, rows].astype(F32)
    return total


def fold(at, low, terms):
    n, _, dim = terms[0][0].shape
    counts = [len(group) for group in terms]
    rows = [group[0].shape[1] for group in terms]

    def kernel(at_ref, *refs):
        ins, (own_ref, *send_refs) = refs[: sum(counts)], refs[sum(counts) :]
        mine = (at_ref[2] >> low) & 3
        k, start = 0, 0
        for count, high in zip(counts, rows):
            for i in range(n // 4):
                for s, to in enumerate([own_ref] + send_refs):
                    block = i * 4 + (mine ^ s)
                    total = ins[k][block].astype(F32)
                    for ref in ins[k + 1 : k + count]:
                        total = total + ref[block].astype(F32)
                    to[i, start : start + high] = total.astype(to.dtype)
            k += count
            start += high

    out = lambda t: jax.ShapeDtypeStruct((n // 4, sum(rows), dim), t)
    return pl.pallas_call(
        kernel,
        out_shape=[out(F32)] + [out(BF)] * 3,
        in_specs=[SMEM] + [VMEM] * sum(counts),
        out_specs=[VMEM] * 4,
        cost_estimate=SMALL,
        compiler_params=pltpu.CompilerParams(vmem_limit_bytes=32 * MIB),
        name="fold",
    )(at, *sum(terms, []))


def split_rows(odd, grad, send_ref, keep_ref):
    parts, rows, _ = send_ref.shape
    for z in range(parts):
        low = grad[2 * z * rows : (2 * z + 1) * rows]
        high = grad[(2 * z + 1) * rows : (2 * z + 2) * rows]
        send_ref[z] = jnp.where(odd, low, high).astype(BF)
        keep_ref[z] = jnp.where(odd, high, low)


def leave(at, table, heads, ffn):
    _, per_ff, unit, dim = ffn.shape
    per = 1 + per_ff

    def kernel(at_ref, table_ref, ffn_ref, *refs):
        terms, outs, all_ref = refs[: len(heads)], refs[len(heads) : -1], refs[-1]
        total = terms[0][0]
        for ref in terms[1:]:
            total = total + ref[0].astype(F32)
        all_ref[0] = total.astype(all_ref.dtype)
        for k in range(per_ff):
            all_ref[k + 1] = ffn_ref[1, k].astype(all_ref.dtype)
        for k in range(per):
            outs[k][...] = all_ref[table_ref[at_ref[0], per + k]].astype(BF)
        for s in range(SLOTS):
            outs[per + s][...] = ffn_ref[0, at_ref[1] ^ s]

    return pl.pallas_call(
        kernel,
        out_shape=[jax.ShapeDtypeStruct((unit, dim), BF)] * (per + SLOTS),
        in_specs=[SMEM] * 2 + [VMEM] * (1 + len(heads)),
        out_specs=[VMEM] * (per + SLOTS),
        scratch_shapes=[pltpu.VMEM((per, unit, dim), F32)],
        cost_estimate=SMALL,
        name="leave",
    )(at, table, ffn, *heads)


def place(at, table, qkv, up, got):
    count, high, width = qkv.shape
    unit, dim = got[0].shape
    nt = len(up)
    nb = count // nt
    per = len(got)
    local = width // 3
    wide = nt * (width + dim)

    def kernel(at_ref, table_ref, qkv_ref, *refs):
        up_refs, got_refs, (in_ref, out_ref, norm_ref, q_ref, k_ref) = refs[:nt], refs[nt : nt + per], refs[nt + per :]
        for s, ref in enumerate(up_refs):
            to = pl.multiple_of(nt * width + (at_ref[1] ^ s) * dim, 128)
            in_ref[:, pl.ds(to, dim)] = ref[...].astype(F32)
        for t in range(nt):
            total = add_blocks(qkv_ref, nb, nt, t, slice(0, unit))
            for k in range(3):
                in_ref[:, k * nt * local + t * local : k * nt * local + (t + 1) * local] = total[:, k * local : (k + 1) * local]
        for k, ref in enumerate(got_refs):
            out_ref[table_ref[at_ref[0], k]] = ref[...].astype(F32)
        small = add_blocks(qkv_ref, count, 1, 0, slice(unit, high))
        small = small[0:2] + small[2:4]
        norm_ref[:, :width] = small[0:1]
        norm_ref[:, width:] = small[1:2, : dim - width]
        q_ref[...] = small[1:2, dim - width : dim - width + HD]
        k_ref[...] = small[1:2, dim - width + HD : dim - width + 2 * HD]

    return pl.pallas_call(
        kernel,
        out_shape=[
            jax.ShapeDtypeStruct((unit, wide), F32),
            jax.ShapeDtypeStruct((per, unit, dim), F32),
            jax.ShapeDtypeStruct((1, dim), F32),
            jax.ShapeDtypeStruct((1, HD), F32),
            jax.ShapeDtypeStruct((1, HD), F32),
        ],
        in_specs=[SMEM] * 2 + [VMEM] * (1 + nt + per),
        out_specs=[VMEM] * 5,
        cost_estimate=SMALL,
        compiler_params=pltpu.CompilerParams(vmem_limit_bytes=32 * MIB),
        name="place",
    )(at, table, qkv, *up, *got)


def after(start, ids, x, cot, gain, keep, near, far, earlier):
    seqs, part, dim = x.shape
    count = far.shape[0]

    def kernel(ids_ref, x_ref, cot_ref, gain_ref, keep_ref, near_ref, far_ref, *rest):
        out_ref, grad_ref = rest[-2:]
        unit, inverse = normalize(x_ref[0].astype(F32))
        live = column(jnp.where(ids_ref[0] >= 0, 1.0, 0.0))
        branch, gn = (keep_ref[0, 0, j].astype(F32) + near_ref[0, 0, j].astype(F32) + far_ref[0, j].astype(F32) for j in range(2))
        out_ref[0] = (live * (x_ref[0].astype(F32) + branch)).astype(BF)
        grad_ref[0] = (live * cot_ref[0].astype(F32) + norm_back(gn * as_row(gain_ref), unit, inverse)).astype(BF)

    one = pl.BlockSpec((1, part, dim), lambda g: (start + g, 0, 0))
    pair = pl.BlockSpec((1, 1, 2, part, dim), lambda g: (0, g, 0, 0, 0))
    lone = pl.BlockSpec((1, 2, part, dim), lambda g: (g, 0, 0, 0))
    return pl.pallas_call(
        kernel,
        grid=(count,),
        out_shape=[jax.ShapeDtypeStruct(x.shape, BF)] * 2,
        in_specs=[
            pl.BlockSpec((1, 1, part), lambda g: (start + g, 0, 0)), one, one,
            pl.BlockSpec(gain.shape, lambda g: (0,)), pair, pair, lone,
        ]
        + [ANY] * len(earlier),
        out_specs=[one, one],
        input_output_aliases={7 + i: i for i in range(len(earlier))},
        cost_estimate=SMALL,
        compiler_params=pltpu.CompilerParams(vmem_limit_bytes=32 * MIB),
        name="after",
    )(ids.reshape(seqs, 1, part), *hbm(x, cot), gain, *hbm(keep, near, far), *earlier)


def attention_kernel(
    heads, block, last, start,
    at_ref, ids_ref, qg_ref, kg_ref, wqkv_hbm, wo_hbm, *refs,
):
    pays, refs = refs[0], refs[1:]
    if last:
        (acc_sums_ref, fnp_ref, gain_ref, accq_hbm, acco_hbm, hid_hbm, gup_hbm, wff_hbm, wup_hbm), refs = refs[:9], refs[9:]
        (keep_hbm, leave_hbm, sendq_ref, sendo_ref, keepo_ref, sums_ref), refs = refs[:6], refs[6:]
        (hid_ref, gup_ref, wff_ref, wup_ref, res_ref, res_sem, act_sem), refs = refs[:7], refs[7:]
    else:
        (o_hbm, grad_hbm, sums_ref, newq_hbm, newo_hbm), refs = refs[:5], refs[5:]
    (
        wqkv_ref, wo_ref, norm_ref, gb_ref, o_ref, grad_ref, gq_ref, go_ref, raw_ref,
        qt_ref, qn_ref, kt_ref, ka_ref, vt_ref, va_ref, do_ref, dq_ref, dk_ref, dv_ref, pad_ref, vm_ref,
        w_sem, sem, out_sem,
    ) = refs
    seqs, length, dim = norm_ref.shape
    part = length // SLOTS
    width = heads * HD
    blocks = length // block
    loads = [pltpu.make_async_copy(wqkv_hbm, wqkv_ref, w_sem.at[0]), pltpu.make_async_copy(wo_hbm, wo_ref, w_sem.at[1])]
    loads[0].start()

    def pay_copy(s, j, t):
        to = (norm_ref, gb_ref)[j].at[s, pl.ds(t * part, part), :]
        return pltpu.make_async_copy(pays.at[t, s, j], to, sem.at[s, j * SLOTS + t])

    for s in range(seqs):
        for j in range(2):
            for t in range(SLOTS):
                pay_copy(s, j, t).start()
            if s + j == 0:
                loads[1].start()
    if last:
        loads.append(pltpu.make_async_copy(accq_hbm, gq_ref, w_sem.at[2]))
        loads.append(pltpu.make_async_copy(acco_hbm, go_ref, w_sem.at[3]))
        loads.append(pltpu.make_async_copy(wff_hbm, wff_ref, act_sem.at[2 * seqs]))
        loads.append(pltpu.make_async_copy(wup_hbm, wup_ref, act_sem.at[2 * seqs + 1]))
        for copy in loads[2:]:
            copy.start()
        skip = hid_hbm.shape[0] // length - seqs

        def act_copies(s):
            rows = pl.ds(pl.multiple_of((skip + s) * length, length), length)
            return [
                pltpu.make_async_copy(hid_hbm.at[rows, :], hid_ref.at[s], act_sem.at[2 * s]),
                pltpu.make_async_copy(gup_hbm.at[rows, :], gup_ref.at[s], act_sem.at[2 * s + 1]),
            ]

        for s in range(seqs):
            for copy in act_copies(s):
                copy.start()
        outs = Outputs(at_ref[1], keep_hbm, leave_hbm, res_ref, res_sem, wo_ref, wff_ref, wqkv_ref, wup_ref)
        sums_ref[...] = acc_sums_ref[...]
    else:
        gq_ref[...] = jnp.zeros_like(gq_ref)
        go_ref[...] = jnp.zeros_like(go_ref)
        sums_ref[...] = jnp.zeros_like(sums_ref)
    gain_q = column(as_row(qg_ref))
    gain_k = column(as_row(kg_ref))
    marks = lax.broadcasted_iota(jnp.int32, (HD, length), 0)
    v_tail = jnp.where(lax.broadcasted_iota(jnp.int32, (length, HD), 1) < 2, 1.0, 0.0).astype(BF)
    ones = jnp.where(lax.broadcasted_iota(jnp.int32, (16, length), 0) == 0, 1.0, 0.0).astype(BF)
    spot = lax.broadcasted_iota(jnp.int32, (HD, block), 0)
    scale = 1.0 / math.sqrt(HD)
    cut = lambda a, i: a[:, i * block : (i + 1) * block]

    def unit_of(row):
        raw = raw_ref[pl.ds(pl.multiple_of(row, HD), HD), :]
        center = raw - jnp.mean(raw, axis=0, keepdims=True)
        inverse = lax.rsqrt(jnp.mean(center * center, axis=0, keepdims=True) + EPS)
        return center * inverse, inverse

    def lanes(a):
        total = a[:, :128]
        for i in range(1, length // 128):
            total = total + a[:, i * 128 : (i + 1) * 128]
        return total

    def stores(s):
        return [
            pltpu.make_async_copy(o_ref.at[s], o_hbm.at[s], out_sem.at[s, 0]),
            pltpu.make_async_copy(grad_ref.at[s], grad_hbm.at[s], out_sem.at[s, 1]),
        ]

    loads[0].wait()
    loads[1].wait()

    def sequence(s, carry):
        ids = ids_ref[start + s]
        same = marks == ids + 1
        k_tail = jnp.where(same, 1.0, 0.0).T.astype(BF)
        q_tail = jnp.where((same & (ids >= 0)) | (marks > 4), 0.0, -BIG).astype(BF)
        pad = jnp.where(ids < 0, 1.0, 0.0)
        for i in range(blocks):
            pad_ref[i] = cut(pad, i)
        for t in range(SLOTS):
            pay_copy(s, 0, t).wait()
        raw_ref[...] = mm(wqkv_ref[...], norm_ref[s], NT)
        for t in range(SLOTS):
            pay_copy(s, 1, t).wait()
        do_all = mm(wo_ref[...], gb_ref[s], NT).astype(BF)
        for h in range(heads):
            for i in range(blocks):
                do_ref[h * blocks + i] = cut(do_all[h * HD : (h + 1) * HD], i)

        def prepare(h, carry):
            q_unit, _ = unit_of(h * HD)
            q = q_unit * gain_q
            qn = q.T.astype(BF)
            for i in range(blocks):
                qt_ref[h * blocks + i, :HD] = cut(q, i).astype(BF)
                qt_ref[h * blocks + i, HD:] = cut(q_tail, i)
                qn_ref[h * blocks + i] = qn[i * block : (i + 1) * block]
            k_unit, _ = unit_of(width + h * HD)
            k = k_unit * gain_k
            kt_ref[h] = k.astype(BF)
            ka_ref[h, :, :HD] = k.T.astype(BF)
            ka_ref[h, :, HD:] = k_tail
            v = raw_ref[pl.ds(pl.multiple_of(2 * width + h * HD, HD), HD), :]
            vb = v.astype(BF)
            vt_ref[h, :HD] = vb
            vt_ref[h, HD:] = ones
            va_ref[h, :, :HD] = v.T.astype(BF)
            va_ref[h, :, HD:] = v_tail
            vm_ref[h] = jnp.mean(vb.astype(F32), axis=1, keepdims=True)
            dk_ref[h] = jnp.zeros(dk_ref.shape[1:], F32)
            dv_ref[h] = jnp.zeros(dv_ref.shape[1:], F32)
            return carry

        lax.fori_loop(0, heads, prepare, 0, unroll=True)

        def step(n, carry):
            h = n // blocks
            padb = pad_ref[n % blocks]
            e = jnp.exp2(mm(ka_ref[h], qt_ref[n]) * (LOG2E * scale))
            eb = e.astype(BF)
            oa = mm(vt_ref[h], eb)
            inv = 1.0 / (oa[HD : HD + 1] + padb)
            o = oa[:HD] * inv
            dos = (do_ref[n].astype(F32) * inv).astype(BF)
            delta = jnp.sum(dos.astype(F32) * o, axis=0, keepdims=True)
            d0 = delta.astype(BF).astype(F32)
            tail = jnp.where(spot == 0, -d0, jnp.where(spot == 1, d0 - delta, 0.0))
            doa = jnp.concatenate([dos.astype(F32), tail], axis=0)
            ds = (e * mm(va_ref[h], doa.astype(BF))).astype(BF)
            dq_ref[n] = mm(kt_ref[h], ds)
            dk_ref[h] += mm(ds, qn_ref[n])
            dv_ref[h] += mm(dos, eb, NT)
            do_ref[n] = jnp.where(padb > 0, vm_ref[h], o).astype(BF)
            return carry

        lax.fori_loop(0, heads * blocks, step, 0)

        def finish(h, carry):
            rows = lambda at: pl.ds(pl.multiple_of(at + h * HD, HD), HD)
            gq = jnp.concatenate([dq_ref[h * blocks + i] for i in range(blocks)], axis=1)
            gk = dk_ref[h].T
            for k, (g, gain_col) in enumerate(((gq, gain_q), (gk, gain_k))):
                unit, inverse = unit_of(k * width + h * HD)
                g = (g * scale).astype(BF).astype(F32)
                sums_ref[k] += lanes(g * unit)
                g = g * gain_col
                back = inverse * (
                    g - jnp.mean(g, axis=0, keepdims=True) - unit * jnp.mean(g * unit, axis=0, keepdims=True)
                )
                grad_ref[s, rows(k * width), :] = back.astype(BF)
            grad_ref[s, rows(2 * width), :] = dv_ref[h].astype(BF)
            for i in range(blocks):
                o_ref[s, rows(0), pl.ds(i * block, block)] = do_ref[h * blocks + i]
            return carry

        lax.fori_loop(0, heads, finish, 0, unroll=True)
        if last:

            @pl.when(s == 0)
            def _():
                for copy in loads[2:]:
                    copy.wait()

            for copy in act_copies(s):
                copy.wait()
            outs.compute(s, o_ref.at[s], hid_ref.at[s], grad_ref.at[s], gup_ref.at[s])
        else:
            for copy in stores(s):
                copy.start()
        gq_ref[...] += mm(grad_ref[s], norm_ref[s])
        go_ref[...] += mm(o_ref[s], gb_ref[s])
        return carry

    lax.fori_loop(0, seqs, sequence, 0)
    if not last:
        ends = [pltpu.make_async_copy(gq_ref, newq_hbm, w_sem.at[2]), pltpu.make_async_copy(go_ref, newo_hbm, w_sem.at[3])]
        for copy in ends:
            copy.start()
        for copy in ends:
            copy.wait()
        for s in range(seqs):
            for copy in stores(s):
                copy.wait()
        return
    outs.wait()
    g_q = gq_ref[...]
    first_row = (jnp.sum(wqkv_ref[...].astype(F32) * g_q, axis=0, keepdims=True) + fnp_ref[...]) / as_row(gain_ref)
    second_row = jnp.concatenate([jnp.sum(sums_ref[k].T, axis=0, keepdims=True) for k in range(2)], axis=1)
    wide = 3 * width
    line = jnp.concatenate([first_row[:, wide:], second_row, jnp.zeros((1, 2 * wide - dim - 2 * HD), F32)], axis=1)
    small = jnp.concatenate([first_row[:, :wide], line], axis=0)
    high = small.astype(BF)
    small = jnp.concatenate([high.astype(F32), small - high.astype(F32)], axis=0).astype(BF)
    g_q = g_q.T.astype(BF)
    count, rows, _ = sendq_ref.shape
    rows = rows - 4
    for i in range(count):
        sendq_ref[i, :rows] = g_q[i * rows : (i + 1) * rows]
        sendq_ref[i, rows:] = small
    split_rows((at_ref[2] & 1) > 0, go_ref[...], sendo_ref, keepo_ref)


def attention(at, start, ids, wqkv, wo, qg, kg, pays, count, more=()):
    wide, dim = wqkv.shape
    width = wo.shape[0]
    heads = width // HD
    _, seqs, _, part, _ = pays.shape
    length = part * SLOTS
    block = 1024
    blocks = length // block
    last = bool(more)
    ins = [at, ids, qg, kg, *hbm(wqkv, wo, pays), *more[:3], *hbm(*more[3:])]
    specs = [SMEM] + [VMEM] * 3 + [HBM] * 3 + ([VMEM] * 3 + [HBM] * 6 if last else [])
    scratch = []
    if last:
        outs = [jax.ShapeDtypeStruct((SLOTS // 2, seqs, 2, part, dim), BF)] * 2
        outs += [jax.ShapeDtypeStruct((count, dim // count + 4, wide), BF)]
        outs += [jax.ShapeDtypeStruct((count // (2 * SLOTS), SLOTS * width // count, dim), t) for t in (BF, F32)]
        scratch = [pltpu.VMEM((2, HD, 128), F32)]
        scratch += [pltpu.VMEM((seqs, length, dim), BF)] * 2 + [pltpu.VMEM((dim, dim), BF)] * 2
        scratch += Outputs.scratch(seqs, length, dim) + [pltpu.SemaphoreType.DMA((2 * seqs + 2,))]
    else:
        outs = [jax.ShapeDtypeStruct((seqs, width, length), BF), jax.ShapeDtypeStruct((seqs, wide, length), BF)]
        outs += [
            jax.ShapeDtypeStruct((2, HD, 128), F32),
            jax.ShapeDtypeStruct((wide, dim), F32),
            jax.ShapeDtypeStruct((width, dim), F32),
        ]
    flops = seqs * (2 * length * dim * width * 8 + heads * 6 * 2 * length * length * HD)
    return pl.pallas_call(
        functools.partial(attention_kernel, heads, block, last, start),
        out_shape=outs,
        in_specs=specs,
        out_specs=[HBM] * 2 + ([VMEM] * 3 if last else [VMEM, HBM, HBM]),
        scratch_shapes=scratch
        + [
            pltpu.VMEM((wide, dim), BF),
            pltpu.VMEM((width, dim), BF),
            pltpu.VMEM((seqs, length, dim), BF),
            pltpu.VMEM((seqs, length, dim), BF),
            pltpu.VMEM((seqs, width, length), BF),
            pltpu.VMEM((seqs, wide, length), BF),
            pltpu.VMEM((wide, dim), F32),
            pltpu.VMEM((width, dim), F32),
            pltpu.VMEM((wide, length), F32),
            pltpu.VMEM((heads * blocks, 2 * HD, block), BF),
            pltpu.VMEM((heads * blocks, block, HD), BF),
            pltpu.VMEM((heads, HD, length), BF),
            pltpu.VMEM((heads, length, 2 * HD), BF),
            pltpu.VMEM((heads, HD + 16, length), BF),
            pltpu.VMEM((heads, length, 2 * HD), BF),
            pltpu.VMEM((heads * blocks, HD, block), BF),
            pltpu.VMEM((heads * blocks, HD, block), F32),
            pltpu.VMEM((heads, length, HD), F32),
            pltpu.VMEM((heads, HD, length), F32),
            pltpu.VMEM((blocks, 1, block), F32),
            pltpu.VMEM((heads, HD, 1), F32),
            pltpu.SemaphoreType.DMA((4,)),
            pltpu.SemaphoreType.DMA((seqs, 2 * SLOTS)),
            pltpu.SemaphoreType.DMA((seqs, 2)),
        ],
        cost_estimate=LARGE,
        compiler_params=pltpu.CompilerParams(vmem_limit_bytes=56 * MIB),
        name="attention",
    )(*ins)


def ffn_kernel(block, groups, plan, at_ref, wup_hbm, wqkv_hbm, wo_hbm, o_hbm, gq_hbm, *refs):
    pieces, refs = refs[: len(plan)], refs[len(plan) :]
    pays, refs = refs[: len(groups)], refs[len(groups) :]
    (hid_hbm, gup_hbm, wff_hbm, keep_hbm, leave_hbm, send_ref, np_ref), refs = refs[:7], refs[7:]
    norm_ref, gb_ref, hid_ref, gup_ref, wup_ref, wff_ref, gin_ref, gff_ref, sem, out_sem, w_sem, *refs = refs
    wqkv_ref, wo_ref, o_ref, gq_ref, res_ref, res_sem, late_sem = refs
    dim = wup_ref.shape[0]
    part = pays[0].shape[3]
    total = norm_ref.shape[0]
    weights = [pltpu.make_async_copy(wup_hbm, wup_ref, w_sem.at[0])]
    rows = send_ref.shape[2]
    for ref, masks in zip(pieces, plan):
        for i, mask in enumerate(masks):
            to = wff_ref.at[pl.ds(pl.multiple_of((at_ref[2] ^ mask) * rows, rows), rows), :]
            weights.append(pltpu.make_async_copy(ref.at[i], to, w_sem.at[len(weights)]))
    for copy in weights:
        copy.start()
    n = 0
    for g, seqs in enumerate(groups):
        for s in range(seqs):
            for t in range(SLOTS):
                for k, to in enumerate((norm_ref, gb_ref)):
                    source = pays[g].at[t, s, k]
                    pltpu.make_async_copy(source, to.at[pl.ds(n * part, part), :], sem.at[k, n]).start()
                n += 1
    late = [
        pltpu.make_async_copy(a, b, late_sem.at[i])
        for i, (a, b) in enumerate(((wqkv_hbm, wqkv_ref), (wo_hbm, wo_ref), (o_hbm, o_ref), (gq_hbm, gq_ref)))
    ]
    for copy in late:
        copy.start()
    gin_ref[...] = jnp.zeros_like(gin_ref)
    gff_ref[...] = jnp.zeros_like(gff_ref)
    for copy in weights:
        copy.wait()
    joined = pltpu.make_async_copy(wff_ref, wff_hbm, w_sem.at[0])
    joined.start()
    c0 = math.sqrt(2.0 / math.pi)
    c1 = 0.044715

    def outs(i):
        at_rows = pl.ds(pl.multiple_of(i * block, block), block)
        return (
            pltpu.make_async_copy(hid_ref.at[at_rows, :], hid_hbm.at[at_rows, :], out_sem.at[0, i]),
            pltpu.make_async_copy(gup_ref.at[at_rows, :], gup_hbm.at[at_rows, :], out_sem.at[1, i]),
        )

    def arrive(i):
        for j in range(block // part):
            for k, to in enumerate((norm_ref, gb_ref)):
                pltpu.make_async_copy(pays[0].at[0, 0, 0], to.at[pl.ds(0, part), :], sem.at[k, i * (block // part) + j]).wait()

    def rows_of(i):
        return pl.ds(pl.multiple_of(i * block, block), block)

    def units(i):
        up = mm(norm_ref[rows_of(i), :], wup_ref[...])
        gh = mm(gb_ref[rows_of(i), :], wff_ref[...], NT)
        sq = up * up
        t = jnp.tanh(up * (c0 + (c0 * c1) * sq))
        half = 0.5 + 0.5 * t
        hid_ref[rows_of(i), :] = (up * half).astype(BF)
        gup_ref[rows_of(i), :] = (gh * (half + (0.5 * up) * (1.0 - t * t) * (c0 + (3.0 * c0 * c1) * sq))).astype(BF)

    def grads(i):
        gin_ref[...] += mm(norm_ref[rows_of(i), :], gup_ref[rows_of(i), :], TN)
        gff_ref[...] += mm(hid_ref[rows_of(i), :], gb_ref[rows_of(i), :], TN)

    count = total // block
    arrive(0)
    units(0)

    def step(i, carry):
        for copy in outs(i - 1):
            copy.start()
        arrive(i)
        grads(i - 1)
        units(i)
        return carry

    lax.fori_loop(1, count, step, 0)
    for copy in outs(count - 1):
        copy.start()
    grads(count - 1)
    for copy in late:
        copy.wait()
    results = Outputs(at_ref[1], keep_hbm, leave_hbm, res_ref, res_sem, wo_ref, wff_ref, wqkv_ref, wup_ref)
    length = SLOTS * part

    def result(s, carry):
        rows_s = pl.ds(pl.multiple_of(s * length, length), length)
        results.compute(s, o_ref.at[s], hid_ref.at[rows_s, :], gq_ref.at[s], gup_ref.at[rows_s, :])
        return carry

    lax.fori_loop(0, results.seqs, result, 0)
    line = jnp.sum(wup_ref[...].astype(F32) * gin_ref[...], axis=1, keepdims=True)
    np_ref[...] = jnp.broadcast_to(line, (dim, 128)).T[0:1]
    for b in range(dim // rows):
        for k, g in enumerate((gin_ref, gff_ref)):
            send_ref[b, k] = g[b * rows : (b + 1) * rows, :].astype(BF)
    joined.wait()
    results.wait()

    def drain(i, carry):
        for copy in outs(i):
            copy.wait()
        return carry

    lax.fori_loop(0, total // block, drain, 0)


def ffn(at, wup, ff_parts, groups, count, wqkv, wo, o, gq, block=512):
    dim, units = wup.shape
    sizes = [g.shape[1] for g in groups]
    part = groups[0].shape[3]
    total = SLOTS * part * sum(sizes)
    pieces = groups
    act = jax.ShapeDtypeStruct((total, units), BF)
    return pl.pallas_call(
        functools.partial(ffn_kernel, block, sizes, [masks for _, masks in ff_parts]),
        out_shape=[
            act,
            act,
            jax.ShapeDtypeStruct((units, dim), BF),
            *[jax.ShapeDtypeStruct((SLOTS // 2, o.shape[0], 2, part, dim), BF)] * 2,
            jax.ShapeDtypeStruct((count, 2, units // count, dim), BF),
            jax.ShapeDtypeStruct((1, dim), F32),
        ],
        in_specs=[SMEM] + [HBM] * (5 + len(ff_parts) + len(pieces)),
        out_specs=[HBM] * 5 + [VMEM] * 2,
        scratch_shapes=[
            pltpu.VMEM((total, dim), BF),
            pltpu.VMEM((total, dim), BF),
            pltpu.VMEM((total, units), BF),
            pltpu.VMEM((total, units), BF),
            pltpu.VMEM((dim, units), BF),
            pltpu.VMEM((units, dim), BF),
            pltpu.VMEM((dim, units), F32),
            pltpu.VMEM((units, dim), F32),
            pltpu.SemaphoreType.DMA((2, total // part)),
            pltpu.SemaphoreType.DMA((2, total // block)),
            pltpu.SemaphoreType.DMA((1 + count,)),
            *[pltpu.VMEM(a.shape, BF) for a in (wqkv, wo, o, gq)],
            *Outputs.scratch(o.shape[0], SLOTS * part, dim),
            pltpu.SemaphoreType.DMA((4,)),
        ],
        cost_estimate=LARGE,
        compiler_params=pltpu.CompilerParams(vmem_limit_bytes=58 * MIB),
        name="ffn",
    )(at, *hbm(wup, wqkv, wo, o, gq, *[a for a, _ in ff_parts], *pieces))


class Outputs:
    def __init__(self, me, keep, send, res, sem, wo, wff, wqkv, wup):
        self.me = me
        self.keep, self.send, self.res, self.sem = keep, send, res, sem
        self.wo, self.wff, self.wqkv, self.wup = wo, wff, wqkv, wup
        self.seqs, _, self.length, _ = res.shape

    @staticmethod
    def scratch(seqs, length, dim):
        return [pltpu.VMEM((seqs, 2, length, dim), BF), pltpu.SemaphoreType.DMA((seqs, 2, SLOTS))]

    def moves(self, s, i):
        half = self.length // 2
        part = half // 2
        out = []
        for j in range(2):
            for k, to in enumerate((self.keep, self.send)):
                rows = pl.ds(pl.multiple_of(i * half + (k ^ (self.me & 1)) * part, part), part)
                source = self.res.at[s, j, rows, :]
                out.append(pltpu.make_async_copy(source, to.at[i ^ (self.me >> 1), s, j], self.sem.at[s, j, 2 * i + k]))
        return out

    def compute(self, s, o, hid, gq, gu):
        half = self.length // 2

        def step(i, carry):
            rows = pl.ds(pl.multiple_of(i * half, half), half)
            branch = mm(o[:, rows], self.wo[...], TN) + mm(hid[rows, :], self.wff[...])
            self.res[s, 0, rows, :] = branch.astype(BF)
            gn = mm(gq[:, rows], self.wqkv[...], TN) + mm(gu[rows, :], self.wup[...], NT)
            self.res[s, 1, rows, :] = gn.astype(BF)
            for copy in self.moves(s, i):
                copy.start()
            return carry

        lax.fori_loop(0, 2, step, 0)

    def wait(self):
        for s in range(self.seqs):
            for i in range(2):
                for copy in self.moves(s, i):
                    copy.wait()


def swap(value, axis, count, mask):
    return lax.ppermute(value, axis, [(i, i ^ mask) for i in range(count)])


def tie(value, *after):
    return lax.optimization_barrier((value,) + after)[0]


def bit_groups(count):
    bits = list(range(count.bit_length() - 1))[::-1]
    groups = []
    while bits:
        take = 2 if len(bits) > 1 else 1
        groups.append(bits[:take])
        bits = bits[take:]
    assert len(groups[-1]) == 1
    return groups


def gather_batch(block, count, groups, hold=None):
    held, masks = block[None], [0]
    for bits in groups:
        low = bits[-1]
        if hold is not None and bits is groups[-1]:
            held = tie(held, hold)
        parts = [(held, masks)]
        for s in range(1, 1 << len(bits)):
            parts.append((swap(held, "batch", count, s << low), [m ^ (s << low) for m in masks]))
        held = jnp.concatenate([a for a, _ in parts], axis=0)
        masks = sum((m for _, m in parts), [])
    return parts


def matchings(edges, devices, per_device):
    left = [[] for _ in range(devices)]
    for e, (source, _, _) in enumerate(edges):
        left[source].append(e)
    rounds = []
    for _ in range(per_device):
        owner = [-1] * devices

        def place(source, seen):
            for e in left[source]:
                target = edges[e][1]
                if target in seen:
                    continue
                seen.add(target)
                if owner[target] < 0 or place(edges[owner[target]][0], seen):
                    owner[target] = e
                    return True
            return False

        for source in range(devices):
            place(source, set())
        rounds.append(list(owner))
        for e in owner:
            left[edges[e][0]].remove(e)
    return rounds


def unit_plan(nb, nt, rows, width, hidden):
    unit = math.gcd(math.gcd(rows, width // nt), hidden // nt)
    per = rows // unit
    head_units, hid_units = width // nt // unit, hidden // nt // unit
    assert head_units == nb and hid_units % nb == 0
    c = hid_units // nb
    edges = []
    for t in range(nt):
        for b in range(nb):
            want = [t * head_units + b]
            want += [nt * head_units + t * hid_units + b * c + i for i in range(c)]
            for slot, u in enumerate(want):
                edges.append((u // per, b * nt + t, (u % per, slot)))
    table = np.zeros((nb * nt, 2 * per), np.int32)
    perms = []
    for k, owner in enumerate(matchings(edges, nb * nt, per)):
        perms.append([(edges[e][0], edges[e][1]) for e in owner])
        for e in owner:
            table[edges[e][0], k] = edges[e][2][0]
            table[edges[e][1], per + k] = edges[e][2][1]
    return unit, per, perms, table


def per_device(
    nb, nt, patches, image_ids, cotangent, norm_gain, query_gain, key_gain, in_weight, out_weight
):
    seqs, part, dim = patches.shape
    width = H * HD
    local = width // nt
    units = (in_weight.shape[1] - 3 * width) // nt
    rows_in = in_weight.shape[0]
    unit, per, perms, table = unit_plan(nb, nt, out_weight.shape[0], width, units * nt)
    assert nt == SLOTS and units == dim and unit == rows_in and dim == nt * local and per == nt + 1
    both = ("batch", "tok")
    me_b = lax.axis_index("batch")
    me_t = lax.axis_index("tok")
    at = jnp.stack([me_b * nt + me_t, me_t, me_b])
    table = jnp.asarray(table)
    gain = norm_gain

    def exchange(value, axis):
        return lax.all_to_all(value, axis, split_axis=0, concat_axis=0, tiled=True)

    groups = bit_groups(nb)

    lead = 2
    a_src, u_src = prepare(image_ids, in_weight, nb, nt)
    a_got = exchange(a_src.reshape(nb * nt, rows_in + 2, 3 * local), both)
    own0, own1, *unit_sends = before(
        at, table, out_weight.reshape(per, unit, dim), image_ids, gain, tie(patches, a_src), cotangent, lead
    )
    got = [lax.ppermute(v, both, perm) for v, perm in zip(unit_sends, perms)]
    wo_src, ff_src = pack_out(at, table, got)
    slots0 = lax.all_gather(own0, "tok", axis=0)
    slots1 = lax.all_gather(own1, "tok", axis=0)
    wo_parts = gather_batch(wo_src, nb, groups, a_got)
    ff_parts = gather_batch(ff_src.reshape((per - 1) * unit, dim), nb, groups[::-1])
    wqkv, wo, ids = join(at, a_got, wo_parts, seqs, part)
    wo = wo.reshape(local, dim)
    wup = exchange(tie(u_src, a_got).reshape(nb * nt, unit, dim), both).reshape(dim, units)

    qg, kg = query_gain, key_gain

    def leave_chip(keep, near, *hold):
        value = (keep[1].astype(F32) + near[1].astype(F32)).astype(BF)
        return value, swap(tie(value, *hold) if hold else value, "tok", nt, 2)

    o0, gq0, sums, acc_q, acc_o = attention(at, 0, ids, wqkv, tie(wo, ff_parts[0][0]), qg, kg, slots0, nb * nt)
    hid, gup, wff, keep0, send0, f_grad, f_np = ffn(
        at, tie(wup, o0), ff_parts, [slots0, slots1], nb, wqkv, wo, o0, gq0
    )
    f_mine = lax.psum_scatter(f_grad, "batch", scatter_dimension=0, tiled=True).reshape(2, nt, unit, dim)
    near0 = swap(send0, "tok", nt, 1)
    value0, away0 = leave_chip(keep0, near0)
    keep1, send1, a_q, a_send, a_keep = attention(
        at, lead, ids, wqkv, tie(wo, value0), qg, kg, slots1, nb * nt,
        (sums, f_np, gain, acc_q, acc_o, hid, gup, wff, wup),
    )
    a_came = swap(a_send, "batch", nb, 1)
    terms = [a_keep, a_came]
    for bits in groups[:-1][::-1]:
        own, *sends = fold(at, bits[-1], [terms])
        terms = [own] + [swap(value, "batch", nb, (s + 1) << bits[-1]) for s, value in enumerate(sends)]
    near1 = swap(tie(send1, away0, *terms[1:]), "tok", nt, 1)
    a_q = exchange(a_q, both)
    value1, away1 = leave_chip(keep1, near1)
    earlier = after(0, image_ids, patches, cotangent, gain, keep0, near0, away0, [])
    outs = leave(at, table, terms, tie(f_mine, *earlier))
    sends, up = outs[:per], outs[per:]
    up = [up[0]] + [swap(up[s], "tok", nt, s) for s in range(1, nt)]
    got = [lax.ppermute(v, both, [(b, a) for a, b in perm]) for v, perm in zip(sends, perms)]
    earlier = after(lead, image_ids, patches, cotangent, gain, keep1, near1, away1, earlier)
    in_grad, out_grad, norm_grad, query_grad, key_grad = place(at, table, tie(a_q, *earlier), up, got)

    block_out, patch_grad = earlier
    return (
        block_out,
        patch_grad,
        norm_grad.reshape(dim),
        query_grad.reshape(HD),
        key_grad.reshape(HD),
        in_grad,
        out_grad.reshape(per * unit, dim),
    )


def solution(mesh):
    rows = P("batch", "tok", None)
    weights = P(("batch", "tok"), None)
    return jax.shard_map(
        functools.partial(per_device, mesh.shape["batch"], mesh.shape["tok"]),
        mesh=mesh,
        in_specs=(rows, P("batch", "tok"), rows, P(), P(), P(), weights, weights),
        out_specs=(rows, rows, P(), P(), P(), weights, weights),
        check_vma=False,
    )
```

```python
import functools
import math

import jax
import jax.numpy as jnp
import numpy as np
from jax import lax
from jax.experimental import pallas as pl
from jax.experimental.pallas import tpu as pltpu
from jax.sharding import PartitionSpec as P

H = 12
HD = 64
SLOTS = 4
EPS = 1e-06
BIG = 2048.0
LOG2E = 1.4426950408889634
BF = jnp.bfloat16
F32 = jnp.float32
NN = (((1,), (0,)), ((), ()))
NT = (((1,), (1,)), ((), ()))
TN = (((0,), (0,)), ((), ()))
MIB = 1 << 20
SMALL = pl.CostEstimate(flops=1, transcendentals=0, bytes_accessed=1)
LARGE = pl.CostEstimate(flops=60_000_000_000, transcendentals=0, bytes_accessed=1)

VMEM = pl.BlockSpec(memory_space=pltpu.VMEM)
SMEM = pl.BlockSpec(memory_space=pltpu.SMEM)
ANY = pl.BlockSpec(memory_space=pl.ANY)
HBM = pl.BlockSpec(memory_space=pltpu.HBM)


def hbm(*arrays):
    return [pltpu.with_memory_space_constraint(a, pltpu.HBM) for a in arrays]


def mm(a, b, dims=NN):
    return lax.dot_general(a, b, dims, preferred_element_type=F32)


def normalize(values):
    center = values - jnp.mean(values, axis=-1, keepdims=True)
    inverse = lax.rsqrt(jnp.mean(center * center, axis=-1, keepdims=True) + EPS)
    return center * inverse, inverse


def norm_back(grad_unit, unit_rows, inverse):
    return inverse * (
        grad_unit
        - jnp.mean(grad_unit, axis=-1, keepdims=True)
        - unit_rows * jnp.mean(grad_unit * unit_rows, axis=-1, keepdims=True)
    )


def as_row(ref):
    return ref[...].reshape(1, ref.shape[0])


def column(row):
    return jnp.broadcast_to(row, (8, row.shape[1])).T[:, 0:1]


def prepare(ids, w_in, nb, nt):
    rows, wide = w_in.shape
    seqs, part = ids.shape
    width = H * HD
    local = width // nt
    units = (wide - 3 * width) // nt

    def kernel(ids_hbm, win_hbm, a_hbm, u_hbm, ids_ref, win_ref, a_ref, u_ref, in_sem, a_sem, u_sem):
        loads = [pltpu.make_async_copy(win_hbm, win_ref, in_sem.at[0]), pltpu.make_async_copy(ids_hbm, ids_ref, in_sem.at[1])]
        for copy in loads:
            copy.start()
        for copy in loads:
            copy.wait()
        row = jnp.concatenate([ids_ref[s : s + 1, :] for s in range(seqs)], axis=1).astype(F32).astype(BF)
        first = 3 * local
        second = jnp.concatenate([row[:, first:].astype(F32), jnp.zeros((1, 2 * first - seqs * part), F32)], axis=1).astype(BF)
        for t in range(nt):
            for k in range(3):
                a_ref[t, :rows, k * local : (k + 1) * local] = win_ref[:, k * width + t * local : k * width + (t + 1) * local]
            a_ref[t, rows : rows + 1] = row[:, :first]
            a_ref[t, rows + 1 :] = second
        for b in range(nb):
            pltpu.make_async_copy(a_ref, a_hbm.at[b], a_sem.at[b]).start()
        for t in range(nt):
            u_ref[t] = win_ref[:, 3 * width + t * units : 3 * width + (t + 1) * units]
        for b in range(nb):
            pltpu.make_async_copy(u_ref, u_hbm.at[b], u_sem.at[b]).start()
        for b in range(nb):
            pltpu.make_async_copy(a_ref, a_hbm.at[b], a_sem.at[b]).wait()
            pltpu.make_async_copy(u_ref, u_hbm.at[b], u_sem.at[b]).wait()

    return pl.pallas_call(
        kernel,
        out_shape=[
            jax.ShapeDtypeStruct((nb, nt, rows + 2, 3 * local), BF),
            jax.ShapeDtypeStruct((nb, nt, rows, units), BF),
        ],
        in_specs=[HBM] * 2,
        out_specs=[HBM] * 2,
        scratch_shapes=[
            pltpu.VMEM(ids.shape, jnp.int32),
            pltpu.VMEM(w_in.shape, BF),
            pltpu.VMEM((nt, rows + 2, 3 * local), BF),
            pltpu.VMEM((nt, rows, units), BF),
            pltpu.SemaphoreType.DMA((2,)),
            pltpu.SemaphoreType.DMA((nb,)),
            pltpu.SemaphoreType.DMA((nb,)),
        ],
        cost_estimate=SMALL,
        compiler_params=pltpu.CompilerParams(vmem_limit_bytes=16 * MIB),
        name="prepare",
    )(*hbm(ids, w_in))


def before(at, table, w_out, ids, gain, x, cot, first):
    seqs, part, dim = x.shape

    per, unit, _ = w_out.shape

    def kernel(at_ref, table_hbm, wout_hbm, ids_hbm, gain_hbm, x_hbm, cot_hbm, out0_hbm, out1_hbm, *refs):
        unit_refs, (table_ref, wout_ref, ids_ref, gain_ref, x_ref, cot_ref, pay_ref, in_sem, x_sem, out_sem) = refs[:per], refs[per:]
        ins = [
            pltpu.make_async_copy(a, b, in_sem.at[i])
            for i, (a, b) in enumerate(((table_hbm, table_ref), (wout_hbm, wout_ref), (ids_hbm, ids_ref), (gain_hbm, gain_ref)))
        ]
        loads = [
            [pltpu.make_async_copy(a.at[s], b.at[s], x_sem.at[s, k]) for k, (a, b) in enumerate(((x_hbm, x_ref), (cot_hbm, cot_ref)))]
            for s in range(seqs)
        ]
        for copy in ins + sum(loads, []):
            copy.start()
        for copy in ins:
            copy.wait()
        for k, ref in enumerate(unit_refs):
            ref[...] = wout_ref[table_ref[at_ref[0], k]]
        copies = []
        for s in range(seqs):
            for copy in loads[s]:
                copy.wait()
            unit, _ = normalize(x_ref[s].astype(F32))
            live = column(jnp.where(ids_ref[s : s + 1, :] >= 0, 1.0, 0.0))
            pay_ref[s, 0] = (unit * as_row(gain_ref)).astype(BF)
            pay_ref[s, 1] = (live * cot_ref[s].astype(F32)).astype(BF)
            to = out0_hbm.at[s] if s < first else out1_hbm.at[s - first]
            copies.append(pltpu.make_async_copy(pay_ref.at[s], to, out_sem.at[s]))
            copies[-1].start()
        for copy in copies:
            copy.wait()

    return pl.pallas_call(
        kernel,
        out_shape=[jax.ShapeDtypeStruct((n, 2, part, dim), BF) for n in (first, seqs - first)]
        + [jax.ShapeDtypeStruct((unit, dim), BF)] * per,
        in_specs=[SMEM] + [HBM] * 6,
        out_specs=[HBM] * 2 + [VMEM] * per,
        scratch_shapes=[
            pltpu.SMEM(table.shape, jnp.int32),
            pltpu.VMEM(w_out.shape, BF),
            pltpu.VMEM(ids.shape, jnp.int32),
            pltpu.VMEM(gain.shape, F32),
            pltpu.VMEM(x.shape, BF),
            pltpu.VMEM(x.shape, BF),
            pltpu.VMEM((seqs, 2, part, dim), BF),
            pltpu.SemaphoreType.DMA((4,)),
            pltpu.SemaphoreType.DMA((seqs, 2)),
            pltpu.SemaphoreType.DMA((seqs,)),
        ],
        cost_estimate=SMALL,
        compiler_params=pltpu.CompilerParams(vmem_limit_bytes=32 * MIB),
        name="before",
    )(at, *hbm(table, w_out, ids, gain, x, cot))


def join(at, got, wo_parts, seqs, part):
    count, high, wide = got.shape
    unit = high - 2
    dim = count * unit
    nb = count // SLOTS

    def kernel(at_ref, got_ref, *refs):
        ins, (w_ref, wo_ref, ids_ref, all_ref) = refs[:-4], refs[-4:]

        def move(i, carry):
            all_ref[i] = got_ref[i, :unit]
            return carry

        lax.fori_loop(0, count, move, 0)
        w_ref[...] = all_ref[...].reshape(dim, wide).T
        for ref, (_, masks) in zip(ins, wo_parts):
            for i, mask in enumerate(masks):
                wo_ref[at_ref[2] ^ mask] = ref[i]
        for slot in range(SLOTS):
            i = at_ref[2] * SLOTS + slot
            row = jnp.concatenate([got_ref[i, unit : unit + 1], got_ref[i, unit + 1 :]], axis=1)
            row = row.astype(F32).astype(jnp.int32)
            for s in range(seqs):
                ids_ref[s, :, slot * part : (slot + 1) * part] = row[:, s * part : (s + 1) * part]

    return pl.pallas_call(
        kernel,
        out_shape=[
            jax.ShapeDtypeStruct((wide, dim), BF),
            jax.ShapeDtypeStruct((nb,) + wo_parts[0][0].shape[1:], BF),
            jax.ShapeDtypeStruct((seqs, 1, SLOTS * part), jnp.int32),
        ],
        in_specs=[SMEM] + [VMEM] * (1 + len(wo_parts)),
        out_specs=[VMEM] * 3,
        scratch_shapes=[pltpu.VMEM((count, unit, wide), BF)],
        cost_estimate=SMALL,
        compiler_params=pltpu.CompilerParams(vmem_limit_bytes=32 * MIB),
        name="join",
    )(at, got, *[a for a, _ in wo_parts])


def pack_out(at, table, got):
    unit, dim = got[0].shape
    per = len(got)

    def kernel(at_ref, table_ref, *refs):
        got_refs, (wo_ref, ff_ref, all_ref) = refs[:per], refs[per:]
        for k, ref in enumerate(got_refs):
            all_ref[table_ref[at_ref[0], per + k]] = ref[...]
        wo_ref[...] = all_ref[0]
        for k in range(per - 1):
            ff_ref[k] = all_ref[k + 1]

    return pl.pallas_call(
        kernel,
        out_shape=[jax.ShapeDtypeStruct((unit, dim), BF), jax.ShapeDtypeStruct((per - 1, unit, dim), BF)],
        in_specs=[SMEM] * 2 + [VMEM] * per,
        out_specs=[VMEM] * 2,
        scratch_shapes=[pltpu.VMEM((per, unit, dim), BF)],
        cost_estimate=SMALL,
        name="pack_out",
    )(at, table, *got)


def add_blocks(ref, count, step, start, rows):
    total = ref[start, rows].astype(F32)
    for i in range(1, count):
        total = total + ref[start + i * step, rows].astype(F32)
    return total


def fold(at, low, terms):
    n, _, dim = terms[0][0].shape
    counts = [len(group) for group in terms]
    rows = [group[0].shape[1] for group in terms]

    def kernel(at_ref, *refs):
        ins, (own_ref, *send_refs) = refs[: sum(counts)], refs[sum(counts) :]
        mine = (at_ref[2] >> low) & 3
        k, start = 0, 0
        for count, high in zip(counts, rows):
            for i in range(n // 4):
                for s, to in enumerate([own_ref] + send_refs):
                    block = i * 4 + (mine ^ s)
                    total = ins[k][block].astype(F32)
                    for ref in ins[k + 1 : k + count]:
                        total = total + ref[block].astype(F32)
                    to[i, start : start + high] = total.astype(to.dtype)
            k += count
            start += high

    out = lambda t: jax.ShapeDtypeStruct((n // 4, sum(rows), dim), t)
    return pl.pallas_call(
        kernel,
        out_shape=[out(F32)] + [out(BF)] * 3,
        in_specs=[SMEM] + [VMEM] * sum(counts),
        out_specs=[VMEM] * 4,
        cost_estimate=SMALL,
        compiler_params=pltpu.CompilerParams(vmem_limit_bytes=32 * MIB),
        name="fold",
    )(at, *sum(terms, []))


def split_rows(odd, grad, send_ref, keep_ref):
    parts, rows, _ = send_ref.shape
    for z in range(parts):
        low = grad[2 * z * rows : (2 * z + 1) * rows]
        high = grad[(2 * z + 1) * rows : (2 * z + 2) * rows]
        send_ref[z] = jnp.where(odd, low, high).astype(BF)
        keep_ref[z] = jnp.where(odd, high, low)


def leave(at, table, heads, ffn):
    _, per_ff, unit, dim = ffn.shape
    per = 1 + per_ff

    def kernel(at_ref, table_ref, ffn_ref, *refs):
        terms, outs, all_ref = refs[: len(heads)], refs[len(heads) : -1], refs[-1]
        total = terms[0][0]
        for ref in terms[1:]:
            total = total + ref[0].astype(F32)
        all_ref[0] = total.astype(all_ref.dtype)
        for k in range(per_ff):
            all_ref[k + 1] = ffn_ref[1, k].astype(all_ref.dtype)
        for k in range(per):
            outs[k][...] = all_ref[table_ref[at_ref[0], per + k]].astype(BF)
        for s in range(SLOTS):
            outs[per + s][...] = ffn_ref[0, at_ref[1] ^ s]

    return pl.pallas_call(
        kernel,
        out_shape=[jax.ShapeDtypeStruct((unit, dim), BF)] * (per + SLOTS),
        in_specs=[SMEM] * 2 + [VMEM] * (1 + len(heads)),
        out_specs=[VMEM] * (per + SLOTS),
        scratch_shapes=[pltpu.VMEM((per, unit, dim), F32)],
        cost_estimate=SMALL,
        name="leave",
    )(at, table, ffn, *heads)


def place(at, table, qkv, up, got):
    count, high, width = qkv.shape
    unit, dim = got[0].shape
    nt = len(up)
    nb = count // nt
    per = len(got)
    local = width // 3
    wide = nt * (width + dim)

    def kernel(at_ref, table_ref, qkv_ref, *refs):
        up_refs, got_refs, (in_ref, out_ref, norm_ref, q_ref, k_ref) = refs[:nt], refs[nt : nt + per], refs[nt + per :]
        for s, ref in enumerate(up_refs):
            to = pl.multiple_of(nt * width + (at_ref[1] ^ s) * dim, 128)
            in_ref[:, pl.ds(to, dim)] = ref[...].astype(F32)
        for t in range(nt):
            total = add_blocks(qkv_ref, nb, nt, t, slice(0, unit))
            for k in range(3):
                in_ref[:, k * nt * local + t * local : k * nt * local + (t + 1) * local] = total[:, k * local : (k + 1) * local]
        for k, ref in enumerate(got_refs):
            out_ref[table_ref[at_ref[0], k]] = ref[...].astype(F32)
        small = add_blocks(qkv_ref, count, 1, 0, slice(unit, high))
        small = small[0:2] + small[2:4]
        tail = dim - width
        norm_ref[...] = jnp.concatenate([small[0:1], small[1:2, :tail]], axis=1).reshape(dim)
        q_ref[...] = small[1:2, tail : tail + HD].reshape(HD)
        k_ref[...] = small[1:2, tail + HD : tail + 2 * HD].reshape(HD)

    return pl.pallas_call(
        kernel,
        out_shape=[
            jax.ShapeDtypeStruct((unit, wide), F32),
            jax.ShapeDtypeStruct((per, unit, dim), F32),
            jax.ShapeDtypeStruct((dim,), F32),
            jax.ShapeDtypeStruct((HD,), F32),
            jax.ShapeDtypeStruct((HD,), F32),
        ],
        in_specs=[SMEM] * 2 + [VMEM] * (1 + nt + per),
        out_specs=[VMEM] * 5,
        cost_estimate=SMALL,
        compiler_params=pltpu.CompilerParams(vmem_limit_bytes=32 * MIB),
        name="place",
    )(at, table, qkv, *up, *got)


def after(start, ids, x, cot, gain, keep, near, far, earlier):
    seqs, part, dim = x.shape
    count = far.shape[0]

    def kernel(ids_ref, x_ref, cot_ref, gain_ref, keep_ref, near_ref, far_ref, *rest):
        out_ref, grad_ref = rest[-2:]
        unit, inverse = normalize(x_ref[0].astype(F32))
        live = column(jnp.where(ids_ref[0] >= 0, 1.0, 0.0))
        branch, gn = (keep_ref[0, 0, j].astype(F32) + near_ref[0, 0, j].astype(F32) + far_ref[0, j].astype(F32) for j in range(2))
        out_ref[0] = (live * (x_ref[0].astype(F32) + branch)).astype(BF)
        grad_ref[0] = (live * cot_ref[0].astype(F32) + norm_back(gn * as_row(gain_ref), unit, inverse)).astype(BF)

    one = pl.BlockSpec((1, part, dim), lambda g: (start + g, 0, 0))
    pair = pl.BlockSpec((1, 1, 2, part, dim), lambda g: (0, g, 0, 0, 0))
    lone = pl.BlockSpec((1, 2, part, dim), lambda g: (g, 0, 0, 0))
    return pl.pallas_call(
        kernel,
        grid=(count,),
        out_shape=[jax.ShapeDtypeStruct(x.shape, BF)] * 2,
        in_specs=[
            pl.BlockSpec((1, 1, part), lambda g: (start + g, 0, 0)), one, one,
            pl.BlockSpec(gain.shape, lambda g: (0,)), pair, pair, lone,
        ]
        + [ANY] * len(earlier),
        out_specs=[one, one],
        input_output_aliases={7 + i: i for i in range(len(earlier))},
        cost_estimate=SMALL,
        compiler_params=pltpu.CompilerParams(vmem_limit_bytes=32 * MIB),
        name="after",
    )(ids.reshape(seqs, 1, part), *hbm(x, cot), gain, *hbm(keep, near, far), *earlier)


def attention_kernel(
    heads, block, last, start,
    at_ref, ids_ref, qg_ref, kg_ref, wqkv_hbm, wo_hbm, *refs,
):
    pays, refs = refs[0], refs[1:]
    if last:
        (acc_sums_ref, fnp_ref, gain_ref, accq_hbm, acco_hbm, hid_hbm, gup_hbm, wff_hbm, wup_hbm), refs = refs[:9], refs[9:]
        (keep_hbm, leave_hbm, sendq_ref, sendo_ref, keepo_ref, sums_ref), refs = refs[:6], refs[6:]
        (hid_ref, gup_ref, wff_ref, wup_ref, res_ref, res_sem, act_sem), refs = refs[:7], refs[7:]
    else:
        (o_hbm, grad_hbm, sums_ref, newq_hbm, newo_hbm), refs = refs[:5], refs[5:]
    (
        wqkv_ref, wo_ref, norm_ref, gb_ref, o_ref, grad_ref, gq_ref, go_ref, raw_ref,
        qt_ref, qn_ref, kt_ref, ka_ref, vt_ref, va_ref, do_ref, dq_ref, dk_ref, dv_ref, pad_ref, vm_ref,
        w_sem, sem, out_sem,
    ) = refs
    seqs, length, dim = norm_ref.shape
    part = length // SLOTS
    width = heads * HD
    blocks = length // block
    loads = [pltpu.make_async_copy(wqkv_hbm, wqkv_ref, w_sem.at[0]), pltpu.make_async_copy(wo_hbm, wo_ref, w_sem.at[1])]
    loads[0].start()

    def pay_copy(s, j, t):
        to = (norm_ref, gb_ref)[j].at[s, pl.ds(t * part, part), :]
        return pltpu.make_async_copy(pays.at[t, s, j], to, sem.at[s, j * SLOTS + t])

    for s in range(seqs):
        for j in range(2):
            for t in range(SLOTS):
                pay_copy(s, j, t).start()
            if s + j == 0:
                loads[1].start()
    if last:
        loads.append(pltpu.make_async_copy(accq_hbm, gq_ref, w_sem.at[2]))
        loads.append(pltpu.make_async_copy(acco_hbm, go_ref, w_sem.at[3]))
        loads.append(pltpu.make_async_copy(wff_hbm, wff_ref, act_sem.at[2 * seqs]))
        loads.append(pltpu.make_async_copy(wup_hbm, wup_ref, act_sem.at[2 * seqs + 1]))
        for copy in loads[2:]:
            copy.start()
        skip = hid_hbm.shape[0] // length - seqs

        def act_copies(s):
            rows = pl.ds(pl.multiple_of((skip + s) * length, length), length)
            return [
                pltpu.make_async_copy(hid_hbm.at[rows, :], hid_ref.at[s], act_sem.at[2 * s]),
                pltpu.make_async_copy(gup_hbm.at[rows, :], gup_ref.at[s], act_sem.at[2 * s + 1]),
            ]

        for s in range(seqs):
            for copy in act_copies(s):
                copy.start()
        outs = Outputs(at_ref[1], keep_hbm, leave_hbm, res_ref, res_sem, wo_ref, wff_ref, wqkv_ref, wup_ref)
        sums_ref[...] = acc_sums_ref[...]
    else:
        gq_ref[...] = jnp.zeros_like(gq_ref)
        go_ref[...] = jnp.zeros_like(go_ref)
        sums_ref[...] = jnp.zeros_like(sums_ref)
    gain_q = column(as_row(qg_ref))
    gain_k = column(as_row(kg_ref))
    marks = lax.broadcasted_iota(jnp.int32, (HD, length), 0)
    v_tail = jnp.where(lax.broadcasted_iota(jnp.int32, (length, HD), 1) < 2, 1.0, 0.0).astype(BF)
    ones = jnp.where(lax.broadcasted_iota(jnp.int32, (16, length), 0) == 0, 1.0, 0.0).astype(BF)
    spot = lax.broadcasted_iota(jnp.int32, (HD, block), 0)
    scale = 1.0 / math.sqrt(HD)
    cut = lambda a, i: a[:, i * block : (i + 1) * block]

    def unit_of(row):
        raw = raw_ref[pl.ds(pl.multiple_of(row, HD), HD), :]
        center = raw - jnp.mean(raw, axis=0, keepdims=True)
        inverse = lax.rsqrt(jnp.mean(center * center, axis=0, keepdims=True) + EPS)
        return center * inverse, inverse

    def lanes(a):
        total = a[:, :128]
        for i in range(1, length // 128):
            total = total + a[:, i * 128 : (i + 1) * 128]
        return total

    def stores(s):
        return [
            pltpu.make_async_copy(o_ref.at[s], o_hbm.at[s], out_sem.at[s, 0]),
            pltpu.make_async_copy(grad_ref.at[s], grad_hbm.at[s], out_sem.at[s, 1]),
        ]

    loads[0].wait()
    loads[1].wait()

    def sequence(s, carry):
        ids = ids_ref[start + s]
        same = marks == ids + 1
        k_tail = jnp.where(same, 1.0, 0.0).T.astype(BF)
        q_tail = jnp.where((same & (ids >= 0)) | (marks > 4), 0.0, -BIG).astype(BF)
        pad = jnp.where(ids < 0, 1.0, 0.0)
        for i in range(blocks):
            pad_ref[i] = cut(pad, i)
        for t in range(SLOTS):
            pay_copy(s, 0, t).wait()
        raw_ref[...] = mm(wqkv_ref[...], norm_ref[s], NT)
        for t in range(SLOTS):
            pay_copy(s, 1, t).wait()
        do_all = mm(wo_ref[...], gb_ref[s], NT).astype(BF)
        for h in range(heads):
            for i in range(blocks):
                do_ref[h * blocks + i] = cut(do_all[h * HD : (h + 1) * HD], i)

        def prepare(h, carry):
            q_unit, _ = unit_of(h * HD)
            q = q_unit * gain_q
            qn = q.T.astype(BF)
            for i in range(blocks):
                qt_ref[h * blocks + i, :HD] = cut(q, i).astype(BF)
                qt_ref[h * blocks + i, HD:] = cut(q_tail, i)
                qn_ref[h * blocks + i] = qn[i * block : (i + 1) * block]
            k_unit, _ = unit_of(width + h * HD)
            k = k_unit * gain_k
            kt_ref[h] = k.astype(BF)
            ka_ref[h, :, :HD] = k.T.astype(BF)
            ka_ref[h, :, HD:] = k_tail
            v = raw_ref[pl.ds(pl.multiple_of(2 * width + h * HD, HD), HD), :]
            vb = v.astype(BF)
            vt_ref[h, :HD] = vb
            vt_ref[h, HD:] = ones
            va_ref[h, :, :HD] = v.T.astype(BF)
            va_ref[h, :, HD:] = v_tail
            vm_ref[h] = jnp.mean(vb.astype(F32), axis=1, keepdims=True)
            dk_ref[h] = jnp.zeros(dk_ref.shape[1:], F32)
            dv_ref[h] = jnp.zeros(dv_ref.shape[1:], F32)
            return carry

        lax.fori_loop(0, heads, prepare, 0, unroll=True)

        def step(n, carry):
            h = n // blocks
            padb = pad_ref[n % blocks]
            e = jnp.exp2(mm(ka_ref[h], qt_ref[n]) * (LOG2E * scale))
            eb = e.astype(BF)
            oa = mm(vt_ref[h], eb)
            inv = 1.0 / (oa[HD : HD + 1] + padb)
            o = oa[:HD] * inv
            dos = (do_ref[n].astype(F32) * inv).astype(BF)
            delta = jnp.sum(dos.astype(F32) * o, axis=0, keepdims=True)
            d0 = delta.astype(BF).astype(F32)
            tail = jnp.where(spot == 0, -d0, jnp.where(spot == 1, d0 - delta, 0.0))
            doa = jnp.concatenate([dos.astype(F32), tail], axis=0)
            ds = (e * mm(va_ref[h], doa.astype(BF))).astype(BF)
            dq_ref[n] = mm(kt_ref[h], ds)
            dk_ref[h] += mm(ds, qn_ref[n])
            dv_ref[h] += mm(dos, eb, NT)
            do_ref[n] = jnp.where(padb > 0, vm_ref[h], o).astype(BF)
            return carry

        lax.fori_loop(0, heads * blocks, step, 0)

        def finish(h, carry):
            rows = lambda at: pl.ds(pl.multiple_of(at + h * HD, HD), HD)
            gq = jnp.concatenate([dq_ref[h * blocks + i] for i in range(blocks)], axis=1)
            gk = dk_ref[h].T
            for k, (g, gain_col) in enumerate(((gq, gain_q), (gk, gain_k))):
                unit, inverse = unit_of(k * width + h * HD)
                g = (g * scale).astype(BF).astype(F32)
                sums_ref[k] += lanes(g * unit)
                g = g * gain_col
                back = inverse * (
                    g - jnp.mean(g, axis=0, keepdims=True) - unit * jnp.mean(g * unit, axis=0, keepdims=True)
                )
                grad_ref[s, rows(k * width), :] = back.astype(BF)
            grad_ref[s, rows(2 * width), :] = dv_ref[h].astype(BF)
            for i in range(blocks):
                o_ref[s, rows(0), pl.ds(i * block, block)] = do_ref[h * blocks + i]
            return carry

        lax.fori_loop(0, heads, finish, 0, unroll=True)
        if last:

            @pl.when(s == 0)
            def _():
                for copy in loads[2:]:
                    copy.wait()

            for copy in act_copies(s):
                copy.wait()
            outs.compute(s, o_ref.at[s], hid_ref.at[s], grad_ref.at[s], gup_ref.at[s])
        else:
            for copy in stores(s):
                copy.start()
        gq_ref[...] += mm(grad_ref[s], norm_ref[s])
        go_ref[...] += mm(o_ref[s], gb_ref[s])
        return carry

    lax.fori_loop(0, seqs, sequence, 0)
    if not last:
        ends = [pltpu.make_async_copy(gq_ref, newq_hbm, w_sem.at[2]), pltpu.make_async_copy(go_ref, newo_hbm, w_sem.at[3])]
        for copy in ends:
            copy.start()
        for copy in ends:
            copy.wait()
        for s in range(seqs):
            for copy in stores(s):
                copy.wait()
        return
    outs.wait()
    g_q = gq_ref[...]
    first_row = (jnp.sum(wqkv_ref[...].astype(F32) * g_q, axis=0, keepdims=True) + fnp_ref[...]) / as_row(gain_ref)
    second_row = jnp.concatenate([jnp.sum(sums_ref[k].T, axis=0, keepdims=True) for k in range(2)], axis=1)
    wide = 3 * width
    line = jnp.concatenate([first_row[:, wide:], second_row, jnp.zeros((1, 2 * wide - dim - 2 * HD), F32)], axis=1)
    small = jnp.concatenate([first_row[:, :wide], line], axis=0)
    high = small.astype(BF)
    small = jnp.concatenate([high.astype(F32), small - high.astype(F32)], axis=0).astype(BF)
    g_q = g_q.T.astype(BF)
    count, rows, _ = sendq_ref.shape
    rows = rows - 4
    for i in range(count):
        sendq_ref[i, :rows] = g_q[i * rows : (i + 1) * rows]
        sendq_ref[i, rows:] = small
    split_rows((at_ref[2] & 1) > 0, go_ref[...], sendo_ref, keepo_ref)


def attention(at, start, ids, wqkv, wo, qg, kg, pays, count, more=()):
    wide, dim = wqkv.shape
    width = wo.shape[0]
    heads = width // HD
    _, seqs, _, part, _ = pays.shape
    length = part * SLOTS
    block = 1024
    blocks = length // block
    last = bool(more)
    ins = [at, ids, qg, kg, wqkv, wo, *hbm(pays), *more[:3], *hbm(*more[3:])]
    specs = [SMEM] + [VMEM] * 3 + [ANY] * 2 + [HBM] + ([VMEM] * 3 + [HBM] * 6 if last else [])
    scratch = []
    if last:
        outs = [jax.ShapeDtypeStruct((SLOTS // 2, seqs, 2, part, dim), BF)] * 2
        outs += [jax.ShapeDtypeStruct((count, dim // count + 4, wide), BF)]
        outs += [jax.ShapeDtypeStruct((count // (2 * SLOTS), SLOTS * width // count, dim), t) for t in (BF, F32)]
        scratch = [pltpu.VMEM((2, HD, 128), F32)]
        scratch += [pltpu.VMEM((seqs, length, dim), BF)] * 2 + [pltpu.VMEM((dim, dim), BF)] * 2
        scratch += Outputs.scratch(seqs, length, dim) + [pltpu.SemaphoreType.DMA((2 * seqs + 2,))]
    else:
        outs = [jax.ShapeDtypeStruct((seqs, width, length), BF), jax.ShapeDtypeStruct((seqs, wide, length), BF)]
        outs += [
            jax.ShapeDtypeStruct((2, HD, 128), F32),
            jax.ShapeDtypeStruct((wide, dim), F32),
            jax.ShapeDtypeStruct((width, dim), F32),
        ]
    flops = seqs * (2 * length * dim * width * 8 + heads * 6 * 2 * length * length * HD)
    return pl.pallas_call(
        functools.partial(attention_kernel, heads, block, last, start),
        out_shape=outs,
        in_specs=specs,
        out_specs=[HBM] * 2 + ([VMEM] * 3 if last else [VMEM, HBM, HBM]),
        scratch_shapes=scratch
        + [
            pltpu.VMEM((wide, dim), BF),
            pltpu.VMEM((width, dim), BF),
            pltpu.VMEM((seqs, length, dim), BF),
            pltpu.VMEM((seqs, length, dim), BF),
            pltpu.VMEM((seqs, width, length), BF),
            pltpu.VMEM((seqs, wide, length), BF),
            pltpu.VMEM((wide, dim), F32),
            pltpu.VMEM((width, dim), F32),
            pltpu.VMEM((wide, length), F32),
            pltpu.VMEM((heads * blocks, 2 * HD, block), BF),
            pltpu.VMEM((heads * blocks, block, HD), BF),
            pltpu.VMEM((heads, HD, length), BF),
            pltpu.VMEM((heads, length, 2 * HD), BF),
            pltpu.VMEM((heads, HD + 16, length), BF),
            pltpu.VMEM((heads, length, 2 * HD), BF),
            pltpu.VMEM((heads * blocks, HD, block), BF),
            pltpu.VMEM((heads * blocks, HD, block), F32),
            pltpu.VMEM((heads, length, HD), F32),
            pltpu.VMEM((heads, HD, length), F32),
            pltpu.VMEM((blocks, 1, block), F32),
            pltpu.VMEM((heads, HD, 1), F32),
            pltpu.SemaphoreType.DMA((4,)),
            pltpu.SemaphoreType.DMA((seqs, 2 * SLOTS)),
            pltpu.SemaphoreType.DMA((seqs, 2)),
        ],
        cost_estimate=LARGE,
        compiler_params=pltpu.CompilerParams(vmem_limit_bytes=40 * MIB),
        name="attention",
    )(*ins)


def ffn_kernel(block, groups, plan, at_ref, wup_hbm, wqkv_hbm, wo_hbm, o_hbm, gq_hbm, *refs):
    pieces, refs = refs[: len(plan)], refs[len(plan) :]
    pays, refs = refs[: len(groups)], refs[len(groups) :]
    (hid_hbm, gup_hbm, wff_hbm, keep_hbm, leave_hbm, send_ref, np_ref), refs = refs[:7], refs[7:]
    norm_ref, gb_ref, hid_ref, gup_ref, wup_ref, wff_ref, gin_ref, gff_ref, sem, out_sem, w_sem, *refs = refs
    wqkv_ref, wo_ref, o_ref, gq_ref, res_ref, res_sem, late_sem = refs
    dim = wup_ref.shape[0]
    part = pays[0].shape[3]
    total = norm_ref.shape[0]
    weights = [pltpu.make_async_copy(wup_hbm, wup_ref, w_sem.at[0])]
    rows = send_ref.shape[2]
    for ref, masks in zip(pieces, plan):
        for i, mask in enumerate(masks):
            to = wff_ref.at[pl.ds(pl.multiple_of((at_ref[2] ^ mask) * rows, rows), rows), :]
            weights.append(pltpu.make_async_copy(ref.at[i], to, w_sem.at[len(weights)]))
    for copy in weights:
        copy.start()
    n = 0
    for g, seqs in enumerate(groups):
        for s in range(seqs):
            for t in range(SLOTS):
                for k, to in enumerate((norm_ref, gb_ref)):
                    source = pays[g].at[t, s, k]
                    pltpu.make_async_copy(source, to.at[pl.ds(n * part, part), :], sem.at[k, n]).start()
                n += 1
    late = [
        pltpu.make_async_copy(a, b, late_sem.at[i])
        for i, (a, b) in enumerate(((wqkv_hbm, wqkv_ref), (wo_hbm, wo_ref), (o_hbm, o_ref), (gq_hbm, gq_ref)))
    ]
    for copy in late:
        copy.start()
    gin_ref[...] = jnp.zeros_like(gin_ref)
    gff_ref[...] = jnp.zeros_like(gff_ref)
    for copy in weights:
        copy.wait()
    joined = pltpu.make_async_copy(wff_ref, wff_hbm, w_sem.at[0])
    joined.start()
    c0 = math.sqrt(2.0 / math.pi)
    c1 = 0.044715

    def outs(i):
        at_rows = pl.ds(pl.multiple_of(i * block, block), block)
        return (
            pltpu.make_async_copy(hid_ref.at[at_rows, :], hid_hbm.at[at_rows, :], out_sem.at[0, i]),
            pltpu.make_async_copy(gup_ref.at[at_rows, :], gup_hbm.at[at_rows, :], out_sem.at[1, i]),
        )

    def arrive(i):
        for j in range(block // part):
            for k, to in enumerate((norm_ref, gb_ref)):
                pltpu.make_async_copy(pays[0].at[0, 0, 0], to.at[pl.ds(0, part), :], sem.at[k, i * (block // part) + j]).wait()

    def rows_of(i):
        return pl.ds(pl.multiple_of(i * block, block), block)

    def units(i):
        up = mm(norm_ref[rows_of(i), :], wup_ref[...])
        gh = mm(gb_ref[rows_of(i), :], wff_ref[...], NT)
        sq = up * up
        t = jnp.tanh(up * (c0 + (c0 * c1) * sq))
        half = 0.5 + 0.5 * t
        hid_ref[rows_of(i), :] = (up * half).astype(BF)
        gup_ref[rows_of(i), :] = (gh * (half + (0.5 * up) * (1.0 - t * t) * (c0 + (3.0 * c0 * c1) * sq))).astype(BF)

    def grads(i):
        gin_ref[...] += mm(norm_ref[rows_of(i), :], gup_ref[rows_of(i), :], TN)
        gff_ref[...] += mm(hid_ref[rows_of(i), :], gb_ref[rows_of(i), :], TN)

    count = total // block
    arrive(0)
    units(0)

    def step(i, carry):
        for copy in outs(i - 1):
            copy.start()
        arrive(i)
        grads(i - 1)
        units(i)
        return carry

    lax.fori_loop(1, count, step, 0)
    for copy in outs(count - 1):
        copy.start()
    grads(count - 1)
    for copy in late:
        copy.wait()
    results = Outputs(at_ref[1], keep_hbm, leave_hbm, res_ref, res_sem, wo_ref, wff_ref, wqkv_ref, wup_ref)
    length = SLOTS * part

    def result(s, carry):
        rows_s = pl.ds(pl.multiple_of(s * length, length), length)
        results.compute(s, o_ref.at[s], hid_ref.at[rows_s, :], gq_ref.at[s], gup_ref.at[rows_s, :])
        return carry

    lax.fori_loop(0, results.seqs, result, 0)
    line = jnp.sum(wup_ref[...].astype(F32) * gin_ref[...], axis=1, keepdims=True)
    np_ref[...] = jnp.broadcast_to(line, (dim, 128)).T[0:1]
    for b in range(dim // rows):
        for k, g in enumerate((gin_ref, gff_ref)):
            send_ref[b, k] = g[b * rows : (b + 1) * rows, :].astype(BF)
    joined.wait()
    results.wait()

    def drain(i, carry):
        for copy in outs(i):
            copy.wait()
        return carry

    lax.fori_loop(0, total // block, drain, 0)


def ffn(at, wup, ff_parts, groups, count, wqkv, wo, o, gq, block=512):
    dim, units = wup.shape
    sizes = [g.shape[1] for g in groups]
    part = groups[0].shape[3]
    total = SLOTS * part * sum(sizes)
    pieces = groups
    act = jax.ShapeDtypeStruct((total, units), BF)
    return pl.pallas_call(
        functools.partial(ffn_kernel, block, sizes, [masks for _, masks in ff_parts]),
        out_shape=[
            act,
            act,
            jax.ShapeDtypeStruct((units, dim), BF),
            *[jax.ShapeDtypeStruct((SLOTS // 2, o.shape[0], 2, part, dim), BF)] * 2,
            jax.ShapeDtypeStruct((count, 2, units // count, dim), BF),
            jax.ShapeDtypeStruct((1, dim), F32),
        ],
        in_specs=[SMEM] + [ANY] * 3 + [HBM] * (2 + len(ff_parts) + len(pieces)),
        out_specs=[HBM] * 5 + [VMEM] * 2,
        scratch_shapes=[
            pltpu.VMEM((total, dim), BF),
            pltpu.VMEM((total, dim), BF),
            pltpu.VMEM((total, units), BF),
            pltpu.VMEM((total, units), BF),
            pltpu.VMEM((dim, units), BF),
            pltpu.VMEM((units, dim), BF),
            pltpu.VMEM((dim, units), F32),
            pltpu.VMEM((units, dim), F32),
            pltpu.SemaphoreType.DMA((2, total // part)),
            pltpu.SemaphoreType.DMA((2, total // block)),
            pltpu.SemaphoreType.DMA((1 + count,)),
            *[pltpu.VMEM(a.shape, BF) for a in (wqkv, wo, o, gq)],
            *Outputs.scratch(o.shape[0], SLOTS * part, dim),
            pltpu.SemaphoreType.DMA((4,)),
        ],
        cost_estimate=LARGE,
        compiler_params=pltpu.CompilerParams(vmem_limit_bytes=58 * MIB),
        name="ffn",
    )(at, wup, wqkv, wo, *hbm(o, gq, *[a for a, _ in ff_parts], *pieces))


class Outputs:
    def __init__(self, me, keep, send, res, sem, wo, wff, wqkv, wup):
        self.me = me
        self.keep, self.send, self.res, self.sem = keep, send, res, sem
        self.wo, self.wff, self.wqkv, self.wup = wo, wff, wqkv, wup
        self.seqs, _, self.length, _ = res.shape

    @staticmethod
    def scratch(seqs, length, dim):
        return [pltpu.VMEM((seqs, 2, length, dim), BF), pltpu.SemaphoreType.DMA((seqs, 2, SLOTS))]

    def moves(self, s, i):
        half = self.length // 2
        part = half // 2
        out = []
        for j in range(2):
            for k, to in enumerate((self.keep, self.send)):
                rows = pl.ds(pl.multiple_of(i * half + (k ^ (self.me & 1)) * part, part), part)
                source = self.res.at[s, j, rows, :]
                out.append(pltpu.make_async_copy(source, to.at[i ^ (self.me >> 1), s, j], self.sem.at[s, j, 2 * i + k]))
        return out

    def compute(self, s, o, hid, gq, gu):
        half = self.length // 2

        def step(i, carry):
            rows = pl.ds(pl.multiple_of(i * half, half), half)
            branch = mm(o[:, rows], self.wo[...], TN) + mm(hid[rows, :], self.wff[...])
            self.res[s, 0, rows, :] = branch.astype(BF)
            gn = mm(gq[:, rows], self.wqkv[...], TN) + mm(gu[rows, :], self.wup[...], NT)
            self.res[s, 1, rows, :] = gn.astype(BF)
            for copy in self.moves(s, i):
                copy.start()
            return carry

        lax.fori_loop(0, 2, step, 0)

    def wait(self):
        for s in range(self.seqs):
            for i in range(2):
                for copy in self.moves(s, i):
                    copy.wait()


def swap(value, axis, count, mask):
    return lax.ppermute(value, axis, [(i, i ^ mask) for i in range(count)])


def tie(value, *after):
    return lax.optimization_barrier((value,) + after)[0]


def bit_groups(count):
    bits = list(range(count.bit_length() - 1))[::-1]
    groups = []
    while bits:
        take = 2 if len(bits) > 1 else 1
        groups.append(bits[:take])
        bits = bits[take:]
    assert len(groups[-1]) == 1
    return groups


def gather_batch(block, count, groups, hold=None):
    held, masks = block[None], [0]
    for bits in groups:
        low = bits[-1]
        if hold is not None and bits is groups[-1]:
            held = tie(held, hold)
        parts = [(held, masks)]
        for s in range(1, 1 << len(bits)):
            parts.append((swap(held, "batch", count, s << low), [m ^ (s << low) for m in masks]))
        held = jnp.concatenate([a for a, _ in parts], axis=0)
        masks = sum((m for _, m in parts), [])
    return parts


def matchings(edges, devices, per_device):
    left = [[] for _ in range(devices)]
    for e, (source, _, _) in enumerate(edges):
        left[source].append(e)
    rounds = []
    for _ in range(per_device):
        owner = [-1] * devices

        def place(source, seen):
            for e in left[source]:
                target = edges[e][1]
                if target in seen:
                    continue
                seen.add(target)
                if owner[target] < 0 or place(edges[owner[target]][0], seen):
                    owner[target] = e
                    return True
            return False

        for source in range(devices):
            place(source, set())
        rounds.append(list(owner))
        for e in owner:
            left[edges[e][0]].remove(e)
    return rounds


def unit_plan(nb, nt, rows, width, hidden):
    unit = math.gcd(math.gcd(rows, width // nt), hidden // nt)
    per = rows // unit
    head_units, hid_units = width // nt // unit, hidden // nt // unit
    assert head_units == nb and hid_units % nb == 0
    c = hid_units // nb
    edges = []
    for t in range(nt):
        for b in range(nb):
            want = [t * head_units + b]
            want += [nt * head_units + t * hid_units + b * c + i for i in range(c)]
            for slot, u in enumerate(want):
                edges.append((u // per, b * nt + t, (u % per, slot)))
    table = np.zeros((nb * nt, 2 * per), np.int32)
    perms = []
    for k, owner in enumerate(matchings(edges, nb * nt, per)):
        perms.append([(edges[e][0], edges[e][1]) for e in owner])
        for e in owner:
            table[edges[e][0], k] = edges[e][2][0]
            table[edges[e][1], per + k] = edges[e][2][1]
    return unit, per, perms, table


def per_device(
    nb, nt, patches, image_ids, cotangent, norm_gain, query_gain, key_gain, in_weight, out_weight
):
    seqs, part, dim = patches.shape
    width = H * HD
    local = width // nt
    units = (in_weight.shape[1] - 3 * width) // nt
    rows_in = in_weight.shape[0]
    unit, per, perms, table = unit_plan(nb, nt, out_weight.shape[0], width, units * nt)
    assert nt == SLOTS and units == dim and unit == rows_in and dim == nt * local and per == nt + 1
    both = ("batch", "tok")
    me_b = lax.axis_index("batch")
    me_t = lax.axis_index("tok")
    at = jnp.stack([me_b * nt + me_t, me_t, me_b])
    table = jnp.asarray(table)
    gain = norm_gain

    def exchange(value, axis):
        return lax.all_to_all(value, axis, split_axis=0, concat_axis=0, tiled=True)

    groups = bit_groups(nb)

    lead = 2
    a_src, u_src = prepare(image_ids, in_weight, nb, nt)
    a_got = exchange(a_src.reshape(nb * nt, rows_in + 2, 3 * local), both)
    own0, own1, *unit_sends = before(
        at, table, out_weight.reshape(per, unit, dim), image_ids, gain, tie(patches, a_src), cotangent, lead
    )
    got = [lax.ppermute(v, both, perm) for v, perm in zip(unit_sends, perms)]
    wo_src, ff_src = pack_out(at, table, got)
    slots0 = lax.all_gather(own0, "tok", axis=0)
    slots1 = lax.all_gather(own1, "tok", axis=0)
    wo_parts = gather_batch(wo_src, nb, groups, a_got)
    ff_parts = gather_batch(ff_src.reshape((per - 1) * unit, dim), nb, groups[::-1])
    wqkv, wo, ids = join(at, a_got, wo_parts, seqs, part)
    wo = wo.reshape(local, dim)
    wup = exchange(tie(u_src, a_got).reshape(nb * nt, unit, dim), both).reshape(dim, units)

    qg, kg = query_gain, key_gain

    def leave_chip(keep, near, *hold):
        value = (keep[1].astype(F32) + near[1].astype(F32)).astype(BF)
        return value, swap(tie(value, *hold) if hold else value, "tok", nt, 2)

    o0, gq0, sums, acc_q, acc_o = attention(at, 0, ids, wqkv, tie(wo, ff_parts[0][0]), qg, kg, slots0, nb * nt)
    hid, gup, wff, keep0, send0, f_grad, f_np = ffn(
        at, tie(wup, o0), ff_parts, [slots0, slots1], nb, wqkv, wo, o0, gq0
    )
    f_mine = lax.psum_scatter(f_grad, "batch", scatter_dimension=0, tiled=True).reshape(2, nt, unit, dim)
    near0 = swap(send0, "tok", nt, 1)
    value0, away0 = leave_chip(keep0, near0)
    keep1, send1, a_q, a_send, a_keep = attention(
        at, lead, ids, wqkv, tie(wo, value0), qg, kg, slots1, nb * nt,
        (sums, f_np, gain, acc_q, acc_o, hid, gup, wff, wup),
    )
    a_came = swap(a_send, "batch", nb, 1)
    terms = [a_keep, a_came]
    for bits in groups[:-1][::-1]:
        own, *sends = fold(at, bits[-1], [terms])
        terms = [own] + [swap(value, "batch", nb, (s + 1) << bits[-1]) for s, value in enumerate(sends)]
    near1 = swap(tie(send1, away0, *terms[1:]), "tok", nt, 1)
    a_q = exchange(a_q, both)
    value1, away1 = leave_chip(keep1, near1)
    earlier = after(0, image_ids, patches, cotangent, gain, keep0, near0, away0, [])
    outs = leave(at, table, terms, tie(f_mine, *earlier))
    sends, up = outs[:per], outs[per:]
    up = [up[0]] + [swap(up[s], "tok", nt, s) for s in range(1, nt)]
    got = [lax.ppermute(v, both, [(b, a) for a, b in perm]) for v, perm in zip(sends, perms)]
    earlier = after(lead, image_ids, patches, cotangent, gain, keep1, near1, away1, earlier)
    in_grad, out_grad, norm_grad, query_grad, key_grad = place(at, table, tie(a_q, *earlier), up, got)

    block_out, patch_grad = earlier
    return (
        block_out,
        patch_grad,
        norm_grad,
        query_grad,
        key_grad,
        in_grad,
        out_grad.reshape(per * unit, dim),
    )


def solution(mesh):
    rows = P("batch", "tok", None)
    weights = P(("batch", "tok"), None)
    return jax.shard_map(
        functools.partial(per_device, mesh.shape["batch"], mesh.shape["tok"]),
        mesh=mesh,
        in_specs=(rows, P("batch", "tok"), rows, P(), P(), P(), weights, weights),
        out_specs=(rows, rows, P(), P(), P(), weights, weights),
        check_vma=False,
    )
```

```python
import functools
import math

import jax
import jax.numpy as jnp
import numpy as np
from jax import lax
from jax.experimental import pallas as pl
from jax.experimental.pallas import tpu as pltpu
from jax.sharding import PartitionSpec as P

H = 12
HD = 64
SLOTS = 4
EPS = 1e-06
BIG = 2048.0
LOG2E = 1.4426950408889634
BF = jnp.bfloat16
F32 = jnp.float32
NN = (((1,), (0,)), ((), ()))
NT = (((1,), (1,)), ((), ()))
TN = (((0,), (0,)), ((), ()))
MIB = 1 << 20
SMALL = pl.CostEstimate(flops=1, transcendentals=0, bytes_accessed=1)
LARGE = pl.CostEstimate(flops=60_000_000_000, transcendentals=0, bytes_accessed=1)

VMEM = pl.BlockSpec(memory_space=pltpu.VMEM)
SMEM = pl.BlockSpec(memory_space=pltpu.SMEM)
ANY = pl.BlockSpec(memory_space=pl.ANY)
HBM = pl.BlockSpec(memory_space=pltpu.HBM)


def hbm(*arrays):
    return [pltpu.with_memory_space_constraint(a, pltpu.HBM) for a in arrays]


def mm(a, b, dims=NN):
    return lax.dot_general(a, b, dims, preferred_element_type=F32)


def normalize(values):
    center = values - jnp.mean(values, axis=-1, keepdims=True)
    inverse = lax.rsqrt(jnp.mean(center * center, axis=-1, keepdims=True) + EPS)
    return center * inverse, inverse


def norm_back(grad_unit, unit_rows, inverse):
    return inverse * (
        grad_unit
        - jnp.mean(grad_unit, axis=-1, keepdims=True)
        - unit_rows * jnp.mean(grad_unit * unit_rows, axis=-1, keepdims=True)
    )


def as_row(ref):
    return ref[...].reshape(1, ref.shape[0])


def column(row):
    return jnp.broadcast_to(row, (8, row.shape[1])).T[:, 0:1]


def prepare(ids, w_in, nb, nt):
    rows, wide = w_in.shape
    seqs, part = ids.shape
    width = H * HD
    local = width // nt
    units = (wide - 3 * width) // nt

    def kernel(ids_hbm, win_hbm, a_hbm, u_hbm, ids_ref, win_ref, a_ref, u_ref, in_sem, a_sem, u_sem):
        loads = [pltpu.make_async_copy(win_hbm, win_ref, in_sem.at[0]), pltpu.make_async_copy(ids_hbm, ids_ref, in_sem.at[1])]
        for copy in loads:
            copy.start()
        for copy in loads:
            copy.wait()
        row = jnp.concatenate([ids_ref[s : s + 1, :] for s in range(seqs)], axis=1).astype(F32).astype(BF)
        first = 3 * local
        second = jnp.concatenate([row[:, first:].astype(F32), jnp.zeros((1, 2 * first - seqs * part), F32)], axis=1).astype(BF)
        for t in range(nt):
            for k in range(3):
                a_ref[t, :rows, k * local : (k + 1) * local] = win_ref[:, k * width + t * local : k * width + (t + 1) * local]
            a_ref[t, rows : rows + 1] = row[:, :first]
            a_ref[t, rows + 1 :] = second
        for b in range(nb):
            pltpu.make_async_copy(a_ref, a_hbm.at[b], a_sem.at[b]).start()
        for t in range(nt):
            u_ref[t] = win_ref[:, 3 * width + t * units : 3 * width + (t + 1) * units]
        for b in range(nb):
            pltpu.make_async_copy(u_ref, u_hbm.at[b], u_sem.at[b]).start()
        for b in range(nb):
            pltpu.make_async_copy(a_ref, a_hbm.at[b], a_sem.at[b]).wait()
            pltpu.make_async_copy(u_ref, u_hbm.at[b], u_sem.at[b]).wait()

    return pl.pallas_call(
        kernel,
        out_shape=[
            jax.ShapeDtypeStruct((nb, nt, rows + 2, 3 * local), BF),
            jax.ShapeDtypeStruct((nb, nt, rows, units), BF),
        ],
        in_specs=[HBM] * 2,
        out_specs=[HBM] * 2,
        scratch_shapes=[
            pltpu.VMEM(ids.shape, jnp.int32),
            pltpu.VMEM(w_in.shape, BF),
            pltpu.VMEM((nt, rows + 2, 3 * local), BF),
            pltpu.VMEM((nt, rows, units), BF),
            pltpu.SemaphoreType.DMA((2,)),
            pltpu.SemaphoreType.DMA((nb,)),
            pltpu.SemaphoreType.DMA((nb,)),
        ],
        cost_estimate=SMALL,
        compiler_params=pltpu.CompilerParams(vmem_limit_bytes=16 * MIB),
        name="prepare",
    )(*hbm(ids, w_in))


def before(at, table, w_out, ids, gain, x, cot, first):
    seqs, part, dim = x.shape

    per, unit, _ = w_out.shape

    def kernel(at_ref, table_hbm, wout_hbm, ids_hbm, gain_hbm, x_hbm, cot_hbm, out0_hbm, out1_hbm, *refs):
        unit_refs, (table_ref, wout_ref, ids_ref, gain_ref, x_ref, cot_ref, pay_ref, in_sem, x_sem, out_sem) = refs[:per], refs[per:]
        ins = [
            pltpu.make_async_copy(a, b, in_sem.at[i])
            for i, (a, b) in enumerate(((table_hbm, table_ref), (wout_hbm, wout_ref), (ids_hbm, ids_ref), (gain_hbm, gain_ref)))
        ]
        loads = [
            [pltpu.make_async_copy(a.at[s], b.at[s], x_sem.at[s, k]) for k, (a, b) in enumerate(((x_hbm, x_ref), (cot_hbm, cot_ref)))]
            for s in range(seqs)
        ]
        for copy in ins + sum(loads, []):
            copy.start()
        for copy in ins:
            copy.wait()
        for k, ref in enumerate(unit_refs):
            ref[...] = wout_ref[table_ref[at_ref[0], k]]
        copies = []
        for s in range(seqs):
            for copy in loads[s]:
                copy.wait()
            unit, _ = normalize(x_ref[s].astype(F32))
            live = column(jnp.where(ids_ref[s : s + 1, :] >= 0, 1.0, 0.0))
            pay_ref[s, 0] = (unit * as_row(gain_ref)).astype(BF)
            pay_ref[s, 1] = (live * cot_ref[s].astype(F32)).astype(BF)
            to = out0_hbm.at[s] if s < first else out1_hbm.at[s - first]
            copies.append(pltpu.make_async_copy(pay_ref.at[s], to, out_sem.at[s]))
            copies[-1].start()
        for copy in copies:
            copy.wait()

    return pl.pallas_call(
        kernel,
        out_shape=[jax.ShapeDtypeStruct((n, 2, part, dim), BF) for n in (first, seqs - first)]
        + [jax.ShapeDtypeStruct((unit, dim), BF)] * per,
        in_specs=[SMEM] + [HBM] * 6,
        out_specs=[HBM] * 2 + [VMEM] * per,
        scratch_shapes=[
            pltpu.SMEM(table.shape, jnp.int32),
            pltpu.VMEM(w_out.shape, BF),
            pltpu.VMEM(ids.shape, jnp.int32),
            pltpu.VMEM(gain.shape, F32),
            pltpu.VMEM(x.shape, BF),
            pltpu.VMEM(x.shape, BF),
            pltpu.VMEM((seqs, 2, part, dim), BF),
            pltpu.SemaphoreType.DMA((4,)),
            pltpu.SemaphoreType.DMA((seqs, 2)),
            pltpu.SemaphoreType.DMA((seqs,)),
        ],
        cost_estimate=SMALL,
        compiler_params=pltpu.CompilerParams(vmem_limit_bytes=32 * MIB),
        name="before",
    )(at, *hbm(table, w_out, ids, gain, x, cot))


def join(at, got, wo_parts, seqs, part):
    count, high, wide = got.shape
    unit = high - 2
    dim = count * unit
    nb = count // SLOTS

    def kernel(at_ref, got_ref, *refs):
        ins, (w_ref, wo_ref, ids_ref, all_ref) = refs[:-4], refs[-4:]

        def move(i, carry):
            all_ref[i] = got_ref[i, :unit]
            return carry

        lax.fori_loop(0, count, move, 0)
        w_ref[...] = all_ref[...].reshape(dim, wide).T
        for ref, (_, masks) in zip(ins, wo_parts):
            for i, mask in enumerate(masks):
                wo_ref[at_ref[2] ^ mask] = ref[i]
        for slot in range(SLOTS):
            i = at_ref[2] * SLOTS + slot
            row = jnp.concatenate([got_ref[i, unit : unit + 1], got_ref[i, unit + 1 :]], axis=1)
            row = row.astype(F32).astype(jnp.int32)
            for s in range(seqs):
                ids_ref[s, :, slot * part : (slot + 1) * part] = row[:, s * part : (s + 1) * part]

    return pl.pallas_call(
        kernel,
        out_shape=[
            jax.ShapeDtypeStruct((wide, dim), BF),
            jax.ShapeDtypeStruct((nb,) + wo_parts[0][0].shape[1:], BF),
            jax.ShapeDtypeStruct((seqs, 1, SLOTS * part), jnp.int32),
        ],
        in_specs=[SMEM] + [VMEM] * (1 + len(wo_parts)),
        out_specs=[VMEM] * 3,
        scratch_shapes=[pltpu.VMEM((count, unit, wide), BF)],
        cost_estimate=SMALL,
        compiler_params=pltpu.CompilerParams(vmem_limit_bytes=32 * MIB),
        name="join",
    )(at, got, *[a for a, _ in wo_parts])


def pack_out(at, table, got):
    unit, dim = got[0].shape
    per = len(got)

    def kernel(at_ref, table_ref, *refs):
        got_refs, (wo_ref, ff_ref, all_ref) = refs[:per], refs[per:]
        for k, ref in enumerate(got_refs):
            all_ref[table_ref[at_ref[0], per + k]] = ref[...]
        wo_ref[...] = all_ref[0]
        for k in range(per - 1):
            ff_ref[k] = all_ref[k + 1]

    return pl.pallas_call(
        kernel,
        out_shape=[jax.ShapeDtypeStruct((unit, dim), BF), jax.ShapeDtypeStruct((per - 1, unit, dim), BF)],
        in_specs=[SMEM] * 2 + [VMEM] * per,
        out_specs=[VMEM] * 2,
        scratch_shapes=[pltpu.VMEM((per, unit, dim), BF)],
        cost_estimate=SMALL,
        name="pack_out",
    )(at, table, *got)


def add_blocks(ref, count, step, start, rows):
    total = ref[start, rows].astype(F32)
    for i in range(1, count):
        total = total + ref[start + i * step, rows].astype(F32)
    return total


def fold(at, low, terms):
    n, _, dim = terms[0][0].shape
    counts = [len(group) for group in terms]
    rows = [group[0].shape[1] for group in terms]

    def kernel(at_ref, *refs):
        ins, (own_ref, *send_refs) = refs[: sum(counts)], refs[sum(counts) :]
        mine = (at_ref[2] >> low) & 3
        k, start = 0, 0
        for count, high in zip(counts, rows):
            for i in range(n // 4):
                for s, to in enumerate([own_ref] + send_refs):
                    block = i * 4 + (mine ^ s)
                    total = ins[k][block].astype(F32)
                    for ref in ins[k + 1 : k + count]:
                        total = total + ref[block].astype(F32)
                    to[i, start : start + high] = total.astype(to.dtype)
            k += count
            start += high

    out = lambda t: jax.ShapeDtypeStruct((n // 4, sum(rows), dim), t)
    return pl.pallas_call(
        kernel,
        out_shape=[out(F32)] + [out(BF)] * 3,
        in_specs=[SMEM] + [VMEM] * sum(counts),
        out_specs=[VMEM] * 4,
        cost_estimate=SMALL,
        compiler_params=pltpu.CompilerParams(vmem_limit_bytes=32 * MIB),
        name="fold",
    )(at, *sum(terms, []))


def split_rows(odd, grad, send_ref, keep_ref):
    parts, rows, _ = send_ref.shape
    for z in range(parts):
        low = grad[2 * z * rows : (2 * z + 1) * rows]
        high = grad[(2 * z + 1) * rows : (2 * z + 2) * rows]
        send_ref[z] = jnp.where(odd, low, high).astype(BF)
        keep_ref[z] = jnp.where(odd, high, low)


def leave(at, table, heads, ffn):
    _, per_ff, unit, dim = ffn.shape
    per = 1 + per_ff

    def kernel(at_ref, table_ref, ffn_ref, *refs):
        terms, outs, all_ref = refs[: len(heads)], refs[len(heads) : -1], refs[-1]
        total = terms[0][0]
        for ref in terms[1:]:
            total = total + ref[0].astype(F32)
        all_ref[0] = total.astype(all_ref.dtype)
        for k in range(per_ff):
            all_ref[k + 1] = ffn_ref[1, k].astype(all_ref.dtype)
        for k in range(per):
            outs[k][...] = all_ref[table_ref[at_ref[0], per + k]].astype(BF)
        for s in range(SLOTS):
            outs[per + s][...] = ffn_ref[0, at_ref[1] ^ s]

    return pl.pallas_call(
        kernel,
        out_shape=[jax.ShapeDtypeStruct((unit, dim), BF)] * (per + SLOTS),
        in_specs=[SMEM] * 2 + [VMEM] * (1 + len(heads)),
        out_specs=[VMEM] * (per + SLOTS),
        scratch_shapes=[pltpu.VMEM((per, unit, dim), F32)],
        cost_estimate=SMALL,
        name="leave",
    )(at, table, ffn, *heads)


def place(at, table, qkv, up, got):
    count, high, width = qkv.shape
    unit, dim = got[0].shape
    nt = len(up)
    nb = count // nt
    per = len(got)
    local = width // 3
    wide = nt * (width + dim)

    def kernel(at_ref, table_ref, qkv_ref, *refs):
        up_refs, got_refs, (in_ref, out_ref, norm_ref, q_ref, k_ref) = refs[:nt], refs[nt : nt + per], refs[nt + per :]
        for s, ref in enumerate(up_refs):
            to = pl.multiple_of(nt * width + (at_ref[1] ^ s) * dim, 128)
            in_ref[:, pl.ds(to, dim)] = ref[...].astype(F32)
        for t in range(nt):
            total = add_blocks(qkv_ref, nb, nt, t, slice(0, unit))
            for k in range(3):
                in_ref[:, k * nt * local + t * local : k * nt * local + (t + 1) * local] = total[:, k * local : (k + 1) * local]
        for k, ref in enumerate(got_refs):
            out_ref[table_ref[at_ref[0], k]] = ref[...].astype(F32)
        small = add_blocks(qkv_ref, count, 1, 0, slice(unit, high))
        small = small[0:2] + small[2:4]
        tail = dim - width
        norm_ref[...] = jnp.concatenate([small[0:1], small[1:2, :tail]], axis=1).reshape(dim)
        q_ref[...] = small[1:2, tail : tail + HD].reshape(HD)
        k_ref[...] = small[1:2, tail + HD : tail + 2 * HD].reshape(HD)

    return pl.pallas_call(
        kernel,
        out_shape=[
            jax.ShapeDtypeStruct((unit, wide), F32),
            jax.ShapeDtypeStruct((per, unit, dim), F32),
            jax.ShapeDtypeStruct((dim,), F32),
            jax.ShapeDtypeStruct((HD,), F32),
            jax.ShapeDtypeStruct((HD,), F32),
        ],
        in_specs=[SMEM] * 2 + [VMEM] * (1 + nt + per),
        out_specs=[VMEM] * 5,
        cost_estimate=SMALL,
        compiler_params=pltpu.CompilerParams(vmem_limit_bytes=32 * MIB),
        name="place",
    )(at, table, qkv, *up, *got)


def after(start, ids, x, cot, gain, keep, near, far, earlier):
    seqs, part, dim = x.shape
    count = far.shape[0]

    def kernel(ids_ref, x_ref, cot_ref, gain_ref, keep_ref, near_ref, far_ref, *rest):
        out_ref, grad_ref = rest[-2:]
        unit, inverse = normalize(x_ref[0].astype(F32))
        live = column(jnp.where(ids_ref[0] >= 0, 1.0, 0.0))
        branch, gn = (keep_ref[0, 0, j].astype(F32) + near_ref[0, 0, j].astype(F32) + far_ref[0, j].astype(F32) for j in range(2))
        out_ref[0] = (live * (x_ref[0].astype(F32) + branch)).astype(BF)
        grad_ref[0] = (live * cot_ref[0].astype(F32) + norm_back(gn * as_row(gain_ref), unit, inverse)).astype(BF)

    one = pl.BlockSpec((1, part, dim), lambda g: (start + g, 0, 0))
    pair = pl.BlockSpec((1, 1, 2, part, dim), lambda g: (0, g, 0, 0, 0))
    lone = pl.BlockSpec((1, 2, part, dim), lambda g: (g, 0, 0, 0))
    return pl.pallas_call(
        kernel,
        grid=(count,),
        out_shape=[jax.ShapeDtypeStruct(x.shape, BF)] * 2,
        in_specs=[
            pl.BlockSpec((1, 1, part), lambda g: (start + g, 0, 0)), one, one,
            pl.BlockSpec(gain.shape, lambda g: (0,)), pair, pair, lone,
        ]
        + [ANY] * len(earlier),
        out_specs=[one, one],
        input_output_aliases={7 + i: i for i in range(len(earlier))},
        cost_estimate=SMALL,
        compiler_params=pltpu.CompilerParams(vmem_limit_bytes=32 * MIB),
        name="after",
    )(ids.reshape(seqs, 1, part), *hbm(x, cot), gain, *hbm(keep, near, far), *earlier)


def attention_kernel(
    heads, block, last, start,
    at_ref, ids_ref, qg_ref, kg_ref, wqkv_hbm, wo_hbm, *refs,
):
    pays, refs = refs[0], refs[1:]
    if last:
        (acc_sums_ref, fnp_ref, gain_ref, accq_hbm, acco_hbm, hid_hbm, gup_hbm, wff_hbm, wup_hbm), refs = refs[:9], refs[9:]
        (keep_hbm, leave_hbm, sendq_ref, sendo_ref, keepo_ref, sums_ref), refs = refs[:6], refs[6:]
        (hid_ref, gup_ref, wff_ref, wup_ref, res_ref, res_sem, act_sem), refs = refs[:7], refs[7:]
    else:
        (o_hbm, grad_hbm, sums_ref, newq_hbm, newo_hbm), refs = refs[:5], refs[5:]
    (
        wqkv_ref, wo_ref, norm_ref, gb_ref, o_ref, grad_ref, gq_ref, go_ref, raw_ref,
        qt_ref, qn_ref, kt_ref, ka_ref, vt_ref, va_ref, do_ref, dq_ref, dk_ref, dv_ref, pad_ref, vm_ref,
        w_sem, sem, out_sem,
    ) = refs
    seqs, length, dim = norm_ref.shape
    part = length // SLOTS
    width = heads * HD
    blocks = length // block
    loads = [pltpu.make_async_copy(wqkv_hbm, wqkv_ref, w_sem.at[0]), pltpu.make_async_copy(wo_hbm, wo_ref, w_sem.at[1])]
    loads[0].start()

    def pay_copy(s, j, t):
        to = (norm_ref, gb_ref)[j].at[s, pl.ds(t * part, part), :]
        return pltpu.make_async_copy(pays.at[t, s, j], to, sem.at[s, j * SLOTS + t])

    for s in range(seqs):
        for j in range(2):
            for t in range(SLOTS):
                pay_copy(s, j, t).start()
            if s + j == 0:
                loads[1].start()
    if last:
        loads.append(pltpu.make_async_copy(accq_hbm, gq_ref, w_sem.at[2]))
        loads.append(pltpu.make_async_copy(acco_hbm, go_ref, w_sem.at[3]))
        loads.append(pltpu.make_async_copy(wff_hbm, wff_ref, act_sem.at[2 * seqs]))
        loads.append(pltpu.make_async_copy(wup_hbm, wup_ref, act_sem.at[2 * seqs + 1]))
        for copy in loads[2:]:
            copy.start()
        skip = hid_hbm.shape[0] // length - seqs

        def act_copies(s):
            rows = pl.ds(pl.multiple_of((skip + s) * length, length), length)
            return [
                pltpu.make_async_copy(hid_hbm.at[rows, :], hid_ref.at[s], act_sem.at[2 * s]),
                pltpu.make_async_copy(gup_hbm.at[rows, :], gup_ref.at[s], act_sem.at[2 * s + 1]),
            ]

        for s in range(seqs):
            for copy in act_copies(s):
                copy.start()
        outs = Outputs(at_ref[1], keep_hbm, leave_hbm, res_ref, res_sem, wo_ref, wff_ref, wqkv_ref, wup_ref)
        sums_ref[...] = acc_sums_ref[...]
    else:
        gq_ref[...] = jnp.zeros_like(gq_ref)
        go_ref[...] = jnp.zeros_like(go_ref)
        sums_ref[...] = jnp.zeros_like(sums_ref)
    gain_q = column(as_row(qg_ref))
    gain_k = column(as_row(kg_ref))
    marks = lax.broadcasted_iota(jnp.int32, (HD, length), 0)
    v_tail = jnp.where(lax.broadcasted_iota(jnp.int32, (length, HD), 1) < 2, 1.0, 0.0).astype(BF)
    ones = jnp.where(lax.broadcasted_iota(jnp.int32, (16, length), 0) == 0, 1.0, 0.0).astype(BF)
    spot = lax.broadcasted_iota(jnp.int32, (HD, block), 0)
    scale = 1.0 / math.sqrt(HD)
    cut = lambda a, i: a[:, i * block : (i + 1) * block]

    def unit_of(row):
        raw = raw_ref[pl.ds(pl.multiple_of(row, HD), HD), :]
        center = raw - jnp.mean(raw, axis=0, keepdims=True)
        inverse = lax.rsqrt(jnp.mean(center * center, axis=0, keepdims=True) + EPS)
        return center * inverse, inverse

    def lanes(a):
        total = a[:, :128]
        for i in range(1, length // 128):
            total = total + a[:, i * 128 : (i + 1) * 128]
        return total

    def stores(s):
        return [
            pltpu.make_async_copy(o_ref.at[s], o_hbm.at[s], out_sem.at[s, 0]),
            pltpu.make_async_copy(grad_ref.at[s], grad_hbm.at[s], out_sem.at[s, 1]),
        ]

    loads[0].wait()
    loads[1].wait()

    def sequence(s, carry):
        ids = ids_ref[start + s]
        same = marks == ids + 1
        k_tail = jnp.where(same, 1.0, 0.0).T.astype(BF)
        q_tail = jnp.where((same & (ids >= 0)) | (marks > 4), 0.0, -BIG).astype(BF)
        pad = jnp.where(ids < 0, 1.0, 0.0)
        for i in range(blocks):
            pad_ref[i] = cut(pad, i)
        for t in range(SLOTS):
            pay_copy(s, 0, t).wait()
        raw_ref[...] = mm(wqkv_ref[...], norm_ref[s], NT)
        for t in range(SLOTS):
            pay_copy(s, 1, t).wait()
        do_all = mm(wo_ref[...], gb_ref[s], NT).astype(BF)
        for h in range(heads):
            for i in range(blocks):
                do_ref[h * blocks + i] = cut(do_all[h * HD : (h + 1) * HD], i)

        def prepare(h, carry):
            q_unit, _ = unit_of(h * HD)
            q = q_unit * gain_q
            qn = q.T.astype(BF)
            for i in range(blocks):
                qt_ref[h * blocks + i, :HD] = cut(q, i).astype(BF)
                qt_ref[h * blocks + i, HD:] = cut(q_tail, i)
                qn_ref[h * blocks + i] = qn[i * block : (i + 1) * block]
            k_unit, _ = unit_of(width + h * HD)
            k = k_unit * gain_k
            kt_ref[h] = k.astype(BF)
            ka_ref[h, :, :HD] = k.T.astype(BF)
            ka_ref[h, :, HD:] = k_tail
            v = raw_ref[pl.ds(pl.multiple_of(2 * width + h * HD, HD), HD), :]
            vb = v.astype(BF)
            vt_ref[h, :HD] = vb
            vt_ref[h, HD:] = ones
            va_ref[h, :, :HD] = v.T.astype(BF)
            va_ref[h, :, HD:] = v_tail
            vm_ref[h] = jnp.mean(vb.astype(F32), axis=1, keepdims=True)
            dk_ref[h] = jnp.zeros(dk_ref.shape[1:], F32)
            dv_ref[h] = jnp.zeros(dv_ref.shape[1:], F32)
            return carry

        lax.fori_loop(0, heads, prepare, 0, unroll=True)

        def step(n, carry):
            h = n // blocks
            padb = pad_ref[n % blocks]
            e = jnp.exp2(mm(ka_ref[h], qt_ref[n]) * (LOG2E * scale))
            eb = e.astype(BF)
            oa = mm(vt_ref[h], eb)
            inv = 1.0 / (oa[HD : HD + 1] + padb)
            o = oa[:HD] * inv
            dos = (do_ref[n].astype(F32) * inv).astype(BF)
            delta = jnp.sum(dos.astype(F32) * o, axis=0, keepdims=True)
            d0 = delta.astype(BF).astype(F32)
            tail = jnp.where(spot == 0, -d0, jnp.where(spot == 1, d0 - delta, 0.0))
            doa = jnp.concatenate([dos.astype(F32), tail], axis=0)
            ds = (e * mm(va_ref[h], doa.astype(BF))).astype(BF)
            dq_ref[n] = mm(kt_ref[h], ds)
            dk_ref[h] += mm(ds, qn_ref[n])
            dv_ref[h] += mm(dos, eb, NT)
            do_ref[n] = jnp.where(padb > 0, vm_ref[h], o).astype(BF)
            return carry

        lax.fori_loop(0, heads * blocks, step, 0, unroll=True)

        def finish(h, carry):
            rows = lambda at: pl.ds(pl.multiple_of(at + h * HD, HD), HD)
            gq = jnp.concatenate([dq_ref[h * blocks + i] for i in range(blocks)], axis=1)
            gk = dk_ref[h].T
            for k, (g, gain_col) in enumerate(((gq, gain_q), (gk, gain_k))):
                unit, inverse = unit_of(k * width + h * HD)
                g = (g * scale).astype(BF).astype(F32)
                sums_ref[k] += lanes(g * unit)
                g = g * gain_col
                back = inverse * (
                    g - jnp.mean(g, axis=0, keepdims=True) - unit * jnp.mean(g * unit, axis=0, keepdims=True)
                )
                grad_ref[s, rows(k * width), :] = back.astype(BF)
            grad_ref[s, rows(2 * width), :] = dv_ref[h].astype(BF)
            for i in range(blocks):
                o_ref[s, rows(0), pl.ds(i * block, block)] = do_ref[h * blocks + i]
            return carry

        lax.fori_loop(0, heads, finish, 0, unroll=True)
        if last:

            @pl.when(s == 0)
            def _():
                for copy in loads[2:]:
                    copy.wait()

            for copy in act_copies(s):
                copy.wait()
            outs.compute(s, o_ref.at[s], hid_ref.at[s], grad_ref.at[s], gup_ref.at[s])
        else:
            for copy in stores(s):
                copy.start()
        gq_ref[...] += mm(grad_ref[s], norm_ref[s])
        go_ref[...] += mm(o_ref[s], gb_ref[s])
        return carry

    lax.fori_loop(0, seqs, sequence, 0)
    if not last:
        ends = [pltpu.make_async_copy(gq_ref, newq_hbm, w_sem.at[2]), pltpu.make_async_copy(go_ref, newo_hbm, w_sem.at[3])]
        for copy in ends:
            copy.start()
        for copy in ends:
            copy.wait()
        for s in range(seqs):
            for copy in stores(s):
                copy.wait()
        return
    outs.wait()
    g_q = gq_ref[...]
    first_row = (jnp.sum(wqkv_ref[...].astype(F32) * g_q, axis=0, keepdims=True) + fnp_ref[...]) / as_row(gain_ref)
    second_row = jnp.concatenate([jnp.sum(sums_ref[k].T, axis=0, keepdims=True) for k in range(2)], axis=1)
    wide = 3 * width
    line = jnp.concatenate([first_row[:, wide:], second_row, jnp.zeros((1, 2 * wide - dim - 2 * HD), F32)], axis=1)
    small = jnp.concatenate([first_row[:, :wide], line], axis=0)
    high = small.astype(BF)
    small = jnp.concatenate([high.astype(F32), small - high.astype(F32)], axis=0).astype(BF)
    g_q = g_q.T.astype(BF)
    count, rows, _ = sendq_ref.shape
    rows = rows - 4
    for i in range(count):
        sendq_ref[i, :rows] = g_q[i * rows : (i + 1) * rows]
        sendq_ref[i, rows:] = small
    split_rows((at_ref[2] & 1) > 0, go_ref[...], sendo_ref, keepo_ref)


def attention(at, start, ids, wqkv, wo, qg, kg, pays, count, more=()):
    wide, dim = wqkv.shape
    width = wo.shape[0]
    heads = width // HD
    _, seqs, _, part, _ = pays.shape
    length = part * SLOTS
    block = 1024
    blocks = length // block
    last = bool(more)
    ins = [at, ids, qg, kg, wqkv, wo, *hbm(pays), *more[:3], *hbm(*more[3:])]
    specs = [SMEM] + [VMEM] * 3 + [ANY] * 2 + [HBM] + ([VMEM] * 3 + [HBM] * 6 if last else [])
    scratch = []
    if last:
        outs = [jax.ShapeDtypeStruct((SLOTS // 2, seqs, 2, part, dim), BF)] * 2
        outs += [jax.ShapeDtypeStruct((count, dim // count + 4, wide), BF)]
        outs += [jax.ShapeDtypeStruct((count // (2 * SLOTS), SLOTS * width // count, dim), t) for t in (BF, F32)]
        scratch = [pltpu.VMEM((2, HD, 128), F32)]
        scratch += [pltpu.VMEM((seqs, length, dim), BF)] * 2 + [pltpu.VMEM((dim, dim), BF)] * 2
        scratch += Outputs.scratch(seqs, length, dim) + [pltpu.SemaphoreType.DMA((2 * seqs + 2,))]
    else:
        outs = [jax.ShapeDtypeStruct((seqs, width, length), BF), jax.ShapeDtypeStruct((seqs, wide, length), BF)]
        outs += [
            jax.ShapeDtypeStruct((2, HD, 128), F32),
            jax.ShapeDtypeStruct((wide, dim), F32),
            jax.ShapeDtypeStruct((width, dim), F32),
        ]
    flops = seqs * (2 * length * dim * width * 8 + heads * 6 * 2 * length * length * HD)
    return pl.pallas_call(
        functools.partial(attention_kernel, heads, block, last, start),
        out_shape=outs,
        in_specs=specs,
        out_specs=[HBM] * 2 + ([VMEM] * 3 if last else [VMEM, HBM, HBM]),
        scratch_shapes=scratch
        + [
            pltpu.VMEM((wide, dim), BF),
            pltpu.VMEM((width, dim), BF),
            pltpu.VMEM((seqs, length, dim), BF),
            pltpu.VMEM((seqs, length, dim), BF),
            pltpu.VMEM((seqs, width, length), BF),
            pltpu.VMEM((seqs, wide, length), BF),
            pltpu.VMEM((wide, dim), F32),
            pltpu.VMEM((width, dim), F32),
            pltpu.VMEM((wide, length), F32),
            pltpu.VMEM((heads * blocks, 2 * HD, block), BF),
            pltpu.VMEM((heads * blocks, block, HD), BF),
            pltpu.VMEM((heads, HD, length), BF),
            pltpu.VMEM((heads, length, 2 * HD), BF),
            pltpu.VMEM((heads, HD + 16, length), BF),
            pltpu.VMEM((heads, length, 2 * HD), BF),
            pltpu.VMEM((heads * blocks, HD, block), BF),
            pltpu.VMEM((heads * blocks, HD, block), F32),
            pltpu.VMEM((heads, length, HD), F32),
            pltpu.VMEM((heads, HD, length), F32),
            pltpu.VMEM((blocks, 1, block), F32),
            pltpu.VMEM((heads, HD, 1), F32),
            pltpu.SemaphoreType.DMA((4,)),
            pltpu.SemaphoreType.DMA((seqs, 2 * SLOTS)),
            pltpu.SemaphoreType.DMA((seqs, 2)),
        ],
        cost_estimate=LARGE,
        compiler_params=pltpu.CompilerParams(vmem_limit_bytes=40 * MIB),
        name="attention",
    )(*ins)


def ffn_kernel(block, groups, plan, at_ref, wup_hbm, wqkv_hbm, wo_hbm, o_hbm, gq_hbm, *refs):
    pieces, refs = refs[: len(plan)], refs[len(plan) :]
    pays, refs = refs[: len(groups)], refs[len(groups) :]
    (hid_hbm, gup_hbm, wff_hbm, keep_hbm, leave_hbm, send_ref, np_ref), refs = refs[:7], refs[7:]
    norm_ref, gb_ref, hid_ref, gup_ref, wup_ref, wff_ref, gin_ref, gff_ref, sem, out_sem, w_sem, *refs = refs
    wqkv_ref, wo_ref, o_ref, gq_ref, res_ref, res_sem, late_sem = refs
    dim = wup_ref.shape[0]
    part = pays[0].shape[3]
    total = norm_ref.shape[0]
    weights = [pltpu.make_async_copy(wup_hbm, wup_ref, w_sem.at[0])]
    rows = send_ref.shape[2]
    for ref, masks in zip(pieces, plan):
        for i, mask in enumerate(masks):
            to = wff_ref.at[pl.ds(pl.multiple_of((at_ref[2] ^ mask) * rows, rows), rows), :]
            weights.append(pltpu.make_async_copy(ref.at[i], to, w_sem.at[len(weights)]))
    for copy in weights:
        copy.start()
    n = 0
    for g, seqs in enumerate(groups):
        for s in range(seqs):
            for t in range(SLOTS):
                for k, to in enumerate((norm_ref, gb_ref)):
                    source = pays[g].at[t, s, k]
                    pltpu.make_async_copy(source, to.at[pl.ds(n * part, part), :], sem.at[k, n]).start()
                n += 1
    late = [
        pltpu.make_async_copy(a, b, late_sem.at[i])
        for i, (a, b) in enumerate(((wqkv_hbm, wqkv_ref), (wo_hbm, wo_ref), (o_hbm, o_ref), (gq_hbm, gq_ref)))
    ]
    for copy in late:
        copy.start()
    gin_ref[...] = jnp.zeros_like(gin_ref)
    gff_ref[...] = jnp.zeros_like(gff_ref)
    for copy in weights:
        copy.wait()
    joined = pltpu.make_async_copy(wff_ref, wff_hbm, w_sem.at[0])
    joined.start()
    c0 = math.sqrt(2.0 / math.pi)
    c1 = 0.044715

    def outs(i):
        at_rows = pl.ds(pl.multiple_of(i * block, block), block)
        return (
            pltpu.make_async_copy(hid_ref.at[at_rows, :], hid_hbm.at[at_rows, :], out_sem.at[0, i]),
            pltpu.make_async_copy(gup_ref.at[at_rows, :], gup_hbm.at[at_rows, :], out_sem.at[1, i]),
        )

    def arrive(i):
        for j in range(block // part):
            for k, to in enumerate((norm_ref, gb_ref)):
                pltpu.make_async_copy(pays[0].at[0, 0, 0], to.at[pl.ds(0, part), :], sem.at[k, i * (block // part) + j]).wait()

    def rows_of(i):
        return pl.ds(pl.multiple_of(i * block, block), block)

    def units(i):
        up = mm(norm_ref[rows_of(i), :], wup_ref[...])
        gh = mm(gb_ref[rows_of(i), :], wff_ref[...], NT)
        sq = up * up
        t = jnp.tanh(up * (c0 + (c0 * c1) * sq))
        half = 0.5 + 0.5 * t
        hid_ref[rows_of(i), :] = (up * half).astype(BF)
        gup_ref[rows_of(i), :] = (gh * (half + (0.5 * up) * (1.0 - t * t) * (c0 + (3.0 * c0 * c1) * sq))).astype(BF)

    def grads(i):
        gin_ref[...] += mm(norm_ref[rows_of(i), :], gup_ref[rows_of(i), :], TN)
        gff_ref[...] += mm(hid_ref[rows_of(i), :], gb_ref[rows_of(i), :], TN)

    count = total // block
    arrive(0)
    units(0)

    def step(i, carry):
        for copy in outs(i - 1):
            copy.start()
        arrive(i)
        grads(i - 1)
        units(i)
        return carry

    lax.fori_loop(1, count, step, 0)
    for copy in outs(count - 1):
        copy.start()
    grads(count - 1)
    for copy in late:
        copy.wait()
    results = Outputs(at_ref[1], keep_hbm, leave_hbm, res_ref, res_sem, wo_ref, wff_ref, wqkv_ref, wup_ref)
    length = SLOTS * part

    def result(s, carry):
        rows_s = pl.ds(pl.multiple_of(s * length, length), length)
        results.compute(s, o_ref.at[s], hid_ref.at[rows_s, :], gq_ref.at[s], gup_ref.at[rows_s, :])
        return carry

    lax.fori_loop(0, results.seqs, result, 0)
    line = jnp.sum(wup_ref[...].astype(F32) * gin_ref[...], axis=1, keepdims=True)
    np_ref[...] = jnp.broadcast_to(line, (dim, 128)).T[0:1]
    for b in range(dim // rows):
        for k, g in enumerate((gin_ref, gff_ref)):
            send_ref[b, k] = g[b * rows : (b + 1) * rows, :].astype(BF)
    joined.wait()
    results.wait()

    def drain(i, carry):
        for copy in outs(i):
            copy.wait()
        return carry

    lax.fori_loop(0, total // block, drain, 0)


def ffn(at, wup, ff_parts, groups, count, wqkv, wo, o, gq, block=512):
    dim, units = wup.shape
    sizes = [g.shape[1] for g in groups]
    part = groups[0].shape[3]
    total = SLOTS * part * sum(sizes)
    pieces = groups
    act = jax.ShapeDtypeStruct((total, units), BF)
    return pl.pallas_call(
        functools.partial(ffn_kernel, block, sizes, [masks for _, masks in ff_parts]),
        out_shape=[
            act,
            act,
            jax.ShapeDtypeStruct((units, dim), BF),
            *[jax.ShapeDtypeStruct((SLOTS // 2, o.shape[0], 2, part, dim), BF)] * 2,
            jax.ShapeDtypeStruct((count, 2, units // count, dim), BF),
            jax.ShapeDtypeStruct((1, dim), F32),
        ],
        in_specs=[SMEM] + [ANY] * 3 + [HBM] * (2 + len(ff_parts) + len(pieces)),
        out_specs=[HBM] * 5 + [VMEM] * 2,
        scratch_shapes=[
            pltpu.VMEM((total, dim), BF),
            pltpu.VMEM((total, dim), BF),
            pltpu.VMEM((total, units), BF),
            pltpu.VMEM((total, units), BF),
            pltpu.VMEM((dim, units), BF),
            pltpu.VMEM((units, dim), BF),
            pltpu.VMEM((dim, units), F32),
            pltpu.VMEM((units, dim), F32),
            pltpu.SemaphoreType.DMA((2, total // part)),
            pltpu.SemaphoreType.DMA((2, total // block)),
            pltpu.SemaphoreType.DMA((1 + count,)),
            *[pltpu.VMEM(a.shape, BF) for a in (wqkv, wo, o, gq)],
            *Outputs.scratch(o.shape[0], SLOTS * part, dim),
            pltpu.SemaphoreType.DMA((4,)),
        ],
        cost_estimate=LARGE,
        compiler_params=pltpu.CompilerParams(vmem_limit_bytes=58 * MIB),
        name="ffn",
    )(at, wup, wqkv, wo, *hbm(o, gq, *[a for a, _ in ff_parts], *pieces))


class Outputs:
    def __init__(self, me, keep, send, res, sem, wo, wff, wqkv, wup):
        self.me = me
        self.keep, self.send, self.res, self.sem = keep, send, res, sem
        self.wo, self.wff, self.wqkv, self.wup = wo, wff, wqkv, wup
        self.seqs, _, self.length, _ = res.shape

    @staticmethod
    def scratch(seqs, length, dim):
        return [pltpu.VMEM((seqs, 2, length, dim), BF), pltpu.SemaphoreType.DMA((seqs, 2, SLOTS))]

    def moves(self, s, i):
        half = self.length // 2
        part = half // 2
        out = []
        for j in range(2):
            for k, to in enumerate((self.keep, self.send)):
                rows = pl.ds(pl.multiple_of(i * half + (k ^ (self.me & 1)) * part, part), part)
                source = self.res.at[s, j, rows, :]
                out.append(pltpu.make_async_copy(source, to.at[i ^ (self.me >> 1), s, j], self.sem.at[s, j, 2 * i + k]))
        return out

    def compute(self, s, o, hid, gq, gu):
        half = self.length // 2

        def step(i, carry):
            rows = pl.ds(pl.multiple_of(i * half, half), half)
            branch = mm(o[:, rows], self.wo[...], TN) + mm(hid[rows, :], self.wff[...])
            self.res[s, 0, rows, :] = branch.astype(BF)
            gn = mm(gq[:, rows], self.wqkv[...], TN) + mm(gu[rows, :], self.wup[...], NT)
            self.res[s, 1, rows, :] = gn.astype(BF)
            for copy in self.moves(s, i):
                copy.start()
            return carry

        lax.fori_loop(0, 2, step, 0)

    def wait(self):
        for s in range(self.seqs):
            for i in range(2):
                for copy in self.moves(s, i):
                    copy.wait()


def swap(value, axis, count, mask):
    return lax.ppermute(value, axis, [(i, i ^ mask) for i in range(count)])


def tie(value, *after):
    return lax.optimization_barrier((value,) + after)[0]


def bit_groups(count):
    bits = list(range(count.bit_length() - 1))[::-1]
    groups = []
    while bits:
        take = 2 if len(bits) > 1 else 1
        groups.append(bits[:take])
        bits = bits[take:]
    assert len(groups[-1]) == 1
    return groups


def gather_batch(block, count, groups, hold=None):
    held, masks = block[None], [0]
    for bits in groups:
        low = bits[-1]
        if hold is not None and bits is groups[-1]:
            held = tie(held, hold)
        parts = [(held, masks)]
        for s in range(1, 1 << len(bits)):
            parts.append((swap(held, "batch", count, s << low), [m ^ (s << low) for m in masks]))
        held = jnp.concatenate([a for a, _ in parts], axis=0)
        masks = sum((m for _, m in parts), [])
    return parts


def matchings(edges, devices, per_device):
    left = [[] for _ in range(devices)]
    for e, (source, _, _) in enumerate(edges):
        left[source].append(e)
    rounds = []
    for _ in range(per_device):
        owner = [-1] * devices

        def place(source, seen):
            for e in left[source]:
                target = edges[e][1]
                if target in seen:
                    continue
                seen.add(target)
                if owner[target] < 0 or place(edges[owner[target]][0], seen):
                    owner[target] = e
                    return True
            return False

        for source in range(devices):
            place(source, set())
        rounds.append(list(owner))
        for e in owner:
            left[edges[e][0]].remove(e)
    return rounds


def unit_plan(nb, nt, rows, width, hidden):
    unit = math.gcd(math.gcd(rows, width // nt), hidden // nt)
    per = rows // unit
    head_units, hid_units = width // nt // unit, hidden // nt // unit
    assert head_units == nb and hid_units % nb == 0
    c = hid_units // nb
    edges = []
    for t in range(nt):
        for b in range(nb):
            want = [t * head_units + b]
            want += [nt * head_units + t * hid_units + b * c + i for i in range(c)]
            for slot, u in enumerate(want):
                edges.append((u // per, b * nt + t, (u % per, slot)))
    table = np.zeros((nb * nt, 2 * per), np.int32)
    perms = []
    for k, owner in enumerate(matchings(edges, nb * nt, per)):
        perms.append([(edges[e][0], edges[e][1]) for e in owner])
        for e in owner:
            table[edges[e][0], k] = edges[e][2][0]
            table[edges[e][1], per + k] = edges[e][2][1]
    return unit, per, perms, table


def per_device(
    nb, nt, patches, image_ids, cotangent, norm_gain, query_gain, key_gain, in_weight, out_weight
):
    seqs, part, dim = patches.shape
    width = H * HD
    local = width // nt
    units = (in_weight.shape[1] - 3 * width) // nt
    rows_in = in_weight.shape[0]
    unit, per, perms, table = unit_plan(nb, nt, out_weight.shape[0], width, units * nt)
    assert nt == SLOTS and units == dim and unit == rows_in and dim == nt * local and per == nt + 1
    both = ("batch", "tok")
    me_b = lax.axis_index("batch")
    me_t = lax.axis_index("tok")
    at = jnp.stack([me_b * nt + me_t, me_t, me_b])
    table = jnp.asarray(table)
    gain = norm_gain

    def exchange(value, axis):
        return lax.all_to_all(value, axis, split_axis=0, concat_axis=0, tiled=True)

    groups = bit_groups(nb)

    lead = 2
    a_src, u_src = prepare(image_ids, in_weight, nb, nt)
    a_got = exchange(a_src.reshape(nb * nt, rows_in + 2, 3 * local), both)
    own0, own1, *unit_sends = before(
        at, table, out_weight.reshape(per, unit, dim), image_ids, gain, tie(patches, a_src), cotangent, lead
    )
    got = [lax.ppermute(v, both, perm) for v, perm in zip(unit_sends, perms)]
    wo_src, ff_src = pack_out(at, table, got)
    slots0 = lax.all_gather(own0, "tok", axis=0)
    slots1 = lax.all_gather(own1, "tok", axis=0)
    wo_parts = gather_batch(wo_src, nb, groups, a_got)
    ff_parts = gather_batch(ff_src.reshape((per - 1) * unit, dim), nb, groups[::-1])
    wqkv, wo, ids = join(at, a_got, wo_parts, seqs, part)
    wo = wo.reshape(local, dim)
    wup = exchange(tie(u_src, a_got).reshape(nb * nt, unit, dim), both).reshape(dim, units)

    qg, kg = query_gain, key_gain

    def leave_chip(keep, near, *hold):
        value = (keep[1].astype(F32) + near[1].astype(F32)).astype(BF)
        return value, swap(tie(value, *hold) if hold else value, "tok", nt, 2)

    o0, gq0, sums, acc_q, acc_o = attention(at, 0, ids, wqkv, tie(wo, ff_parts[0][0]), qg, kg, slots0, nb * nt)
    hid, gup, wff, keep0, send0, f_grad, f_np = ffn(
        at, tie(wup, o0), ff_parts, [slots0, slots1], nb, wqkv, wo, o0, gq0
    )
    f_mine = lax.psum_scatter(f_grad, "batch", scatter_dimension=0, tiled=True).reshape(2, nt, unit, dim)
    near0 = swap(send0, "tok", nt, 1)
    value0, away0 = leave_chip(keep0, near0)
    keep1, send1, a_q, a_send, a_keep = attention(
        at, lead, ids, wqkv, tie(wo, value0), qg, kg, slots1, nb * nt,
        (sums, f_np, gain, acc_q, acc_o, hid, gup, wff, wup),
    )
    a_came = swap(a_send, "batch", nb, 1)
    terms = [a_keep, a_came]
    for bits in groups[:-1][::-1]:
        own, *sends = fold(at, bits[-1], [terms])
        terms = [own] + [swap(value, "batch", nb, (s + 1) << bits[-1]) for s, value in enumerate(sends)]
    near1 = swap(tie(send1, away0, *terms[1:]), "tok", nt, 1)
    a_q = exchange(a_q, both)
    value1, away1 = leave_chip(keep1, near1)
    earlier = after(0, image_ids, patches, cotangent, gain, keep0, near0, away0, [])
    outs = leave(at, table, terms, tie(f_mine, *earlier))
    sends, up = outs[:per], outs[per:]
    up = [up[0]] + [swap(up[s], "tok", nt, s) for s in range(1, nt)]
    got = [lax.ppermute(v, both, [(b, a) for a, b in perm]) for v, perm in zip(sends, perms)]
    earlier = after(lead, image_ids, patches, cotangent, gain, keep1, near1, away1, earlier)
    in_grad, out_grad, norm_grad, query_grad, key_grad = place(at, table, tie(a_q, *earlier), up, got)

    block_out, patch_grad = earlier
    return (
        block_out,
        patch_grad,
        norm_grad,
        query_grad,
        key_grad,
        in_grad,
        out_grad.reshape(per * unit, dim),
    )


def solution(mesh):
    rows = P("batch", "tok", None)
    weights = P(("batch", "tok"), None)
    return jax.shard_map(
        functools.partial(per_device, mesh.shape["batch"], mesh.shape["tok"]),
        mesh=mesh,
        in_specs=(rows, P("batch", "tok"), rows, P(), P(), P(), weights, weights),
        out_specs=(rows, rows, P(), P(), P(), weights, weights),
        check_vma=False,
    )
```
